32 devices in a mesh: dp: 8 (over z, y), seq: 4 (over x, core).
Axes of the slice: x: 2, y: 2, z: 4, core: 2. Of those that a mesh axis runs over, the one named last changes fastest.
Arguments:
- patches: bfloat16 [24, 896, 768], P('dp', 'seq'), may hold values from -6 to 6
- cotangent: bfloat16 [24, 896, 768], P('dp', 'seq'), may hold values from -6 to 6
- time_ids: int32 [24, 896], P('dp', 'seq'), may hold values from 0 to 100
- freq_ids: int32 [24, 896], P('dp', 'seq'), may hold values from 0 to 11
- lengths: int32 [24], P('dp'), may hold values from 300 to 700, as said below
- qkv_weight: bfloat16 [768, 2304], replicated, may hold values from -0.21875 to 0.21875
- query_bias: float32 [768], replicated, may hold values from -3 to 3
- value_bias: float32 [768], replicated, may hold values from -3 to 3
- out_weight: bfloat16 [768, 768], replicated, may hold values from -0.875 to 0.875
- out_bias: float32 [768], replicated, may hold values from -3 to 3
- norm1_gain: float32 [768], replicated, may hold values from 0.25 to 1.75
- norm1_shift: float32 [768], replicated, may hold values from -3 to 3
- norm2_gain: float32 [768], replicated, may hold values from 0.25 to 1.75
- norm2_shift: float32 [768], replicated, may hold values from -3 to 3
- up_weight: bfloat16 [768, 3072], replicated, may hold values from -0.21875 to 0.21875
- up_bias: float32 [3072], replicated, may hold values from -3 to 3
- down_weight: bfloat16 [3072, 768], replicated, may hold values from -0.109375 to 0.109375
- down_bias: float32 [768], replicated, may hold values from -3 to 3
- time_table: float32 [101, 768], replicated, may hold values from -3 to 3
- freq_table: float32 [12, 768], replicated, may hold values from -3 to 3
Outputs:
- output: bfloat16 [24, 896, 768], P('dp', 'seq')
- d_patches: bfloat16 [24, 896, 768], P('dp', 'seq')
- grad_qkv_weight: float32 [768, 2304], P('dp')
- grad_query_bias: float32 [768], P('dp')
- grad_value_bias: float32 [768], P('dp')
- grad_out_weight: float32 [768, 768], P('dp')
- grad_out_bias: float32 [768], P('dp')
- grad_norm1_gain: float32 [768], P('dp')
- grad_norm1_shift: float32 [768], P('dp')
- grad_norm2_gain: float32 [768], P('dp')
- grad_norm2_shift: float32 [768], P('dp')
- grad_up_weight: float32 [768, 3072], P('dp')
- grad_up_bias: float32 [3072], P('dp')
- grad_down_weight: float32 [3072, 768], P('dp')
- grad_down_bias: float32 [768], P('dp')
- grad_time_table: float32 [101, 768], P(None, 'dp')
- grad_freq_table: float32 [12, 768], P(None, 'dp')
The draws below stay inside these ranges and needn't reach their ends.
Inputs may be any that keep to these rules, and one draw needn't show every extreme that they name: `lengths`: at least one clip keeps exactly 700 patches.
All inputs are finite; a program needn't handle non-finite values.
Results may differ from the reference program's by a relative error of at most 0.015.
Values may be sent and summed in bfloat16 or wider, within the bound.
A program may use at most 192 MiB of HBM per device.

```python
import math
import jax
import jax.numpy as jnp
from jax import lax

D = 768
HEADS = 12
FF = 3072
TGRID = 101
FGRID = 12
CLIP = 896
KEEP_MIN = 300
KEEP_MAX = 700
CLIPS = 24


def draw_lengths(key, part):
    first, second = jax.random.split(jax.random.fold_in(key, 17))
    counts = jax.random.randint(first, (CLIPS,), KEEP_MIN, KEEP_MAX + 1)
    chosen = jax.random.randint(second, (), 0, CLIPS)
    return jnp.where(jnp.arange(CLIPS) == chosen, KEEP_MAX, counts).astype(jnp.int32)


def place_ends(values, key, least, high):
    shape = values.shape
    spot = [jax.random.randint(jax.random.fold_in(key, axis), (), 0, shape[axis]) for axis in range(len(shape))]
    values = values.at[tuple(spot)].set(least)
    longest = shape.index(max(shape))
    spot[longest] = (spot[longest] + 1) % shape[longest]
    return values.at[tuple(spot)].set(high)


def level_of(rng, extent, cuts, smallest, largest):
    level, own = 1.0, jax.random.fold_in(rng, 6)
    for position, parts in cuts:
        steps = jnp.exp(jax.random.uniform(jax.random.fold_in(own, position), (parts,), jnp.float32, smallest / len(cuts), largest / len(cuts)))
        level = level * jnp.repeat(steps, extent[position] // parts).reshape([-1 if axis == position else 1 for axis in range(len(extent))])
    return level


def bell_draw(own_key, dims, width, bound, cuts=(), kind=jnp.bfloat16):
    drawn = width * jax.random.normal(own_key, dims, jnp.float32)
    if cuts:
        drawn = drawn * level_of(own_key, dims, cuts, -0.22, 0.18)
    return jnp.clip(drawn, -bound, bound).astype(kind)


def setup_inputs(seed: int = 0) -> dict:
    key_of = jax.random.split(jax.random.key(seed), 21)
    return {
        "patches": bell_draw(key_of[0], (CLIPS, CLIP, D), 1.0, 6.0, ((0, 8), (1, 4))),
        "cotangent": bell_draw(key_of[1], (CLIPS, CLIP, D), 1.0, 6.0, ((0, 8), (1, 4))),
        "time_ids": place_ends(jax.random.randint(key_of[2], (CLIPS, CLIP), 0, TGRID), jax.random.fold_in(key_of[2], 1), 0, TGRID - 1).astype(jnp.int32),
        "freq_ids": place_ends(jax.random.randint(key_of[3], (CLIPS, CLIP), 0, FGRID), jax.random.fold_in(key_of[3], 1), 0, FGRID - 1).astype(jnp.int32),
        "lengths": draw_lengths(jax.random.fold_in(key_of[20], 71), 0),
        "qkv_weight": bell_draw(key_of[5], (D, 3 * D), D ** -0.5, 0.21875),
        "query_bias": bell_draw(key_of[6], (D,), 0.3, 3.0, (), jnp.float32),
        "value_bias": bell_draw(key_of[7], (D,), 0.5, 3.0, (), jnp.float32),
        "out_weight": bell_draw(key_of[8], (D, D), (D // 16) ** -0.5, 0.875),
        "out_bias": bell_draw(key_of[9], (D,), 0.5, 3.0, (), jnp.float32),
        "norm1_gain": jnp.clip(1.0 + 0.15 * jax.random.normal(key_of[10], (D,), jnp.float32), 0.25, 1.75),
        "norm1_shift": bell_draw(key_of[11], (D,), 0.3, 3.0, (), jnp.float32),
        "norm2_gain": jnp.clip(1.0 + 0.15 * jax.random.normal(key_of[12], (D,), jnp.float32), 0.25, 1.75),
        "norm2_shift": bell_draw(key_of[13], (D,), 0.3, 3.0, (), jnp.float32),
        "up_weight": bell_draw(key_of[14], (D, FF), D ** -0.5, 0.21875),
        "up_bias": bell_draw(key_of[15], (FF,), 0.5, 3.0, (), jnp.float32),
        "down_weight": bell_draw(key_of[16], (FF, D), FF ** -0.5, 0.109375),
        "down_bias": bell_draw(key_of[17], (D,), 0.5, 3.0, (), jnp.float32),
        "time_table": bell_draw(key_of[18], (TGRID, D), 0.5, 3.0, (), jnp.float32),
        "freq_table": bell_draw(key_of[19], (FGRID, D), 0.5, 3.0, (), jnp.float32),
    }


EPS = 1e-06
NEGATIVE = -1000000000.0

@jax.custom_vjp
def low(v):
    return lax.optimization_barrier(v.astype(jnp.bfloat16)).astype(jnp.float32)

@jax.custom_vjp
def low_back(v):
    return v

def low_keep(v):
    return (low(v), None)

def low_pass(kept, grad):
    return (grad,)

def back_keep(v):
    return (v, None)

def back_low(kept, grad):
    return (low(grad),)
low.defvjp(low_keep, low_pass)
low_back.defvjp(back_keep, back_low)

def product(form, left, right):
    return jnp.einsum(form, left, right, precision=lax.Precision.HIGHEST)

def layer_norm(values, gain, shift):
    center = values - lax.optimization_barrier(jnp.mean(values, -1, keepdims=True))
    spread = lax.optimization_barrier(jnp.mean(center * center, -1, keepdims=True))
    return center * lax.rsqrt(spread + EPS) * gain + shift

def forward(weights, patch, time_ids, freq_ids, valid):
    qkv_weight, query_bias, value_bias, out_weight, out_bias, norm1_gain, norm1_shift, norm2_gain, norm2_shift, up_weight, up_bias, down_weight, down_bias, time_table, freq_table = weights
    group, slots, features = patch.shape
    head_dim = features // HEADS
    scale = 1.0 / math.sqrt(head_dim)
    start = patch + time_table[time_ids] + freq_table[freq_ids]
    normed = low(layer_norm(start, norm1_gain, norm1_shift))
    bias = jnp.concatenate([query_bias, jnp.zeros_like(query_bias), value_bias])
    qkv = low(low_back(product('gtd,de->gte', normed, qkv_weight) + bias))
    qkv = qkv.reshape(group, slots, 3, HEADS, head_dim)
    scores = product('gqhd,gkhd->ghqk', qkv[:, :, 0], qkv[:, :, 1]) * scale
    key_valid = valid[:, None, None, :] > 0.5
    scores = low_back(jnp.where(key_valid, scores, NEGATIVE))
    probs = jax.nn.softmax(scores, -1)
    mixed = product('ghqk,gkhd->gqhd', low(probs), qkv[:, :, 2])
    mixed = low(low_back(mixed.reshape(group, slots, features)))
    after_attn = start + low_back(product('gtd,de->gte', mixed, out_weight) + out_bias)
    normed_two = low(layer_norm(after_attn, norm2_gain, norm2_shift))
    hidden = low_back(product('gtd,df->gtf', normed_two, up_weight) + up_bias)
    act = low(jax.nn.gelu(hidden, approximate=False))
    after_mlp = after_attn + low_back(product('gtf,fd->gtd', act, down_weight) + down_bias)
    return valid[..., None] * after_mlp

def reference(patches, cotangent, time_ids, freq_ids, lengths, qkv_weight, query_bias, value_bias, out_weight, out_bias, norm1_gain, norm1_shift, norm2_gain, norm2_shift, up_weight, up_bias, down_weight, down_bias, time_table, freq_table):
    weights = tuple((w.astype(jnp.float32) for w in (qkv_weight, query_bias, value_bias, out_weight, out_bias, norm1_gain, norm1_shift, norm2_gain, norm2_shift, up_weight, up_bias, down_weight, down_bias, time_table, freq_table)))
    group = math.gcd(CLIPS, 4)
    turns = CLIPS // group

    def split(array):
        return array.reshape((turns, group) + array.shape[1:])
    zeros = tuple((jnp.zeros_like(w) for w in weights))

    def step(totals, item):
        patch, cot, time_part, freq_part, length_part = item
        slots = jnp.arange(CLIP, dtype=jnp.int32)
        valid = (slots[None, :] < length_part[:, None]).astype(jnp.float32)

        def run(params, values):
            return forward(params, values, time_part, freq_part, valid)
        result, pull = jax.vjp(run, weights, patch.astype(jnp.float32))
        grads, d_patch = pull(cot.astype(jnp.float32))
        totals = tuple((a + b for a, b in zip(totals, grads)))
        return (totals, (result.astype(jnp.bfloat16), d_patch.astype(jnp.bfloat16)))
    totals, (results, d_results) = lax.scan(step, zeros, (split(patches), split(cotangent), split(time_ids), split(freq_ids), split(lengths)))
    return (results.reshape(CLIPS, CLIP, D), d_results.reshape(CLIPS, CLIP, D), totals[0], totals[1], totals[2], totals[3], totals[4], totals[5], totals[6], totals[7], totals[8], totals[9], totals[10], totals[11], totals[12], totals[13], totals[14])
```

```python
import functools
import math

import jax
import jax.numpy as jnp
from jax import lax
from jax.experimental import pallas as pl
from jax.experimental.pallas import tpu as pltpu
from jax.sharding import PartitionSpec as P

HEADS = 12
KEEP_MAX = 700
EPS = 1e-06
NEGATIVE = -1000000000.0
FREQ_ROW = 104
TABLE_ROWS = 128
SMALL_ROWS = 16 + TABLE_ROWS
F32 = jnp.float32
BF16 = jnp.bfloat16
NN = (((1,), (0,)), ((), ()))
NT = (((1,), (1,)), ((), ()))
TN = (((0,), (0,)), ((), ()))
MIB = 1 << 20


def mm(left, right, dims=NN):
    return lax.dot_general(left, right, dims, preferred_element_type=F32)


def params(limit=60):
    return pltpu.CompilerParams(vmem_limit_bytes=limit * MIB)


def row_sum(values):
    return jnp.sum(values, 0, keepdims=True)


def normalize(values):
    center = values - jnp.mean(values, -1, keepdims=True)
    rstd = lax.rsqrt(jnp.mean(center * center, -1, keepdims=True) + EPS)
    return center * rstd, rstd


def norm_back(d_out, gain, xhat, rstd):
    u = d_out * gain
    inner = jnp.mean(u * xhat, -1, keepdims=True)
    return rstd * (u - jnp.mean(u, -1, keepdims=True) - xhat * inner)


def split_high_low(values):
    high = values.astype(BF16)
    return high, (values - high.astype(F32)).astype(BF16)


def one_hot(time_row, freq_row):
    spot = lax.broadcasted_iota(jnp.int32, (TABLE_ROWS, time_row.shape[1]), 0)
    hit = (spot == time_row) | (spot == freq_row + FREQ_ROW)
    return jnp.where(hit, 1.0, 0.0).astype(BF16)


def project_body(groups, patch, time_ids, freq_ids, time_table, freq_table, gain, shift, weight, bias, x_out, n_out, heads_out, table):
    features = patch.shape[2]
    width = features // groups

    @pl.when(pl.program_id(0) == 0)
    def _():
        full = jnp.zeros((TABLE_ROWS, features), F32)
        table_f32 = x_out.at[0, 0:TABLE_ROWS]
        table_f32[...] = full
        x_out[0, 0:time_table.shape[0], :] = time_table[...]
        x_out[0, FREQ_ROW:FREQ_ROW + freq_table.shape[0], :] = freq_table[...]
        high, low = split_high_low(x_out[0, 0:TABLE_ROWS, :])
        table[0:TABLE_ROWS, :] = high
        table[TABLE_ROWS:, :] = low

    hot = one_hot(time_ids[0], freq_ids[0])
    x = patch[0].astype(F32) + mm(jnp.concatenate([hot, hot], 0), table[...], TN)
    x_out[0] = x
    xhat, _ = normalize(x)
    normed = (xhat * gain[...] + shift[...]).astype(BF16)
    n_out[0] = normed
    for part in range(3):
        cols = slice(part * features, (part + 1) * features)
        out = (mm(normed, weight[:, cols]) + bias[:, cols]).astype(BF16)
        for g in range(groups):
            heads_out[g, 0, :, part * width:(part + 1) * width] = out[:, g * width:(g + 1) * width]


def project(patch, time_ids, freq_ids, time_table, freq_table, gain, shift, weight, bias, groups):
    clips, rows, features = patch.shape
    width = features // groups
    whole = lambda a: pl.BlockSpec(a.shape, lambda c: (0,) * a.ndim)
    per_clip = lambda *tail: pl.BlockSpec((1,) + tail, lambda c: (c,) + (0,) * len(tail))
    return pl.pallas_call(
        functools.partial(project_body, groups),
        grid=(clips,),
        in_specs=[per_clip(rows, features), per_clip(1, rows), per_clip(1, rows)]
        + [whole(a) for a in (time_table, freq_table, gain, shift, weight, bias)],
        out_specs=[per_clip(rows, features), per_clip(rows, features), pl.BlockSpec((groups, 1, rows, 3 * width), lambda c: (0, c, 0, 0))],
        out_shape=[
            jax.ShapeDtypeStruct((clips, rows, features), F32),
            jax.ShapeDtypeStruct((clips, rows, features), BF16),
            jax.ShapeDtypeStruct((groups, clips, rows, 3 * width), BF16),
        ],
        scratch_shapes=[pltpu.VMEM((2 * TABLE_ROWS, features), BF16)],
        compiler_params=params(),
    )(patch, time_ids, freq_ids, time_table, freq_table, gain, shift, weight, bias)


def attend_body(used, head_dim, block, lengths, heads, mixed_out, log_out):
    groups, _, rows, width3 = heads.shape
    width = width3 // 3
    here = width // head_dim
    length = lengths[pl.program_id(0)]
    joined = heads[...].reshape(groups * rows, width3)[0:used]
    query = joined[:, 0:width] * BF16(1.0 / math.sqrt(head_dim))
    keys = joined[:, width:2 * width]
    values = joined[:, 2 * width:]
    lane = lax.broadcasted_iota(jnp.int32, (1, width), 1) // head_dim
    wide_lane = lax.broadcasted_iota(jnp.int32, (block, 128), 1)
    key_ok = lax.broadcasted_iota(jnp.int32, (1, used), 1) < length
    pieces = []
    logs = []
    for first in range(0, used, block):
        q_block = query[first:first + block]
        mixed = jnp.zeros((block, width), F32)
        log_wide = jnp.zeros((block, 128), F32)
        for h in range(here):
            q_head = jnp.where(lane == h, q_block, BF16(0))
            scores = jnp.where(key_ok, mm(q_head, keys, NT), NEGATIVE)
            highest = jnp.max(scores, -1, keepdims=True)
            powers = jnp.exp(scores - highest)
            total = jnp.sum(powers, -1, keepdims=True)
            out = mm(powers.astype(BF16), values) * (1.0 / total)
            mixed = mixed + jnp.where(lane == h, out, 0.0)
            log_wide = jnp.where(wide_lane == h, highest + jnp.log(total), log_wide)
        pieces.append(mixed.astype(BF16))
        logs.append(log_wide)
    tail = groups * rows - used
    pieces.append(jnp.zeros((tail, width), BF16))
    mixed_out[...] = jnp.concatenate(pieces, 0).reshape(mixed_out.shape)
    log_out[0] = jnp.concatenate(logs, 0).T[0:8]


def attend(heads, lengths, head_dim, used, block):
    groups, clips, rows, width3 = heads.shape
    width = width3 // 3
    return pl.pallas_call(
        functools.partial(attend_body, used, head_dim, block),
        grid_spec=pltpu.PrefetchScalarGridSpec(
            num_scalar_prefetch=1,
            grid=(clips,),
            in_specs=[pl.BlockSpec((groups, 1, rows, width3), lambda c, s: (0, c, 0, 0))],
            out_specs=[
                pl.BlockSpec((groups, 1, rows, width), lambda c, s: (0, c, 0, 0)),
                pl.BlockSpec((1, 8, used), lambda c, s: (c, 0, 0)),
            ],
        ),
        out_shape=[
            jax.ShapeDtypeStruct((groups, clips, rows, width), BF16),
            jax.ShapeDtypeStruct((clips, 8, used), F32),
        ],
        compiler_params=params(),
    )(lengths, heads)


def middle_body(clips, limits, x_in, mixed_in, cot, out_weight, out_bias, gain, shift, up, up_bias, down, down_bias,
                out_ref, d_mixed_ref, d_x1_ref, g_down_t, g_up, g_out, small, up_bias_grad,
                mixed, x1, n2, n2_t, dm, dm_t, acc, d_n2, act_all, d_hidden_all):
    step = pl.program_id(0)
    groups, total, width = mixed_in.shape
    rows = total // clips
    features = x_in.shape[1]

    def valid_rows(c):
        return lax.broadcasted_iota(jnp.int32, (rows, 1), 0) < limits[c]

    @pl.when(step == 0)
    def _():
        small[...] = jnp.zeros_like(small)
        for c in range(clips):
            span = slice(c * rows, (c + 1) * rows)
            for g in range(groups):
                mixed[span, g * width:(g + 1) * width] = mixed_in[g, span, :]
            after = x_in[span] + (mm(mixed[span], out_weight[...]) + out_bias[...])
            x1[span] = after
            xhat, _ = normalize(after)
            n2[span] = (xhat * gain[...] + shift[...]).astype(BF16)
            dm[span] = jnp.where(valid_rows(c), cot[span], BF16(0))
        n2_t[...] = n2[...].T
        dm_t[...] = dm[...].T
        acc[...] = jnp.zeros_like(acc)
        d_n2[...] = jnp.zeros_like(d_n2)
        small[7:8, :] = row_sum(dm[...].astype(F32))

    bias_sum = None
    for c in range(clips):
        span = slice(c * rows, (c + 1) * rows)
        hidden = mm(n2[span], up[...]) + up_bias[...]
        half = 0.5 * (1.0 + lax.erf(hidden * (1.0 / math.sqrt(2.0))))
        act = (hidden * half).astype(BF16)
        slope = half + hidden * jnp.exp(hidden * hidden * -0.5) * (1.0 / math.sqrt(2.0 * math.pi))
        d_hidden = (slope * mm(dm[span], down[...], NT)).astype(BF16)
        act_all[span] = act
        d_hidden_all[span] = d_hidden
        acc[span] += mm(act, down[...])
        d_n2[span] += mm(d_hidden, up[...], NT)
        part = row_sum(d_hidden.astype(F32))
        bias_sum = part if bias_sum is None else bias_sum + part
    up_bias_grad[...] = bias_sum
    g_down_t[...] = mm(dm_t[...], act_all[...]).astype(BF16)
    g_up[...] = mm(n2_t[...], d_hidden_all[...]).astype(BF16)

    @pl.when(step == pl.num_programs(0) - 1)
    def _():
        gain_sum = jnp.zeros((1, features), F32)
        shift_sum = jnp.zeros((1, features), F32)
        bias_out = jnp.zeros((1, features), F32)
        for c in range(clips):
            span = slice(c * rows, (c + 1) * rows)
            ok = valid_rows(c)
            after = x1[span]
            out_ref[span] = jnp.where(ok, after + (acc[span] + down_bias[...]), 0.0).astype(BF16)
            xhat, rstd = normalize(after)
            d_norm = d_n2[span]
            gain_sum += row_sum(d_norm * xhat)
            shift_sum += row_sum(d_norm)
            d_x1 = dm[span].astype(F32) + norm_back(d_norm, gain[...], xhat, rstd)
            d_x1_ref[span] = d_x1
            d_a = d_x1.astype(BF16)
            n2[span] = d_a
            bias_out += row_sum(d_a.astype(F32))
            d_mixed = mm(d_a, out_weight[...], NT).astype(BF16)
            for g in range(groups):
                d_mixed_ref[g, span, :] = d_mixed[:, g * width:(g + 1) * width]
        g_out[...] = mm(mixed[...].T, n2[...]).astype(BF16)
        small[2:3, :] = bias_out
        small[5:6, :] = gain_sum
        small[6:7, :] = shift_sum


def middle(limits, x, mixed, cot, out_weight, out_bias, gain, shift, up, up_bias, down, down_bias, clips, tile):
    total, features = x.shape
    groups, _, width = mixed.shape
    hidden = up.shape[1]
    whole = lambda a: pl.BlockSpec(a.shape, lambda j, s: (0,) * len(a.shape))
    outs = [
        jax.ShapeDtypeStruct((total, features), BF16),
        jax.ShapeDtypeStruct((groups, total, width), BF16),
        jax.ShapeDtypeStruct((total, features), F32),
        jax.ShapeDtypeStruct((features, hidden), BF16),
        jax.ShapeDtypeStruct((features, hidden), BF16),
        jax.ShapeDtypeStruct((features, features), BF16),
        jax.ShapeDtypeStruct((8, features), F32),
        jax.ShapeDtypeStruct((1, hidden), F32),
    ]
    cols = lambda height: pl.BlockSpec((height, tile), lambda j, s: (0, j))
    return pl.pallas_call(
        functools.partial(middle_body, clips),
        grid_spec=pltpu.PrefetchScalarGridSpec(
            num_scalar_prefetch=1,
            grid=(hidden // tile,),
            in_specs=[whole(x), whole(mixed), whole(cot), whole(out_weight), whole(out_bias), whole(gain), whole(shift),
                      cols(features), cols(1), pl.BlockSpec((tile, features), lambda j, s: (j, 0)), whole(down_bias)],
            out_specs=[whole(outs[0]), whole(outs[1]), whole(outs[2]), cols(features), cols(features), whole(outs[5]), whole(outs[6]), cols(1)],
            scratch_shapes=[
                pltpu.VMEM((total, features), BF16),
                pltpu.VMEM((total, features), F32),
                pltpu.VMEM((total, features), BF16),
                pltpu.VMEM((features, total), BF16),
                pltpu.VMEM((total, features), BF16),
                pltpu.VMEM((features, total), BF16),
                pltpu.VMEM((total, features), F32),
                pltpu.VMEM((total, features), F32),
                pltpu.VMEM((total, tile), BF16),
                pltpu.VMEM((total, tile), BF16),
            ],
        ),
        out_shape=outs,
        compiler_params=params(),
    )(limits, x, mixed, cot, out_weight, out_bias, gain, shift, up, up_bias, down, down_bias)


def attend_back_body(used, head_dim, block, lengths, heads, d_mixed_in, logs, d_heads):
    groups, _, rows, width3 = heads.shape
    width = width3 // 3
    here = width // head_dim
    length = lengths[pl.program_id(0)]
    scale = BF16(1.0 / math.sqrt(head_dim))
    joined = heads[...].reshape(groups * rows, width3)[0:used]
    d_mixed = d_mixed_in[...].reshape(groups * rows, width)[0:used]
    query = joined[:, 0:width] * scale
    keys = joined[:, width:2 * width]
    values = joined[:, 2 * width:]
    keys_t = (keys * scale).T
    lane = lax.broadcasted_iota(jnp.int32, (1, width), 1) // head_dim
    key_ok = lax.broadcasted_iota(jnp.int32, (used, 1), 0) < length
    d_keys = jnp.zeros((used, width), F32)
    d_values = jnp.zeros((used, width), F32)
    d_query_t = []
    for first in range(0, used, block):
        last = min(first + block, used)
        q_block = query[first:last]
        m_block = d_mixed[first:last]
        d_q_parts = []
        for h in range(here):
            q_head = jnp.where(lane == h, q_block, BF16(0))
            m_head = jnp.where(lane == h, m_block, BF16(0))
            scores = jnp.where(key_ok, mm(keys, q_head, NT), NEGATIVE)
            probs = jnp.exp(scores - logs[0, h:h + 1, first:last])
            d_values = d_values + mm(probs.astype(BF16), m_head)
            weighted = probs * mm(values, m_head, NT)
            d_scores = (weighted - probs * row_sum(weighted)).astype(BF16)
            d_keys = d_keys + mm(d_scores, q_head)
            d_q_parts.append(mm(keys_t[h * head_dim:(h + 1) * head_dim], d_scores))
        d_query_t.append(jnp.concatenate(d_q_parts, 0))
    d_query = jnp.concatenate(d_query_t, 1).T
    tail = jnp.zeros((groups * rows - used, width), BF16)
    for part, value in enumerate((d_query, d_keys, d_values)):
        full = jnp.concatenate([value.astype(BF16), tail], 0)
        d_heads[:, 0, :, part * width:(part + 1) * width] = full.reshape(groups, rows, width)


def attend_back(heads, d_mixed, logs, lengths, head_dim, used, block):
    groups, clips, rows, width3 = heads.shape
    width = width3 // 3
    spec = lambda cols: pl.BlockSpec((groups, 1, rows, cols), lambda c, s: (0, c, 0, 0))
    return pl.pallas_call(
        functools.partial(attend_back_body, used, head_dim, block),
        grid_spec=pltpu.PrefetchScalarGridSpec(
            num_scalar_prefetch=1,
            grid=(clips,),
            in_specs=[spec(width3), spec(width), pl.BlockSpec((1, 8, used), lambda c, s: (c, 0, 0))],
            out_specs=spec(width3),
        ),
        out_shape=jax.ShapeDtypeStruct((groups, clips, rows, width3), BF16),
        compiler_params=params(),
    )(lengths, heads, d_mixed, logs)


def finish_body(clips, d_heads, weight, normed, x_in, d_x1, time_ids, freq_ids, gain, small_in, d_patch, g_qkv, small, joined, high_low, hot):
    groups, total, width3 = d_heads.shape
    width = width3 // 3
    rows = total // clips
    features = x_in.shape[1]
    for part in range(3):
        for g in range(groups):
            first = part * features + g * width
            joined[:, first:first + width] = d_heads[g, :, part * width:(part + 1) * width]
    small[0:8, :] = small_in[...]
    small[8:16, :] = jnp.zeros((8, features), F32)
    gain_sum = jnp.zeros((1, features), F32)
    shift_sum = jnp.zeros((1, features), F32)
    query_sum = jnp.zeros((1, features), F32)
    value_sum = jnp.zeros((1, features), F32)
    for c in range(clips):
        span = slice(c * rows, (c + 1) * rows)
        d_norm = mm(joined[span], weight[...], NT)
        query_sum += row_sum(joined[span, 0:features].astype(F32))
        value_sum += row_sum(joined[span, 2 * features:].astype(F32))
        xhat, rstd = normalize(x_in[span])
        gain_sum += row_sum(d_norm * xhat)
        shift_sum += row_sum(d_norm)
        d_x = d_x1[span] + norm_back(d_norm, gain[...], xhat, rstd)
        high, low = split_high_low(d_x)
        d_patch[span] = high
        high_low[span, 0:features] = high
        high_low[span, features:] = low
    normed_t = normed[...].T
    for part in range(3):
        cols = slice(part * features, (part + 1) * features)
        g_qkv[:, cols] = mm(normed_t, joined[:, cols]).astype(BF16)
    tables = jnp.zeros((TABLE_ROWS, 2 * features), F32)
    for c in range(clips):
        tables = tables + mm(one_hot(time_ids[c], freq_ids[c]), high_low[c * rows:(c + 1) * rows])
    small[16:, :] = tables[:, 0:features] + tables[:, features:]
    small[0:1, :] = query_sum
    small[1:2, :] = value_sum
    small[3:4, :] = gain_sum
    small[4:5, :] = shift_sum


def finish(d_heads, weight, normed, x, d_x1, time_ids, freq_ids, gain, small, clips):
    total, features = x.shape
    return pl.pallas_call(
        functools.partial(finish_body, clips),
        out_shape=[
            jax.ShapeDtypeStruct((total, features), BF16),
            jax.ShapeDtypeStruct((features, 3 * features), BF16),
            jax.ShapeDtypeStruct((SMALL_ROWS, features), F32),
        ],
        scratch_shapes=[
            pltpu.VMEM((total, 3 * features), BF16),
            pltpu.VMEM((total, 2 * features), BF16),
            pltpu.VMEM((8, 128), F32),
        ],
        compiler_params=params(),
    )(d_heads, weight, normed, x, d_x1, time_ids, freq_ids, gain, small)


def exchange(array):
    return lax.all_to_all(array, "seq", split_axis=0, concat_axis=0, tiled=True)


def reduce_all(g_qkv, g_out, g_up, g_down_t, small, up_bias_grad):
    shares = lax.axis_size("dp")
    features = small.shape[1]
    hidden = up_bias_grad.shape[1]
    repeat = hidden // features
    chunks = up_bias_grad.reshape(shares, repeat, features // shares)
    small = small.at[8:8 + repeat].set(jnp.swapaxes(chunks, 0, 1).reshape(repeat, features))

    def total(part, axis):
        return lax.psum(lax.psum_scatter(part, "dp", scatter_dimension=axis, tiled=True), "seq").astype(F32)

    small = total(small, 1)
    up_bias = small[8:8 + repeat].reshape(hidden // shares)
    return (
        total(g_qkv, 0), small[0], small[1], total(g_out, 0), small[2], small[3], small[4], small[5], small[6],
        total(g_up, 0), up_bias, total(g_down_t, 1).T, small[7],
        small[16:16 + 101], small[16 + FREQ_ROW:16 + FREQ_ROW + 12],
    )


def shards(
    patches,
    cotangent,
    time_ids,
    freq_ids,
    lengths,
    qkv_weight,
    query_bias,
    value_bias,
    out_weight,
    out_bias,
    norm1_gain,
    norm1_shift,
    norm2_gain,
    norm2_shift,
    up_weight,
    up_bias,
    down_weight,
    down_bias,
    time_table,
    freq_table,
):
    groups = lax.axis_size("seq")
    clips, rows, features = patches.shape
    head_dim = features // HEADS
    width = features // groups
    total = clips * rows
    used = min(-(-KEEP_MAX // 16) * 16, rows * groups)
    limits = lengths - lax.axis_index("seq") * rows
    line = lambda v: v.reshape(1, -1)
    bias = line(jnp.concatenate([query_bias, jnp.zeros_like(query_bias), value_bias]))
    time_rows = time_ids.reshape(clips, 1, rows)
    freq_rows = freq_ids.reshape(clips, 1, rows)
    x, normed, heads = project(
        patches, time_rows, freq_rows, time_table, freq_table, line(norm1_gain), line(norm1_shift), qkv_weight, bias, groups
    )
    heads = exchange(heads)
    mixed, logs = attend(heads, lengths, head_dim, used, used // 4)
    mixed = exchange(mixed)
    x = x.reshape(total, features)
    output, d_mixed, d_x1, g_down_t, g_up, g_out, small, up_bias_grad = middle(
        limits, x, mixed.reshape(groups, total, width), cotangent.reshape(total, features), out_weight, line(out_bias),
        line(norm2_gain), line(norm2_shift), up_weight, line(up_bias), down_weight, line(down_bias), clips, 512
    )
    d_mixed = exchange(d_mixed.reshape(groups, clips, rows, width))
    d_heads = attend_back(heads, d_mixed, logs, lengths, head_dim, used, 256)
    d_heads = exchange(d_heads)
    d_patch, g_qkv, small = finish(
        d_heads.reshape(groups, total, 3 * width), qkv_weight, normed.reshape(total, features), x, d_x1, time_rows, freq_rows,
        line(norm1_gain), small, clips
    )
    shape = patches.shape
    return (output.reshape(shape), d_patch.reshape(shape)) + reduce_all(g_qkv, g_out, g_up, g_down_t, small, up_bias_grad)


def solution(mesh):
    clip_spec, row_spec, one = P("dp", "seq", None), P("dp", "seq"), P("dp")
    matrix = P("dp", None)
    return jax.shard_map(
        shards,
        mesh=mesh,
        in_specs=(clip_spec, clip_spec, row_spec, row_spec, one) + (P(),) * 15,
        out_specs=(clip_spec, clip_spec, matrix, one, one, matrix, one, one, one, one, one, matrix, one, matrix, one, P(None, "dp"), P(None, "dp")),
        check_vma=False,
    )
```

```python
import functools
import math

import jax
import jax.numpy as jnp
from jax import lax
from jax.experimental import pallas as pl
from jax.experimental.pallas import tpu as pltpu
from jax.sharding import PartitionSpec as P

HEADS = 12
KEEP_MAX = 700
EPS = 1e-06
NEGATIVE = -1000000000.0
FREQ_ROW = 104
TABLE_ROWS = 128
SMALL_ROWS = 32 + TABLE_ROWS
F32 = jnp.float32
BF16 = jnp.bfloat16
NN = (((1,), (0,)), ((), ()))
NT = (((1,), (1,)), ((), ()))
TN = (((0,), (0,)), ((), ()))
MIB = 1 << 20


def mm(left, right, dims=NN):
    return lax.dot_general(left, right, dims, preferred_element_type=F32)


def params(limit=60):
    return pltpu.CompilerParams(vmem_limit_bytes=limit * MIB)


def row_sum(values):
    return jnp.sum(values, 0, keepdims=True)


def normalize(values):
    center = values - jnp.mean(values, -1, keepdims=True)
    rstd = lax.rsqrt(jnp.mean(center * center, -1, keepdims=True) + EPS)
    return center * rstd, rstd


def norm_back(d_out, gain, xhat, rstd):
    u = d_out * gain
    inner = jnp.mean(u * xhat, -1, keepdims=True)
    return rstd * (u - jnp.mean(u, -1, keepdims=True) - xhat * inner)


def split_high_low(values):
    high = values.astype(BF16)
    return high, (values - high.astype(F32)).astype(BF16)


def one_hot(time_row, freq_row):
    spot = lax.broadcasted_iota(jnp.int32, (TABLE_ROWS, time_row.shape[1]), 0)
    hit = (spot == time_row) | (spot == freq_row + FREQ_ROW)
    return jnp.where(hit, 1.0, 0.0).astype(BF16)


def project_body(groups, patch, time_ids, freq_ids, time_table, freq_table, gain, shift, weight, bias, x_out, n_out, heads_out, table):
    features = patch.shape[2]
    width = features // groups

    @pl.when(pl.program_id(0) == 0)
    def _():
        full = jnp.zeros((TABLE_ROWS, features), F32)
        table_f32 = x_out.at[0, 0:TABLE_ROWS]
        table_f32[...] = full
        x_out[0, 0:time_table.shape[0], :] = time_table[...]
        x_out[0, FREQ_ROW:FREQ_ROW + freq_table.shape[0], :] = freq_table[...]
        high, low = split_high_low(x_out[0, 0:TABLE_ROWS, :])
        table[0:TABLE_ROWS, :] = high
        table[TABLE_ROWS:, :] = low

    hot = one_hot(time_ids[0], freq_ids[0])
    x = patch[0].astype(F32) + mm(jnp.concatenate([hot, hot], 0), table[...], TN)
    x_out[0] = x
    xhat, _ = normalize(x)
    normed = (xhat * gain[...] + shift[...]).astype(BF16)
    n_out[0] = normed
    for part in range(3):
        cols = slice(part * features, (part + 1) * features)
        out = (mm(normed, weight[:, cols]) + bias[:, cols]).astype(BF16)
        for g in range(groups):
            heads_out[g, 0, :, part * width:(part + 1) * width] = out[:, g * width:(g + 1) * width]


def project(patch, time_ids, freq_ids, time_table, freq_table, gain, shift, weight, bias, groups):
    clips, rows, features = patch.shape
    width = features // groups
    whole = lambda a: pl.BlockSpec(a.shape, lambda c: (0,) * a.ndim)
    per_clip = lambda *tail: pl.BlockSpec((1,) + tail, lambda c: (c,) + (0,) * len(tail))
    return pl.pallas_call(
        functools.partial(project_body, groups),
        grid=(clips,),
        in_specs=[per_clip(rows, features), per_clip(1, rows), per_clip(1, rows)]
        + [whole(a) for a in (time_table, freq_table, gain, shift, weight, bias)],
        out_specs=[per_clip(rows, features), per_clip(rows, features), pl.BlockSpec((groups, 1, rows, 3 * width), lambda c: (0, c, 0, 0))],
        out_shape=[
            jax.ShapeDtypeStruct((clips, rows, features), F32),
            jax.ShapeDtypeStruct((clips, rows, features), BF16),
            jax.ShapeDtypeStruct((groups, clips, rows, 3 * width), BF16),
        ],
        scratch_shapes=[pltpu.VMEM((2 * TABLE_ROWS, features), BF16)],
        compiler_params=params(),
    )(patch, time_ids, freq_ids, time_table, freq_table, gain, shift, weight, bias)


def attend_body(used, head_dim, block, lengths, heads, mixed_out, log_out):
    groups, _, rows, width3 = heads.shape
    width = width3 // 3
    here = width // head_dim
    length = lengths[pl.program_id(0)]
    joined = heads[...].reshape(groups * rows, width3)[0:used]
    query = joined[:, 0:width] * BF16(1.0 / math.sqrt(head_dim))
    keys = joined[:, width:2 * width]
    values = joined[:, 2 * width:]
    lane = lax.broadcasted_iota(jnp.int32, (1, width), 1) // head_dim
    wide_lane = lax.broadcasted_iota(jnp.int32, (block, 128), 1)
    key_ok = lax.broadcasted_iota(jnp.int32, (1, used), 1) < length
    pieces = []
    logs = []
    for first in range(0, used, block):
        q_block = query[first:first + block]
        mixed = jnp.zeros((block, width), F32)
        log_wide = jnp.zeros((block, 128), F32)
        for h in range(here):
            q_head = jnp.where(lane == h, q_block, BF16(0))
            scores = jnp.where(key_ok, mm(q_head, keys, NT), NEGATIVE)
            highest = jnp.max(scores, -1, keepdims=True)
            powers = jnp.exp(scores - highest)
            total = jnp.sum(powers, -1, keepdims=True)
            out = mm(powers.astype(BF16), values) * (1.0 / total)
            mixed = mixed + jnp.where(lane == h, out, 0.0)
            log_wide = jnp.where(wide_lane == h, highest + jnp.log(total), log_wide)
        pieces.append(mixed.astype(BF16))
        logs.append(log_wide)
    tail = groups * rows - used
    pieces.append(jnp.zeros((tail, width), BF16))
    mixed_out[...] = jnp.concatenate(pieces, 0).reshape(mixed_out.shape)
    log_out[0] = jnp.concatenate(logs, 0).T[0:8]


def attend(heads, lengths, head_dim, used, block):
    groups, clips, rows, width3 = heads.shape
    width = width3 // 3
    return pl.pallas_call(
        functools.partial(attend_body, used, head_dim, block),
        grid_spec=pltpu.PrefetchScalarGridSpec(
            num_scalar_prefetch=1,
            grid=(clips,),
            in_specs=[pl.BlockSpec((groups, 1, rows, width3), lambda c, s: (0, c, 0, 0))],
            out_specs=[
                pl.BlockSpec((groups, 1, rows, width), lambda c, s: (0, c, 0, 0)),
                pl.BlockSpec((1, 8, used), lambda c, s: (c, 0, 0)),
            ],
        ),
        out_shape=[
            jax.ShapeDtypeStruct((groups, clips, rows, width), BF16),
            jax.ShapeDtypeStruct((clips, 8, used), F32),
        ],
        compiler_params=params(),
    )(lengths, heads)


def middle_body(clips, shares, limits, x_in, mixed_in, cot, out_weight, out_bias, gain, shift, up, up_bias, down, down_bias,
                out_ref, d_mixed_ref, d_x1_ref, g_down_a, g_down_b, g_up_a, g_up_b, g_out, small, up_bias_grad,
                mixed, x1, n2, n2_t, dm, dm_t, acc, d_n2, act_all, d_hidden_all):
    step = pl.program_id(0)
    groups, total, width = mixed_in.shape
    rows = total // clips
    features = x_in.shape[1]
    share = features // shares

    def valid_rows(c):
        return lax.broadcasted_iota(jnp.int32, (rows, 1), 0) < limits[c]

    @pl.when(step == 0)
    def _():
        small[...] = jnp.zeros_like(small)
        for c in range(clips):
            span = slice(c * rows, (c + 1) * rows)
            for g in range(groups):
                mixed[span, g * width:(g + 1) * width] = mixed_in[g, span, :]
            after = x_in[span] + (mm(mixed[span], out_weight[...]) + out_bias[...])
            x1[span] = after
            xhat, _ = normalize(after)
            n2[span] = (xhat * gain[...] + shift[...]).astype(BF16)
            dm[span] = jnp.where(valid_rows(c), cot[span], BF16(0))
        n2_t[...] = n2[...].T
        dm_t[...] = dm[...].T
        acc[...] = jnp.zeros_like(acc)
        d_n2[...] = jnp.zeros_like(d_n2)
        small[7:8, :] = row_sum(dm[...].astype(F32))

    bias_sum = None
    for c in range(clips):
        span = slice(c * rows, (c + 1) * rows)
        hidden = mm(n2[span], up[...]) + up_bias[...]
        half = 0.5 * (1.0 + lax.erf(hidden * (1.0 / math.sqrt(2.0))))
        act = (hidden * half).astype(BF16)
        slope = half + hidden * jnp.exp(hidden * hidden * -0.5) * (1.0 / math.sqrt(2.0 * math.pi))
        d_hidden = (slope * mm(dm[span], down[...], NT)).astype(BF16)
        act_all[span] = act
        d_hidden_all[span] = d_hidden
        acc[span] += mm(act, down[...])
        d_n2[span] += mm(d_hidden, up[...], NT)
        part = row_sum(d_hidden.astype(F32))
        bias_sum = part if bias_sum is None else bias_sum + part
    up_bias_grad[...] = bias_sum
    tile = up.shape[1]
    heights = g_down_a.shape[3], g_down_b.shape[2]
    reach = g_down_a.shape[4]
    for core in range(2):
        first = core * (features // 2)
        out = mm(dm_t[first:first + features // 2], act_all[...]).astype(BF16)
        for d in range(tile // reach):
            cols = slice(d * reach, (d + 1) * reach)
            for half_x in range(2):
                g_down_a[d, core, half_x] = out[half_x * heights[0]:(half_x + 1) * heights[0], cols]
            g_down_b[d, core] = out[2 * heights[0]:, cols]
    g_up_tile = mm(n2_t[...], d_hidden_all[...]).astype(BF16)

    @pl.when(step % 2 == 0)
    def _():
        wide = tile // 2
        for d in range(shares):
            for half_x in range(2):
                g_up_a[d, 0, half_x] = g_up_tile[d * share:(d + 1) * share, half_x * wide:(half_x + 1) * wide]

    @pl.when(step % 2 == 1)
    def _():
        for d in range(shares):
            g_up_b[d, 0] = g_up_tile[d * share:(d + 1) * share]

    @pl.when(step == pl.num_programs(0) - 1)
    def _():
        gain_sum = jnp.zeros((1, features), F32)
        shift_sum = jnp.zeros((1, features), F32)
        bias_out = jnp.zeros((1, features), F32)
        for c in range(clips):
            span = slice(c * rows, (c + 1) * rows)
            ok = valid_rows(c)
            after = x1[span]
            out_ref[span] = jnp.where(ok, after + (acc[span] + down_bias[...]), 0.0).astype(BF16)
            xhat, rstd = normalize(after)
            d_norm = d_n2[span]
            gain_sum += row_sum(d_norm * xhat)
            shift_sum += row_sum(d_norm)
            d_x1 = dm[span].astype(F32) + norm_back(d_norm, gain[...], xhat, rstd)
            d_x1_ref[span] = d_x1
            d_a = d_x1.astype(BF16)
            n2[span] = d_a
            bias_out += row_sum(d_a.astype(F32))
            d_mixed = mm(d_a, out_weight[...], NT).astype(BF16)
            for g in range(groups):
                d_mixed_ref[g, span, :] = d_mixed[:, g * width:(g + 1) * width]
        out = mm(mixed[...].T, n2[...]).astype(BF16)
        for d in range(shares):
            for core in range(2):
                g_out[d, core] = out[d * share:(d + 1) * share, core * (features // 2):(core + 1) * (features // 2)]
        small[2:3, :] = bias_out
        small[5:6, :] = gain_sum
        small[6:7, :] = shift_sum


def middle(limits, x, mixed, cot, out_weight, out_bias, gain, shift, up, up_bias, down, down_bias, clips, tile, shares):
    total, features = x.shape
    groups, _, width = mixed.shape
    hidden = up.shape[1]
    share, reach, half = features // shares, hidden // shares, features // 2
    spread = max(tile // reach, 1)
    whole = lambda a: pl.BlockSpec(a.shape, lambda j, s: (0,) * len(a.shape))
    outs = [
        jax.ShapeDtypeStruct((total, features), BF16),
        jax.ShapeDtypeStruct((groups, total, width), BF16),
        jax.ShapeDtypeStruct((total, features), F32),
        jax.ShapeDtypeStruct((shares, 2, 2, half // 4, reach), BF16),
        jax.ShapeDtypeStruct((shares, 2, half // 2, reach), BF16),
        jax.ShapeDtypeStruct((shares, 2, 2, share, hidden // 8), BF16),
        jax.ShapeDtypeStruct((shares, 2, share, hidden // 4), BF16),
        jax.ShapeDtypeStruct((shares, 2, share, half), BF16),
        jax.ShapeDtypeStruct((8, features), F32),
        jax.ShapeDtypeStruct((1, hidden), F32),
    ]
    cols = lambda height: pl.BlockSpec((height, tile), lambda j, s: (0, j))
    if tile >= reach:
        down_spec = lambda *mid: pl.BlockSpec((spread,) + mid + (reach,), lambda j, s: (j,) + (0,) * (len(mid) + 1))
    else:
        down_spec = lambda *mid: pl.BlockSpec((1,) + mid + (tile,), lambda j, s: (0,) * (len(mid) + 1) + (j,))
    return pl.pallas_call(
        functools.partial(middle_body, clips, shares),
        grid_spec=pltpu.PrefetchScalarGridSpec(
            num_scalar_prefetch=1,
            grid=(hidden // tile,),
            in_specs=[whole(x), whole(mixed), whole(cot), whole(out_weight), whole(out_bias), whole(gain), whole(shift),
                      cols(features), cols(1), pl.BlockSpec((tile, features), lambda j, s: (j, 0)), whole(down_bias)],
            out_specs=[whole(outs[0]), whole(outs[1]), whole(outs[2]), down_spec(2, 2, half // 4), down_spec(2, half // 2),
                       pl.BlockSpec((shares, 1, 2, share, tile // 2), lambda j, s: (0, j // 2, 0, 0, 0)),
                       pl.BlockSpec((shares, 1, share, tile), lambda j, s: (0, j // 2, 0, 0)),
                       whole(outs[7]), whole(outs[8]), cols(1)],
            scratch_shapes=[
                pltpu.VMEM((total, features), BF16),
                pltpu.VMEM((total, features), F32),
                pltpu.VMEM((total, features), BF16),
                pltpu.VMEM((features, total), BF16),
                pltpu.VMEM((total, features), BF16),
                pltpu.VMEM((features, total), BF16),
                pltpu.VMEM((total, features), F32),
                pltpu.VMEM((total, features), F32),
                pltpu.VMEM((total, tile), BF16),
                pltpu.VMEM((total, tile), BF16),
            ],
        ),
        out_shape=outs,
        compiler_params=params(),
    )(limits, x, mixed, cot, out_weight, out_bias, gain, shift, up, up_bias, down, down_bias)


def attend_back_body(used, head_dim, block, lengths, heads, d_mixed_in, logs, d_heads):
    groups, _, rows, width3 = heads.shape
    width = width3 // 3
    here = width // head_dim
    length = lengths[pl.program_id(0)]
    scale = BF16(1.0 / math.sqrt(head_dim))
    joined = heads[...].reshape(groups * rows, width3)[0:used]
    d_mixed = d_mixed_in[...].reshape(groups * rows, width)[0:used]
    query = joined[:, 0:width] * scale
    keys = joined[:, width:2 * width]
    values = joined[:, 2 * width:]
    keys_t = (keys * scale).T
    lane = lax.broadcasted_iota(jnp.int32, (1, width), 1) // head_dim
    key_ok = lax.broadcasted_iota(jnp.int32, (used, 1), 0) < length
    d_keys = jnp.zeros((used, width), F32)
    d_values = jnp.zeros((used, width), F32)
    d_query_t = []
    for first in range(0, used, block):
        last = min(first + block, used)
        q_block = query[first:last]
        m_block = d_mixed[first:last]
        d_q_parts = []
        for h in range(here):
            q_head = jnp.where(lane == h, q_block, BF16(0))
            m_head = jnp.where(lane == h, m_block, BF16(0))
            scores = jnp.where(key_ok, mm(keys, q_head, NT), NEGATIVE)
            probs = jnp.exp(scores - logs[0, h:h + 1, first:last])
            d_values = d_values + mm(probs.astype(BF16), m_head)
            weighted = probs * mm(values, m_head, NT)
            d_scores = (weighted - probs * row_sum(weighted)).astype(BF16)
            d_keys = d_keys + mm(d_scores, q_head)
            d_q_parts.append(mm(keys_t[h * head_dim:(h + 1) * head_dim], d_scores))
        d_query_t.append(jnp.concatenate(d_q_parts, 0))
    d_query = jnp.concatenate(d_query_t, 1).T
    tail = jnp.zeros((groups * rows - used, width), BF16)
    for part, value in enumerate((d_query, d_keys, d_values)):
        full = jnp.concatenate([value.astype(BF16), tail], 0)
        d_heads[:, 0, :, part * width:(part + 1) * width] = full.reshape(groups, rows, width)


def attend_back(heads, d_mixed, logs, lengths, head_dim, used, block):
    groups, clips, rows, width3 = heads.shape
    width = width3 // 3
    spec = lambda cols: pl.BlockSpec((groups, 1, rows, cols), lambda c, s: (0, c, 0, 0))
    return pl.pallas_call(
        functools.partial(attend_back_body, used, head_dim, block),
        grid_spec=pltpu.PrefetchScalarGridSpec(
            num_scalar_prefetch=1,
            grid=(clips,),
            in_specs=[spec(width3), spec(width), pl.BlockSpec((1, 8, used), lambda c, s: (c, 0, 0))],
            out_specs=spec(width3),
        ),
        out_shape=jax.ShapeDtypeStruct((groups, clips, rows, width3), BF16),
        compiler_params=params(),
    )(lengths, heads, d_mixed, logs)


def finish_body(clips, shares, d_heads, weight, normed, x_in, d_x1, time_ids, freq_ids, gain, small_in, up_bias_grad,
                d_patch, g_qkv_a, g_qkv_b, packed, joined, high_low, small):
    groups, total, width3 = d_heads.shape
    width = width3 // 3
    rows = total // clips
    features = x_in.shape[1]
    share = features // shares
    for part in range(3):
        for g in range(groups):
            first = part * features + g * width
            joined[:, first:first + width] = d_heads[g, :, part * width:(part + 1) * width]
    small[0:8, :] = small_in[...]
    small[8:, :] = jnp.zeros((small.shape[0] - 8, features), F32)
    gain_sum = jnp.zeros((1, features), F32)
    shift_sum = jnp.zeros((1, features), F32)
    query_sum = jnp.zeros((1, features), F32)
    value_sum = jnp.zeros((1, features), F32)
    for c in range(clips):
        span = slice(c * rows, (c + 1) * rows)
        d_norm = mm(joined[span], weight[...], NT)
        query_sum += row_sum(joined[span, 0:features].astype(F32))
        value_sum += row_sum(joined[span, 2 * features:].astype(F32))
        xhat, rstd = normalize(x_in[span])
        gain_sum += row_sum(d_norm * xhat)
        shift_sum += row_sum(d_norm)
        d_x = d_x1[span] + norm_back(d_norm, gain[...], xhat, rstd)
        high, low = split_high_low(d_x)
        d_patch[span] = high
        high_low[span, 0:features] = high
        high_low[span, features:] = low
    normed_t = normed[...].T
    half = 3 * features // 2
    wide = g_qkv_a.shape[4]
    for core in range(2):
        out = mm(normed_t, joined[:, core * half:(core + 1) * half]).astype(BF16)
        for d in range(shares):
            span = slice(d * share, (d + 1) * share)
            for half_x in range(2):
                g_qkv_a[d, core, half_x] = out[span, half_x * wide:(half_x + 1) * wide]
            g_qkv_b[d, core] = out[span, 2 * wide:]
    tables = jnp.zeros((TABLE_ROWS, 2 * features), F32)
    for c in range(clips):
        tables = tables + mm(one_hot(time_ids[c], freq_ids[c]), high_low[c * rows:(c + 1) * rows])
    small[16:16 + TABLE_ROWS, :] = tables[:, 0:features] + tables[:, features:]
    small[0:1, :] = query_sum
    small[1:2, :] = value_sum
    small[3:4, :] = gain_sum
    small[4:5, :] = shift_sum
    repeat = up_bias_grad.shape[1] // features
    height = packed.shape[2]
    if share != packed.shape[3]:
        packed[...] = jnp.zeros_like(packed)
    for d in range(shares):
        for r in range(repeat):
            first = (d * repeat + r) * share
            small[8 + r:9 + r, d * share:(d + 1) * share] = up_bias_grad[:, first:first + share]
        for core in range(2):
            packed[d, core, :, 0:share] = small[core * height:(core + 1) * height, d * share:(d + 1) * share].astype(BF16)


def finish(d_heads, weight, normed, x, d_x1, time_ids, freq_ids, gain, small, up_bias_grad, clips, shares):
    total, features = x.shape
    share = features // shares
    half = 3 * features // 2
    wide = half * 2 // 9
    return pl.pallas_call(
        functools.partial(finish_body, clips, shares),
        out_shape=[
            jax.ShapeDtypeStruct((total, features), BF16),
            jax.ShapeDtypeStruct((shares, 2, 2, share, wide), BF16),
            jax.ShapeDtypeStruct((shares, 2, share, half - 2 * wide), BF16),
            jax.ShapeDtypeStruct((shares, 2, SMALL_ROWS // 2, -(-share // 128) * 128), BF16),
        ],
        scratch_shapes=[
            pltpu.VMEM((total, 3 * features), BF16),
            pltpu.VMEM((total, 2 * features), BF16),
            pltpu.VMEM((SMALL_ROWS, features), F32),
        ],
        compiler_params=params(),
    )(d_heads, weight, normed, x, d_x1, time_ids, freq_ids, gain, small, up_bias_grad)


class Flow:
    def __init__(self, source, result, refs, place):
        self.source, self.result = source, result
        self.split = len(source.shape) == 5
        self.own, self.got, self.x_got, self.y_got, self.z_got, self.send, self.recv = refs
        self.z, self.y, self.x, self.c = place
        self.open = {}
        if self.split:
            self.stages = [self.begin, self.cores_x, self.x_y, self.y_z, self.z_fill, self.fill_cores, self.end]
        else:
            self.stages = [self.begin, self.cores_y, self.y_z, self.z_x, self.x_cores, self.end]
        self.used = 0

    def copy(self, key, source, target, peer):
        z, y, x, c = peer
        slot = self.used
        self.used += 1
        made = pltpu.make_async_remote_copy(
            src_ref=source, dst_ref=target, send_sem=self.send.at[slot], recv_sem=self.recv.at[slot],
            device_id=(z * 2 + y, x * 2 + c), device_id_type=pl.DeviceIdType.MESH)
        made.start()
        self.open.setdefault(key, []).append(made)

    def wait(self, key):
        for made in self.open.pop(key):
            made.wait()

    def at(self, ref, z, y):
        return ref.at[z * 2 + y, self.x] if self.split else ref.at[z * 2 + y]

    def begin(self):
        made = pltpu.make_async_copy(self.source.at[:, self.c], self.own, self.send.at[self.used])
        self.used += 1
        made.start()
        self.open["own"] = [made]
        self.copy("core", self.source.at[:, 1 - self.c], self.got, (self.z, self.y, self.x, 1 - self.c))

    def cores(self):
        self.wait("own")
        self.wait("core")

        def add(i, _):
            self.own[i] = self.own[i] + self.got[i]
            return 0

        lax.fori_loop(0, self.own.shape[0], add, 0)

    def cores_x(self):
        self.cores()
        self.copy("x", self.own.at[:, 1 - self.x], self.x_got, (self.z, self.y, 1 - self.x, self.c))

    def cores_y(self):
        self.cores()
        self.to_y()

    def to_y(self):
        for z in range(4):
            self.copy("y", self.at(self.own, z, 1 - self.y), self.y_got.at[z], (self.z, 1 - self.y, self.x, self.c))

    def x_y(self):
        self.wait("x")

        def add(i, _):
            self.own[i, self.x] = self.own[i, self.x] + self.x_got[i]
            return 0

        lax.fori_loop(0, self.own.shape[0], add, 0)
        self.to_y()

    def y_z(self):
        self.wait("y")

        def add(z, _):
            spot = self.at(self.own, z, self.y)
            spot[...] = spot[...] + self.y_got[z]
            return 0

        lax.fori_loop(0, 4, add, 0)
        for ahead in range(1, 4):
            z = lax.rem(self.z + ahead, 4)
            self.copy("z", self.at(self.own, z, self.y), self.z_got.at[ahead - 1], (z, self.y, self.x, self.c))

    def z_sum(self):
        self.wait("z")
        total = self.at(self.own, self.z, self.y)[...].astype(F32)
        for i in range(3):
            total = total + self.z_got[i].astype(F32)
        return total.astype(BF16)

    def z_fill(self):
        self.result[self.c, self.x] = self.z_sum()
        spot = self.result.at[self.c, self.x]
        self.copy("fill", spot, spot, (self.z, self.y, 1 - self.x, self.c))

    def fill_cores(self):
        self.wait("fill")
        self.to_core()

    def z_x(self):
        spot = self.at(self.own, self.z, self.y)
        spot[...] = self.z_sum()
        self.copy("x", spot, self.x_got, (self.z, self.y, 1 - self.x, self.c))

    def x_cores(self):
        self.wait("x")
        self.result[self.c] = self.at(self.own, self.z, self.y)[...] + self.x_got[...]
        self.to_core()

    def to_core(self):
        spot = self.result.at[self.c]
        self.copy("end", spot, spot, (self.z, self.y, self.x, 1 - self.c))

    def end(self):
        self.wait("end")


def flow_scratch(shape):
    shares, tail = shape[0], shape[2:]
    block = tail[-2:]
    first = (shares,) + block if len(tail) == 3 else block
    slots = 16
    return [pltpu.VMEM((shares,) + tail, BF16), pltpu.VMEM((shares,) + tail, BF16), pltpu.VMEM(first, BF16),
            pltpu.VMEM((4,) + block, BF16), pltpu.VMEM((3,) + block, BF16),
            pltpu.SemaphoreType.DMA((slots,)), pltpu.SemaphoreType.DMA((slots,))]


FLOW_REFS = 7


def place_of():
    d, s = lax.axis_index("dp"), lax.axis_index("seq")
    return d // 2, d % 2, s // 2, s % 2


def greet(place):
    z, y, x, c = place
    peers = [(z, y, x, 1 - c), (z, y, 1 - x, c), (z, 1 - y, x, c)] + [(lax.rem(z + i, 4), y, x, c) for i in range(1, 4)]
    barrier = pltpu.get_barrier_semaphore()
    for pz, py, px, pc in peers:
        pl.semaphore_signal(barrier, inc=1, device_id=(pz * 2 + py, px * 2 + pc), device_id_type=pl.DeviceIdType.MESH)
    pl.semaphore_wait(barrier, len(peers))


def reduce_body(count, *refs):
    sources, results, rest = refs[:count], refs[count:2 * count], refs[2 * count:]
    place = place_of()
    greet(place)
    flows = [Flow(sources[i], results[i], rest[i * FLOW_REFS:(i + 1) * FLOW_REFS], place) for i in range(count)]
    for level in range(7):
        for flow in flows:
            if level < len(flow.stages):
                flow.stages[level]()


def reduce_pieces(pieces):
    return pl.pallas_call(
        functools.partial(reduce_body, len(pieces)),
        in_specs=[pl.BlockSpec(memory_space=pl.ANY)] * len(pieces),
        out_shape=[jax.ShapeDtypeStruct(p.shape[1:], BF16) for p in pieces],
        scratch_shapes=[ref for p in pieces for ref in flow_scratch(p.shape)],
        compiler_params=pltpu.CompilerParams(collective_id=0, has_side_effects=True, vmem_limit_bytes=60 * MIB),
    )(*pieces)


def join_columns(halves, rest):
    parts = []
    for core in range(2):
        parts += [halves[core, 0], halves[core, 1], rest[core]]
    return jnp.concatenate(parts, 1)


def join_rows(halves, rest):
    parts = []
    for core in range(2):
        parts += [halves[core, 0], halves[core, 1], rest[core]]
    return jnp.concatenate(parts, 0)


def collect(down_a, down_b, up_a, up_b, out, qkv_a, qkv_b, packed, finish_part):
    small = packed.reshape(SMALL_ROWS, packed.shape[2])
    return (
        finish_part(join_columns(qkv_a, qkv_b), 0),
        finish_part(jnp.concatenate([out[0], out[1]], 1), 0),
        finish_part(join_columns(up_a, up_b), 0),
        finish_part(join_rows(down_a, down_b), 1).T,
        finish_part(small, 1),
    )


def exchange(array):
    return lax.all_to_all(array, "seq", split_axis=0, concat_axis=0, tiled=True)


def reduce_all(pieces, custom, features, hidden, time_count, freq_count):
    if custom:
        qkv, out, up, down, small = collect(*reduce_pieces(pieces), lambda v, axis: v.astype(F32))
        small = small[:, 0:features // lax.axis_size("dp")]
    else:
        def total(part, axis):
            return lax.psum(lax.psum_scatter(part, "dp", scatter_dimension=axis, tiled=True), "seq").astype(F32)

        qkv, out, up, down, small = collect(*(p[0] for p in pieces), total)
    repeat = hidden // features
    up_bias = small[8:8 + repeat].reshape(-1)
    return (
        qkv, small[0], small[1], out, small[2], small[3], small[4], small[5], small[6], up, up_bias, down, small[7],
        small[16:16 + time_count], small[16 + FREQ_ROW:16 + FREQ_ROW + freq_count],
    )


def shards(
    patches,
    cotangent,
    time_ids,
    freq_ids,
    lengths,
    qkv_weight,
    query_bias,
    value_bias,
    out_weight,
    out_bias,
    norm1_gain,
    norm1_shift,
    norm2_gain,
    norm2_shift,
    up_weight,
    up_bias,
    down_weight,
    down_bias,
    time_table,
    freq_table,
):
    groups = lax.axis_size("seq")
    clips, rows, features = patches.shape
    head_dim = features // HEADS
    width = features // groups
    total = clips * rows
    used = min(-(-KEEP_MAX // 16) * 16, rows * groups)
    limits = lengths - lax.axis_index("seq") * rows
    line = lambda v: v.reshape(1, -1)
    bias = line(jnp.concatenate([query_bias, jnp.zeros_like(query_bias), value_bias]))
    time_rows = time_ids.reshape(clips, 1, rows)
    freq_rows = freq_ids.reshape(clips, 1, rows)
    x, normed, heads = project(
        patches, time_rows, freq_rows, time_table, freq_table, line(norm1_gain), line(norm1_shift), qkv_weight, bias, groups
    )
    heads = exchange(heads)
    mixed, logs = attend(heads, lengths, head_dim, used, used // 4)
    mixed = exchange(mixed)
    x = x.reshape(total, features)
    custom = lax.axis_size("dp") == 8 and groups == 4
    shares = 8 if custom else 1
    output, d_mixed, d_x1, down_a, down_b, up_a, up_b, g_out, small, up_bias_grad = middle(
        limits, x, mixed.reshape(groups, total, width), cotangent.reshape(total, features), out_weight, line(out_bias),
        line(norm2_gain), line(norm2_shift), up_weight, line(up_bias), down_weight, line(down_bias), clips, up_weight.shape[1] // 4, shares
    )
    d_mixed = exchange(d_mixed.reshape(groups, clips, rows, width))
    d_heads = attend_back(heads, d_mixed, logs, lengths, head_dim, used, 256)
    d_heads = exchange(d_heads)
    d_patch, qkv_a, qkv_b, packed = finish(
        d_heads.reshape(groups, total, 3 * width), qkv_weight, normed.reshape(total, features), x, d_x1, time_rows, freq_rows,
        line(norm1_gain), small, up_bias_grad, clips, shares
    )
    shape = patches.shape
    return (output.reshape(shape), d_patch.reshape(shape)) + reduce_all(
        (down_a, down_b, up_a, up_b, g_out, qkv_a, qkv_b, packed), custom, features, up_weight.shape[1], time_table.shape[0], freq_table.shape[0]
    )


def solution(mesh):
    clip_spec, row_spec, one = P("dp", "seq", None), P("dp", "seq"), P("dp")
    matrix = P("dp", None)
    return jax.shard_map(
        shards,
        mesh=mesh,
        in_specs=(clip_spec, clip_spec, row_spec, row_spec, one) + (P(),) * 15,
        out_specs=(clip_spec, clip_spec, matrix, one, one, matrix, one, one, one, one, one, matrix, one, matrix, one, P(None, "dp"), P(None, "dp")),
        check_vma=False,
    )
```

```python
import functools
import math

import jax
import jax.numpy as jnp
from jax import lax
from jax.experimental import pallas as pl
from jax.experimental.pallas import tpu as pltpu
from jax.sharding import PartitionSpec as P

HEADS = 12
EPS = 1e-06
NEGATIVE = -1000000000.0
FREQ_ROW = 104
TABLE_ROWS = 128
SMALL_ROWS = 32 + TABLE_ROWS
F32 = jnp.float32
BF16 = jnp.bfloat16
NN = (((1,), (0,)), ((), ()))
NT = (((1,), (1,)), ((), ()))
TN = (((0,), (0,)), ((), ()))
MIB = 1 << 20


def mm(left, right, dims=NN):
    return lax.dot_general(left, right, dims, preferred_element_type=F32)


def params(limit=60):
    return pltpu.CompilerParams(vmem_limit_bytes=limit * MIB)


def row_sum(values):
    return jnp.sum(values, 0, keepdims=True)


def normalize(values):
    center = values - jnp.mean(values, -1, keepdims=True)
    rstd = lax.rsqrt(jnp.mean(center * center, -1, keepdims=True) + EPS)
    return center * rstd, rstd


def norm_back(d_out, gain, xhat, rstd):
    u = d_out * gain
    inner = jnp.mean(u * xhat, -1, keepdims=True)
    return rstd * (u - jnp.mean(u, -1, keepdims=True) - xhat * inner)


def split_high_low(values):
    high = values.astype(BF16)
    return high, (values - high.astype(F32)).astype(BF16)


def one_hot(time_row, freq_row):
    spot = lax.broadcasted_iota(jnp.int32, (TABLE_ROWS, time_row.shape[1]), 0)
    hit = (spot == time_row) | (spot == freq_row + FREQ_ROW)
    return jnp.where(hit, 1.0, 0.0).astype(BF16)


ROWS = 224
OWN = 352
SHARED = 176
WORK = OWN + SHARED
KEYS = 2 * OWN
SHARED_MOVES = (
    (0, 2, 176, 48, 3, 384), (1, 2, 176, 48, 3, 432), (2, 2, 176, 48, 3, 480), (3, 2, 0, 32, 3, 352),
    (0, 2, 0, 176, 0, 352), (1, 2, 0, 176, 1, 352), (2, 2, 0, 176, 2, 352),
)
OWN_MOVES = (
    (2, 0, 0, 128, 0, 224), (2, 0, 128, 96, 1, 224), (3, 0, 0, 32, 1, 320), (0, 1, 0, 224, 2, 0), (1, 1, 0, 224, 3, 0),
    (2, 1, 128, 96, 3, 224), (2, 1, 0, 128, 2, 224), (3, 1, 0, 32, 3, 320), (0, 0, 0, 224, 0, 0), (1, 0, 0, 224, 1, 0),
)
MOVES = SHARED_MOVES + OWN_MOVES
UNUSED = (3, 32)


def seq_place():
    s = lax.axis_index("seq")
    return s, s // 2, lax.rem(s, 2)


def seq_peer(s):
    return {"seq": s}


def greet_group(s):
    barrier = pltpu.get_barrier_semaphore()
    for ahead in range(1, 4):
        pl.semaphore_signal(barrier, inc=1, device_id=seq_peer(lax.rem(s + ahead, 4)), device_id_type=pl.DeviceIdType.MESH)
    pl.semaphore_wait(barrier, 3)


class Mover:
    def __init__(self, s, at_home, at_work, send, recv, back=False):
        self.s, self.at_home, self.at_work, self.send, self.recv, self.back = s, at_home, at_work, send, recv, back

    def ends(self, move):
        home, clip, first, count, work, spot = move
        a, b = self.at_home.at[clip, pl.ds(first, count)], self.at_work.at[pl.ds(spot, count)]
        return (work, b, home, a) if self.back else (home, a, work, b)

    def each(self, moves, which, act, near=True):
        for device in range(4):
            chosen = [m for m in moves if self.ends(m)[which] == device and (near or self.ends(m)[0] != self.ends(m)[2])]
            if not chosen:
                continue

            @pl.when(self.s == device)
            def _(chosen=chosen):
                for m in chosen:
                    src_device, src, dst_device, dst = self.ends(m)
                    slot = MOVES.index(m)
                    if src_device == dst_device:
                        act(False, pltpu.make_async_copy(src, dst, self.recv.at[slot]))
                    else:
                        act(True, pltpu.make_async_remote_copy(
                            src_ref=src, dst_ref=dst, send_sem=self.send.at[slot], recv_sem=self.recv.at[slot],
                            device_id=seq_peer(dst_device), device_id_type=pl.DeviceIdType.MESH))

    def start(self, moves):
        self.each(moves, 0, lambda far, made: made.start())

    def wait(self, moves):
        self.each(moves, 2, lambda far, made: made.wait_recv() if far else made.wait())

    def drain(self, moves):
        self.each(moves, 0, lambda far, made: made.wait_send(), False)


class Sender:
    def __init__(self, send, recv):
        self.send, self.recv, self.used = send, recv, 0

    def far(self, source, target, peer):
        made = pltpu.make_async_remote_copy(
            src_ref=source, dst_ref=target, send_sem=self.send.at[self.used], recv_sem=self.recv.at[self.used],
            device_id=seq_peer(peer), device_id_type=pl.DeviceIdType.MESH)
        self.used += 1
        made.start()
        return made

    def near(self, source, target):
        made = pltpu.make_async_copy(source, target, self.recv.at[self.used])
        self.used += 1
        made.start()
        return made


def wait_all(copies):
    for made in copies:
        made.wait()


def shift_between(spot, cuts):
    slot = spot
    for low, high, shift in cuts:
        slot = jnp.where((spot >= low) & (spot < high), spot + shift, slot)
    return slot


def own_slots(spot):
    return shift_between(spot, ((224, 352, 224), (352, 576, -128)))


def shared_slots(spot):
    return shift_between(spot, ((176, 352, 48), (352, 528, 96), (528, 560, 144), (560, 608, -384), (608, 656, -208), (656, 704, -32)))


def span(first, size):
    return pl.ds(pl.multiple_of(first, 16), size)


def attend(query, keys, values, key_ok, mixed_out, log_out, log_wide, head_dim):
    count = query.shape[1]
    lane = lax.broadcasted_iota(jnp.int32, (1, 128), 1) // head_dim
    wide = lax.broadcasted_iota(jnp.int32, (SHARED, 128), 1)
    scale = BF16(1.0 / math.sqrt(head_dim))

    def pair(p, _):
        k, v = keys[p], values[p]
        for first in range(0, count, SHARED):
            q = query[p, first:first + SHARED] * scale
            mixed = jnp.zeros((SHARED, 128), F32)
            logs = jnp.zeros((SHARED, 128), F32)
            for h in range(128 // head_dim):
                scores = jnp.where(key_ok, mm(jnp.where(lane == h, q, BF16(0)), k, NT), NEGATIVE)
                highest = jnp.max(scores, -1, keepdims=True)
                powers = jnp.exp(scores - highest)
                total = jnp.sum(powers, -1, keepdims=True)
                out = mm(powers.astype(BF16), v) * (1.0 / total)
                mixed = jnp.where(lane == h, out, mixed)
                logs = jnp.where(wide == h, highest + jnp.log(total), logs)
            mixed_out[p, first:first + SHARED] = mixed.astype(BF16)
            log_wide[first:first + SHARED] = logs
        log_out[p] = log_wide[0:count].T[0:8]
        return 0

    lax.fori_loop(0, query.shape[0], pair, 0)


def forward_body(head_dim, lengths, patches, cot, time_ids, freq_ids, time_table, freq_table, gain, shift, weight, query_bias, value_bias,
                 x_out, n_out, own_out, shared_q_out, shared_kv_out, own_log, shared_log, mixed_out, cot_out, id_out, valid_out,
                 work, table_f32, table, ids, matrix, own_stage, shared_stage, own_mixed, shared_mixed, log_wide,
                 patch_send, patch_recv, cot_send, cot_recv, send, recv, weight_sem):
    s, x, c = seq_place()
    features = x_out.shape[1]
    groups = own_out.shape[1]
    other = 1 - c
    loads = [pltpu.make_async_copy(weight.at[:, pl.ds(p * features, features)], matrix.at[:, pl.ds(p * features, features)], weight_sem.at[p])
             for p in range(3)]
    for load in loads:
        load.start()
    greet_group(s)
    patch_mover = Mover(s, patches, work, patch_send, patch_recv)
    cot_mover = Mover(s, cot, cot_out, cot_send, cot_recv)
    sender = Sender(send, recv)
    id_copies = []
    for i, source in enumerate((time_ids, freq_ids)):
        id_copies.append(sender.near(source, ids.at[s, i]))
        for ahead in range(1, 4):
            id_copies.append(sender.far(source, ids.at[s, i], lax.rem(s + ahead, 4)))
    patch_mover.start(MOVES)

    table_f32[...] = jnp.zeros_like(table_f32)
    table_f32[0:time_table.shape[0], :] = time_table[...]
    table_f32[FREQ_ROW:FREQ_ROW + freq_table.shape[0], :] = freq_table[...]
    high, low = split_high_low(table_f32[...])
    table[0:TABLE_ROWS, :] = high
    table[TABLE_ROWS:, :] = low
    spot = lax.broadcasted_iota(jnp.int32, (WORK, 1), 0)
    place = jnp.where(spot < OWN, jnp.where(spot < ROWS, spot + ROWS * c, spot + ROWS + 128 * c), shared_slots(spot - OWN + SHARED * s))
    limit = jnp.where(spot < OWN, jnp.where(x == 0, lengths[0], lengths[1]), lengths[2])
    valid_out[...] = jnp.broadcast_to(jnp.where(place < limit, 1.0, 0.0), valid_out.shape)
    id_out[...] = jnp.zeros_like(id_out)
    wait_all(id_copies)
    for device in range(4):
        @pl.when(s == device)
        def _(device=device):
            for home, clip, first, count, target, at in MOVES:
                if target == device:
                    for i in range(2):
                        id_out[i:i + 1, at:at + count] = ids[home, i, clip:clip + 1, first:first + count]

    bias = (query_bias[...].reshape(1, features), None, value_bias[...].reshape(1, features))

    def project(first, stage, at):
        rows = slice(first, first + SHARED)
        hot = one_hot(id_out[0:1, rows], id_out[1:2, rows])
        value = work[rows].astype(F32) + mm(jnp.concatenate([hot, hot], 0), table[...], TN)
        x_out[rows] = value
        xhat, _ = normalize(value)
        normed = (xhat * gain[...].reshape(1, features) + shift[...].reshape(1, features)).astype(BF16)
        n_out[rows] = normed
        for part in range(3):
            out = mm(normed, matrix[:, part * features:(part + 1) * features])
            if bias[part] is not None:
                out = out + bias[part]
            out = out.astype(BF16)
            for g in range(2 * groups):
                stage[part, g, at:at + SHARED] = out[:, g * 128:(g + 1) * 128]

    patch_mover.wait(SHARED_MOVES)
    wait_all(loads)
    project(OWN, shared_stage, 0)
    q_rows, kv_rows = span(SHARED * c, SHARED), span(SHARED * s, SHARED)
    mine, theirs = pl.ds(groups * c, groups), pl.ds(groups * other, groups)
    partner, across, diagonal = 2 * x + other, 2 * (1 - x) + c, 2 * (1 - x) + other
    shared_copies = [
        sender.far(shared_stage.at[0, theirs], shared_q_out.at[:, q_rows], partner),
        sender.far(shared_stage.at[1:3, theirs], shared_kv_out.at[:, :, kv_rows], partner),
        sender.far(shared_stage.at[1:3, mine], shared_kv_out.at[:, :, kv_rows], across),
        sender.far(shared_stage.at[1:3, theirs], shared_kv_out.at[:, :, kv_rows], diagonal),
        sender.near(shared_stage.at[0, mine], shared_q_out.at[:, q_rows]),
        sender.near(shared_stage.at[1:3, mine], shared_kv_out.at[:, :, kv_rows]),
    ]
    patch_mover.wait(OWN_MOVES)
    project(0, own_stage, 0)
    project(SHARED, own_stage, SHARED)
    own_rows = span(OWN * c, OWN)
    own_copies = [
        sender.far(own_stage.at[:, theirs], own_out.at[:, :, own_rows], partner),
        sender.near(own_stage.at[:, mine], own_out.at[:, :, own_rows]),
    ]
    cot_mover.start(MOVES)
    wait_all(own_copies)
    key_spot = lax.broadcasted_iota(jnp.int32, (1, KEYS), 1)
    attend(own_out.at[0], own_out.at[1], own_out.at[2], own_slots(key_spot) < jnp.where(x == 0, lengths[0], lengths[1]),
           own_mixed, own_log, log_wide, head_dim)
    mixed_copies = [
        sender.far(own_mixed.at[:, span(OWN * other, OWN)], mixed_out.at[mine, 0:OWN], partner),
        sender.near(own_mixed.at[:, own_rows], mixed_out.at[mine, 0:OWN]),
    ]
    wait_all(shared_copies)
    attend(shared_q_out, shared_kv_out.at[0], shared_kv_out.at[1], shared_slots(key_spot) < lengths[2],
           shared_mixed, shared_log, log_wide, head_dim)
    mixed_copies += [
        sender.far(shared_mixed.at[:, span(SHARED * other, SHARED)], mixed_out.at[mine, OWN:WORK], partner),
        sender.near(shared_mixed.at[:, q_rows], mixed_out.at[mine, OWN:WORK]),
    ]
    wait_all(mixed_copies)
    cot_mover.wait(MOVES)
    patch_mover.drain(MOVES)
    cot_mover.drain(MOVES)


def forward(lengths, patches, cot, time_ids, freq_ids, time_table, freq_table, gain, shift, weight, query_bias, value_bias, head_dim):
    features = patches.shape[2]
    groups = features // 256
    anywhere, vmem = pl.BlockSpec(memory_space=pl.ANY), pl.BlockSpec(memory_space=pltpu.VMEM)
    lanes = lambda *lead: jax.ShapeDtypeStruct(lead + (128,), BF16)
    dma = pltpu.SemaphoreType.DMA
    return pl.pallas_call(
        functools.partial(forward_body, head_dim),
        in_specs=[pl.BlockSpec(memory_space=pltpu.SMEM)] + [anywhere] * 4 + [vmem] * 4 + [anywhere] + [vmem] * 2,
        out_specs=[vmem] * 8 + [anywhere] + [vmem] * 2,
        out_shape=[
            jax.ShapeDtypeStruct((WORK, features), F32),
            jax.ShapeDtypeStruct((WORK, features), BF16),
            lanes(3, groups, KEYS),
            lanes(groups, OWN),
            lanes(2, groups, KEYS),
            jax.ShapeDtypeStruct((groups, 8, KEYS), F32),
            jax.ShapeDtypeStruct((groups, 8, OWN), F32),
            lanes(2 * groups, WORK),
            jax.ShapeDtypeStruct((WORK, features), BF16),
            jax.ShapeDtypeStruct((8, WORK), jnp.int32),
            jax.ShapeDtypeStruct((WORK, 128), F32),
        ],
        scratch_shapes=[
            pltpu.VMEM((WORK, features), BF16),
            pltpu.VMEM((TABLE_ROWS, features), F32),
            pltpu.VMEM((2 * TABLE_ROWS, features), BF16),
            pltpu.VMEM((4, 2) + time_ids.shape, jnp.int32),
            pltpu.VMEM(weight.shape, BF16),
            pltpu.VMEM((3, 2 * groups, OWN, 128), BF16),
            pltpu.VMEM((3, 2 * groups, SHARED, 128), BF16),
            pltpu.VMEM((groups, KEYS, 128), BF16),
            pltpu.VMEM((groups, OWN, 128), BF16),
            pltpu.VMEM((KEYS, 128), F32),
            dma((len(MOVES),)), dma((len(MOVES),)), dma((len(MOVES),)), dma((len(MOVES),)), dma((24,)), dma((24,)), dma((3,)),
        ],
        compiler_params=pltpu.CompilerParams(collective_id=1, has_side_effects=True, vmem_limit_bytes=60 * MIB),
    )(lengths, patches, cot, time_ids, freq_ids, time_table, freq_table, gain, shift, weight, query_bias, value_bias)


def middle_body(blocks, shares, valid, x_in, mixed_in, cot, out_weight, out_bias, gain, shift, up, up_bias, down, down_bias,
                out_ref, d_mixed_ref, d_x1_ref, g_down_a, g_down_b, g_up_a, g_up_b, g_out, small, up_bias_grad,
                mixed, x1, n2, n2_t, dm, dm_t, acc, d_n2, act_all, d_hidden_all):
    step = pl.program_id(0)
    groups, total, width = mixed_in.shape
    rows = total // blocks
    features = x_in.shape[1]
    share = features // shares

    flat = lambda ref: ref[...].reshape(1, ref.shape[0])

    @pl.when(step == 0)
    def _():
        small[...] = jnp.zeros_like(small)
        for c in range(blocks):
            span = slice(c * rows, (c + 1) * rows)
            for g in range(groups):
                mixed[span, g * width:(g + 1) * width] = mixed_in[g, span, :]
            after = x_in[span] + (mm(mixed[span], out_weight[...]) + flat(out_bias))
            x1[span] = after
            xhat, _ = normalize(after)
            n2[span] = (xhat * flat(gain) + flat(shift)).astype(BF16)
            dm[span] = (cot[span].astype(F32) * valid[span, 0:1]).astype(BF16)
        n2_t[...] = n2[...].T
        dm_t[...] = dm[...].T
        acc[...] = jnp.zeros_like(acc)
        d_n2[...] = jnp.zeros_like(d_n2)
        small[7:8, :] = row_sum(dm[...].astype(F32))

    tile_bias = up_bias[pl.ds(pl.multiple_of(step * up.shape[1], 128), up.shape[1])].reshape(1, up.shape[1])
    bias_sum = None
    for c in range(blocks):
        span = slice(c * rows, (c + 1) * rows)
        hidden = mm(n2[span], up[...]) + tile_bias
        half = 0.5 * (1.0 + lax.erf(hidden * (1.0 / math.sqrt(2.0))))
        act = (hidden * half).astype(BF16)
        slope = half + hidden * jnp.exp(hidden * hidden * -0.5) * (1.0 / math.sqrt(2.0 * math.pi))
        d_hidden = (slope * mm(dm[span], down[...], NT)).astype(BF16)
        act_all[span] = act
        d_hidden_all[span] = d_hidden
        acc[span] += mm(act, down[...])
        d_n2[span] += mm(d_hidden, up[...], NT)
        part = row_sum(d_hidden.astype(F32))
        bias_sum = part if bias_sum is None else bias_sum + part
    up_bias_grad[...] = bias_sum
    tile = up.shape[1]
    heights = g_down_a.shape[3], g_down_b.shape[2]
    reach = g_down_a.shape[4]
    for core in range(2):
        first = core * (features // 2)
        out = mm(dm_t[first:first + features // 2], act_all[...]).astype(BF16)
        for d in range(tile // reach):
            cols = slice(d * reach, (d + 1) * reach)
            for half_x in range(2):
                g_down_a[d, core, half_x] = out[half_x * heights[0]:(half_x + 1) * heights[0], cols]
            g_down_b[d, core] = out[2 * heights[0]:, cols]
    g_up_tile = mm(n2_t[...], d_hidden_all[...]).astype(BF16)

    @pl.when(step % 2 == 0)
    def _():
        wide = tile // 2
        for d in range(shares):
            for half_x in range(2):
                g_up_a[d, 0, half_x] = g_up_tile[d * share:(d + 1) * share, half_x * wide:(half_x + 1) * wide]

    @pl.when(step % 2 == 1)
    def _():
        for d in range(shares):
            g_up_b[d, 0] = g_up_tile[d * share:(d + 1) * share]

    @pl.when(step == pl.num_programs(0) - 1)
    def _():
        gain_sum = jnp.zeros((1, features), F32)
        shift_sum = jnp.zeros((1, features), F32)
        bias_out = jnp.zeros((1, features), F32)
        for c in range(blocks):
            span = slice(c * rows, (c + 1) * rows)
            ok = valid[span, 0:1]
            after = x1[span]
            out_ref[span] = (ok * (after + (acc[span] + flat(down_bias)))).astype(BF16)
            xhat, rstd = normalize(after)
            d_norm = d_n2[span]
            gain_sum += row_sum(d_norm * xhat)
            shift_sum += row_sum(d_norm)
            d_x1 = dm[span].astype(F32) + norm_back(d_norm, flat(gain), xhat, rstd)
            d_x1_ref[span] = d_x1
            d_a = d_x1.astype(BF16)
            n2[span] = d_a
            bias_out += row_sum(d_a.astype(F32))
            d_mixed = mm(d_a, out_weight[...], NT).astype(BF16)
            for g in range(groups):
                d_mixed_ref[g, span, :] = d_mixed[:, g * width:(g + 1) * width]
        out = mm(mixed[...].T, n2[...]).astype(BF16)
        for d in range(shares):
            for core in range(2):
                g_out[d, core] = out[d * share:(d + 1) * share, core * (features // 2):(core + 1) * (features // 2)]
        small[2:3, :] = bias_out
        small[5:6, :] = gain_sum
        small[6:7, :] = shift_sum


def middle(valid, x, mixed, cot, out_weight, out_bias, gain, shift, up, up_bias, down, down_bias, blocks, tile, shares):
    total, features = x.shape
    groups, _, width = mixed.shape
    hidden = up.shape[1]
    share, reach, half = features // shares, hidden // shares, features // 2
    spread = max(tile // reach, 1)
    whole = lambda a: pl.BlockSpec(a.shape, lambda j: (0,) * len(a.shape))
    outs = [
        jax.ShapeDtypeStruct((total, features), BF16),
        jax.ShapeDtypeStruct((groups, total, width), BF16),
        jax.ShapeDtypeStruct((total, features), F32),
        jax.ShapeDtypeStruct((shares, 2, 2, half // 4, reach), BF16),
        jax.ShapeDtypeStruct((shares, 2, half // 2, reach), BF16),
        jax.ShapeDtypeStruct((shares, 2, 2, share, hidden // 8), BF16),
        jax.ShapeDtypeStruct((shares, 2, share, hidden // 4), BF16),
        jax.ShapeDtypeStruct((shares, 2, share, half), BF16),
        jax.ShapeDtypeStruct((8, features), F32),
        jax.ShapeDtypeStruct((1, hidden), F32),
    ]
    cols = lambda height: pl.BlockSpec((height, tile), lambda j: (0, j))
    if tile >= reach:
        down_spec = lambda *mid: pl.BlockSpec((spread,) + mid + (reach,), lambda j: (j,) + (0,) * (len(mid) + 1))
    else:
        down_spec = lambda *mid: pl.BlockSpec((1,) + mid + (tile,), lambda j: (0,) * (len(mid) + 1) + (j,))
    return pl.pallas_call(
        functools.partial(middle_body, blocks, shares),
        grid_spec=pl.GridSpec(
            grid=(hidden // tile,),
            in_specs=[whole(valid), whole(x), whole(mixed), whole(cot), whole(out_weight), whole(out_bias), whole(gain), whole(shift),
                      cols(features), whole(up_bias), pl.BlockSpec((tile, features), lambda j: (j, 0)), whole(down_bias)],
            out_specs=[whole(outs[0]), whole(outs[1]), whole(outs[2]), down_spec(2, 2, half // 4), down_spec(2, half // 2),
                       pl.BlockSpec((shares, 1, 2, share, tile // 2), lambda j: (0, j // 2, 0, 0, 0)),
                       pl.BlockSpec((shares, 1, share, tile), lambda j: (0, j // 2, 0, 0)),
                       whole(outs[7]), whole(outs[8]), cols(1)],
            scratch_shapes=[
                pltpu.VMEM((total, features), BF16),
                pltpu.VMEM((total, features), F32),
                pltpu.VMEM((total, features), BF16),
                pltpu.VMEM((features, total), BF16),
                pltpu.VMEM((total, features), BF16),
                pltpu.VMEM((features, total), BF16),
                pltpu.VMEM((total, features), F32),
                pltpu.VMEM((total, features), F32),
                pltpu.VMEM((total, tile), BF16),
                pltpu.VMEM((total, tile), BF16),
            ],
        ),
        out_shape=outs,
        compiler_params=params(),
    )(valid, x, mixed, cot, out_weight, out_bias, gain, shift, up, up_bias, down, down_bias)


def attend_back(query, keys, values, d_mixed, logs, key_ok, d_query, d_keys, d_values, head_dim, block):
    count = query.shape[1]
    lane = lax.broadcasted_iota(jnp.int32, (1, 128), 1) // head_dim
    scale = BF16(1.0 / math.sqrt(head_dim))

    def pair(p, _):
        k, v = keys[p], values[p]
        k_t = (k * scale).T
        total_k = jnp.zeros((KEYS, 128), F32)
        total_v = jnp.zeros((KEYS, 128), F32)
        for first in range(0, count, block):
            last = min(first + block, count)
            q_block = query[p, first:last] * scale
            m_block = d_mixed[p, first:last]
            parts = []
            for h in range(128 // head_dim):
                q_head = jnp.where(lane == h, q_block, BF16(0))
                m_head = jnp.where(lane == h, m_block, BF16(0))
                scores = jnp.where(key_ok, mm(k, q_head, NT), NEGATIVE)
                probs = jnp.exp(scores - logs[p, h:h + 1, first:last])
                total_v = total_v + mm(probs.astype(BF16), m_head)
                weighted = probs * mm(v, m_head, NT)
                d_scores = (weighted - probs * row_sum(weighted)).astype(BF16)
                total_k = total_k + mm(d_scores, q_head)
                parts.append(mm(k_t[h * head_dim:(h + 1) * head_dim], d_scores))
            d_query[p, first:last] = jnp.concatenate(parts, 0).T.astype(BF16)
        d_keys[p] = total_k.astype(BF16)
        d_values[p] = total_v.astype(BF16)
        return 0

    lax.fori_loop(0, query.shape[0], pair, 0)


def backward_body(head_dim, shares, lengths, d_mixed, own, shared_q, shared_kv, own_log, shared_log, weight, normed, x_in, d_x1, ids, gain,
                  small_in, up_bias_grad, out_work,
                  output, d_patches, g_qkv_a, g_qkv_b, packed,
                  own_dm, shared_dm, own_d, shared_dq, shared_dkv, other_dkv, joined_lanes, joined, d_work, high_low, small, zeros, matrix,
                  out_send, out_recv, d_send, d_recv, send, recv, weight_sem, zero_sem):
    s, x, c = seq_place()
    total, features = x_in.shape
    groups = own.shape[1]
    other = 1 - c
    partner, across = 2 * x + other, 2 * (1 - x) + c
    mine, theirs = pl.ds(groups * c, groups), pl.ds(groups * other, groups)
    own_rows, q_rows = span(OWN * c, OWN), span(SHARED * c, SHARED)
    load = pltpu.make_async_copy(weight, matrix, weight_sem.at[0])
    load.start()
    zeros[...] = jnp.zeros_like(zeros)
    greet_group(s)
    sender = Sender(send, recv)
    shared_copies = [
        sender.far(d_mixed.at[theirs, OWN:WORK], shared_dm.at[:, q_rows], partner),
        sender.near(d_mixed.at[mine, OWN:WORK], shared_dm.at[:, q_rows]),
    ]
    own_copies = [
        sender.far(d_mixed.at[theirs, 0:OWN], own_dm.at[:, own_rows], partner),
        sender.near(d_mixed.at[mine, 0:OWN], own_dm.at[:, own_rows]),
    ]
    out_mover = Mover(s, output, out_work, out_send, out_recv, True)
    d_mover = Mover(s, d_patches, d_work, d_send, d_recv, True)

    def fill(act):
        @pl.when(s == UNUSED[0])
        def _():
            for i, array in enumerate((output, d_patches)):
                for clip in range(3):
                    act(pltpu.make_async_copy(zeros, array.at[clip, pl.ds(UNUSED[1], ROWS - UNUSED[1])], zero_sem.at[3 * i + clip]))

    fill(lambda made: made.start())
    key_spot = lax.broadcasted_iota(jnp.int32, (KEYS, 1), 0)
    wait_all(shared_copies)
    attend_back(shared_q, shared_kv.at[0], shared_kv.at[1], shared_dm, shared_log, shared_slots(key_spot) < lengths[2],
                shared_dq, shared_dkv.at[0], shared_dkv.at[1], head_dim, 256)
    kv_copy = sender.far(shared_dkv.at[:, :, span(OWN * (1 - x), OWN)], other_dkv, across)
    out_mover.start(MOVES)
    wait_all(own_copies)
    attend_back(own.at[0], own.at[1], own.at[2], own_dm, own_log, own_slots(key_spot) < jnp.where(x == 0, lengths[0], lengths[1]),
                own_d.at[0], own_d.at[1], own_d.at[2], head_dim, 256)
    own_copies = [
        sender.far(own_d.at[:, :, span(OWN * other, OWN)], joined_lanes.at[:, mine, 0:OWN], partner),
        sender.near(own_d.at[:, :, own_rows], joined_lanes.at[:, mine, 0:OWN]),
    ]
    kv_copy.wait()
    for i in range(2):
        for g in range(groups):
            rows = span(OWN * x, OWN)
            shared_dkv[i, g, rows] = shared_dkv[i, g, rows] + other_dkv[i, g]
    shared_copies = []
    for to, peer in ((other, partner), (c, None)):
        q_part = shared_dq.at[:, span(SHARED * to, SHARED)]
        kv_part = shared_dkv.at[:, :, span(OWN * x + SHARED * to, SHARED)]
        q_place, kv_place = joined_lanes.at[0, mine, OWN:WORK], joined_lanes.at[1:3, mine, OWN:WORK]
        if peer is None:
            shared_copies += [sender.near(q_part, q_place), sender.near(kv_part, kv_place)]
        else:
            shared_copies += [sender.far(q_part, q_place, peer), sender.far(kv_part, kv_place, peer)]
    load.wait()
    small[0:8, :] = small_in[...]
    small[8:, :] = jnp.zeros((small.shape[0] - 8, features), F32)
    sums = [jnp.zeros((1, features), F32)] * 4
    tables = jnp.zeros((TABLE_ROWS, 2 * features), F32)
    wait_all(own_copies)
    for first in range(0, total, SHARED):
        if first == OWN:
            wait_all(shared_copies)
        rows = slice(first, first + SHARED)
        for part in range(3):
            for g in range(2 * groups):
                at = (part * 2 * groups + g) * 128
                joined[rows, at:at + 128] = joined_lanes[part, g, rows]
        d_norm = mm(joined[rows], matrix[...], NT)
        xhat, rstd = normalize(x_in[rows])
        terms = (joined[rows, 0:features].astype(F32), joined[rows, 2 * features:].astype(F32), d_norm * xhat, d_norm)
        sums = [a + row_sum(b) for a, b in zip(sums, terms)]
        d_x = d_x1[rows] + norm_back(d_norm, gain[...].reshape(1, features), xhat, rstd)
        high, low = split_high_low(d_x)
        d_work[rows] = high
        tables = tables + mm(one_hot(ids[0:1, rows], ids[1:2, rows]), jnp.concatenate([high, low], 1))
        if first + SHARED == OWN:
            d_mover.start(OWN_MOVES)
    d_mover.start(SHARED_MOVES)
    normed_t = normed[...].T
    half = 3 * features // 2
    wide = g_qkv_a.shape[4]
    share = features // shares
    for core in range(2):
        out = mm(normed_t, joined[:, core * half:(core + 1) * half]).astype(BF16)
        for d in range(shares):
            rows = slice(d * share, (d + 1) * share)
            for half_x in range(2):
                g_qkv_a[d, core, half_x] = out[rows, half_x * wide:(half_x + 1) * wide]
            g_qkv_b[d, core] = out[rows, 2 * wide:]
    small[16:16 + TABLE_ROWS, :] = tables[:, 0:features] + tables[:, features:]
    for row, value in zip((0, 1, 3, 4), sums):
        small[row:row + 1, :] = value
    repeat = up_bias_grad.shape[1] // features
    height = packed.shape[2]
    if share != packed.shape[3]:
        packed[...] = jnp.zeros_like(packed)
    for d in range(shares):
        for r in range(repeat):
            first = (d * repeat + r) * share
            small[8 + r:9 + r, d * share:(d + 1) * share] = up_bias_grad[:, first:first + share]
        for core in range(2):
            packed[d, core, :, 0:share] = small[core * height:(core + 1) * height, d * share:(d + 1) * share].astype(BF16)
    out_mover.wait(MOVES)
    d_mover.wait(MOVES)
    out_mover.drain(MOVES)
    d_mover.drain(MOVES)
    fill(lambda made: made.wait())


def backward(lengths, d_mixed, own, shared_q, shared_kv, own_log, shared_log, weight, normed, x, d_x1, ids, gain, small, up_bias_grad, out_work,
             head_dim, shares):
    total, features = x.shape
    groups = own.shape[1]
    share = features // shares
    half = 3 * features // 2
    wide = half * 2 // 9
    anywhere, vmem = pl.BlockSpec(memory_space=pl.ANY), pl.BlockSpec(memory_space=pltpu.VMEM)
    dma = pltpu.SemaphoreType.DMA
    lanes = lambda *lead: pltpu.VMEM(lead + (128,), BF16)
    moves = len(MOVES)
    return pl.pallas_call(
        functools.partial(backward_body, head_dim, shares),
        in_specs=[pl.BlockSpec(memory_space=pltpu.SMEM), anywhere] + [vmem] * 5 + [anywhere] + [vmem] * 7 + [anywhere],
        out_specs=[anywhere] * 2 + [vmem] * 3,
        out_shape=[
            jax.ShapeDtypeStruct((3, ROWS, features), BF16),
            jax.ShapeDtypeStruct((3, ROWS, features), BF16),
            jax.ShapeDtypeStruct((shares, 2, 2, share, wide), BF16),
            jax.ShapeDtypeStruct((shares, 2, share, half - 2 * wide), BF16),
            jax.ShapeDtypeStruct((shares, 2, SMALL_ROWS // 2, -(-share // 128) * 128), BF16),
        ],
        scratch_shapes=[
            lanes(groups, KEYS), lanes(groups, OWN), lanes(3, groups, KEYS), lanes(groups, OWN), lanes(2, groups, KEYS), lanes(2, groups, OWN),
            lanes(3, 2 * groups, WORK),
            pltpu.VMEM((total, 3 * features), BF16),
            pltpu.VMEM((total, features), BF16),
            pltpu.VMEM((8, 128), BF16),
            pltpu.VMEM((SMALL_ROWS, features), F32),
            pltpu.VMEM((ROWS - UNUSED[1], features), BF16),
            pltpu.VMEM(weight.shape, BF16),
            dma((moves,)), dma((moves,)), dma((moves,)), dma((moves,)), dma((16,)), dma((16,)), dma((1,)), dma((6,)),
        ],
        compiler_params=pltpu.CompilerParams(collective_id=2, has_side_effects=True, vmem_limit_bytes=60 * MIB),
    )(lengths, d_mixed, own, shared_q, shared_kv, own_log, shared_log, weight, normed, x, d_x1, ids, gain, small, up_bias_grad, out_work)


class Flow:
    def __init__(self, source, result, refs, place):
        self.source, self.result = source, result
        self.split = len(source.shape) == 5
        self.own, self.got, self.x_got, self.y_got, self.z_got, self.send, self.recv = refs
        self.z, self.y, self.x, self.c = place
        self.open = {}
        if self.split:
            self.stages = [self.begin, self.cores_x, self.x_y, self.y_z, self.z_fill, self.fill_cores, self.end]
        else:
            self.stages = [self.begin, self.cores_y, self.y_z, self.z_x, self.x_cores, self.end]
        self.used = 0

    def copy(self, key, source, target, peer):
        z, y, x, c = peer
        slot = self.used
        self.used += 1
        made = pltpu.make_async_remote_copy(
            src_ref=source, dst_ref=target, send_sem=self.send.at[slot], recv_sem=self.recv.at[slot],
            device_id=(z * 2 + y, x * 2 + c), device_id_type=pl.DeviceIdType.MESH)
        made.start()
        self.open.setdefault(key, []).append(made)

    def wait(self, key):
        for made in self.open.pop(key):
            made.wait()

    def at(self, ref, z, y):
        return ref.at[z * 2 + y, self.x] if self.split else ref.at[z * 2 + y]

    def begin(self):
        made = pltpu.make_async_copy(self.source.at[:, self.c], self.own, self.send.at[self.used])
        self.used += 1
        made.start()
        self.open["own"] = [made]
        self.copy("core", self.source.at[:, 1 - self.c], self.got, (self.z, self.y, self.x, 1 - self.c))

    def cores(self):
        self.wait("own")
        self.wait("core")

        def add(i, _):
            self.own[i] = self.own[i] + self.got[i]
            return 0

        lax.fori_loop(0, self.own.shape[0], add, 0)

    def cores_x(self):
        self.cores()
        self.copy("x", self.own.at[:, 1 - self.x], self.x_got, (self.z, self.y, 1 - self.x, self.c))

    def cores_y(self):
        self.cores()
        self.to_y()

    def to_y(self):
        for z in range(4):
            self.copy("y", self.at(self.own, z, 1 - self.y), self.y_got.at[z], (self.z, 1 - self.y, self.x, self.c))

    def x_y(self):
        self.wait("x")

        def add(i, _):
            self.own[i, self.x] = self.own[i, self.x] + self.x_got[i]
            return 0

        lax.fori_loop(0, self.own.shape[0], add, 0)
        self.to_y()

    def y_z(self):
        self.wait("y")

        def add(z, _):
            spot = self.at(self.own, z, self.y)
            spot[...] = spot[...] + self.y_got[z]
            return 0

        lax.fori_loop(0, 4, add, 0)
        for ahead in range(1, 4):
            z = lax.rem(self.z + ahead, 4)
            self.copy("z", self.at(self.own, z, self.y), self.z_got.at[ahead - 1], (z, self.y, self.x, self.c))

    def z_sum(self):
        self.wait("z")
        total = self.at(self.own, self.z, self.y)[...].astype(F32)
        for i in range(3):
            total = total + self.z_got[i].astype(F32)
        return total.astype(BF16)

    def z_fill(self):
        self.result[self.c, self.x] = self.z_sum()
        spot = self.result.at[self.c, self.x]
        self.copy("fill", spot, spot, (self.z, self.y, 1 - self.x, self.c))

    def fill_cores(self):
        self.wait("fill")
        self.to_core()

    def z_x(self):
        spot = self.at(self.own, self.z, self.y)
        spot[...] = self.z_sum()
        self.copy("x", spot, self.x_got, (self.z, self.y, 1 - self.x, self.c))

    def x_cores(self):
        self.wait("x")
        self.result[self.c] = self.at(self.own, self.z, self.y)[...] + self.x_got[...]
        self.to_core()

    def to_core(self):
        spot = self.result.at[self.c]
        self.copy("end", spot, spot, (self.z, self.y, self.x, 1 - self.c))

    def end(self):
        self.wait("end")


def flow_scratch(shape):
    shares, tail = shape[0], shape[2:]
    block = tail[-2:]
    first = (shares,) + block if len(tail) == 3 else block
    slots = 16
    return [pltpu.VMEM((shares,) + tail, BF16), pltpu.VMEM((shares,) + tail, BF16), pltpu.VMEM(first, BF16),
            pltpu.VMEM((4,) + block, BF16), pltpu.VMEM((3,) + block, BF16),
            pltpu.SemaphoreType.DMA((slots,)), pltpu.SemaphoreType.DMA((slots,))]


FLOW_REFS = 7


def place_of():
    d, s = lax.axis_index("dp"), lax.axis_index("seq")
    return d // 2, d % 2, s // 2, s % 2


def greet(place):
    z, y, x, c = place
    peers = [(z, y, x, 1 - c), (z, y, 1 - x, c), (z, 1 - y, x, c)] + [(lax.rem(z + i, 4), y, x, c) for i in range(1, 4)]
    barrier = pltpu.get_barrier_semaphore()
    for pz, py, px, pc in peers:
        pl.semaphore_signal(barrier, inc=1, device_id=(pz * 2 + py, px * 2 + pc), device_id_type=pl.DeviceIdType.MESH)
    pl.semaphore_wait(barrier, len(peers))


def reduce_body(count, *refs):
    sources, results, rest = refs[:count], refs[count:2 * count], refs[2 * count:]
    place = place_of()
    greet(place)
    flows = [Flow(sources[i], results[i], rest[i * FLOW_REFS:(i + 1) * FLOW_REFS], place) for i in range(count)]
    for level in range(7):
        for flow in flows:
            if level < len(flow.stages):
                flow.stages[level]()


def reduce_pieces(pieces):
    return pl.pallas_call(
        functools.partial(reduce_body, len(pieces)),
        in_specs=[pl.BlockSpec(memory_space=pl.ANY)] * len(pieces),
        out_shape=[jax.ShapeDtypeStruct(p.shape[1:], BF16) for p in pieces],
        scratch_shapes=[ref for p in pieces for ref in flow_scratch(p.shape)],
        compiler_params=pltpu.CompilerParams(collective_id=0, has_side_effects=True, vmem_limit_bytes=60 * MIB),
    )(*pieces)


def join_columns(halves, rest):
    parts = []
    for core in range(2):
        parts += [halves[core, 0], halves[core, 1], rest[core]]
    return jnp.concatenate(parts, 1)


def join_rows(halves, rest):
    parts = []
    for core in range(2):
        parts += [halves[core, 0], halves[core, 1], rest[core]]
    return jnp.concatenate(parts, 0)


def collect(down_a, down_b, up_a, up_b, out, qkv_a, qkv_b, packed, finish_part):
    small = packed.reshape(SMALL_ROWS, packed.shape[2])
    return (
        finish_part(join_columns(qkv_a, qkv_b), 0),
        finish_part(jnp.concatenate([out[0], out[1]], 1), 0),
        finish_part(join_columns(up_a, up_b), 0),
        finish_part(join_rows(down_a, down_b), 1).T,
        finish_part(small, 1),
    )


def reduce_all(pieces, custom, features, hidden, time_count, freq_count):
    if custom:
        qkv, out, up, down, small = collect(*reduce_pieces(pieces), lambda v, axis: v.astype(F32))
        small = small[:, 0:features // lax.axis_size("dp")]
    else:
        def total(part, axis):
            return lax.psum(lax.psum_scatter(part, "dp", scatter_dimension=axis, tiled=True), "seq").astype(F32)

        qkv, out, up, down, small = collect(*(p[0] for p in pieces), total)
    repeat = hidden // features
    up_bias = small[8:8 + repeat].reshape(-1)
    return (
        qkv, small[0], small[1], out, small[2], small[3], small[4], small[5], small[6], up, up_bias, down, small[7],
        small[16:16 + time_count], small[16 + FREQ_ROW:16 + FREQ_ROW + freq_count],
    )


def shards(
    patches,
    cotangent,
    time_ids,
    freq_ids,
    lengths,
    qkv_weight,
    query_bias,
    value_bias,
    out_weight,
    out_bias,
    norm1_gain,
    norm1_shift,
    norm2_gain,
    norm2_shift,
    up_weight,
    up_bias,
    down_weight,
    down_bias,
    time_table,
    freq_table,
):
    features = patches.shape[2]
    head_dim = features // HEADS
    assert patches.shape[:2] == (3, ROWS) and lax.axis_size("seq") == 4
    custom = lax.axis_size("dp") == 8
    shares = 8 if custom else 1
    x, normed, own, shared_q, shared_kv, own_log, shared_log, mixed, cot, ids, valid = forward(
        lengths, patches, cotangent, time_ids, freq_ids, time_table, freq_table, norm1_gain, norm1_shift, qkv_weight, query_bias, value_bias,
        head_dim
    )
    out_work, d_mixed, d_x1, down_a, down_b, up_a, up_b, g_out, small, up_bias_grad = middle(
        valid, x, mixed, cot, out_weight, out_bias, norm2_gain, norm2_shift, up_weight, up_bias, down_weight, down_bias, 3,
        up_weight.shape[1] // 4, shares
    )
    output, d_patch, qkv_a, qkv_b, packed = backward(
        lengths, d_mixed, own, shared_q, shared_kv, own_log, shared_log, qkv_weight, normed, x, d_x1, ids, norm1_gain, small, up_bias_grad,
        out_work, head_dim, shares
    )
    return (output, d_patch) + reduce_all(
        (down_a, down_b, up_a, up_b, g_out, qkv_a, qkv_b, packed), custom, features, up_weight.shape[1], time_table.shape[0],
        freq_table.shape[0]
    )


def solution(mesh):
    clip_spec, row_spec, one = P("dp", "seq", None), P("dp", "seq"), P("dp")
    matrix = P("dp", None)
    return jax.shard_map(
        shards,
        mesh=mesh,
        in_specs=(clip_spec, clip_spec, row_spec, row_spec, one) + (P(),) * 15,
        out_specs=(clip_spec, clip_spec, matrix, one, one, matrix, one, one, one, one, one, matrix, one, matrix, one, P(None, "dp"), P(None, "dp")),
        check_vma=False,
    )
```

```python
import functools
import math

import jax
import jax.numpy as jnp
from jax import lax
from jax.experimental import pallas as pl
from jax.experimental.pallas import tpu as pltpu
from jax.sharding import PartitionSpec as P

HEADS = 12
EPS = 1e-06
NEGATIVE = -1000000000.0
FREQ_ROW = 104
TABLE_ROWS = 128
SMALL_ROWS = 32 + TABLE_ROWS
TILES = 3
F32 = jnp.float32
BF16 = jnp.bfloat16
NN = (((1,), (0,)), ((), ()))
NT = (((1,), (1,)), ((), ()))
TN = (((0,), (0,)), ((), ()))
MIB = 1 << 20


def mm(left, right, dims=NN):
    return lax.dot_general(left, right, dims, preferred_element_type=F32)


def params(limit=60):
    return pltpu.CompilerParams(vmem_limit_bytes=limit * MIB)


def row_sum(values):
    return jnp.sum(values, 0, keepdims=True)


def normalize(values):
    center = values - jnp.mean(values, -1, keepdims=True)
    rstd = lax.rsqrt(jnp.mean(center * center, -1, keepdims=True) + EPS)
    return center * rstd, rstd


def norm_back(d_out, gain, xhat, rstd):
    u = d_out * gain
    inner = jnp.mean(u * xhat, -1, keepdims=True)
    return rstd * (u - jnp.mean(u, -1, keepdims=True) - xhat * inner)


def split_high_low(values):
    high = values.astype(BF16)
    return high, (values - high.astype(F32)).astype(BF16)


def one_hot(time_row, freq_row):
    spot = lax.broadcasted_iota(jnp.int32, (TABLE_ROWS, time_row.shape[1]), 0)
    hit = (spot == time_row) | (spot == freq_row + FREQ_ROW)
    return jnp.where(hit, 1.0, 0.0).astype(BF16)


ROWS = 224
OWN = 352
SHARED = 176
WORK = OWN + SHARED
KEYS = 2 * OWN
SHARED_MOVES = (
    (0, 2, 176, 48, 3, 384), (1, 2, 176, 48, 3, 432), (2, 2, 176, 48, 3, 480), (3, 2, 0, 32, 3, 352),
    (0, 2, 0, 176, 0, 352), (1, 2, 0, 176, 1, 352), (2, 2, 0, 176, 2, 352),
)
OWN_MOVES = (
    (2, 0, 0, 128, 0, 224), (2, 0, 128, 96, 1, 224), (3, 0, 0, 32, 1, 320), (0, 1, 0, 224, 2, 0), (1, 1, 0, 224, 3, 0),
    (2, 1, 128, 96, 3, 224), (2, 1, 0, 128, 2, 224), (3, 1, 0, 32, 3, 320), (0, 0, 0, 224, 0, 0), (1, 0, 0, 224, 1, 0),
)
MOVES = SHARED_MOVES + OWN_MOVES
UNUSED = (3, 32)


def seq_place():
    s = lax.axis_index("seq")
    return s, s // 2, lax.rem(s, 2)


def seq_peer(s):
    return {"seq": s}


def greet_group(s):
    barrier = pltpu.get_barrier_semaphore()
    for ahead in range(1, 4):
        pl.semaphore_signal(barrier, inc=1, device_id=seq_peer(lax.rem(s + ahead, 4)), device_id_type=pl.DeviceIdType.MESH)
    pl.semaphore_wait(barrier, 3)


class Mover:
    def __init__(self, s, at_home, at_work, send, recv, back=False):
        self.s, self.at_home, self.at_work, self.send, self.recv, self.back = s, at_home, at_work, send, recv, back

    def ends(self, move):
        home, clip, first, count, work, spot = move
        a, b = self.at_home.at[clip, pl.ds(first, count)], self.at_work.at[pl.ds(spot, count)]
        return (work, b, home, a) if self.back else (home, a, work, b)

    def each(self, moves, which, act, near=True):
        for device in range(4):
            chosen = [m for m in moves if self.ends(m)[which] == device and (near or self.ends(m)[0] != self.ends(m)[2])]
            if not chosen:
                continue

            @pl.when(self.s == device)
            def _(chosen=chosen):
                for m in chosen:
                    src_device, src, dst_device, dst = self.ends(m)
                    slot = MOVES.index(m)
                    if src_device == dst_device:
                        act(False, pltpu.make_async_copy(src, dst, self.recv.at[slot]))
                    else:
                        act(True, pltpu.make_async_remote_copy(
                            src_ref=src, dst_ref=dst, send_sem=self.send.at[slot], recv_sem=self.recv.at[slot],
                            device_id=seq_peer(dst_device), device_id_type=pl.DeviceIdType.MESH))

    def start(self, moves):
        self.each(moves, 0, lambda far, made: made.start())

    def wait(self, moves):
        self.each(moves, 2, lambda far, made: made.wait_recv() if far else made.wait())

    def drain(self, moves):
        self.each(moves, 0, lambda far, made: made.wait_send(), False)


class Sender:
    def __init__(self, send, recv):
        self.send, self.recv, self.used = send, recv, 0

    def far(self, source, target, peer, begin=True):
        made = pltpu.make_async_remote_copy(
            src_ref=source, dst_ref=target, send_sem=self.send.at[self.used], recv_sem=self.recv.at[self.used],
            device_id=seq_peer(peer), device_id_type=pl.DeviceIdType.MESH)
        self.used += 1
        if begin:
            made.start()
        return made

    def near(self, source, target, begin=True):
        made = pltpu.make_async_copy(source, target, self.recv.at[self.used])
        self.used += 1
        if begin:
            made.start()
        return made


def wait_all(copies):
    for made in copies:
        made.wait()


def shift_between(spot, cuts):
    slot = spot
    for low, high, shift in cuts:
        slot = jnp.where((spot >= low) & (spot < high), spot + shift, slot)
    return slot


def own_slots(spot):
    return shift_between(spot, ((224, 352, 224), (352, 576, -128)))


def shared_slots(spot):
    return shift_between(spot, ((176, 352, 48), (352, 528, 96), (528, 560, 144), (560, 608, -384), (608, 656, -208), (656, 704, -32)))


def span(first, size):
    return pl.ds(pl.multiple_of(first, 16), size)


def attend(query, keys, values, key_ok, mixed_out, log_out, log_wide, head_dim):
    count = query.shape[1]
    lane = lax.broadcasted_iota(jnp.int32, (1, 128), 1) // head_dim
    wide = lax.broadcasted_iota(jnp.int32, (SHARED, 128), 1)
    scale = BF16(1.0 / math.sqrt(head_dim))

    def pair(p, _):
        k, v = keys[p], values[p]
        for first in range(0, count, SHARED):
            q = query[p, first:first + SHARED] * scale
            mixed = jnp.zeros((SHARED, 128), F32)
            logs = jnp.zeros((SHARED, 128), F32)
            for h in range(128 // head_dim):
                scores = jnp.where(key_ok, mm(jnp.where(lane == h, q, BF16(0)), k, NT), NEGATIVE)
                highest = jnp.max(scores, -1, keepdims=True)
                powers = jnp.exp(scores - highest)
                total = jnp.sum(powers, -1, keepdims=True)
                out = mm(powers.astype(BF16), v) * (1.0 / total)
                mixed = jnp.where(lane == h, out, mixed)
                logs = jnp.where(wide == h, highest + jnp.log(total), logs)
            mixed_out[p, first:first + SHARED] = mixed.astype(BF16)
            log_wide[first:first + SHARED] = logs
        log_out[p] = log_wide[0:count].T[0:8]
        return 0

    lax.fori_loop(0, query.shape[0], pair, 0)


def forward_body(head_dim, lengths, patches, cot, time_ids, freq_ids, time_table, freq_table, gain, shift, weight, query_bias, value_bias,
                 x_out, n_out, own_out, shared_q_out, shared_kv_out, own_log, shared_log, mixed_out, cot_out, id_out, valid_out,
                 work, table_f32, table, ids, matrix, own_stage, shared_stage, own_mixed, shared_mixed, log_wide,
                 patch_send, patch_recv, cot_send, cot_recv, send, recv, weight_sem):
    s, x, c = seq_place()
    features = x_out.shape[1]
    groups = own_out.shape[1]
    other = 1 - c
    loads = [pltpu.make_async_copy(weight.at[:, pl.ds(p * features, features)], matrix.at[:, pl.ds(p * features, features)], weight_sem.at[p])
             for p in range(3)]
    for load in loads:
        load.start()
    greet_group(s)
    patch_mover = Mover(s, patches, work, patch_send, patch_recv)
    cot_mover = Mover(s, cot, cot_out, cot_send, cot_recv)
    sender = Sender(send, recv)
    id_copies = []
    for i, source in enumerate((time_ids, freq_ids)):
        id_copies.append(sender.near(source, ids.at[s, i]))
        for ahead in range(1, 4):
            id_copies.append(sender.far(source, ids.at[s, i], lax.rem(s + ahead, 4)))
    patch_mover.start(MOVES)

    table_f32[...] = jnp.zeros_like(table_f32)
    table_f32[0:time_table.shape[0], :] = time_table[...]
    table_f32[FREQ_ROW:FREQ_ROW + freq_table.shape[0], :] = freq_table[...]
    high, low = split_high_low(table_f32[...])
    table[0:TABLE_ROWS, :] = high
    table[TABLE_ROWS:, :] = low
    spot = lax.broadcasted_iota(jnp.int32, (WORK, 1), 0)
    place = jnp.where(spot < OWN, jnp.where(spot < ROWS, spot + ROWS * c, spot + ROWS + 128 * c), shared_slots(spot - OWN + SHARED * s))
    limit = jnp.where(spot < OWN, jnp.where(x == 0, lengths[0], lengths[1]), lengths[2])
    valid_out[...] = jnp.broadcast_to(jnp.where(place < limit, 1.0, 0.0), valid_out.shape)
    id_out[...] = jnp.zeros_like(id_out)
    wait_all(id_copies)
    for device in range(4):
        @pl.when(s == device)
        def _(device=device):
            for home, clip, first, count, target, at in MOVES:
                if target == device:
                    for i in range(2):
                        id_out[i:i + 1, at:at + count] = ids[home, i, clip:clip + 1, first:first + count]

    bias = (query_bias[...].reshape(1, features), None, value_bias[...].reshape(1, features))

    def project(first, stage, at):
        rows = slice(first, first + SHARED)
        hot = one_hot(id_out[0:1, rows], id_out[1:2, rows])
        value = work[rows].astype(F32) + mm(jnp.concatenate([hot, hot], 0), table[...], TN)
        x_out[rows] = value
        xhat, _ = normalize(value)
        normed = (xhat * gain[...].reshape(1, features) + shift[...].reshape(1, features)).astype(BF16)
        n_out[rows] = normed
        for part in range(3):
            out = mm(normed, matrix[:, part * features:(part + 1) * features])
            if bias[part] is not None:
                out = out + bias[part]
            out = out.astype(BF16)
            for g in range(2 * groups):
                stage[part, g, at:at + SHARED] = out[:, g * 128:(g + 1) * 128]

    patch_mover.wait(SHARED_MOVES)
    wait_all(loads)
    project(OWN, shared_stage, 0)
    q_rows, kv_rows = span(SHARED * c, SHARED), span(SHARED * s, SHARED)
    mine, theirs = pl.ds(groups * c, groups), pl.ds(groups * other, groups)
    partner, across, diagonal = 2 * x + other, 2 * (1 - x) + c, 2 * (1 - x) + other
    shared_copies = [
        sender.far(shared_stage.at[0, theirs], shared_q_out.at[:, q_rows], partner),
        sender.far(shared_stage.at[1:3, theirs], shared_kv_out.at[:, :, kv_rows], partner),
        sender.far(shared_stage.at[1:3, mine], shared_kv_out.at[:, :, kv_rows], across),
        sender.far(shared_stage.at[1:3, theirs], shared_kv_out.at[:, :, kv_rows], diagonal),
        sender.near(shared_stage.at[0, mine], shared_q_out.at[:, q_rows]),
        sender.near(shared_stage.at[1:3, mine], shared_kv_out.at[:, :, kv_rows]),
    ]
    patch_mover.wait(OWN_MOVES)
    project(0, own_stage, 0)
    project(SHARED, own_stage, SHARED)
    own_rows = span(OWN * c, OWN)
    own_copies = [
        sender.far(own_stage.at[:, theirs], own_out.at[:, :, own_rows], partner),
        sender.near(own_stage.at[:, mine], own_out.at[:, :, own_rows]),
    ]
    cot_mover.start(MOVES)
    wait_all(own_copies)
    key_spot = lax.broadcasted_iota(jnp.int32, (1, KEYS), 1)
    attend(own_out.at[0], own_out.at[1], own_out.at[2], own_slots(key_spot) < jnp.where(x == 0, lengths[0], lengths[1]),
           own_mixed, own_log, log_wide, head_dim)
    mixed_copies = [
        sender.far(own_mixed.at[:, span(OWN * other, OWN)], mixed_out.at[mine, 0:OWN], partner),
        sender.near(own_mixed.at[:, own_rows], mixed_out.at[mine, 0:OWN]),
    ]
    wait_all(shared_copies)
    attend(shared_q_out, shared_kv_out.at[0], shared_kv_out.at[1], shared_slots(key_spot) < lengths[2],
           shared_mixed, shared_log, log_wide, head_dim)
    mixed_copies += [
        sender.far(shared_mixed.at[:, span(SHARED * other, SHARED)], mixed_out.at[mine, OWN:WORK], partner),
        sender.near(shared_mixed.at[:, q_rows], mixed_out.at[mine, OWN:WORK]),
    ]
    wait_all(mixed_copies)
    cot_mover.wait(MOVES)
    patch_mover.drain(MOVES)
    cot_mover.drain(MOVES)


def forward(lengths, patches, cot, time_ids, freq_ids, time_table, freq_table, gain, shift, weight, query_bias, value_bias, head_dim):
    features = patches.shape[2]
    groups = features // 256
    anywhere, vmem = pl.BlockSpec(memory_space=pl.ANY), pl.BlockSpec(memory_space=pltpu.VMEM)
    lanes = lambda *lead: jax.ShapeDtypeStruct(lead + (128,), BF16)
    dma = pltpu.SemaphoreType.DMA
    return pl.pallas_call(
        functools.partial(forward_body, head_dim),
        in_specs=[pl.BlockSpec(memory_space=pltpu.SMEM)] + [anywhere] * 4 + [vmem] * 4 + [anywhere] + [vmem] * 2,
        out_specs=[vmem] * 11,
        out_shape=[
            jax.ShapeDtypeStruct((WORK, features), F32),
            jax.ShapeDtypeStruct((WORK, features), BF16),
            lanes(3, groups, KEYS),
            lanes(groups, OWN),
            lanes(2, groups, KEYS),
            jax.ShapeDtypeStruct((groups, 8, KEYS), F32),
            jax.ShapeDtypeStruct((groups, 8, OWN), F32),
            lanes(2 * groups, WORK),
            jax.ShapeDtypeStruct((WORK, features), BF16),
            jax.ShapeDtypeStruct((8, WORK), jnp.int32),
            jax.ShapeDtypeStruct((WORK, 128), F32),
        ],
        scratch_shapes=[
            pltpu.VMEM((WORK, features), BF16),
            pltpu.VMEM((TABLE_ROWS, features), F32),
            pltpu.VMEM((2 * TABLE_ROWS, features), BF16),
            pltpu.VMEM((4, 2) + time_ids.shape, jnp.int32),
            pltpu.VMEM(weight.shape, BF16),
            pltpu.VMEM((3, 2 * groups, OWN, 128), BF16),
            pltpu.VMEM((3, 2 * groups, SHARED, 128), BF16),
            pltpu.VMEM((groups, KEYS, 128), BF16),
            pltpu.VMEM((groups, OWN, 128), BF16),
            pltpu.VMEM((KEYS, 128), F32),
            dma((len(MOVES),)), dma((len(MOVES),)), dma((len(MOVES),)), dma((len(MOVES),)), dma((24,)), dma((24,)), dma((3,)),
        ],
        compiler_params=pltpu.CompilerParams(collective_id=1, has_side_effects=True, vmem_limit_bytes=60 * MIB),
    )(lengths, patches, cot, time_ids, freq_ids, time_table, freq_table, gain, shift, weight, query_bias, value_bias)


def attend_back(p, query, keys, values, d_mixed, logs, key_ok, d_query, d_keys, d_values, head_dim, block, tick):
    count = query.shape[1]
    lane = lax.broadcasted_iota(jnp.int32, (1, 128), 1) // head_dim
    scale = BF16(1.0 / math.sqrt(head_dim))

    k, v = keys[p], values[p]
    k_t = (k * scale).T
    total_k = jnp.zeros((KEYS, 128), F32)
    total_v = jnp.zeros((KEYS, 128), F32)
    for first in range(0, count, block):
        last = min(first + block, count)
        q_block = query[p, first:last] * scale
        m_block = d_mixed[p, first:last]
        parts = []
        for h in range(128 // head_dim):
            q_head = jnp.where(lane == h, q_block, BF16(0))
            m_head = jnp.where(lane == h, m_block, BF16(0))
            scores = jnp.where(key_ok, mm(k, q_head, NT), NEGATIVE)
            probs = jnp.exp(scores - logs[p, h:h + 1, first:last])
            total_v = total_v + mm(probs.astype(BF16), m_head)
            weighted = probs * mm(v, m_head, NT)
            d_scores = (weighted - probs * row_sum(weighted)).astype(BF16)
            total_k = total_k + mm(d_scores, q_head)
            parts.append(mm(k_t[h * head_dim:(h + 1) * head_dim], d_scores))
        d_query[p, first:last] = jnp.concatenate(parts, 0).T.astype(BF16)
        tick(first // block)
    d_keys[p] = total_k.astype(BF16)
    d_values[p] = total_v.astype(BF16)


class Flow:
    def __init__(self, source, result, refs, place):
        self.source, self.result = source, result
        self.split = len(source.shape) == 5
        self.got, self.x_got, self.y_got, self.z_got, self.send, self.recv = refs
        self.z, self.y, self.x, self.c = place
        self.open = {}
        if self.split:
            self.stages = [self.begin, self.cores_x, self.x_y, self.y_z, self.z_fill, self.fill_cores, self.end]
        else:
            self.stages = [self.begin, self.cores_y, self.y_z, self.z_x, self.x_cores, self.end]
        self.used = 0
        self.done = 0

    def advance(self):
        self.stages[self.done]()
        self.done += 1

    def copy(self, key, ends):
        slot = self.used
        self.used += 1

        def make():
            source, target, (z, y, x, c) = ends()
            return pltpu.make_async_remote_copy(
                src_ref=source, dst_ref=target, send_sem=self.send.at[slot], recv_sem=self.recv.at[slot],
                device_id=(z * 2 + y, x * 2 + c), device_id_type=pl.DeviceIdType.MESH)

        make().start()
        self.open.setdefault(key, []).append(make)

    def wait(self, key):
        for make in self.open.pop(key):
            make().wait()

    def at(self, z, y):
        return self.source.at[z * 2 + y, self.c, self.x] if self.split else self.source.at[z * 2 + y, self.c]

    def begin(self):
        self.copy("core", lambda: (self.source.at[:, 1 - self.c], self.got, (self.z, self.y, self.x, 1 - self.c)))

    def cores(self):
        self.wait("core")

        def add(i, _):
            self.source[i, self.c] = self.source[i, self.c] + self.got[i]
            return 0

        lax.fori_loop(0, self.got.shape[0], add, 0)

    def cores_x(self):
        self.cores()
        self.copy("x", lambda: (self.source.at[:, self.c, 1 - self.x], self.x_got, (self.z, self.y, 1 - self.x, self.c)))

    def cores_y(self):
        self.cores()
        self.to_y()

    def to_y(self):
        for z in range(4):
            self.copy("y", lambda z=z: (self.at(z, 1 - self.y), self.y_got.at[z], (self.z, 1 - self.y, self.x, self.c)))

    def x_y(self):
        self.wait("x")

        def add(i, _):
            self.source[i, self.c, self.x] = self.source[i, self.c, self.x] + self.x_got[i]
            return 0

        lax.fori_loop(0, self.got.shape[0], add, 0)
        self.to_y()

    def y_z(self):
        self.wait("y")

        def add(z, _):
            spot = self.at(z, self.y)
            spot[...] = spot[...] + self.y_got[z]
            return 0

        lax.fori_loop(0, 4, add, 0)
        for ahead in range(1, 4):
            def ends(ahead=ahead):
                z = lax.rem(self.z + ahead, 4)
                return self.at(z, self.y), self.z_got.at[ahead - 1], (z, self.y, self.x, self.c)

            self.copy("z", ends)

    def z_sum(self):
        self.wait("z")
        total = self.at(self.z, self.y)[...].astype(F32)
        for i in range(3):
            total = total + self.z_got[i].astype(F32)
        return total.astype(BF16)

    def z_fill(self):
        self.result[self.c, self.x] = self.z_sum()
        spot = lambda: self.result.at[self.c, self.x]
        self.copy("fill", lambda: (spot(), spot(), (self.z, self.y, 1 - self.x, self.c)))

    def fill_cores(self):
        self.wait("fill")
        self.to_core()

    def z_x(self):
        spot = self.at(self.z, self.y)
        spot[...] = self.z_sum()
        self.copy("x", lambda: (self.at(self.z, self.y), self.x_got, (self.z, self.y, 1 - self.x, self.c)))

    def x_cores(self):
        self.wait("x")
        self.result[self.c] = self.at(self.z, self.y)[...] + self.x_got[...]
        self.to_core()

    def to_core(self):
        spot = lambda: self.result.at[self.c]
        self.copy("end", lambda: (spot(), spot(), (self.z, self.y, self.x, 1 - self.c)))

    def end(self):
        self.wait("end")


FLOW_REFS = 6
FLOW_NAMES = ("D0", "D1", "D2", "U0", "U1", "U2", "O", "A", "B", "S")
SCHEDULE = {
    "d0": ("D0",),
    "u0": ("U0",),
    "1b0": ("D0",),
    "1b1": ("U0",),
    "d1": ("D1",),
    "u1": ("U1",),
    "2b0": ("D1", "D0",),
    "2b1": ("U0", "U1",),
    "d2": ("D2",),
    "u2": ("U2",),
    "e": ("D0", "D1", "D2", "U1", "U2", "O",),
    "s00": ("U0",),
    "s10": ("D0", "O",),
    "s20": ("D0",),
    "o01": ("D1", "D2",),
    "o02": ("U2",),
    "o10": ("U0", "U1",),
    "o21": ("O",),
    "q": ("B", "A", "U1", "D2", "U2",),
    "f0": ("B",),
    "f1": ("A", "U0", "D1", "O",),
    "f2": ("S", "U0", "D1", "U1", "D2", "U2",),
    "tail": ("S", "U1", "D2", "B", "S", "A", "O", "O", "A", "B", "S", "U2", "U2", "B", "S", "A", "B", "S", "A", "A",),
}


def flow_scratch(shape):
    shares, tail = shape[0], shape[2:]
    block = tail[-2:]
    first = (shares,) + block if len(tail) == 3 else block
    slots = 16
    return [pltpu.VMEM((shares,) + tail, BF16), pltpu.VMEM(first, BF16), pltpu.VMEM((4,) + block, BF16), pltpu.VMEM((3,) + block, BF16),
            pltpu.SemaphoreType.DMA((slots,)), pltpu.SemaphoreType.DMA((slots,))]


def place_of():
    d, s = lax.axis_index("dp"), lax.axis_index("seq")
    return d // 2, lax.rem(d, 2), s // 2, lax.rem(s, 2)


def greet(place):
    z, y, x, c = place
    peers = [(z, y, x, 1 - c), (z, y, 1 - x, c), (z, 1 - y, x, c)] + [(lax.rem(z + i, 4), y, x, c) for i in range(1, 4)]
    peers.append((z, y, 1 - x, 1 - c))
    barrier = pltpu.get_barrier_semaphore()
    for pz, py, px, pc in peers:
        pl.semaphore_signal(barrier, inc=1, device_id=(pz * 2 + py, px * 2 + pc), device_id_type=pl.DeviceIdType.MESH)
    pl.semaphore_wait(barrier, len(peers))


def piece_shapes(shares, features, hidden):
    share = features // shares
    down = (shares, 2, features // 2, hidden // shares // TILES)
    up = (shares, 2, 2, share, hidden // TILES // 4)
    wide = features // 3
    return (down,) * TILES + (up,) * TILES + (
        (shares, 2, share, features // 2), (shares, 2, 2, share, wide), (shares, 2, share, 3 * features // 2 - 2 * wide),
        (shares, 2, SMALL_ROWS // 2, -(-share // 128) * 128))


def middle_part(env, out_weight, up, down, mixed, x1, n2, n2_t, dm, dm_t, acc, d_n2, act_all, d_hidden_all, load_sem, weight_sem):
    total, features = x1.shape
    hidden = env.up.shape[1]
    tile = hidden // TILES
    shares = env.shares
    reach = hidden // shares
    width = reach // TILES
    share = features // shares
    line = lambda ref: ref[...].reshape(1, ref.shape[0])
    blocks = [slice(i, i + SHARED) for i in range(0, total, SHARED)]

    def weight_loads(j):
        made = []
        for d in range(shares):
            first = d * reach + j * width
            k = 2 * (shares * (j % 2) + d)
            made.append(pltpu.make_async_copy(env.up.at[:, pl.ds(first, width)], up.at[j % 2, :, pl.ds(d * width, width)], weight_sem.at[k]))
            made.append(pltpu.make_async_copy(env.down.at[pl.ds(first, width)], down.at[j % 2, pl.ds(d * width, width)], weight_sem.at[k + 1]))
        return made

    first_loads = [pltpu.make_async_copy(env.out_weight, out_weight, load_sem.at[0]), pltpu.make_async_copy(env.x, x1, load_sem.at[1]),
                   pltpu.make_async_copy(env.cot, dm, load_sem.at[2])]
    for g in range(env.mixed.shape[0]):
        first_loads.append(pltpu.make_async_copy(env.mixed.at[g], mixed.at[:, pl.ds(g * 128, 128)], load_sem.at[3 + g]))
    pending = {0: weight_loads(0), 1: weight_loads(1)}
    for made in first_loads + pending[0] + pending[1]:
        made.start()
    env.greet()
    wait_all(first_loads)
    for rows in blocks:
        after = x1[rows] + (mm(mixed[rows], out_weight[...]) + line(env.out_bias))
        x1[rows] = after
        xhat, _ = normalize(after)
        n2[rows] = (xhat * line(env.gain2) + line(env.shift2)).astype(BF16)
        dm[rows] = (dm[rows].astype(F32) * env.valid[rows, 0:1]).astype(BF16)
    n2_t[...] = n2[...].T
    dm_t[...] = dm[...].T
    acc[...] = jnp.zeros_like(acc)
    d_n2[...] = jnp.zeros_like(d_n2)
    env.small[7:8, :] = row_sum(dm[...].astype(F32))
    for j in range(TILES):
        up_j, down_j = up.at[j % 2], down.at[j % 2]
        wait_all(pending[j])
        tile_bias = jnp.concatenate([env.up_bias[d * reach + j * width:d * reach + (j + 1) * width].reshape(1, width) for d in range(shares)], 1)
        bias_sum = jnp.zeros((1, tile), F32)
        for i, rows in enumerate(blocks):
            h = mm(n2[rows], up_j[...]) + tile_bias
            half = 0.5 * (1.0 + lax.erf(h * (1.0 / math.sqrt(2.0))))
            act = (h * half).astype(BF16)
            slope = half + h * jnp.exp(h * h * -0.5) * (1.0 / math.sqrt(2.0 * math.pi))
            d_hidden = (slope * mm(dm[rows], down_j[...], NT)).astype(BF16)
            act_all[rows] = act
            d_hidden_all[rows] = d_hidden
            acc[rows] += mm(act, down_j[...])
            d_n2[rows] += mm(d_hidden, up_j[...], NT)
            bias_sum += row_sum(d_hidden.astype(F32))
            env.tick(f"{j}b{i}")
        if j + 2 < TILES:
            pending[j + 2] = weight_loads(j + 2)
            for made in pending[j + 2]:
                made.start()
        for d in range(shares):
            env.up_bias_grad[:, d * reach + j * width:d * reach + (j + 1) * width] = bias_sum[:, d * width:(d + 1) * width]
        g_down, g_up = env.pieces[j], env.pieces[TILES + j]
        for core in range(2):
            rows = slice(core * (features // 2), (core + 1) * (features // 2))
            out = mm(dm_t[rows], act_all[...]).astype(BF16)
            for d in range(shares):
                g_down[d, core] = out[:, d * width:(d + 1) * width]
        env.tick(f"d{j}")
        wide = g_up.shape[4]
        out = mm(n2_t[...], d_hidden_all[...]).astype(BF16)
        for d in range(shares):
            rows = slice(d * share, (d + 1) * share)
            for core in range(2):
                for half_x in range(2):
                    first = (2 * core + half_x) * wide
                    g_up[d, core, half_x] = out[rows, first:first + wide]
        env.tick(f"u{j}")
    sums = [jnp.zeros((1, features), F32)] * 3
    for rows in blocks:
        after = x1[rows]
        env.out_work[rows] = (env.valid[rows, 0:1] * (after + (acc[rows] + line(env.down_bias)))).astype(BF16)
        xhat, rstd = normalize(after)
        d_norm = d_n2[rows]
        d_x1 = dm[rows].astype(F32) + norm_back(d_norm, line(env.gain2), xhat, rstd)
        env.d_x1[rows] = d_x1
        d_a = d_x1.astype(BF16)
        n2[rows] = d_a
        sums = [a + row_sum(b) for a, b in zip(sums, (d_a.astype(F32), d_norm * xhat, d_norm))]
        d_mixed = mm(d_a, out_weight[...], NT).astype(BF16)
        for g in range(features // 128):
            env.d_mixed[g, rows] = d_mixed[:, g * 128:(g + 1) * 128]
    env.after_middle()
    out = mm(mixed[...].T, n2[...]).astype(BF16)
    g_out = env.pieces[2 * TILES]
    for d in range(shares):
        for core in range(2):
            g_out[d, core] = out[d * share:(d + 1) * share, core * (features // 2):(core + 1) * (features // 2)]
    for row, value in zip((2, 5, 6), sums):
        env.small[row:row + 1, :] = value
    env.tick("e")


def attention_part(env, matrix, own, shared_q, shared_kv, own_d, shared_dq, shared_dkv, joined, normed, x_in, d_work, weight_sem):
    s, x, c = env.s, env.x_at, env.c
    other = 1 - c
    total, features = x_in.shape
    groups = own.shape[1]
    partner, across = 2 * x + other, 2 * (1 - x) + c
    mine = pl.ds(groups * c, groups)
    own_rows = span(OWN * c, OWN)
    sender = env.sender
    loads = [pltpu.make_async_copy(a, b, weight_sem.at[i]) for i, (a, b) in enumerate((
        (env.shared_q, shared_q), (env.shared_kv, shared_kv), (env.own, own), (env.weight, matrix), (env.normed, normed), (env.x, x_in)))]
    for load in loads:
        load.start()
    key_spot = lax.broadcasted_iota(jnp.int32, (KEYS, 1), 0)
    shared_dm_copies, own_dm_copies = env.exchange_copies()
    wait_all(shared_dm_copies + loads[0:2])
    for p in range(groups):
        attend_back(p, shared_q, shared_kv.at[0], shared_kv.at[1], env.shared_dm, env.shared_log, shared_slots(key_spot) < env.lengths[2],
                    shared_dq, shared_dkv.at[0], shared_dkv.at[1], env.head_dim, 256, lambda i: env.tick(f"s{p}{i}"))
    kv_copy = sender.far(shared_dkv.at[:, :, span(OWN * (1 - x), OWN)], env.other_dkv, across)
    env.out_mover.start(MOVES)
    wait_all(own_dm_copies + loads[2:3])
    for p in range(groups):
        attend_back(p, own.at[0], own.at[1], own.at[2], env.own_dm, env.own_log,
                    own_slots(key_spot) < jnp.where(x == 0, env.lengths[0], env.lengths[1]),
                    own_d.at[0], own_d.at[1], own_d.at[2], env.head_dim, 256, lambda i: env.tick(f"o{p}{i}"))
    own_copies = [
        sender.far(own_d.at[:, :, span(OWN * other, OWN)], env.joined_lanes.at[:, mine, 0:OWN], partner),
        sender.near(own_d.at[:, :, own_rows], env.joined_lanes.at[:, mine, 0:OWN]),
    ]
    kv_copy.wait()
    for i in range(2):
        for g in range(groups):
            rows = span(OWN * x, OWN)
            shared_dkv[i, g, rows] = shared_dkv[i, g, rows] + env.other_dkv[i, g]
    shared_copies = []
    for to, peer in ((other, partner), (c, None)):
        q_part = shared_dq.at[:, span(SHARED * to, SHARED)]
        kv_part = shared_dkv.at[:, :, span(OWN * x + SHARED * to, SHARED)]
        q_place, kv_place = env.joined_lanes.at[0, mine, OWN:WORK], env.joined_lanes.at[1:3, mine, OWN:WORK]
        if peer is None:
            shared_copies += [sender.near(q_part, q_place), sender.near(kv_part, kv_place)]
        else:
            shared_copies += [sender.far(q_part, q_place, peer), sender.far(kv_part, kv_place, peer)]
    wait_all(loads[3:])
    normed_t = normed[...].T
    wait_all(own_copies + shared_copies)
    blocks = [slice(i, i + SHARED) for i in range(0, total, SHARED)]
    for part in range(3):
        for g in range(2 * groups):
            at = (part * 2 * groups + g) * 128
            joined[:, at:at + 128] = env.joined_lanes[part, g]
    half = 3 * features // 2
    g_a, g_b, packed = env.pieces[2 * TILES + 1:]
    wide = g_a.shape[4]
    share = features // env.shares
    for core in range(2):
        out = mm(normed_t, joined[:, core * half:(core + 1) * half]).astype(BF16)
        for d in range(env.shares):
            rows = slice(d * share, (d + 1) * share)
            for half_x in range(2):
                g_a[d, core, half_x] = out[rows, half_x * wide:(half_x + 1) * wide]
            g_b[d, core] = out[rows, 2 * wide:]
    env.tick("q")
    sums = [jnp.zeros((1, features), F32)] * 4
    tables = jnp.zeros((TABLE_ROWS, 2 * features), F32)
    for i, rows in enumerate(blocks):
        d_norm = mm(joined[rows], matrix[...], NT)
        xhat, rstd = normalize(x_in[rows])
        terms = (joined[rows, 0:features].astype(F32), joined[rows, 2 * features:].astype(F32), d_norm * xhat, d_norm)
        sums = [a + row_sum(b) for a, b in zip(sums, terms)]
        d_x = env.d_x1[rows] + norm_back(d_norm, env.gain1[...].reshape(1, features), xhat, rstd)
        high, low = split_high_low(d_x)
        d_work[rows] = high
        tables = tables + mm(one_hot(env.ids[0:1, rows], env.ids[1:2, rows]), jnp.concatenate([high, low], 1))
        if i < 2:
            env.tick(f"f{i}")
    d_mover = Mover(s, env.d_patches, d_work, env.d_send, env.d_recv, True)
    d_mover.start(MOVES)
    small = env.small
    small[16:16 + TABLE_ROWS, :] = tables[:, 0:features] + tables[:, features:]
    for row, value in zip((0, 1, 3, 4), sums):
        small[row:row + 1, :] = value
    repeat = env.up_bias_grad.shape[1] // features
    height = packed.shape[2]
    if share != packed.shape[3]:
        packed[...] = jnp.zeros_like(packed)
    for d in range(env.shares):
        for r in range(repeat):
            first = (d * repeat + r) * share
            small[8 + r:9 + r, d * share:(d + 1) * share] = env.up_bias_grad[:, first:first + share]
        for core in range(2):
            packed[d, core, :, 0:share] = small[core * height:(core + 1) * height, d * share:(d + 1) * share].astype(BF16)
    env.tick("f2")
    env.tick("tail")
    for mover in (env.out_mover, d_mover):
        mover.wait(MOVES)
        mover.drain(MOVES)


class Env:
    pass


BACK_INPUTS = ("lengths", "valid", "x", "mixed", "cot", "out_weight", "out_bias", "gain2", "shift2", "up", "up_bias", "down", "down_bias",
               "own", "shared_q", "shared_kv", "own_log", "shared_log", "weight", "normed", "ids", "gain1")
IN_VMEM = ("valid", "out_bias", "gain2", "shift2", "up_bias", "down_bias", "own_log", "shared_log", "ids", "gain1")
BACK_SCRATCH = ("d_mixed", "own_dm", "shared_dm", "other_dkv", "joined_lanes", "d_x1", "out_work", "small", "up_bias_grad", "zeros",
                "out_send", "out_recv", "d_send", "d_recv", "send", "recv", "dm_send", "dm_recv", "zero_sem")


def backward_body(head_dim, shares, custom, features, hidden, *refs):
    env = Env()
    refs = list(refs)
    take = lambda count: [refs.pop(0) for _ in range(count)]
    for name, ref in zip(BACK_INPUTS, take(len(BACK_INPUTS))):
        setattr(env, name, ref)
    count = len(FLOW_NAMES)
    env.output, env.d_patches = take(2)
    outs = take(count)
    for name, ref in zip(BACK_SCRATCH, take(len(BACK_SCRATCH))):
        setattr(env, name, ref)
    env.head_dim, env.shares = head_dim, shares
    env.s, env.x_at, env.c = seq_place()
    flows = {}
    if custom:
        place = place_of()
        env.pieces = take(count)
        for i, name in enumerate(FLOW_NAMES):
            flows[name] = Flow(env.pieces[i], outs[i], take(FLOW_REFS), place)
        env.greet = lambda: greet(place)
    else:
        env.pieces = outs
        env.greet = lambda: greet_group(env.s)

    def tick(point):
        for name in SCHEDULE.get(point, ()):
            if custom:
                flows[name].advance()

    env.tick = tick
    env.sender = Sender(env.send, env.recv)
    env.out_mover = Mover(env.s, env.output, env.out_work, env.out_send, env.out_recv, True)
    env.zeros[...] = jnp.zeros_like(env.zeros)
    env.small[...] = jnp.zeros_like(env.small)

    def fill(act):
        @pl.when(env.s == UNUSED[0])
        def _():
            for i, array in enumerate((env.output, env.d_patches)):
                for clip in range(3):
                    act(pltpu.make_async_copy(env.zeros, array.at[clip, pl.ds(UNUSED[1], ROWS - UNUSED[1])], env.zero_sem.at[3 * i + clip]))

    fill(lambda made: made.start())

    groups = features // 256

    def exchange_copies():
        other = 1 - env.c
        partner = 2 * env.x_at + other
        mine, theirs = pl.ds(groups * env.c, groups), pl.ds(groups * other, groups)
        places = ((env.shared_dm.at[:, span(SHARED * env.c, SHARED)], slice(OWN, WORK)), (env.own_dm.at[:, span(OWN * env.c, OWN)], slice(0, OWN)))
        sender = Sender(env.dm_send, env.dm_recv)
        return [[sender.far(env.d_mixed.at[theirs, rows], place, partner, False), sender.near(env.d_mixed.at[mine, rows], place, False)]
                for place, rows in places]

    def after_middle():
        for made in sum(exchange_copies(), []):
            made.start()

    env.exchange_copies = exchange_copies
    env.after_middle = after_middle
    tile = hidden // TILES
    dma = pltpu.SemaphoreType.DMA
    wide, tall = lambda kind: pltpu.VMEM((WORK, features), kind), pltpu.VMEM((features, WORK), BF16)
    lanes = lambda *lead: pltpu.VMEM(lead + (128,), BF16)
    pl.run_scoped(
        functools.partial(middle_part, env), pltpu.VMEM((features, features), BF16), pltpu.VMEM((2, features, tile), BF16),
        pltpu.VMEM((2, tile, features), BF16), wide(BF16), wide(F32), wide(BF16), tall, wide(BF16), tall, wide(F32), wide(F32),
        pltpu.VMEM((WORK, tile), BF16), pltpu.VMEM((WORK, tile), BF16), dma((3 + 2 * groups,)), dma((4 * shares,)))
    pl.run_scoped(
        functools.partial(attention_part, env), pltpu.VMEM((features, 3 * features), BF16), lanes(3, groups, KEYS), lanes(groups, OWN),
        lanes(2, groups, KEYS), lanes(3, groups, KEYS), lanes(groups, OWN), lanes(2, groups, KEYS), pltpu.VMEM((WORK, 3 * features), BF16),
        wide(BF16), wide(F32), wide(BF16), dma((6,)))
    fill(lambda made: made.wait())


def backward(inputs, head_dim, shares, custom):
    features, hidden = inputs["up"].shape
    groups = features // 256
    anywhere, vmem = pl.BlockSpec(memory_space=pl.ANY), pl.BlockSpec(memory_space=pltpu.VMEM)
    dma = pltpu.SemaphoreType.DMA
    lanes = lambda *lead: pltpu.VMEM(lead + (128,), BF16)
    moves = len(MOVES)
    shapes = piece_shapes(shares, features, hidden)
    specs = [vmem if name in IN_VMEM else anywhere for name in BACK_INPUTS]
    specs[0] = pl.BlockSpec(memory_space=pltpu.SMEM)
    scratch = [
        lanes(2 * groups, WORK), lanes(groups, KEYS), lanes(groups, OWN), lanes(2, groups, OWN), lanes(3, 2 * groups, WORK),
        pltpu.VMEM((WORK, features), F32), pltpu.VMEM((WORK, features), BF16), pltpu.VMEM((SMALL_ROWS, features), F32),
        pltpu.VMEM((1, hidden), F32), pltpu.VMEM((ROWS - UNUSED[1], features), BF16),
        dma((moves,)), dma((moves,)), dma((moves,)), dma((moves,)), dma((24,)), dma((24,)), dma((4,)), dma((4,)), dma((6,)),
    ]
    if custom:
        scratch += [pltpu.VMEM(shape, BF16) for shape in shapes]
        scratch += [ref for shape in shapes for ref in flow_scratch(shape)]
    rows = jax.ShapeDtypeStruct((3, ROWS, features), BF16)
    return pl.pallas_call(
        functools.partial(backward_body, head_dim, shares, custom, features, hidden),
        in_specs=specs,
        out_specs=[anywhere] * 2 + [vmem] * len(shapes),
        out_shape=[rows, rows] + [jax.ShapeDtypeStruct(shape[1:] if custom else shape, BF16) for shape in shapes],
        scratch_shapes=scratch,
        compiler_params=pltpu.CompilerParams(collective_id=0, has_side_effects=True, vmem_limit_bytes=63 * MIB),
    )(*(inputs[name] for name in BACK_INPUTS))


def assemble_body(time_count, freq_count, *refs):
    count = len(FLOW_NAMES)
    pieces = refs[0:count]
    outs = refs[count:]
    down, up, out, qkv_a, qkv_b, packed = pieces[0:TILES], pieces[TILES:2 * TILES], *pieces[2 * TILES:]
    (qkv_out, qb, vb, out_out, ob, n1g, n1s, n2g, n2s, up_out, up_b, down_out, db, time_out, freq_out) = outs
    wide, rest = qkv_a.shape[3], qkv_b.shape[2]
    half = 2 * wide + rest
    for core in range(2):
        for half_x in range(2):
            first = core * half + half_x * wide
            qkv_out[:, first:first + wide] = qkv_a[core, half_x].astype(F32)
        qkv_out[:, core * half + 2 * wide:(core + 1) * half] = qkv_b[core].astype(F32)
        cols = out.shape[2]
        out_out[:, core * cols:(core + 1) * cols] = out[core].astype(F32)
    width = down[0].shape[2]
    for j in range(TILES):
        for core in range(2):
            high = down[j].shape[1]
            down_out[j * width:(j + 1) * width, core * high:(core + 1) * high] = down[j][core].astype(F32).T
            for half_x in range(2):
                span_x = up[j].shape[3]
                for k in range(span_x // width):
                    block = ((2 * core + half_x) * span_x) // width + k
                    first = (block * TILES + j) * width
                    up_out[:, first:first + width] = up[j][core, half_x, :, k * width:(k + 1) * width].astype(F32)
    small = jnp.concatenate([packed[0], packed[1]], 0).astype(F32)
    share = qb.shape[0]
    for row, ref in ((0, qb), (1, vb), (2, ob), (3, n1g), (4, n1s), (5, n2g), (6, n2s), (7, db)):
        ref[...] = small[row, 0:share]
    for r in range(up_b.shape[0] // share):
        up_b[r * share:(r + 1) * share] = small[8 + r, 0:share]
    time_out[...] = small[16:16 + time_count, 0:share]
    freq_out[...] = small[16 + FREQ_ROW:16 + FREQ_ROW + freq_count, 0:share]


def assemble(pieces, features, hidden, shares, time_count, freq_count):
    share = features // shares
    line = (share,)
    shapes = [(share, 3 * features), line, line, (share, features), line, line, line, line, line, (share, hidden), (hidden // shares,),
              (hidden // shares, features), line, (time_count, share), (freq_count, share)]
    return pl.pallas_call(
        functools.partial(assemble_body, time_count, freq_count),
        out_shape=[jax.ShapeDtypeStruct(shape, F32) for shape in shapes],
        compiler_params=params(),
    )(*pieces)


def reduce_native(pieces, time_count, freq_count):
    def total(part, axis):
        return lax.psum(lax.psum_scatter(part, "dp", scatter_dimension=axis, tiled=True), "seq").astype(F32)

    pieces = [p[0] for p in pieces]
    down = jnp.concatenate([p.reshape(-1, p.shape[2]) for p in pieces[0:TILES]], 1)
    up = jnp.concatenate([p[c, h] for p in pieces[TILES:2 * TILES] for c in range(2) for h in range(2)], 1)
    out, qkv_a, qkv_b, packed = pieces[2 * TILES:]
    qkv = jnp.concatenate([part for c in range(2) for part in (qkv_a[c, 0], qkv_a[c, 1], qkv_b[c])], 1)
    small = packed.reshape(SMALL_ROWS, -1)
    repeat = up.shape[1] // small.shape[1]
    up_bias = total(small[8:8 + repeat].reshape(-1), 0)
    small = total(small, 1)
    return (
        total(qkv, 0), small[0], small[1], total(jnp.concatenate([out[0], out[1]], 1), 0), small[2], small[3], small[4], small[5], small[6],
        total(up, 0), up_bias, total(down, 1).T, small[7], small[16:16 + time_count], small[16 + FREQ_ROW:16 + FREQ_ROW + freq_count],
    )


def shards(
    patches,
    cotangent,
    time_ids,
    freq_ids,
    lengths,
    qkv_weight,
    query_bias,
    value_bias,
    out_weight,
    out_bias,
    norm1_gain,
    norm1_shift,
    norm2_gain,
    norm2_shift,
    up_weight,
    up_bias,
    down_weight,
    down_bias,
    time_table,
    freq_table,
):
    features = patches.shape[2]
    head_dim = features // HEADS
    assert patches.shape[:2] == (3, ROWS) and lax.axis_size("seq") == 4
    custom = lax.axis_size("dp") == 8
    shares = 8 if custom else 1
    x, normed, own, shared_q, shared_kv, own_log, shared_log, mixed, cot, ids, valid = forward(
        lengths, patches, cotangent, time_ids, freq_ids, time_table, freq_table, norm1_gain, norm1_shift, qkv_weight, query_bias, value_bias,
        head_dim
    )
    inputs = dict(
        lengths=lengths, valid=valid, x=x, mixed=mixed, cot=cot, out_weight=out_weight, out_bias=out_bias, gain2=norm2_gain,
        shift2=norm2_shift, up=up_weight, up_bias=up_bias, down=down_weight, down_bias=down_bias, own=own, shared_q=shared_q,
        shared_kv=shared_kv, own_log=own_log, shared_log=shared_log, weight=qkv_weight, normed=normed, ids=ids, gain1=norm1_gain)
    output, d_patch, *pieces = backward(inputs, head_dim, shares, custom)
    counts = time_table.shape[0], freq_table.shape[0]
    if custom:
        return (output, d_patch) + tuple(assemble(pieces, features, up_weight.shape[1], shares, *counts))
    return (output, d_patch) + reduce_native(pieces, *counts)


def solution(mesh):
    clip_spec, row_spec, one = P("dp", "seq", None), P("dp", "seq"), P("dp")
    matrix = P("dp", None)
    return jax.shard_map(
        shards,
        mesh=mesh,
        in_specs=(clip_spec, clip_spec, row_spec, row_spec, one) + (P(),) * 15,
        out_specs=(clip_spec, clip_spec, matrix, one, one, matrix, one, one, one, one, one, matrix, one, matrix, one, P(None, "dp"), P(None, "dp")),
        check_vma=False,
    )
```

```python
import functools
import math

import jax
import jax.numpy as jnp
from jax import lax
from jax.experimental import pallas as pl
from jax.experimental.pallas import tpu as pltpu
from jax.sharding import PartitionSpec as P

HEADS = 12
EPS = 1e-06
NEGATIVE = -1000000000.0
FREQ_ROW = 104
TABLE_ROWS = 128
SMALL_ROWS = 32 + TABLE_ROWS
TILES = 3
CHUNKS = 2
F32 = jnp.float32
BF16 = jnp.bfloat16
NN = (((1,), (0,)), ((), ()))
NT = (((1,), (1,)), ((), ()))
TN = (((0,), (0,)), ((), ()))
MIB = 1 << 20


def mm(left, right, dims=NN):
    return lax.dot_general(left, right, dims, preferred_element_type=F32)


def params(limit=60):
    return pltpu.CompilerParams(vmem_limit_bytes=limit * MIB)


def row_sum(values):
    return jnp.sum(values, 0, keepdims=True)


def normalize(values):
    center = values - jnp.mean(values, -1, keepdims=True)
    rstd = lax.rsqrt(jnp.mean(center * center, -1, keepdims=True) + EPS)
    return center * rstd, rstd


def norm_back(d_out, gain, xhat, rstd):
    u = d_out * gain
    inner = jnp.mean(u * xhat, -1, keepdims=True)
    return rstd * (u - jnp.mean(u, -1, keepdims=True) - xhat * inner)


def gelu_parts(h):
    half = 0.5 * (1.0 + lax.erf(h * (1.0 / math.sqrt(2.0))))
    return half, half + h * jnp.exp(h * h * -0.5) * (1.0 / math.sqrt(2.0 * math.pi))


def split_high_low(values):
    high = values.astype(BF16)
    return high, (values - high.astype(F32)).astype(BF16)


def one_hot(time_row, freq_row):
    spot = lax.broadcasted_iota(jnp.int32, (TABLE_ROWS, time_row.shape[1]), 0)
    hit = (spot == time_row) | (spot == freq_row + FREQ_ROW)
    return jnp.where(hit, 1.0, 0.0).astype(BF16)


ROWS = 224
OWN = 352
SHARED = 176
WORK = OWN + SHARED
KEYS = 2 * OWN
TALL = WORK + SHARED
SHARED_MOVES = (
    (0, 2, 176, 48, 3, 384), (1, 2, 176, 48, 3, 432), (2, 2, 176, 48, 3, 480), (3, 2, 0, 32, 3, 352),
    (0, 2, 0, 176, 0, 352), (1, 2, 0, 176, 1, 352), (2, 2, 0, 176, 2, 352),
)
OWN_MOVES = (
    (2, 0, 0, 128, 0, 224), (2, 0, 128, 96, 1, 224), (3, 0, 0, 32, 1, 320), (0, 1, 0, 224, 2, 0), (1, 1, 0, 224, 3, 0),
    (2, 1, 128, 96, 3, 224), (2, 1, 0, 128, 2, 224), (3, 1, 0, 32, 3, 320), (0, 0, 0, 224, 0, 0), (1, 0, 0, 224, 1, 0),
)
MIRROR_MOVES = (
    (0, 2, 0, 176, 2, 528), (1, 2, 0, 176, 3, 528), (2, 2, 0, 176, 0, 528), (0, 2, 176, 48, 1, 560), (2, 2, 176, 48, 1, 656),
    (1, 2, 176, 48, 1, 608), (3, 2, 0, 32, 1, 528),
)
MOVES = SHARED_MOVES + OWN_MOVES
ALL_MOVES = MOVES + MIRROR_MOVES
UNUSED = (3, 32)


def seq_place():
    s = lax.axis_index("seq")
    return s, s // 2, lax.rem(s, 2)


def seq_peer(s):
    return {"seq": s}


def greet_group(s):
    barrier = pltpu.get_barrier_semaphore()
    for ahead in range(1, 4):
        pl.semaphore_signal(barrier, inc=1, device_id=seq_peer(lax.rem(s + ahead, 4)), device_id_type=pl.DeviceIdType.MESH)
    pl.semaphore_wait(barrier, 3)


class Mover:
    def __init__(self, s, at_home, at_work, send, recv, back=False):
        self.s, self.at_home, self.at_work, self.send, self.recv, self.back = s, at_home, at_work, send, recv, back

    def ends(self, move):
        home, clip, first, count, work, spot = move
        a, b = self.at_home.at[clip, pl.ds(first, count)], self.at_work.at[pl.ds(spot, count)]
        return (work, b, home, a) if self.back else (home, a, work, b)

    def each(self, moves, which, act, near=True):
        for device in range(4):
            chosen = [m for m in moves if self.ends(m)[which] == device and (near or self.ends(m)[0] != self.ends(m)[2])]
            if not chosen:
                continue

            @pl.when(self.s == device)
            def _(chosen=chosen):
                for m in chosen:
                    src_device, src, dst_device, dst = self.ends(m)
                    slot = ALL_MOVES.index(m)
                    if src_device == dst_device:
                        act(False, pltpu.make_async_copy(src, dst, self.recv.at[slot]))
                    else:
                        act(True, pltpu.make_async_remote_copy(
                            src_ref=src, dst_ref=dst, send_sem=self.send.at[slot], recv_sem=self.recv.at[slot],
                            device_id=seq_peer(dst_device), device_id_type=pl.DeviceIdType.MESH))

    def start(self, moves):
        self.each(moves, 0, lambda far, made: made.start())

    def wait(self, moves):
        self.each(moves, 2, lambda far, made: made.wait_recv() if far else made.wait())

    def drain(self, moves):
        self.each(moves, 0, lambda far, made: made.wait_send(), False)


class Sender:
    def __init__(self, send, recv):
        self.send, self.recv, self.used = send, recv, 0

    def far(self, source, target, peer, begin=True):
        made = pltpu.make_async_remote_copy(
            src_ref=source, dst_ref=target, send_sem=self.send.at[self.used], recv_sem=self.recv.at[self.used],
            device_id=seq_peer(peer), device_id_type=pl.DeviceIdType.MESH)
        self.used += 1
        if begin:
            made.start()
        return made

    def near(self, source, target, begin=True):
        made = pltpu.make_async_copy(source, target, self.recv.at[self.used])
        self.used += 1
        if begin:
            made.start()
        return made


def wait_all(copies):
    for made in copies:
        made.wait()


def shift_between(spot, cuts):
    slot = spot
    for low, high, shift in cuts:
        slot = jnp.where((spot >= low) & (spot < high), spot + shift, slot)
    return slot


def own_slots(spot):
    return shift_between(spot, ((224, 352, 224), (352, 576, -128)))


def shared_slots(spot):
    return shift_between(spot, ((176, 352, 48), (352, 528, 96), (528, 560, 144), (560, 608, -384), (608, 656, -208), (656, 704, -32)))


def span(first, size):
    return pl.ds(pl.multiple_of(first, 16), size)


def lane_parts(value):
    high, rest = split_high_low(value)
    low = (value - high.astype(F32) - rest.astype(F32)).astype(BF16)
    return high, rest, low


def with_lanes(base, lane, first, columns):
    for i, column in enumerate(columns):
        base = jnp.where(lane == first + i, column, base)
    return base


def attend(query, keys, values, key_ok, mixed_out, log_out, head_dim):
    count = query.shape[1]
    lane = lax.broadcasted_iota(jnp.int32, (1, 128), 1)
    head = lane // head_dim
    scale = BF16(1.0 / math.sqrt(head_dim))
    key_bias = jnp.where(key_ok, 0.0, NEGATIVE).astype(BF16)
    per_pair = 128 // head_dim
    units = [(first, h) for first in range(0, count, OWN) for h in range(per_pair)]
    log_out[...] = jnp.zeros_like(log_out)

    def pair(p, _):
        k, v = keys[p], values[p]
        biased = [with_lanes(k, lane, free_lane(h, head_dim), (key_bias,)) for h in range(per_pair)]

        def score(unit):
            first, h = unit
            q = jnp.where(head == h, query[p, first:first + OWN] * scale, BF16(0))
            return mm(with_lanes(q, lane, free_lane(h, head_dim), (BF16(1),)), biased[h], NT)

        ready = score(units[0])
        for i, (first, h) in enumerate(units):
            scores = ready
            if i + 1 < len(units):
                ready = score(units[i + 1])
            rows = slice(first, first + OWN)
            highest = jnp.max(scores, -1, keepdims=True)
            powers = jnp.exp(scores - highest)
            total = jnp.sum(powers, -1, keepdims=True)
            out = mm(powers.astype(BF16), v) * (1.0 / total)
            mixed = out if h == 0 else jnp.where(head == h, out, mixed)
            log_out[rows] = jnp.where(lane == per_pair * p + h, highest + jnp.log(total), log_out[rows])
            if h == per_pair - 1:
                mixed_out[p, rows] = mixed.astype(BF16)
        return 0

    lax.fori_loop(0, query.shape[0], pair, 0)


def free_lane(h, head_dim):
    return (h + 1) * head_dim % 128


def forward_body(head_dim, lengths, patches, cot, time_ids, freq_ids, time_table, freq_table, gain, shift, weight, query_bias, value_bias,
                 x_out, n_out, own_out, shared_q_out, shared_kv_out, own_log, shared_log, own_mixed, shared_mixed, mixed_out, cot_out, id_out,
                 valid_out,
                 work, table_f32, table, ids, matrix, own_stage, shared_stage, mirror_stage,
                 patch_send, patch_recv, cot_send, cot_recv, send, recv, weight_sem):
    s, x, c = seq_place()
    features = x_out.shape[1]
    groups = own_out.shape[1]
    other = 1 - c
    loads = [pltpu.make_async_copy(weight.at[:, pl.ds(p * features, features)], matrix.at[:, pl.ds(p * features, features)], weight_sem.at[p])
             for p in range(3)]
    for load in loads:
        load.start()
    greet_group(s)
    patch_mover = Mover(s, patches, work, patch_send, patch_recv)
    cot_mover = Mover(s, cot, cot_out, cot_send, cot_recv)
    sender = Sender(send, recv)
    id_copies = []
    for i, source in enumerate((time_ids, freq_ids)):
        id_copies.append(sender.near(source, ids.at[s, i]))
        for ahead in range(1, 4):
            id_copies.append(sender.far(source, ids.at[s, i], lax.rem(s + ahead, 4)))
    patch_mover.start(ALL_MOVES)

    table_f32[...] = jnp.zeros_like(table_f32)
    table_f32[0:time_table.shape[0], :] = time_table[...]
    table_f32[FREQ_ROW:FREQ_ROW + freq_table.shape[0], :] = freq_table[...]
    high, low = split_high_low(table_f32[...])
    table[0:TABLE_ROWS, :] = high
    table[TABLE_ROWS:, :] = low
    spot = lax.broadcasted_iota(jnp.int32, (WORK, 1), 0)
    place = jnp.where(spot < OWN, jnp.where(spot < ROWS, spot + ROWS * c, spot + ROWS + 128 * c), shared_slots(spot - OWN + SHARED * s))
    limit = jnp.where(spot < OWN, jnp.where(x == 0, lengths[0], lengths[1]), lengths[2])
    valid_out[...] = jnp.broadcast_to(jnp.where(place < limit, 1.0, 0.0), valid_out.shape)
    id_out[...] = jnp.zeros_like(id_out)
    wait_all(id_copies)
    for device in range(4):
        @pl.when(s == device)
        def _(device=device):
            for home, clip, first, count, target, at in ALL_MOVES:
                if target == device:
                    for i in range(2):
                        id_out[i:i + 1, at:at + count] = ids[home, i, clip:clip + 1, first:first + count]

    bias = (query_bias[...].reshape(1, features), None, value_bias[...].reshape(1, features))

    def project(first, count, stage, own=True):
        rows = slice(first, first + count)
        hot = one_hot(id_out[0:1, rows], id_out[1:2, rows])
        value = work[rows].astype(F32) + mm(jnp.concatenate([hot, hot], 0), table[...], TN)
        if own:
            x_out[rows] = value
        xhat, _ = normalize(value)
        normed = (xhat * gain[...].reshape(1, features) + shift[...].reshape(1, features)).astype(BF16)
        n_out[rows] = normed
        for part in range(0 if own else 1, 3):
            out = mm(normed, matrix[:, part * features:(part + 1) * features])
            if bias[part] is not None:
                out = out + bias[part]
            out = out.astype(BF16)
            for g in range(2 * groups):
                stage[part if own else part - 1, g] = out[:, g * 128:(g + 1) * 128]

    patch_mover.wait(SHARED_MOVES)
    wait_all(loads)
    project(OWN, SHARED, shared_stage)
    q_rows, kv_rows = span(SHARED * c, SHARED), span(SHARED * s, SHARED)
    mine, theirs = pl.ds(groups * c, groups), pl.ds(groups * other, groups)
    mirror_rows = span(SHARED * (2 * (1 - x) + c), SHARED)
    partner = 2 * x + other
    shared_copies = [
        sender.far(shared_stage.at[0, theirs], shared_q_out.at[:, q_rows], partner),
        sender.far(shared_stage.at[1:3, theirs], shared_kv_out.at[:, :, kv_rows], partner),
        sender.near(shared_stage.at[0, mine], shared_q_out.at[:, q_rows]),
        sender.near(shared_stage.at[1:3, mine], shared_kv_out.at[:, :, kv_rows]),
    ]
    patch_mover.wait(OWN_MOVES)
    project(0, OWN, own_stage)
    own_rows = span(OWN * c, OWN)
    own_copies = [
        sender.far(own_stage.at[:, theirs], own_out.at[:, :, own_rows], partner),
        sender.near(own_stage.at[:, mine], own_out.at[:, :, own_rows]),
    ]
    cot_mover.start(MOVES)
    patch_mover.wait(MIRROR_MOVES)
    project(WORK, SHARED, mirror_stage, False)
    shared_copies += [
        sender.far(mirror_stage.at[:, theirs], shared_kv_out.at[:, :, mirror_rows], partner),
        sender.near(mirror_stage.at[:, mine], shared_kv_out.at[:, :, mirror_rows]),
    ]
    wait_all(own_copies)
    key_spot = lax.broadcasted_iota(jnp.int32, (KEYS, 1), 0)
    attend(own_out.at[0], own_out.at[1], own_out.at[2], own_slots(key_spot) < jnp.where(x == 0, lengths[0], lengths[1]),
           own_mixed, own_log, head_dim)
    mixed_copies = [
        sender.far(own_mixed.at[:, span(OWN * other, OWN)], mixed_out.at[mine, 0:OWN], partner),
        sender.near(own_mixed.at[:, own_rows], mixed_out.at[mine, 0:OWN]),
    ]
    wait_all(shared_copies)
    attend(shared_q_out, shared_kv_out.at[0], shared_kv_out.at[1], shared_slots(key_spot) < lengths[2],
           shared_mixed, shared_log, head_dim)
    mixed_copies += [
        sender.far(shared_mixed.at[:, span(SHARED * other, SHARED)], mixed_out.at[mine, OWN:WORK], partner),
        sender.near(shared_mixed.at[:, q_rows], mixed_out.at[mine, OWN:WORK]),
    ]
    wait_all(mixed_copies)
    cot_mover.wait(MOVES)
    patch_mover.drain(ALL_MOVES)
    cot_mover.drain(MOVES)


def forward(lengths, patches, cot, time_ids, freq_ids, time_table, freq_table, gain, shift, weight, query_bias, value_bias, head_dim):
    features = patches.shape[2]
    groups = features // 256
    anywhere, vmem = pl.BlockSpec(memory_space=pl.ANY), pl.BlockSpec(memory_space=pltpu.VMEM)
    lanes = lambda *lead: jax.ShapeDtypeStruct(lead + (128,), BF16)
    dma = pltpu.SemaphoreType.DMA
    return pl.pallas_call(
        functools.partial(forward_body, head_dim),
        in_specs=[pl.BlockSpec(memory_space=pltpu.SMEM)] + [anywhere] * 4 + [vmem] * 4 + [anywhere] + [vmem] * 2,
        out_specs=[vmem] * 13,
        out_shape=[
            jax.ShapeDtypeStruct((WORK, features), F32),
            jax.ShapeDtypeStruct((TALL, features), BF16),
            lanes(3, groups, KEYS),
            lanes(groups, OWN),
            lanes(2, groups, KEYS),
            jax.ShapeDtypeStruct((KEYS, 128), F32),
            jax.ShapeDtypeStruct((OWN, 128), F32),
            lanes(groups, KEYS),
            lanes(groups, OWN),
            lanes(2 * groups, WORK),
            jax.ShapeDtypeStruct((WORK, features), BF16),
            jax.ShapeDtypeStruct((8, TALL), jnp.int32),
            jax.ShapeDtypeStruct((WORK, 128), F32),
        ],
        scratch_shapes=[
            pltpu.VMEM((TALL, features), BF16),
            pltpu.VMEM((TABLE_ROWS, features), F32),
            pltpu.VMEM((2 * TABLE_ROWS, features), BF16),
            pltpu.VMEM((4, 2) + time_ids.shape, jnp.int32),
            pltpu.VMEM(weight.shape, BF16),
            pltpu.VMEM((3, 2 * groups, OWN, 128), BF16),
            pltpu.VMEM((3, 2 * groups, SHARED, 128), BF16),
            pltpu.VMEM((2, 2 * groups, SHARED, 128), BF16),
            dma((len(ALL_MOVES),)), dma((len(ALL_MOVES),)), dma((len(MOVES),)), dma((len(MOVES),)), dma((24,)), dma((24,)), dma((3,)),
        ],
        compiler_params=pltpu.CompilerParams(collective_id=1, has_side_effects=True, vmem_limit_bytes=60 * MIB),
    )(lengths, patches, cot, time_ids, freq_ids, time_table, freq_table, gain, shift, weight, query_bias, value_bias)


def attend_back(p, query, keys, values, d_mixed, mixed, logs, key_ok, d_query, d_keys, d_values, head_dim, block, tick):
    count = query.shape[1]
    lane = lax.broadcasted_iota(jnp.int32, (1, 128), 1)
    head = lane // head_dim
    scale = BF16(1.0 / math.sqrt(head_dim))
    key_bias = jnp.where(key_ok, 0.0, NEGATIVE).astype(BF16)
    k, v = keys[p], values[p]
    k_t = (k * scale).T
    per_pair = 128 // head_dim
    one = BF16(1)
    k_wide = [with_lanes(k, lane, free_lane(h, head_dim), (key_bias, one, one, one)) for h in range(per_pair)]
    v_wide = [with_lanes(v, lane, free_lane(h, head_dim), (one, one, one)) for h in range(per_pair)]
    total_k = jnp.zeros((KEYS, 128), F32)
    total_v = jnp.zeros((KEYS, 128), F32)
    units = [(first, min(first + block, count), h) for first in range(0, count, block) for h in range(per_pair)]

    def products(unit):
        first, last, h = unit
        rows = slice(first, last)
        d_m = d_mixed[p, rows]
        q_head = jnp.where(head == h, query[p, rows] * scale, BF16(0))
        m_head = jnp.where(head == h, d_m, BF16(0))
        delta = jnp.sum(m_head.astype(F32) * mixed[p, rows].astype(F32), -1, keepdims=True)
        at = per_pair * p + h
        q_wide = with_lanes(q_head, lane, free_lane(h, head_dim), (one,) + lane_parts(-logs[rows, at:at + 1]))
        m_wide = with_lanes(m_head, lane, free_lane(h, head_dim), lane_parts(-delta))
        return q_head, m_head, mm(k_wide[h], q_wide, NT), mm(v_wide[h], m_wide, NT)

    ready = products(units[0])
    parts = []
    for i, (first, last, h) in enumerate(units):
        q_head, m_head, scores, d_probs = ready
        if i + 1 < len(units):
            ready = products(units[i + 1])
        probs = jnp.exp(scores)
        d_scores = (probs * d_probs).astype(BF16)
        total_v = total_v + mm(probs.astype(BF16), m_head)
        total_k = total_k + mm(d_scores, q_head)
        parts.append(mm(k_t[h * head_dim:(h + 1) * head_dim], d_scores))
        if h == per_pair - 1:
            d_query[p, first:last] = jnp.concatenate(parts, 0).T.astype(BF16)
            parts = []
            tick(first // block)
    d_keys[p] = total_k.astype(BF16)
    d_values[p] = total_v.astype(BF16)


class Flow:
    def __init__(self, source, result, refs, place):
        self.source, self.result = source, result
        self.split = len(source.shape) == 5
        self.got, self.x_got, self.y_got, self.z_got, self.send, self.recv = refs
        self.z, self.y, self.x, self.c = place
        self.open = {}
        if self.split:
            self.stages = [self.begin, self.cores_x, self.x_y, self.y_z, self.z_fill, self.fill_cores, self.end]
        else:
            self.stages = [self.begin, self.cores_y, self.y_z, self.z_x, self.x_cores, self.end]
        self.used = 0
        self.done = 0

    def advance(self):
        self.stages[self.done]()
        self.done += 1

    def copy(self, key, ends):
        slot = self.used
        self.used += 1

        def make():
            source, target, (z, y, x, c) = ends()
            return pltpu.make_async_remote_copy(
                src_ref=source, dst_ref=target, send_sem=self.send.at[slot], recv_sem=self.recv.at[slot],
                device_id=(z * 2 + y, x * 2 + c), device_id_type=pl.DeviceIdType.MESH)

        make().start()
        self.open.setdefault(key, []).append(make)

    def wait(self, key):
        for make in self.open.pop(key):
            make().wait()

    def at(self, z, y):
        return self.source.at[z * 2 + y, self.c, self.x] if self.split else self.source.at[z * 2 + y, self.c]

    def begin(self):
        self.copy("core", lambda: (self.source.at[:, 1 - self.c], self.got, (self.z, self.y, self.x, 1 - self.c)))

    def cores(self):
        self.wait("core")

        def add(i, _):
            self.source[i, self.c] = self.source[i, self.c] + self.got[i]
            return 0

        lax.fori_loop(0, self.got.shape[0], add, 0)

    def cores_x(self):
        self.cores()
        self.copy("x", lambda: (self.source.at[:, self.c, 1 - self.x], self.x_got, (self.z, self.y, 1 - self.x, self.c)))

    def cores_y(self):
        self.cores()
        self.to_y()

    def to_y(self):
        for z in range(4):
            self.copy("y", lambda z=z: (self.at(z, 1 - self.y), self.y_got.at[z], (self.z, 1 - self.y, self.x, self.c)))

    def x_y(self):
        self.wait("x")

        def add(i, _):
            self.source[i, self.c, self.x] = self.source[i, self.c, self.x] + self.x_got[i]
            return 0

        lax.fori_loop(0, self.got.shape[0], add, 0)
        self.to_y()

    def y_z(self):
        self.wait("y")

        def add(z, _):
            spot = self.at(z, self.y)
            spot[...] = spot[...] + self.y_got[z]
            return 0

        lax.fori_loop(0, 4, add, 0)
        for ahead in range(1, 4):
            def ends(ahead=ahead):
                z = lax.rem(self.z + ahead, 4)
                return self.at(z, self.y), self.z_got.at[ahead - 1], (z, self.y, self.x, self.c)

            self.copy("z", ends)

    def z_sum(self):
        self.wait("z")
        total = self.at(self.z, self.y)[...].astype(F32)
        for i in range(3):
            total = total + self.z_got[i].astype(F32)
        return total.astype(BF16)

    def z_fill(self):
        self.result[self.c, self.x] = self.z_sum()
        spot = lambda: self.result.at[self.c, self.x]
        self.copy("fill", lambda: (spot(), spot(), (self.z, self.y, 1 - self.x, self.c)))

    def fill_cores(self):
        self.wait("fill")
        self.to_core()

    def z_x(self):
        spot = self.at(self.z, self.y)
        spot[...] = self.z_sum()
        self.copy("x", lambda: (self.at(self.z, self.y), self.x_got, (self.z, self.y, 1 - self.x, self.c)))

    def x_cores(self):
        self.wait("x")
        self.result[self.c] = self.at(self.z, self.y)[...] + self.x_got[...]
        self.to_core()

    def to_core(self):
        spot = lambda: self.result.at[self.c]
        self.copy("end", lambda: (spot(), spot(), (self.z, self.y, self.x, 1 - self.c)))

    def end(self):
        self.wait("end")


FLOW_REFS = 6
FLOW_NAMES = ("D0", "D1", "D2", "U0", "U1", "U2", "O", "A", "B", "S")
SCHEDULE = {
    "d0": ("D0",),
    "u0": ("U0",),
    "1b1": ("D0", "U0",),
    "d1": ("D1",),
    "u1": ("U1",),
    "2b1": ("U1", "D1",),
    "d2": ("D0", "U0", "D2",),
    "u2": ("U2",),
    "e": ("U2", "D2", "O",),
    "s01": ("U1", "D1",),
    "s10": ("O",),
    "s11": ("D0",),
    "s21": ("U0",),
    "o11": ("D1",),
    "o12": ("D2",),
    "o21": ("U0",),
    "m": ("U1", "D0", "U2",),
    "q": ("B", "D0", "D1", "U0", "A", "O",),
    "n": ("D2",),
    "f0": ("B", "U1", "U2", "D1", "U0",),
    "f1": ("A", "D2",),
    "f2": ("U1", "D2", "S",),
    "tail": ("O", "U1", "S", "U2", "B", "A", "S", "A", "O", "U2", "B", "O", "U2", "S", "B", "S", "A", "B", "S", "A", "A",),
}


def flow_scratch(shape):
    shares, tail = shape[0], shape[2:]
    block = tail[-2:]
    first = (shares,) + block if len(tail) == 3 else block
    slots = 16
    return [pltpu.VMEM((shares,) + tail, BF16), pltpu.VMEM(first, BF16), pltpu.VMEM((4,) + block, BF16), pltpu.VMEM((3,) + block, BF16),
            pltpu.SemaphoreType.DMA((slots,)), pltpu.SemaphoreType.DMA((slots,))]


def place_of():
    d, s = lax.axis_index("dp"), lax.axis_index("seq")
    return d // 2, lax.rem(d, 2), s // 2, lax.rem(s, 2)


def greet(place):
    z, y, x, c = place
    peers = [(z, y, x, 1 - c), (z, y, 1 - x, c), (z, 1 - y, x, c)] + [(lax.rem(z + i, 4), y, x, c) for i in range(1, 4)]
    peers.append((z, y, 1 - x, 1 - c))
    barrier = pltpu.get_barrier_semaphore()
    for pz, py, px, pc in peers:
        pl.semaphore_signal(barrier, inc=1, device_id=(pz * 2 + py, px * 2 + pc), device_id_type=pl.DeviceIdType.MESH)
    pl.semaphore_wait(barrier, len(peers))


def piece_shapes(shares, features, hidden):
    share = features // shares
    down = (shares, 2, features // 2, hidden // shares // TILES)
    up = (shares, 2, 2, share, hidden // TILES // 4)
    wide = features // 3
    return (down,) * TILES + (up,) * TILES + (
        (shares, 2, share, features // 2), (shares, 2, 2, share, wide), (shares, 2, share, 3 * features // 2 - 2 * wide),
        (shares, 2, SMALL_ROWS // 2, -(-share // 128) * 128))


def middle_part(env, out_weight, up, down, mixed, x1, n2, n2_t, dm, dm_t, acc, d_n2, act_all, d_hidden_all, load_sem, weight_sem):
    total, features = x1.shape
    hidden = env.up.shape[1]
    tile = hidden // TILES
    shares = env.shares
    reach = hidden // shares
    width = reach // TILES
    share = features // shares
    line = lambda ref: ref[...].reshape(1, ref.shape[0])
    blocks = [slice(i, i + SHARED) for i in range(0, total, SHARED)]

    def weight_loads(j):
        made = []
        for d in range(shares):
            first = d * reach + j * width
            k = 2 * (shares * (j % 2) + d)
            made.append(pltpu.make_async_copy(env.up.at[:, pl.ds(first, width)], up.at[j % 2, :, pl.ds(d * width, width)], weight_sem.at[k]))
            made.append(pltpu.make_async_copy(env.down.at[pl.ds(first, width)], down.at[j % 2, pl.ds(d * width, width)], weight_sem.at[k + 1]))
        return made

    first_loads = [pltpu.make_async_copy(env.out_weight, out_weight, load_sem.at[0]), pltpu.make_async_copy(env.x, x1, load_sem.at[1]),
                   pltpu.make_async_copy(env.cot, dm, load_sem.at[2])]
    for g in range(env.mixed.shape[0]):
        first_loads.append(pltpu.make_async_copy(env.mixed.at[g], mixed.at[:, pl.ds(g * 128, 128)], load_sem.at[3 + g]))
    pending = {0: weight_loads(0), 1: weight_loads(1)}
    for made in first_loads + pending[0] + pending[1]:
        made.start()
    env.greet()
    wait_all(first_loads)
    x1[...] = x1[...] + (mm(mixed[...], out_weight[...]) + line(env.out_bias))
    for rows in blocks:
        after = x1[rows]
        xhat, _ = normalize(after)
        n2[rows] = (xhat * line(env.gain2) + line(env.shift2)).astype(BF16)
        dm[rows] = (dm[rows].astype(F32) * env.valid[rows, 0:1]).astype(BF16)
    n2_t[...] = n2[...].T
    dm_t[...] = dm[...].T
    acc[...] = jnp.zeros_like(acc)
    d_n2[...] = jnp.zeros_like(d_n2)
    env.small[7:8, :] = row_sum(dm[...].astype(F32))
    for j in range(TILES):
        up_j, down_j = up.at[j % 2], down.at[j % 2]
        wait_all(pending[j])
        tile_bias = jnp.concatenate([env.up_bias[d * reach + j * width:d * reach + (j + 1) * width].reshape(1, width) for d in range(shares)], 1)
        chunk = tile // CHUNKS
        products = lambda cols: (mm(n2[...], up_j[:, cols]), mm(dm[...], down_j[cols], NT))
        parts = [slice(i, i + chunk) for i in range(0, tile, chunk)]
        ready = products(parts[0])
        sums = []
        for i, cols in enumerate(parts):
            h, d_act = ready[0] + tile_bias[:, cols], ready[1]
            if i + 1 < len(parts):
                ready = products(parts[i + 1])
            half, slope = gelu_parts(h)
            d_hidden = (slope * d_act).astype(BF16)
            act_all[:, cols] = (h * half).astype(BF16)
            d_hidden_all[:, cols] = d_hidden
            sums.append(row_sum(d_hidden.astype(F32)))
            env.tick(f"{j}b{i}")
        bias_sum = jnp.concatenate(sums, 1)
        acc[...] += mm(act_all[...], down_j[...])
        d_n2[...] += mm(d_hidden_all[...], up_j[...], NT)
        env.tick(f"{j}c")
        if j + 2 < TILES:
            pending[j + 2] = weight_loads(j + 2)
            for made in pending[j + 2]:
                made.start()
        for d in range(shares):
            env.up_bias_grad[:, d * reach + j * width:d * reach + (j + 1) * width] = bias_sum[:, d * width:(d + 1) * width]
        g_down, g_up = env.pieces[j], env.pieces[TILES + j]
        for core in range(2):
            rows = slice(core * (features // 2), (core + 1) * (features // 2))
            out = mm(dm_t[rows], act_all[...]).astype(BF16)
            for d in range(shares):
                g_down[d, core] = out[:, d * width:(d + 1) * width]
        env.tick(f"d{j}")
        wide = g_up.shape[4]
        out = mm(n2_t[...], d_hidden_all[...]).astype(BF16)
        for d in range(shares):
            rows = slice(d * share, (d + 1) * share)
            for core in range(2):
                for half_x in range(2):
                    first = (2 * core + half_x) * wide
                    g_up[d, core, half_x] = out[rows, first:first + wide]
        env.tick(f"u{j}")
    sums = [jnp.zeros((1, features), F32)] * 3
    for rows in blocks:
        after = x1[rows]
        env.out_work[rows] = (env.valid[rows, 0:1] * (after + (acc[rows] + line(env.down_bias)))).astype(BF16)
        xhat, rstd = normalize(after)
        d_norm = d_n2[rows]
        d_x1 = dm[rows].astype(F32) + norm_back(d_norm, line(env.gain2), xhat, rstd)
        env.d_x1[rows] = d_x1
        d_a = d_x1.astype(BF16)
        n2[rows] = d_a
        sums = [a + row_sum(b) for a, b in zip(sums, (d_a.astype(F32), d_norm * xhat, d_norm))]
    d_mixed = mm(n2[...], out_weight[...], NT).astype(BF16)
    for g in range(features // 128):
        env.d_mixed[g] = d_mixed[:, g * 128:(g + 1) * 128]
    env.after_middle()
    out = mm(mixed[...].T, n2[...]).astype(BF16)
    g_out = env.pieces[2 * TILES]
    for d in range(shares):
        for core in range(2):
            g_out[d, core] = out[d * share:(d + 1) * share, core * (features // 2):(core + 1) * (features // 2)]
    for row, value in zip((2, 5, 6), sums):
        env.small[row:row + 1, :] = value
    env.tick("e")


def attention_part(env, matrix, own, shared_q, shared_kv, own_mixed, shared_mixed, own_d, shared_dq, shared_dkv, joined, normed, x_in, d_work,
                   d_mirror, weight_sem):
    s, x, c = env.s, env.x_at, env.c
    other = 1 - c
    total, features = x_in.shape
    groups = own.shape[1]
    partner, across = 2 * x + other, 2 * (1 - x) + c
    mine = pl.ds(groups * c, groups)
    own_rows = span(OWN * c, OWN)
    sender = env.sender
    env.out_mover.start(MOVES)
    loads = [pltpu.make_async_copy(a, b, weight_sem.at[i]) for i, (a, b) in enumerate((
        (env.shared_q, shared_q), (env.shared_kv, shared_kv), (env.shared_mixed, shared_mixed), (env.own, own), (env.own_mixed, own_mixed), (env.weight, matrix), (env.normed, normed), (env.x, x_in)))]
    for load in loads:
        load.start()
    key_spot = lax.broadcasted_iota(jnp.int32, (KEYS, 1), 0)
    shared_dm_copies, own_dm_copies = env.exchange_copies()
    wait_all(shared_dm_copies + loads[0:3])
    for p in range(groups):
        attend_back(p, shared_q, shared_kv.at[0], shared_kv.at[1], env.shared_dm, shared_mixed, env.shared_log, shared_slots(key_spot) < env.lengths[2],
                    shared_dq, shared_dkv.at[0], shared_dkv.at[1], env.head_dim, 256, lambda i: env.tick(f"s{p}{i}"))
    shared_copies = []
    for to, peer in ((other, partner), (c, None)):
        ends = [(shared_dq.at[:, span(SHARED * to, SHARED)], env.joined_lanes.at[0, mine, OWN:WORK])]
        for chip, rows in ((x, slice(OWN, WORK)), (1 - x, slice(WORK, TALL))):
            ends.append((shared_dkv.at[:, :, span(OWN * chip + SHARED * to, SHARED)], env.joined_lanes.at[1:3, mine, rows]))
        shared_copies += [sender.near(*pair) if peer is None else sender.far(*pair, peer) for pair in ends]
    wait_all(own_dm_copies + loads[3:5])
    for p in range(groups):
        attend_back(p, own.at[0], own.at[1], own.at[2], env.own_dm, own_mixed, env.own_log,
                    own_slots(key_spot) < jnp.where(x == 0, env.lengths[0], env.lengths[1]),
                    own_d.at[0], own_d.at[1], own_d.at[2], env.head_dim, 256, lambda i: env.tick(f"o{p}{i}"))
    own_copies = [
        sender.far(own_d.at[:, :, span(OWN * other, OWN)], env.joined_lanes.at[:, mine, 0:OWN], partner),
        sender.near(own_d.at[:, :, own_rows], env.joined_lanes.at[:, mine, 0:OWN]),
    ]
    wait_all(loads[5:])
    normed_t = normed[...].T
    wait_all(own_copies + shared_copies)
    blocks = [slice(i, i + SHARED) for i in range(0, total, SHARED)]
    joined[WORK:TALL, 0:features] = jnp.zeros((SHARED, features), BF16)
    for part in range(3):
        height = TALL if part else WORK
        for g in range(2 * groups):
            at = (part * 2 * groups + g) * 128
            joined[0:height, at:at + 128] = env.joined_lanes[part, g, 0:height]
    d_mirror[...] = mm(joined[WORK:TALL, features:], matrix[:, features:], NT).astype(BF16)
    mirror_copy = sender.far(d_mirror, env.other_mirror, across)
    env.tick("m")
    half = 3 * features // 2
    g_a, g_b, packed = env.pieces[2 * TILES + 1:]
    wide = g_a.shape[4]
    share = features // env.shares
    for core in range(2):
        out = mm(normed_t, joined[:, core * half:(core + 1) * half]).astype(BF16)
        for d in range(env.shares):
            rows = slice(d * share, (d + 1) * share)
            for half_x in range(2):
                g_a[d, core, half_x] = out[rows, half_x * wide:(half_x + 1) * wide]
            g_b[d, core] = out[rows, 2 * wide:]
    env.tick("q")
    sums = [jnp.zeros((1, features), F32)] * 4
    tables = jnp.zeros((TABLE_ROWS, 2 * features), F32)
    d_norms = mm(joined[0:WORK], matrix[...], NT)
    env.tick("n")
    for i, rows in enumerate(blocks):
        d_norm = d_norms[rows]
        if rows.start == OWN:
            mirror_copy.wait()
            d_norm = d_norm + env.other_mirror[...].astype(F32)
        xhat, rstd = normalize(x_in[rows])
        terms = (joined[rows, 0:features].astype(F32), joined[rows, 2 * features:].astype(F32), d_norm * xhat, d_norm)
        sums = [a + row_sum(b) for a, b in zip(sums, terms)]
        d_x = env.d_x1[rows] + norm_back(d_norm, env.gain1[...].reshape(1, features), xhat, rstd)
        high, low = split_high_low(d_x)
        d_work[rows] = high
        tables = tables + mm(one_hot(env.ids[0:1, rows], env.ids[1:2, rows]), jnp.concatenate([high, low], 1))
        if i < 2:
            env.tick(f"f{i}")
    d_mover = Mover(s, env.d_patches, d_work, env.d_send, env.d_recv, True)
    sums[1] = sums[1] + row_sum(joined[WORK:TALL, 2 * features:].astype(F32))
    d_mover.start(MOVES)
    small = env.small
    small[16:16 + TABLE_ROWS, :] = tables[:, 0:features] + tables[:, features:]
    for row, value in zip((0, 1, 3, 4), sums):
        small[row:row + 1, :] = value
    repeat = env.up_bias_grad.shape[1] // features
    height = packed.shape[2]
    if share != packed.shape[3]:
        packed[...] = jnp.zeros_like(packed)
    for d in range(env.shares):
        for r in range(repeat):
            first = (d * repeat + r) * share
            small[8 + r:9 + r, d * share:(d + 1) * share] = env.up_bias_grad[:, first:first + share]
        for core in range(2):
            packed[d, core, :, 0:share] = small[core * height:(core + 1) * height, d * share:(d + 1) * share].astype(BF16)
    env.tick("f2")
    env.tick("tail")
    for mover in (env.out_mover, d_mover):
        mover.wait(MOVES)
        mover.drain(MOVES)


class Env:
    pass


BACK_INPUTS = ("lengths", "valid", "x", "mixed", "cot", "out_weight", "out_bias", "gain2", "shift2", "up", "up_bias", "down", "down_bias",
               "own", "shared_q", "shared_kv", "own_mixed", "shared_mixed", "own_log", "shared_log", "weight", "normed", "ids", "gain1")
IN_VMEM = ("valid", "out_bias", "gain2", "shift2", "up_bias", "down_bias", "own_log", "shared_log", "ids", "gain1")
BACK_SCRATCH = ("d_mixed", "own_dm", "shared_dm", "other_mirror", "joined_lanes", "d_x1", "out_work", "small", "up_bias_grad", "zeros",
                "out_send", "out_recv", "d_send", "d_recv", "send", "recv", "dm_send", "dm_recv", "zero_sem")


def backward_body(head_dim, shares, custom, features, hidden, *refs):
    env = Env()
    refs = list(refs)
    take = lambda count: [refs.pop(0) for _ in range(count)]
    for name, ref in zip(BACK_INPUTS, take(len(BACK_INPUTS))):
        setattr(env, name, ref)
    count = len(FLOW_NAMES)
    env.output, env.d_patches = take(2)
    outs = take(count)
    for name, ref in zip(BACK_SCRATCH, take(len(BACK_SCRATCH))):
        setattr(env, name, ref)
    env.head_dim, env.shares = head_dim, shares
    env.s, env.x_at, env.c = seq_place()
    flows = {}
    if custom:
        place = place_of()
        env.pieces = take(count)
        for i, name in enumerate(FLOW_NAMES):
            flows[name] = Flow(env.pieces[i], outs[i], take(FLOW_REFS), place)
        env.greet = lambda: greet(place)
    else:
        env.pieces = outs
        env.greet = lambda: greet_group(env.s)

    def tick(point):
        for name in SCHEDULE.get(point, ()):
            if custom:
                flows[name].advance()

    env.tick = tick
    env.sender = Sender(env.send, env.recv)
    env.out_mover = Mover(env.s, env.output, env.out_work, env.out_send, env.out_recv, True)
    env.zeros[...] = jnp.zeros_like(env.zeros)
    env.small[...] = jnp.zeros_like(env.small)

    def fill(act):
        @pl.when(env.s == UNUSED[0])
        def _():
            for i, array in enumerate((env.output, env.d_patches)):
                for clip in range(3):
                    act(pltpu.make_async_copy(env.zeros, array.at[clip, pl.ds(UNUSED[1], ROWS - UNUSED[1])], env.zero_sem.at[3 * i + clip]))

    fill(lambda made: made.start())

    groups = features // 256

    def exchange_copies():
        other = 1 - env.c
        partner = 2 * env.x_at + other
        mine, theirs = pl.ds(groups * env.c, groups), pl.ds(groups * other, groups)
        places = ((env.shared_dm.at[:, span(SHARED * env.c, SHARED)], slice(OWN, WORK)), (env.own_dm.at[:, span(OWN * env.c, OWN)], slice(0, OWN)))
        sender = Sender(env.dm_send, env.dm_recv)
        return [[sender.far(env.d_mixed.at[theirs, rows], place, partner, False), sender.near(env.d_mixed.at[mine, rows], place, False)]
                for place, rows in places]

    def after_middle():
        for made in sum(exchange_copies(), []):
            made.start()

    env.exchange_copies = exchange_copies
    env.after_middle = after_middle
    tile = hidden // TILES
    dma = pltpu.SemaphoreType.DMA
    wide, tall = lambda kind: pltpu.VMEM((WORK, features), kind), pltpu.VMEM((features, WORK), BF16)
    lanes = lambda *lead: pltpu.VMEM(lead + (128,), BF16)
    pl.run_scoped(
        functools.partial(middle_part, env), pltpu.VMEM((features, features), BF16), pltpu.VMEM((2, features, tile), BF16),
        pltpu.VMEM((2, tile, features), BF16), wide(BF16), wide(F32), wide(BF16), tall, wide(BF16), tall, wide(F32), wide(F32),
        pltpu.VMEM((WORK, tile), BF16), pltpu.VMEM((WORK, tile), BF16), dma((3 + 2 * groups,)), dma((4 * shares,)))
    pl.run_scoped(
        functools.partial(attention_part, env), pltpu.VMEM((features, 3 * features), BF16), lanes(3, groups, KEYS), lanes(groups, OWN),
        lanes(2, groups, KEYS), lanes(groups, KEYS), lanes(groups, OWN), lanes(3, groups, KEYS), lanes(groups, OWN), lanes(2, groups, KEYS),
        pltpu.VMEM((TALL, 3 * features), BF16), pltpu.VMEM((TALL, features), BF16), wide(F32), wide(BF16),
        pltpu.VMEM((SHARED, features), BF16), dma((8,)))
    fill(lambda made: made.wait())
    assert all(flow.done == len(flow.stages) for flow in flows.values())


def backward(inputs, head_dim, shares, custom):
    features, hidden = inputs["up"].shape
    groups = features // 256
    anywhere, vmem = pl.BlockSpec(memory_space=pl.ANY), pl.BlockSpec(memory_space=pltpu.VMEM)
    dma = pltpu.SemaphoreType.DMA
    lanes = lambda *lead: pltpu.VMEM(lead + (128,), BF16)
    moves = len(MOVES)
    shapes = piece_shapes(shares, features, hidden)
    specs = [vmem if name in IN_VMEM else anywhere for name in BACK_INPUTS]
    specs[0] = pl.BlockSpec(memory_space=pltpu.SMEM)
    scratch = [
        lanes(2 * groups, WORK), lanes(groups, KEYS), lanes(groups, OWN), pltpu.VMEM((SHARED, features), BF16), lanes(3, 2 * groups, TALL),
        pltpu.VMEM((WORK, features), F32), pltpu.VMEM((WORK, features), BF16), pltpu.VMEM((SMALL_ROWS, features), F32),
        pltpu.VMEM((1, hidden), F32), pltpu.VMEM((ROWS - UNUSED[1], features), BF16),
        dma((moves,)), dma((moves,)), dma((moves,)), dma((moves,)), dma((24,)), dma((24,)), dma((4,)), dma((4,)), dma((6,)),
    ]
    if custom:
        scratch += [pltpu.VMEM(shape, BF16) for shape in shapes]
        scratch += [ref for shape in shapes for ref in flow_scratch(shape)]
    rows = jax.ShapeDtypeStruct((3, ROWS, features), BF16)
    return pl.pallas_call(
        functools.partial(backward_body, head_dim, shares, custom, features, hidden),
        in_specs=specs,
        out_specs=[anywhere] * 2 + [vmem] * len(shapes),
        out_shape=[rows, rows] + [jax.ShapeDtypeStruct(shape[1:] if custom else shape, BF16) for shape in shapes],
        scratch_shapes=scratch,
        compiler_params=pltpu.CompilerParams(collective_id=0, has_side_effects=True, vmem_limit_bytes=63 * MIB),
    )(*(inputs[name] for name in BACK_INPUTS))


def assemble_body(time_count, freq_count, *refs):
    count = len(FLOW_NAMES)
    pieces = refs[0:count]
    outs = refs[count:]
    down, up, out, qkv_a, qkv_b, packed = pieces[0:TILES], pieces[TILES:2 * TILES], *pieces[2 * TILES:]
    (qkv_out, qb, vb, out_out, ob, n1g, n1s, n2g, n2s, up_out, up_b, down_out, db, time_out, freq_out) = outs
    wide, rest = qkv_a.shape[3], qkv_b.shape[2]
    half = 2 * wide + rest
    for core in range(2):
        for half_x in range(2):
            first = core * half + half_x * wide
            qkv_out[:, first:first + wide] = qkv_a[core, half_x].astype(F32)
        qkv_out[:, core * half + 2 * wide:(core + 1) * half] = qkv_b[core].astype(F32)
        cols = out.shape[2]
        out_out[:, core * cols:(core + 1) * cols] = out[core].astype(F32)
    width = down[0].shape[2]
    for j in range(TILES):
        for core in range(2):
            high = down[j].shape[1]
            down_out[j * width:(j + 1) * width, core * high:(core + 1) * high] = down[j][core].astype(F32).T
            for half_x in range(2):
                span_x = up[j].shape[3]
                for k in range(span_x // width):
                    block = ((2 * core + half_x) * span_x) // width + k
                    first = (block * TILES + j) * width
                    up_out[:, first:first + width] = up[j][core, half_x, :, k * width:(k + 1) * width].astype(F32)
    small = jnp.concatenate([packed[0], packed[1]], 0).astype(F32)
    share = qb.shape[0]
    for row, ref in ((0, qb), (1, vb), (2, ob), (3, n1g), (4, n1s), (5, n2g), (6, n2s), (7, db)):
        ref[...] = small[row, 0:share]
    for r in range(up_b.shape[0] // share):
        up_b[r * share:(r + 1) * share] = small[8 + r, 0:share]
    time_out[...] = small[16:16 + TABLE_ROWS].T[0:share, 0:time_count]
    freq_out[...] = small[16 + FREQ_ROW:16 + FREQ_ROW + freq_count, 0:share]


def assemble(pieces, features, hidden, shares, time_count, freq_count):
    share = features // shares
    line = (share,)
    shapes = [(share, 3 * features), line, line, (share, features), line, line, line, line, line, (share, hidden), (hidden // shares,),
              (hidden // shares, features), line, (share, time_count), (freq_count, share)]
    return pl.pallas_call(
        functools.partial(assemble_body, time_count, freq_count),
        out_shape=[jax.ShapeDtypeStruct(shape, F32) for shape in shapes],
        compiler_params=params(),
    )(*pieces)


def reduce_native(pieces, time_count, freq_count):
    def total(part, axis):
        return lax.psum(lax.psum_scatter(part, "dp", scatter_dimension=axis, tiled=True), "seq").astype(F32)

    pieces = [p[0] for p in pieces]
    down = jnp.concatenate([p.reshape(-1, p.shape[2]) for p in pieces[0:TILES]], 1)
    up = jnp.concatenate([p[c, h] for p in pieces[TILES:2 * TILES] for c in range(2) for h in range(2)], 1)
    out, qkv_a, qkv_b, packed = pieces[2 * TILES:]
    qkv = jnp.concatenate([part for c in range(2) for part in (qkv_a[c, 0], qkv_a[c, 1], qkv_b[c])], 1)
    small = packed.reshape(SMALL_ROWS, -1)
    repeat = up.shape[1] // small.shape[1]
    up_bias = total(small[8:8 + repeat].reshape(-1), 0)
    small = total(small, 1)
    return (
        total(qkv, 0), small[0], small[1], total(jnp.concatenate([out[0], out[1]], 1), 0), small[2], small[3], small[4], small[5], small[6],
        total(up, 0), up_bias, total(down, 1).T, small[7], small[16:16 + time_count], small[16 + FREQ_ROW:16 + FREQ_ROW + freq_count],
    )


def shards(
    patches,
    cotangent,
    time_ids,
    freq_ids,
    lengths,
    qkv_weight,
    query_bias,
    value_bias,
    out_weight,
    out_bias,
    norm1_gain,
    norm1_shift,
    norm2_gain,
    norm2_shift,
    up_weight,
    up_bias,
    down_weight,
    down_bias,
    time_table,
    freq_table,
):
    features = patches.shape[2]
    head_dim = features // HEADS
    assert patches.shape[:2] == (3, ROWS) and lax.axis_size("seq") == 4
    custom = lax.axis_size("dp") == 8
    shares = 8 if custom else 1
    x, normed, own, shared_q, shared_kv, own_log, shared_log, own_mixed, shared_mixed, mixed, cot, ids, valid = forward(
        lengths, patches, cotangent, time_ids, freq_ids, time_table, freq_table, norm1_gain, norm1_shift, qkv_weight, query_bias, value_bias,
        head_dim
    )
    inputs = dict(
        lengths=lengths, valid=valid, x=x, mixed=mixed, cot=cot, out_weight=out_weight, out_bias=out_bias, gain2=norm2_gain,
        shift2=norm2_shift, up=up_weight, up_bias=up_bias, down=down_weight, down_bias=down_bias, own=own, shared_q=shared_q,
        shared_kv=shared_kv, own_mixed=own_mixed, shared_mixed=shared_mixed, own_log=own_log, shared_log=shared_log, weight=qkv_weight, normed=normed, ids=ids, gain1=norm1_gain)
    output, d_patch, *pieces = backward(inputs, head_dim, shares, custom)
    counts = time_table.shape[0], freq_table.shape[0]
    if custom:
        *rest, time_grad, freq_grad = assemble(pieces, features, up_weight.shape[1], shares, *counts)
        return (output, d_patch, *rest, time_grad.T, freq_grad)
    return (output, d_patch) + reduce_native(pieces, *counts)


def solution(mesh):
    clip_spec, row_spec, one = P("dp", "seq", None), P("dp", "seq"), P("dp")
    matrix = P("dp", None)
    return jax.shard_map(
        shards,
        mesh=mesh,
        in_specs=(clip_spec, clip_spec, row_spec, row_spec, one) + (P(),) * 15,
        out_specs=(clip_spec, clip_spec, matrix, one, one, matrix, one, one, one, one, one, matrix, one, matrix, one, P(None, "dp"), P(None, "dp")),
        check_vma=False,
    )
```

```python
import functools
import math

import jax
import jax.numpy as jnp
from jax import lax
from jax.experimental import pallas as pl
from jax.experimental.pallas import tpu as pltpu
from jax.sharding import PartitionSpec as P

HEADS = 12
EPS = 1e-06
NEGATIVE = -1000000000.0
FREQ_ROW = 104
TABLE_ROWS = 128
SMALL_ROWS = 32 + TABLE_ROWS
TILES = 3
CHUNKS = 2
UP_SPLIT = (False, True, False)
PAIR_SPLIT = (True, True, False)
F32 = jnp.float32
BF16 = jnp.bfloat16
NN = (((1,), (0,)), ((), ()))
NT = (((1,), (1,)), ((), ()))
TN = (((0,), (0,)), ((), ()))
MIB = 1 << 20


def mm(left, right, dims=NN):
    return lax.dot_general(left, right, dims, preferred_element_type=F32)


def params(limit=60):
    return pltpu.CompilerParams(vmem_limit_bytes=limit * MIB)


def row_sum(values):
    return jnp.sum(values, 0, keepdims=True)


def normalize(values):
    center = values - jnp.mean(values, -1, keepdims=True)
    rstd = lax.rsqrt(jnp.mean(center * center, -1, keepdims=True) + EPS)
    return center * rstd, rstd


def norm_back(d_out, gain, xhat, rstd):
    u = d_out * gain
    inner = jnp.mean(u * xhat, -1, keepdims=True)
    return rstd * (u - jnp.mean(u, -1, keepdims=True) - xhat * inner)


def gelu_parts(h):
    half = 0.5 * (1.0 + lax.erf(h * (1.0 / math.sqrt(2.0))))
    return half, half + h * jnp.exp(h * h * -0.5) * (1.0 / math.sqrt(2.0 * math.pi))


def split_high_low(values):
    high = values.astype(BF16)
    return high, (values - high.astype(F32)).astype(BF16)


def one_hot(time_row, freq_row):
    spot = lax.broadcasted_iota(jnp.int32, (TABLE_ROWS, time_row.shape[1]), 0)
    hit = (spot == time_row) | (spot == freq_row + FREQ_ROW)
    return jnp.where(hit, 1.0, 0.0).astype(BF16)


ROWS = 224
OWN = 352
SHARED = 176
WORK = OWN + SHARED
KEYS = 2 * OWN
TALL = WORK + SHARED
SHARED_MOVES = (
    (0, 2, 176, 48, 3, 384), (1, 2, 176, 48, 3, 432), (2, 2, 176, 48, 3, 480), (3, 2, 0, 32, 3, 352),
    (0, 2, 0, 176, 0, 352), (1, 2, 0, 176, 1, 352), (2, 2, 0, 176, 2, 352),
)
OWN_MOVES = (
    (2, 0, 0, 128, 0, 224), (2, 0, 128, 96, 1, 224), (3, 0, 0, 32, 1, 320), (0, 1, 0, 224, 2, 0), (1, 1, 0, 224, 3, 0),
    (2, 1, 128, 96, 3, 224), (2, 1, 0, 128, 2, 224), (3, 1, 0, 32, 3, 320), (0, 0, 0, 224, 0, 0), (1, 0, 0, 224, 1, 0),
)
MIRROR_MOVES = (
    (0, 2, 0, 176, 2, 528), (1, 2, 0, 176, 3, 528), (2, 2, 0, 176, 0, 528), (0, 2, 176, 48, 1, 560), (2, 2, 176, 48, 1, 656),
    (1, 2, 176, 48, 1, 608), (3, 2, 0, 32, 1, 528),
)
MOVES = SHARED_MOVES + OWN_MOVES
ALL_MOVES = MOVES + MIRROR_MOVES
UNUSED = (3, 32)


def seq_place():
    s = lax.axis_index("seq")
    return s, s // 2, lax.rem(s, 2)


def seq_peer(s):
    return {"seq": s}


def greet_group(s):
    barrier = pltpu.get_barrier_semaphore()
    for ahead in range(1, 4):
        pl.semaphore_signal(barrier, inc=1, device_id=seq_peer(lax.rem(s + ahead, 4)), device_id_type=pl.DeviceIdType.MESH)
    pl.semaphore_wait(barrier, 3)


class Mover:
    def __init__(self, s, at_home, at_work, send, recv, back=False):
        self.s, self.at_home, self.at_work, self.send, self.recv, self.back = s, at_home, at_work, send, recv, back

    def ends(self, move):
        home, clip, first, count, work, spot = move
        a, b = self.at_home.at[clip, pl.ds(first, count)], self.at_work.at[pl.ds(spot, count)]
        return (work, b, home, a) if self.back else (home, a, work, b)

    def each(self, moves, which, act, near=True):
        for device in range(4):
            chosen = [m for m in moves if self.ends(m)[which] == device and (near or self.ends(m)[0] != self.ends(m)[2])]
            if not chosen:
                continue

            @pl.when(self.s == device)
            def _(chosen=chosen):
                for m in chosen:
                    src_device, src, dst_device, dst = self.ends(m)
                    slot = ALL_MOVES.index(m)
                    if src_device == dst_device:
                        act(False, pltpu.make_async_copy(src, dst, self.recv.at[slot]))
                    else:
                        act(True, pltpu.make_async_remote_copy(
                            src_ref=src, dst_ref=dst, send_sem=self.send.at[slot], recv_sem=self.recv.at[slot],
                            device_id=seq_peer(dst_device), device_id_type=pl.DeviceIdType.MESH))

    def start(self, moves):
        self.each(moves, 0, lambda far, made: made.start())

    def wait(self, moves):
        self.each(moves, 2, lambda far, made: made.wait_recv() if far else made.wait())

    def drain(self, moves):
        self.each(moves, 0, lambda far, made: made.wait_send(), False)


class Sender:
    def __init__(self, send, recv):
        self.send, self.recv, self.used = send, recv, 0

    def far(self, source, target, peer, begin=True):
        made = pltpu.make_async_remote_copy(
            src_ref=source, dst_ref=target, send_sem=self.send.at[self.used], recv_sem=self.recv.at[self.used],
            device_id=seq_peer(peer), device_id_type=pl.DeviceIdType.MESH)
        self.used += 1
        if begin:
            made.start()
        return made

    def near(self, source, target, begin=True):
        made = pltpu.make_async_copy(source, target, self.recv.at[self.used])
        self.used += 1
        if begin:
            made.start()
        return made


def wait_all(copies):
    for made in copies:
        made.wait()


def shift_between(spot, cuts):
    slot = spot
    for low, high, shift in cuts:
        slot = jnp.where((spot >= low) & (spot < high), spot + shift, slot)
    return slot


def own_slots(spot):
    return shift_between(spot, ((224, 352, 224), (352, 576, -128)))


def shared_slots(spot):
    return shift_between(spot, ((176, 352, 48), (352, 528, 96), (528, 560, 144), (560, 608, -384), (608, 656, -208), (656, 704, -32)))


def span(first, size):
    return pl.ds(pl.multiple_of(first, 16), size)


def lane_parts(value):
    high, rest = split_high_low(value)
    low = (value - high.astype(F32) - rest.astype(F32)).astype(BF16)
    return high, rest, low


def with_lanes(base, lane, first, columns):
    for i, column in enumerate(columns):
        base = jnp.where(lane == first + i, column, base)
    return base


def attend(query, keys, values, key_ok, mixed_out, log_out, head_dim):
    count = query.shape[1]
    lane = lax.broadcasted_iota(jnp.int32, (1, 128), 1)
    head = lane // head_dim
    scale = BF16(1.0 / math.sqrt(head_dim))
    key_bias = jnp.where(key_ok, 0.0, NEGATIVE).astype(BF16)
    per_pair = 128 // head_dim
    units = [(first, h) for first in range(0, count, OWN) for h in range(per_pair)]
    log_out[...] = jnp.zeros_like(log_out)

    def pair(p, _):
        k, v = keys[p], values[p]
        biased = [with_lanes(k, lane, free_lane(h, head_dim), (key_bias,)) for h in range(per_pair)]
        counted = [with_lanes(v, lane, free_lane(h, head_dim), (BF16(1),)) for h in range(per_pair)]

        def score(unit):
            first, h = unit
            q = jnp.where(head == h, query[p, first:first + OWN] * scale, BF16(0))
            return mm(with_lanes(q, lane, free_lane(h, head_dim), (BF16(1),)), biased[h], NT)

        ready = score(units[0])
        for i, (first, h) in enumerate(units):
            scores = ready
            if i + 1 < len(units):
                ready = score(units[i + 1])
            rows = slice(first, first + OWN)
            highest = jnp.max(scores, -1, keepdims=True)
            powers = jnp.exp(scores - highest)
            out = mm(powers.astype(BF16), counted[h])
            first_free = free_lane(h, head_dim)
            total = out[:, first_free:first_free + 1]
            out = out * (1.0 / total)
            mixed = out if h == 0 else jnp.where(head == h, out, mixed)
            log_out[rows] = jnp.where(lane == per_pair * p + h, highest + jnp.log(total), log_out[rows])
            if h == per_pair - 1:
                mixed_out[p, rows] = mixed.astype(BF16)
        return 0

    lax.fori_loop(0, query.shape[0], pair, 0)


def free_lane(h, head_dim):
    return (h + 1) * head_dim % 128


def forward_body(head_dim, lengths, patches, cot, time_ids, freq_ids, time_table, freq_table, gain, shift, weight, query_bias, value_bias,
                 x_out, n_out, own_out, shared_q_out, shared_kv_out, own_log, shared_log, own_mixed, shared_mixed, mixed_out, cot_out, id_out,
                 valid_out,
                 work, table_f32, table, ids, matrix, own_stage, shared_stage, mirror_stage,
                 patch_send, patch_recv, cot_send, cot_recv, send, recv, weight_sem):
    s, x, c = seq_place()
    features = x_out.shape[1]
    groups = own_out.shape[1]
    other = 1 - c
    loads = [pltpu.make_async_copy(weight.at[:, pl.ds(p * features, features)], matrix.at[:, pl.ds(p * features, features)], weight_sem.at[p])
             for p in range(3)]
    for load in loads:
        load.start()
    greet_group(s)
    patch_mover = Mover(s, patches, work, patch_send, patch_recv)
    cot_mover = Mover(s, cot, cot_out, cot_send, cot_recv)
    sender = Sender(send, recv)
    id_copies = []
    for i, source in enumerate((time_ids, freq_ids)):
        id_copies.append(sender.near(source, ids.at[s, i]))
        for ahead in range(1, 4):
            id_copies.append(sender.far(source, ids.at[s, i], lax.rem(s + ahead, 4)))
    patch_mover.start(ALL_MOVES)

    table_f32[...] = jnp.zeros_like(table_f32)
    table_f32[0:time_table.shape[0], :] = time_table[...]
    table_f32[FREQ_ROW:FREQ_ROW + freq_table.shape[0], :] = freq_table[...]
    high, low = split_high_low(table_f32[...])
    table[0:TABLE_ROWS, :] = high
    table[TABLE_ROWS:, :] = low
    spot = lax.broadcasted_iota(jnp.int32, (WORK, 1), 0)
    place = jnp.where(spot < OWN, jnp.where(spot < ROWS, spot + ROWS * c, spot + ROWS + 128 * c), shared_slots(spot - OWN + SHARED * s))
    limit = jnp.where(spot < OWN, jnp.where(x == 0, lengths[0], lengths[1]), lengths[2])
    valid_out[...] = jnp.broadcast_to(jnp.where(place < limit, 1.0, 0.0), valid_out.shape)
    id_out[...] = jnp.zeros_like(id_out)
    wait_all(id_copies)
    for device in range(4):
        @pl.when(s == device)
        def _(device=device):
            for home, clip, first, count, target, at in ALL_MOVES:
                if target == device:
                    for i in range(2):
                        id_out[i:i + 1, at:at + count] = ids[home, i, clip:clip + 1, first:first + count]

    bias = (query_bias[...].reshape(1, features), None, value_bias[...].reshape(1, features))

    def project(first, count, stage, own=True):
        rows = slice(first, first + count)
        hot = one_hot(id_out[0:1, rows], id_out[1:2, rows])
        value = work[rows].astype(F32) + mm(jnp.concatenate([hot, hot], 0), table[...], TN)
        if own:
            x_out[rows] = value
        xhat, _ = normalize(value)
        normed = (xhat * gain[...].reshape(1, features) + shift[...].reshape(1, features)).astype(BF16)
        n_out[c, rows] = normed
        for part in range(0 if own else 1, 3):
            out = mm(normed, matrix[:, part * features:(part + 1) * features])
            if bias[part] is not None:
                out = out + bias[part]
            out = out.astype(BF16)
            for g in range(2 * groups):
                stage[part if own else part - 1, g] = out[:, g * 128:(g + 1) * 128]

    patch_mover.wait(SHARED_MOVES)
    wait_all(loads)
    project(OWN, SHARED, shared_stage)
    q_rows, kv_rows = span(SHARED * c, SHARED), span(SHARED * s, SHARED)
    mine, theirs = pl.ds(groups * c, groups), pl.ds(groups * other, groups)
    mirror_rows = span(SHARED * (2 * (1 - x) + c), SHARED)
    partner = 2 * x + other
    shared_copies = [
        sender.far(shared_stage.at[0, theirs], shared_q_out.at[:, q_rows], partner),
        sender.far(shared_stage.at[1:3, theirs], shared_kv_out.at[:, :, kv_rows], partner),
        sender.near(shared_stage.at[0, mine], shared_q_out.at[:, q_rows]),
        sender.near(shared_stage.at[1:3, mine], shared_kv_out.at[:, :, kv_rows]),
    ]
    patch_mover.wait(OWN_MOVES)
    project(0, OWN, own_stage)
    own_rows = span(OWN * c, OWN)
    own_copies = [
        sender.far(own_stage.at[:, theirs], own_out.at[:, :, own_rows], partner),
        sender.near(own_stage.at[:, mine], own_out.at[:, :, own_rows]),
    ]
    cot_mover.start(MOVES)
    patch_mover.wait(MIRROR_MOVES)
    project(WORK, SHARED, mirror_stage, False)
    shared_copies += [
        sender.far(mirror_stage.at[:, theirs], shared_kv_out.at[:, :, mirror_rows], partner),
        sender.near(mirror_stage.at[:, mine], shared_kv_out.at[:, :, mirror_rows]),
    ]
    normed_copy = sender.far(n_out.at[c], n_out.at[c], partner)
    wait_all(own_copies)
    key_spot = lax.broadcasted_iota(jnp.int32, (KEYS, 1), 0)
    attend(own_out.at[0], own_out.at[1], own_out.at[2], own_slots(key_spot) < jnp.where(x == 0, lengths[0], lengths[1]),
           own_mixed, own_log, head_dim)
    mixed_copies = [
        sender.far(own_mixed.at[:, span(OWN * other, OWN)], mixed_out.at[mine, 0:OWN], partner),
        sender.near(own_mixed.at[:, own_rows], mixed_out.at[mine, 0:OWN]),
    ]
    wait_all(shared_copies)
    attend(shared_q_out, shared_kv_out.at[0], shared_kv_out.at[1], shared_slots(key_spot) < lengths[2],
           shared_mixed, shared_log, head_dim)
    mixed_copies += [
        sender.far(shared_mixed.at[:, span(SHARED * other, SHARED)], mixed_out.at[mine, OWN:WORK], partner),
        sender.near(shared_mixed.at[:, q_rows], mixed_out.at[mine, OWN:WORK]),
    ]
    wait_all(mixed_copies + [normed_copy])
    cot_mover.wait(MOVES)
    patch_mover.drain(ALL_MOVES)
    cot_mover.drain(MOVES)


def forward(lengths, patches, cot, time_ids, freq_ids, time_table, freq_table, gain, shift, weight, query_bias, value_bias, head_dim):
    features = patches.shape[2]
    groups = features // 256
    anywhere, vmem = pl.BlockSpec(memory_space=pl.ANY), pl.BlockSpec(memory_space=pltpu.VMEM)
    lanes = lambda *lead: jax.ShapeDtypeStruct(lead + (128,), BF16)
    dma = pltpu.SemaphoreType.DMA
    return pl.pallas_call(
        functools.partial(forward_body, head_dim),
        in_specs=[pl.BlockSpec(memory_space=pltpu.SMEM)] + [anywhere] * 4 + [vmem] * 4 + [anywhere] + [vmem] * 2,
        out_specs=[vmem] * 13,
        out_shape=[
            jax.ShapeDtypeStruct((WORK, features), F32),
            jax.ShapeDtypeStruct((2, TALL, features), BF16),
            lanes(3, groups, KEYS),
            lanes(groups, OWN),
            lanes(2, groups, KEYS),
            jax.ShapeDtypeStruct((KEYS, 128), F32),
            jax.ShapeDtypeStruct((OWN, 128), F32),
            lanes(groups, KEYS),
            lanes(groups, OWN),
            lanes(2 * groups, WORK),
            jax.ShapeDtypeStruct((WORK, features), BF16),
            jax.ShapeDtypeStruct((8, TALL), jnp.int32),
            jax.ShapeDtypeStruct((WORK, 128), F32),
        ],
        scratch_shapes=[
            pltpu.VMEM((TALL, features), BF16),
            pltpu.VMEM((TABLE_ROWS, features), F32),
            pltpu.VMEM((2 * TABLE_ROWS, features), BF16),
            pltpu.VMEM((4, 2) + time_ids.shape, jnp.int32),
            pltpu.VMEM(weight.shape, BF16),
            pltpu.VMEM((3, 2 * groups, OWN, 128), BF16),
            pltpu.VMEM((3, 2 * groups, SHARED, 128), BF16),
            pltpu.VMEM((2, 2 * groups, SHARED, 128), BF16),
            dma((len(ALL_MOVES),)), dma((len(ALL_MOVES),)), dma((len(MOVES),)), dma((len(MOVES),)), dma((24,)), dma((24,)), dma((3,)),
        ],
        compiler_params=pltpu.CompilerParams(collective_id=1, has_side_effects=True, vmem_limit_bytes=60 * MIB),
    )(lengths, patches, cot, time_ids, freq_ids, time_table, freq_table, gain, shift, weight, query_bias, value_bias)


def attend_back(p, query, keys, values, d_mixed, mixed, logs, key_ok, d_query, d_keys, d_values, head_dim, block, tick):
    count = query.shape[1]
    lane = lax.broadcasted_iota(jnp.int32, (1, 128), 1)
    head = lane // head_dim
    scale = BF16(1.0 / math.sqrt(head_dim))
    key_bias = jnp.where(key_ok, 0.0, NEGATIVE).astype(BF16)
    k, v = keys[p], values[p]
    k_t = (k * scale).T
    per_pair = 128 // head_dim
    one = BF16(1)
    k_wide = [with_lanes(k, lane, free_lane(h, head_dim), (key_bias, one, one, one)) for h in range(per_pair)]
    v_wide = [with_lanes(v, lane, free_lane(h, head_dim), (one, one, one)) for h in range(per_pair)]
    total_k = jnp.zeros((KEYS, 128), F32)
    total_v = jnp.zeros((KEYS, 128), F32)
    units = [(first, min(first + block, count), h) for first in range(0, count, block) for h in range(per_pair)]

    def products(unit):
        first, last, h = unit
        rows = slice(first, last)
        d_m = d_mixed[p, rows]
        q_head = jnp.where(head == h, query[p, rows] * scale, BF16(0))
        m_head = jnp.where(head == h, d_m, BF16(0))
        delta = jnp.sum(m_head.astype(F32) * mixed[p, rows].astype(F32), -1, keepdims=True)
        at = per_pair * p + h
        q_wide = with_lanes(q_head, lane, free_lane(h, head_dim), (one,) + lane_parts(-logs[rows, at:at + 1]))
        m_wide = with_lanes(m_head, lane, free_lane(h, head_dim), lane_parts(-delta))
        return q_head, m_head, mm(k_wide[h], q_wide, NT), mm(v_wide[h], m_wide, NT)

    ready = products(units[0])
    parts = []
    for i, (first, last, h) in enumerate(units):
        q_head, m_head, scores, d_probs = ready
        if i + 1 < len(units):
            ready = products(units[i + 1])
        probs = jnp.exp(scores)
        d_scores = (probs * d_probs).astype(BF16)
        total_v = total_v + mm(probs.astype(BF16), m_head)
        total_k = total_k + mm(d_scores, q_head)
        parts.append(mm(k_t[h * head_dim:(h + 1) * head_dim], d_scores))
        if h == per_pair - 1:
            d_query[p, first:last] = jnp.concatenate(parts, 0).T.astype(BF16)
            parts = []
            tick(first // block)
    d_keys[p] = total_k.astype(BF16)
    d_values[p] = total_v.astype(BF16)


class Flow:
    def __init__(self, source, result, refs, place, single):
        self.source, self.result, self.single = source, result, single
        self.split = len(source.shape) == (4 if single else 5)
        self.got, self.x_got, self.y_got, self.z_got, self.send, self.recv = refs
        self.z, self.y, self.x, self.c = place
        self.open = {}
        if self.split:
            self.stages = [self.begin, self.cores_x, self.x_y, self.y_z, self.z_fill, self.fill_cores, self.end]
        else:
            self.stages = [self.begin, self.cores_y, self.y_z, self.z_x, self.x_cores, self.end]
        if single:
            self.stages = [self.to_x if self.split else self.to_y] + self.stages[2:]
        self.used = 0
        self.done = 0

    def advance(self):
        self.stages[self.done]()
        self.done += 1

    def copy(self, key, ends):
        slot = self.used
        self.used += 1

        def make():
            source, target, (z, y, x, c) = ends()
            return pltpu.make_async_remote_copy(
                src_ref=source, dst_ref=target, send_sem=self.send.at[slot], recv_sem=self.recv.at[slot],
                device_id=(z * 2 + y, x * 2 + c), device_id_type=pl.DeviceIdType.MESH)

        make().start()
        self.open.setdefault(key, []).append(make)

    def wait(self, key):
        for make in self.open.pop(key):
            make().wait()

    def at(self, z, y):
        row = self.row(z * 2 + y)
        return row.at[self.x] if self.split else row

    def row(self, i):
        return self.source.at[i] if self.single else self.source.at[i, self.c]

    def begin(self):
        self.copy("core", lambda: (self.source.at[:, 1 - self.c], self.got, (self.z, self.y, self.x, 1 - self.c)))

    def cores(self):
        self.wait("core")

        def add(i, _):
            self.source[i, self.c] = self.source[i, self.c] + self.got[i]
            return 0

        lax.fori_loop(0, self.got.shape[0], add, 0)

    def cores_x(self):
        self.cores()
        self.to_x()

    def to_x(self):
        part = lambda: self.source.at[:, 1 - self.x] if self.single else self.source.at[:, self.c, 1 - self.x]
        self.copy("x", lambda: (part(), self.x_got, (self.z, self.y, 1 - self.x, self.c)))

    def cores_y(self):
        self.cores()
        self.to_y()

    def to_y(self):
        for z in range(4):
            self.copy("y", lambda z=z: (self.at(z, 1 - self.y), self.y_got.at[z], (self.z, 1 - self.y, self.x, self.c)))

    def x_y(self):
        self.wait("x")

        def add(i, _):
            spot = self.row(i).at[self.x]
            spot[...] = spot[...] + self.x_got[i]
            return 0

        lax.fori_loop(0, self.source.shape[0], add, 0)
        self.to_y()

    def y_z(self):
        self.wait("y")

        def add(z, _):
            spot = self.at(z, self.y)
            spot[...] = spot[...] + self.y_got[z]
            return 0

        lax.fori_loop(0, 4, add, 0)
        for ahead in range(1, 4):
            def ends(ahead=ahead):
                z = lax.rem(self.z + ahead, 4)
                return self.at(z, self.y), self.z_got.at[ahead - 1], (z, self.y, self.x, self.c)

            self.copy("z", ends)

    def z_sum(self):
        self.wait("z")
        total = self.at(self.z, self.y)[...].astype(F32)
        for i in range(3):
            total = total + self.z_got[i].astype(F32)
        return total.astype(BF16)

    def z_fill(self):
        self.result[self.c, self.x] = self.z_sum()
        spot = lambda: self.result.at[self.c, self.x]
        self.copy("fill", lambda: (spot(), spot(), (self.z, self.y, 1 - self.x, self.c)))

    def fill_cores(self):
        self.wait("fill")
        self.to_core()

    def z_x(self):
        spot = self.at(self.z, self.y)
        spot[...] = self.z_sum()
        self.copy("x", lambda: (self.at(self.z, self.y), self.x_got, (self.z, self.y, 1 - self.x, self.c)))

    def x_cores(self):
        self.wait("x")
        self.result[self.c] = self.at(self.z, self.y)[...] + self.x_got[...]
        self.to_core()

    def to_core(self):
        spot = lambda: self.result.at[self.c]
        self.copy("end", lambda: (spot(), spot(), (self.z, self.y, self.x, 1 - self.c)))

    def end(self):
        self.wait("end")


FLOW_REFS = 6
FLOW_NAMES = ("D0", "D1", "D2", "E0", "E1", "E2", "U0", "U1", "U2", "O", "Q0", "Q1", "Q2", "S")
SCHEDULE = {
    "d0": ("D0", "E0",),
    "u0": ("U0",),
    "1b0": ("D0", "U0",),
    "d1": ("D1",),
    "u1": ("U1", "D1", "D0", "E1",),
    "2b0": ("E0", "U1",),
    "2b1": ("U0",),
    "2e1": ("D2",),
    "u2": ("E1", "D1",),
    "2c": ("D2", "E0", "E2", "U2",),
    "e": ("R", "D0", "U0", "U2",),
    "s00": ("U1", "D1", "O",),
    "s01": ("E1",),
    "o02": ("D0", "D2", "E2", "U2",),
    "q0": ("O", "Q0", "E1",),
    "o12": ("U1",),
    "q1": ("Q1",),
    "o21": ("E2",),
    "q2": ("D1", "D2", "Q2", "E0", "D0",),
    "m": ("O",),
    "f0": ("U2", "Q1", "E2", "Q0", "D1", "D2", "U1",),
    "f1": ("Q2",),
    "f2": ("O", "E1", "S", "S", "U0", "Q1", "Q2", "U1", "Q0",),
    "tail": ("E2", "E2", "U2", "U2", "E0", "S", "D2", "Q0", "Q1", "D0", "S", "E0", "Q2", "O", "Q1", "U1", "Q0", "S", "D2", "Q1", "Q2", "S", "E1", "O", "Q0", "U0", "D1",),
}


def flow_scratch(name, shape):
    single = name[0] == "Q"
    shares, tail = shape[0], shape[1 if single else 2:]
    block = tail[-2:]
    first = (shares,) + block if len(tail) == 3 else block
    slots = 16
    return [pltpu.VMEM((8, 128) if single else (shares,) + tail, BF16), pltpu.VMEM(first, BF16), pltpu.VMEM((4,) + block, BF16), pltpu.VMEM((3,) + block, BF16),
            pltpu.SemaphoreType.DMA((slots,)), pltpu.SemaphoreType.DMA((slots,))]


def result_shape(name, shape):
    return (2,) + shape[1:] if name[0] == "Q" else shape[1:]


def place_of():
    d, s = lax.axis_index("dp"), lax.axis_index("seq")
    return d // 2, lax.rem(d, 2), s // 2, lax.rem(s, 2)


def greet(place):
    z, y, x, c = place
    peers = [(z, y, x, 1 - c), (z, y, 1 - x, c), (z, 1 - y, x, c)] + [(lax.rem(z + i, 4), y, x, c) for i in range(1, 4)]
    peers.append((z, y, 1 - x, 1 - c))
    barrier = pltpu.get_barrier_semaphore()
    for pz, py, px, pc in peers:
        pl.semaphore_signal(barrier, inc=1, device_id=(pz * 2 + py, px * 2 + pc), device_id_type=pl.DeviceIdType.MESH)
    pl.semaphore_wait(barrier, len(peers))


def piece_shapes(shares, features, hidden):
    share = features // shares
    width, tile = hidden // shares // TILES, hidden // TILES
    halved = (shares, 2, 2, features // 8, width)
    whole = (shares, 2, features // 4, width)
    up = tuple((shares, 2, 2, share, tile // 4) if split else (shares, 2, share, tile // 2) for split in UP_SPLIT)
    pairs = tuple((shares, 2, share // 2, features // 2) if split else (shares, share, features // 2) for split in PAIR_SPLIT)
    out = (shares, 2, share, features // 2)
    return (halved,) * TILES + (whole,) * TILES + up + (out,) + pairs + ((shares, 2, SMALL_ROWS // 2, -(-share // 128) * 128),)


def middle_part(env, out_weight, up, down, mixed, x1, n2, n2_t, dm, dm_t, acc, d_n2, act_all, d_hidden_all, slope_all, load_sem,
                weight_sem):
    total, features = x1.shape
    hidden = env.up.shape[1]
    tile = hidden // TILES
    shares = env.shares
    reach = hidden // shares
    width = reach // TILES
    share = features // shares
    line = lambda ref: ref[...].reshape(1, ref.shape[0])
    blocks = [slice(i, i + SHARED) for i in range(0, total, SHARED)]

    def weight_loads(j):
        made = []
        for d in range(shares):
            first = d * reach + j * width
            k = 2 * (shares * (j % 2) + d)
            made.append(pltpu.make_async_copy(env.up.at[:, pl.ds(first, width)], up.at[j % 2, :, pl.ds(d * width, width)], weight_sem.at[k]))
            made.append(pltpu.make_async_copy(env.down.at[pl.ds(first, width)], down.at[j % 2, pl.ds(d * width, width)], weight_sem.at[k + 1]))
        return made

    first_loads = [pltpu.make_async_copy(env.out_weight, out_weight, load_sem.at[0]), pltpu.make_async_copy(env.x, x1, load_sem.at[1]),
                   pltpu.make_async_copy(env.cot, dm, load_sem.at[2])]
    for g in range(env.mixed.shape[0]):
        first_loads.append(pltpu.make_async_copy(env.mixed.at[g], mixed.at[:, pl.ds(g * 128, 128)], load_sem.at[3 + g]))
    pending = {0: weight_loads(0), 1: weight_loads(1)}
    for made in first_loads + pending[0] + pending[1]:
        made.start()
    env.greet()
    wait_all(first_loads)
    x1[...] = x1[...] + (mm(mixed[...], out_weight[...]) + line(env.out_bias))
    for rows in blocks:
        after = x1[rows]
        xhat, _ = normalize(after)
        n2[rows] = (xhat * line(env.gain2) + line(env.shift2)).astype(BF16)
        dm[rows] = (dm[rows].astype(F32) * env.valid[rows, 0:1]).astype(BF16)
    n2_t[...] = n2[...].T
    dm_t[...] = dm[...].T
    acc[...] = jnp.zeros_like(acc)
    d_n2[...] = jnp.zeros_like(d_n2)
    env.small[7:8, :] = row_sum(dm[...].astype(F32))
    for j in range(TILES):
        up_j, down_j = up.at[j % 2], down.at[j % 2]
        wait_all(pending[j])
        tile_bias = jnp.concatenate([env.up_bias[d * reach + j * width:d * reach + (j + 1) * width].reshape(1, width) for d in range(shares)], 1)
        chunk = tile // CHUNKS
        parts = [slice(i, i + chunk) for i in range(0, tile, chunk)]
        forth = lambda cols: mm(n2[...], up_j[:, cols])
        back = lambda cols: mm(dm[...], down_j[cols], NT)
        ready = forth(parts[0])
        for i, cols in enumerate(parts):
            h = ready + tile_bias[:, cols]
            if i + 1 < len(parts):
                ready = forth(parts[i + 1])
            half, slope = gelu_parts(h)
            act_all[:, cols] = (h * half).astype(BF16)
            slope_all[:, cols] = slope
            env.tick(f"{j}b{i}")
        halved, whole = env.pieces[j], env.pieces[TILES + j]
        high = halved.shape[3]
        for core in range(2):
            rows = slice(core * (features // 2), (core + 1) * (features // 2))
            out = mm(dm_t[rows], act_all[...]).astype(BF16)
            for d in range(shares):
                cols = slice(d * width, (d + 1) * width)
                for half_x in range(2):
                    halved[d, core, half_x] = out[half_x * high:(half_x + 1) * high, cols]
                whole[d, core] = out[2 * high:, cols]
        env.tick(f"d{j}")
        sums = []
        ready = back(parts[0])
        for i, cols in enumerate(parts):
            d_act = ready
            if i + 1 < len(parts):
                ready = back(parts[i + 1])
            d_hidden = (slope_all[:, cols] * d_act).astype(BF16)
            d_hidden_all[:, cols] = d_hidden
            sums.append(row_sum(d_hidden.astype(F32)))
            env.tick(f"{j}e{i}")
        bias_sum = jnp.concatenate(sums, 1)
        for d in range(shares):
            env.up_bias_grad[:, d * reach + j * width:d * reach + (j + 1) * width] = bias_sum[:, d * width:(d + 1) * width]
        out = mm(n2_t[...], d_hidden_all[...]).astype(BF16)
        g_up = env.pieces[2 * TILES + j]
        for d in range(shares):
            rows = slice(d * share, (d + 1) * share)
            for core in range(2):
                first = core * (tile // 2)
                if UP_SPLIT[j]:
                    for half_x in range(2):
                        g_up[d, core, half_x] = out[rows, first + half_x * (tile // 4):first + (half_x + 1) * (tile // 4)]
                else:
                    g_up[d, core] = out[rows, first:first + tile // 2]
        env.tick(f"u{j}")
        acc[...] += mm(act_all[...], down_j[...])
        d_n2[...] += mm(d_hidden_all[...], up_j[...], NT)
        env.tick(f"{j}c")
        if j + 2 < TILES:
            pending[j + 2] = weight_loads(j + 2)
            for made in pending[j + 2]:
                made.start()
    sums = [jnp.zeros((1, features), F32)] * 3
    for rows in blocks:
        after = x1[rows]
        env.out_work[rows] = (env.valid[rows, 0:1] * (after + (acc[rows] + line(env.down_bias)))).astype(BF16)
        xhat, rstd = normalize(after)
        d_norm = d_n2[rows]
        d_x1 = dm[rows].astype(F32) + norm_back(d_norm, line(env.gain2), xhat, rstd)
        env.d_x1[rows] = d_x1
        d_a = d_x1.astype(BF16)
        n2[rows] = d_a
        sums = [a + row_sum(b) for a, b in zip(sums, (d_a.astype(F32), d_norm * xhat, d_norm))]
    d_mixed = mm(n2[...], out_weight[...], NT).astype(BF16)
    for g in range(features // 128):
        env.d_mixed[g] = d_mixed[:, g * 128:(g + 1) * 128]
    env.after_middle()
    out = mm(mixed[...].T, n2[...]).astype(BF16)
    g_out = env.pieces[3 * TILES]
    for d in range(shares):
        for core in range(2):
            g_out[d, core] = out[d * share:(d + 1) * share, core * (features // 2):(core + 1) * (features // 2)]
    for row, value in zip((2, 5, 6), sums):
        env.small[row:row + 1, :] = value
    env.tick("e")


def attention_part(env, matrix, own, shared_q, shared_kv, own_mixed, shared_mixed, own_d, shared_dq, shared_dkv, joined, normed, normed_t, pair_d, x_in,
                   d_work, d_mirror, weight_sem):
    s, x, c = env.s, env.x_at, env.c
    other = 1 - c
    total, features = x_in.shape
    groups = own.shape[1]
    partner, across = 2 * x + other, 2 * (1 - x) + c
    mine = pl.ds(groups * c, groups)
    own_rows = span(OWN * c, OWN)
    sender = env.sender
    loads = [pltpu.make_async_copy(a, b, weight_sem.at[i]) for i, (a, b) in enumerate((
        (env.shared_q, shared_q), (env.shared_kv, shared_kv), (env.shared_mixed, shared_mixed), (env.own, own), (env.own_mixed, own_mixed), (env.weight, matrix), (env.x, x_in)))]
    at = 0
    for rows in (slice(0, OWN), slice(OWN, WORK), slice(WORK, TALL)):
        for core in range(2):
            count = rows.stop - rows.start
            loads.append(pltpu.make_async_copy(env.normed.at[core, rows], normed.at[pl.ds(at, count)], weight_sem.at[len(loads)]))
            at += count
    for load in loads:
        load.start()
    key_spot = lax.broadcasted_iota(jnp.int32, (KEYS, 1), 0)
    shared_dm_copies, own_dm_copies = env.exchange_copies()
    wait_all(shared_dm_copies + loads[0:3])
    for p in range(groups):
        attend_back(p, shared_q, shared_kv.at[0], shared_kv.at[1], env.shared_dm, shared_mixed, env.shared_log, shared_slots(key_spot) < env.lengths[2],
                    shared_dq, shared_dkv.at[0], shared_dkv.at[1], env.head_dim, 256, lambda i: env.tick(f"s{p}{i}"))
    shared_copies = []
    for to, peer in ((other, partner), (c, None)):
        ends = [(shared_dq.at[:, span(SHARED * to, SHARED)], env.joined_lanes.at[0, mine, OWN:WORK])]
        for chip, rows in ((x, slice(OWN, WORK)), (1 - x, slice(WORK, TALL))):
            ends.append((shared_dkv.at[:, :, span(OWN * chip + SHARED * to, SHARED)], env.joined_lanes.at[1:3, mine, rows]))
        shared_copies += [sender.near(*pair) if peer is None else sender.far(*pair, peer) for pair in ends]
    wait_all(own_dm_copies + loads[3:5] + loads[7:])
    normed_t[...] = normed[...].T
    share = features // env.shares
    pair_d[KEYS + OWN:, 0:128] = jnp.zeros((OWN, 128), BF16)
    for p in range(groups):
        attend_back(p, own.at[0], own.at[1], own.at[2], env.own_dm, own_mixed, env.own_log,
                    own_slots(key_spot) < jnp.where(x == 0, env.lengths[0], env.lengths[1]),
                    own_d.at[0], own_d.at[1], own_d.at[2], env.head_dim, 256, lambda i: env.tick(f"o{p}{i}"))
        here, there = span(OWN * x, OWN), span(OWN * (1 - x), OWN)
        pair_d[KEYS:KEYS + OWN, 0:128] = shared_dq[p]
        for part in range(3):
            cols = slice(part * 128, (part + 1) * 128)
            pair_d[0:KEYS, cols] = own_d[part, p]
            if part:
                pair_d[KEYS:KEYS + OWN, cols] = shared_dkv[part - 1, p, here]
                pair_d[KEYS + OWN:, cols] = shared_dkv[part - 1, p, there]
        out = mm(normed_t[...], pair_d[...]).astype(BF16)
        piece = env.pieces[3 * TILES + 1 + p]
        for d in range(env.shares):
            if PAIR_SPLIT[p]:
                for half_x in range(2):
                    first = (2 * d + half_x) * (share // 2)
                    piece[d, half_x] = out[first:first + share // 2]
            else:
                piece[d] = out[d * share:(d + 1) * share]
        env.tick(f"q{p}")
    own_copies = [
        sender.far(own_d.at[:, :, span(OWN * other, OWN)], env.joined_lanes.at[:, mine, 0:OWN], partner),
        sender.near(own_d.at[:, :, own_rows], env.joined_lanes.at[:, mine, 0:OWN]),
    ]
    wait_all(loads[5:7])
    wait_all(own_copies + shared_copies)
    blocks = [slice(i, i + SHARED) for i in range(0, total, SHARED)]
    joined[WORK:TALL, 0:features] = jnp.zeros((SHARED, features), BF16)
    for part in range(3):
        height = TALL if part else WORK
        for g in range(2 * groups):
            at = (part * 2 * groups + g) * 128
            joined[0:height, at:at + 128] = env.joined_lanes[part, g, 0:height]
    d_mirror[...] = mm(joined[WORK:TALL, features:], matrix[:, features:], NT).astype(BF16)
    mirror_copy = sender.far(d_mirror, env.other_mirror, across)
    env.tick("m")
    packed = env.pieces[-1]
    sums = [jnp.zeros((1, features), F32)] * 4
    tables = jnp.zeros((TABLE_ROWS, 2 * features), F32)
    d_norms = mm(joined[0:WORK], matrix[...], NT)
    env.tick("n")
    for i, rows in enumerate(blocks):
        d_norm = d_norms[rows]
        if rows.start == OWN:
            mirror_copy.wait()
            d_norm = d_norm + env.other_mirror[...].astype(F32)
        xhat, rstd = normalize(x_in[rows])
        terms = (joined[rows, 0:features].astype(F32), joined[rows, 2 * features:].astype(F32), d_norm * xhat, d_norm)
        sums = [a + row_sum(b) for a, b in zip(sums, terms)]
        d_x = env.d_x1[rows] + norm_back(d_norm, env.gain1[...].reshape(1, features), xhat, rstd)
        high, low = split_high_low(d_x)
        d_work[rows] = high
        tables = tables + mm(one_hot(env.ids[0:1, rows], env.ids[1:2, rows]), jnp.concatenate([high, low], 1))
        if i < 2:
            env.tick(f"f{i}")
    d_mover = Mover(s, env.d_patches, d_work, env.d_send, env.d_recv, True)
    sums[1] = sums[1] + row_sum(joined[WORK:TALL, 2 * features:].astype(F32))
    d_mover.start(MOVES)
    small = env.small
    small[16:16 + TABLE_ROWS, :] = tables[:, 0:features] + tables[:, features:]
    for row, value in zip((0, 1, 3, 4), sums):
        small[row:row + 1, :] = value
    repeat = env.up_bias_grad.shape[1] // features
    height = packed.shape[2]
    if share != packed.shape[3]:
        packed[...] = jnp.zeros_like(packed)
    for d in range(env.shares):
        for r in range(repeat):
            first = (d * repeat + r) * share
            small[8 + r:9 + r, d * share:(d + 1) * share] = env.up_bias_grad[:, first:first + share]
        for core in range(2):
            packed[d, core, :, 0:share] = small[core * height:(core + 1) * height, d * share:(d + 1) * share].astype(BF16)
    env.tick("f2")
    env.tick("tail")
    for mover in (env.out_mover, d_mover):
        mover.wait(MOVES)
        mover.drain(MOVES)


class Env:
    pass


BACK_INPUTS = ("lengths", "valid", "x", "mixed", "cot", "out_weight", "out_bias", "gain2", "shift2", "up", "up_bias", "down", "down_bias",
               "own", "shared_q", "shared_kv", "own_mixed", "shared_mixed", "own_log", "shared_log", "weight", "normed", "ids", "gain1")
IN_VMEM = ("valid", "out_bias", "gain2", "shift2", "up_bias", "down_bias", "own_log", "shared_log", "ids", "gain1")
BACK_SCRATCH = ("d_mixed", "own_dm", "shared_dm", "other_mirror", "joined_lanes", "d_x1", "out_work", "small", "up_bias_grad", "zeros",
                "out_send", "out_recv", "d_send", "d_recv", "send", "recv", "dm_send", "dm_recv", "zero_sem")


def backward_body(head_dim, shares, custom, features, hidden, *refs):
    env = Env()
    refs = list(refs)
    take = lambda count: [refs.pop(0) for _ in range(count)]
    for name, ref in zip(BACK_INPUTS, take(len(BACK_INPUTS))):
        setattr(env, name, ref)
    count = len(FLOW_NAMES)
    env.output, env.d_patches = take(2)
    outs = take(count)
    for name, ref in zip(BACK_SCRATCH, take(len(BACK_SCRATCH))):
        setattr(env, name, ref)
    env.head_dim, env.shares = head_dim, shares
    env.s, env.x_at, env.c = seq_place()
    flows = {}
    if custom:
        place = place_of()
        env.pieces = take(count)
        for i, name in enumerate(FLOW_NAMES):
            flows[name] = Flow(env.pieces[i], outs[i], take(FLOW_REFS), place, name[0] == "Q")
        env.greet = lambda: greet(place)
    else:
        env.pieces = outs
        env.greet = lambda: greet_group(env.s)

    def tick(point):
        for name in SCHEDULE.get(point, ()):
            if name == "R":
                env.out_mover.start(MOVES)
            elif custom:
                flows[name].advance()

    env.tick = tick
    env.sender = Sender(env.send, env.recv)
    env.out_mover = Mover(env.s, env.output, env.out_work, env.out_send, env.out_recv, True)
    env.zeros[...] = jnp.zeros_like(env.zeros)
    env.small[...] = jnp.zeros_like(env.small)

    def fill(act):
        @pl.when(env.s == UNUSED[0])
        def _():
            for i, array in enumerate((env.output, env.d_patches)):
                for clip in range(3):
                    act(pltpu.make_async_copy(env.zeros, array.at[clip, pl.ds(UNUSED[1], ROWS - UNUSED[1])], env.zero_sem.at[3 * i + clip]))

    fill(lambda made: made.start())

    groups = features // 256

    def exchange_copies():
        other = 1 - env.c
        partner = 2 * env.x_at + other
        mine, theirs = pl.ds(groups * env.c, groups), pl.ds(groups * other, groups)
        places = ((env.shared_dm.at[:, span(SHARED * env.c, SHARED)], slice(OWN, WORK)), (env.own_dm.at[:, span(OWN * env.c, OWN)], slice(0, OWN)))
        sender = Sender(env.dm_send, env.dm_recv)
        return [[sender.far(env.d_mixed.at[theirs, rows], place, partner, False), sender.near(env.d_mixed.at[mine, rows], place, False)]
                for place, rows in places]

    def after_middle():
        for made in sum(exchange_copies(), []):
            made.start()

    env.exchange_copies = exchange_copies
    env.after_middle = after_middle
    tile = hidden // TILES
    dma = pltpu.SemaphoreType.DMA
    wide, tall = lambda kind: pltpu.VMEM((WORK, features), kind), pltpu.VMEM((features, WORK), BF16)
    lanes = lambda *lead: pltpu.VMEM(lead + (128,), BF16)
    pl.run_scoped(
        functools.partial(middle_part, env), pltpu.VMEM((features, features), BF16), pltpu.VMEM((2, features, tile), BF16),
        pltpu.VMEM((2, tile, features), BF16), wide(BF16), wide(F32), wide(BF16), tall, wide(BF16), tall, wide(F32), wide(F32),
        pltpu.VMEM((WORK, tile), BF16), pltpu.VMEM((WORK, tile), BF16), pltpu.VMEM((WORK, tile), F32), dma((3 + 2 * groups,)), dma((4 * shares,)))
    pl.run_scoped(
        functools.partial(attention_part, env), pltpu.VMEM((features, 3 * features), BF16), lanes(3, groups, KEYS), lanes(groups, OWN),
        lanes(2, groups, KEYS), lanes(groups, KEYS), lanes(groups, OWN), lanes(3, groups, KEYS), lanes(groups, OWN), lanes(2, groups, KEYS),
        pltpu.VMEM((TALL, 3 * features), BF16), pltpu.VMEM((2 * KEYS, features), BF16), pltpu.VMEM((features, 2 * KEYS), BF16),
        pltpu.VMEM((2 * KEYS, 384), BF16), wide(F32), wide(BF16), pltpu.VMEM((SHARED, features), BF16), dma((13,)))
    fill(lambda made: made.wait())
    assert all(flow.done == len(flow.stages) for flow in flows.values())


def backward(inputs, head_dim, shares, custom):
    features, hidden = inputs["up"].shape
    groups = features // 256
    anywhere, vmem = pl.BlockSpec(memory_space=pl.ANY), pl.BlockSpec(memory_space=pltpu.VMEM)
    dma = pltpu.SemaphoreType.DMA
    lanes = lambda *lead: pltpu.VMEM(lead + (128,), BF16)
    moves = len(MOVES)
    shapes = piece_shapes(shares, features, hidden)
    specs = [vmem if name in IN_VMEM else anywhere for name in BACK_INPUTS]
    specs[0] = pl.BlockSpec(memory_space=pltpu.SMEM)
    scratch = [
        lanes(2 * groups, WORK), lanes(groups, KEYS), lanes(groups, OWN), pltpu.VMEM((SHARED, features), BF16), lanes(3, 2 * groups, TALL),
        pltpu.VMEM((WORK, features), F32), pltpu.VMEM((WORK, features), BF16), pltpu.VMEM((SMALL_ROWS, features), F32),
        pltpu.VMEM((1, hidden), F32), pltpu.VMEM((ROWS - UNUSED[1], features), BF16),
        dma((moves,)), dma((moves,)), dma((moves,)), dma((moves,)), dma((24,)), dma((24,)), dma((4,)), dma((4,)), dma((6,)),
    ]
    if custom:
        scratch += [pltpu.VMEM(shape, BF16) for shape in shapes]
        scratch += [ref for name, shape in zip(FLOW_NAMES, shapes) for ref in flow_scratch(name, shape)]
    rows = jax.ShapeDtypeStruct((3, ROWS, features), BF16)
    return pl.pallas_call(
        functools.partial(backward_body, head_dim, shares, custom, features, hidden),
        in_specs=specs,
        out_specs=[anywhere] * 2 + [vmem] * len(shapes),
        out_shape=[rows, rows] + [jax.ShapeDtypeStruct(result_shape(name, shape) if custom else shape, BF16) for name, shape in zip(FLOW_NAMES, shapes)],
        scratch_shapes=scratch,
        compiler_params=pltpu.CompilerParams(collective_id=0, has_side_effects=True, vmem_limit_bytes=63 * MIB),
    )(*(inputs[name] for name in BACK_INPUTS))


def assemble_body(time_count, freq_count, *refs):
    count = len(FLOW_NAMES)
    pieces = refs[0:count]
    outs = refs[count:]
    halved, whole, up = pieces[0:TILES], pieces[TILES:2 * TILES], pieces[2 * TILES:3 * TILES]
    out, *pairs, packed = pieces[3 * TILES:]
    (qkv_out, qb, vb, out_out, ob, n1g, n1s, n2g, n2s, up_out, up_b, down_out, db, time_out, freq_out) = outs
    third = qkv_out.shape[1] // 3
    for core in range(2):
        for p, pair in enumerate(pairs):
            for part in range(3):
                first = part * third + core * (third // 2) + p * 128
                cols = slice(part * 128, (part + 1) * 128)
                if PAIR_SPLIT[p]:
                    high = pair.shape[2]
                    for half_x in range(2):
                        qkv_out[half_x * high:(half_x + 1) * high, first:first + 128] = pair[core, half_x, :, cols].astype(F32)
                else:
                    qkv_out[:, first:first + 128] = pair[core, :, cols].astype(F32)
        cols = out.shape[2]
        out_out[:, core * cols:(core + 1) * cols] = out[core].astype(F32)
    width = whole[0].shape[2]
    half = down_out.shape[1] // 2
    for j in range(TILES):
        for core in range(2):
            grad = jnp.concatenate([halved[j][core, 0], halved[j][core, 1], whole[j][core]], 0)
            down_out[j * width:(j + 1) * width, core * half:(core + 1) * half] = grad.astype(F32).T
            if UP_SPLIT[j]:
                grad = jnp.concatenate([up[j][core, 0], up[j][core, 1]], 1)
            else:
                grad = up[j][core]
            blocks = grad.shape[1] // width
            for k in range(blocks):
                first = ((core * blocks + k) * TILES + j) * width
                up_out[:, first:first + width] = grad[:, k * width:(k + 1) * width].astype(F32)
    small = jnp.concatenate([packed[0], packed[1]], 0).astype(F32)
    share = qb.shape[0]
    for row, ref in ((0, qb), (1, vb), (2, ob), (3, n1g), (4, n1s), (5, n2g), (6, n2s), (7, db)):
        ref[...] = small[row, 0:share]
    for r in range(up_b.shape[0] // share):
        up_b[r * share:(r + 1) * share] = small[8 + r, 0:share]
    time_out[...] = small[16:16 + TABLE_ROWS].T[0:share, 0:time_count]
    freq_out[...] = small[16 + FREQ_ROW:16 + FREQ_ROW + freq_count, 0:share]


def assemble(pieces, features, hidden, shares, time_count, freq_count):
    share = features // shares
    line = (share,)
    shapes = [(share, 3 * features), line, line, (share, features), line, line, line, line, line, (share, hidden), (hidden // shares,),
              (hidden // shares, features), line, (share, time_count), (freq_count, share)]
    return pl.pallas_call(
        functools.partial(assemble_body, time_count, freq_count),
        out_shape=[jax.ShapeDtypeStruct(shape, F32) for shape in shapes],
        compiler_params=params(),
    )(*pieces)


def reduce_native(pieces, time_count, freq_count):
    def total(part, axis):
        return lax.psum(lax.psum_scatter(part, "dp", scatter_dimension=axis, tiled=True), "seq").astype(F32)

    pieces = [p[0] for p in pieces]
    down = jnp.concatenate([jnp.concatenate([part for c in range(2) for part in (a[c, 0], a[c, 1], b[c])], 0)
                            for a, b in zip(pieces[0:TILES], pieces[TILES:2 * TILES])], 1)
    ups = []
    for piece, split in zip(pieces[2 * TILES:3 * TILES], UP_SPLIT):
        ups += [part for c in range(2) for part in ((piece[c, 0], piece[c, 1]) if split else (piece[c],))]
    up = jnp.concatenate(ups, 1)
    out, *pairs, packed = pieces[3 * TILES:]
    here = lax.rem(lax.axis_index("seq"), 2)
    pairs = [jnp.concatenate([p[0], p[1]], 0) if split else p for p, split in zip(pairs, PAIR_SPLIT)]
    qkv = jnp.concatenate([jnp.where(here == core, p[:, part * 128:(part + 1) * 128], BF16(0))
                           for part in range(3) for core in range(2) for p in pairs], 1)
    small = packed.reshape(SMALL_ROWS, -1)
    repeat = up.shape[1] // small.shape[1]
    up_bias = total(small[8:8 + repeat].reshape(-1), 0)
    small = total(small, 1)
    return (
        total(qkv, 0), small[0], small[1], total(jnp.concatenate([out[0], out[1]], 1), 0), small[2], small[3], small[4], small[5], small[6],
        total(up, 0), up_bias, total(down, 1).T, small[7], small[16:16 + time_count], small[16 + FREQ_ROW:16 + FREQ_ROW + freq_count],
    )


def shards(
    patches,
    cotangent,
    time_ids,
    freq_ids,
    lengths,
    qkv_weight,
    query_bias,
    value_bias,
    out_weight,
    out_bias,
    norm1_gain,
    norm1_shift,
    norm2_gain,
    norm2_shift,
    up_weight,
    up_bias,
    down_weight,
    down_bias,
    time_table,
    freq_table,
):
    features = patches.shape[2]
    head_dim = features // HEADS
    assert patches.shape[:2] == (3, ROWS) and lax.axis_size("seq") == 4
    custom = lax.axis_size("dp") == 8
    shares = 8 if custom else 1
    x, normed, own, shared_q, shared_kv, own_log, shared_log, own_mixed, shared_mixed, mixed, cot, ids, valid = forward(
        lengths, patches, cotangent, time_ids, freq_ids, time_table, freq_table, norm1_gain, norm1_shift, qkv_weight, query_bias, value_bias,
        head_dim
    )
    inputs = dict(
        lengths=lengths, valid=valid, x=x, mixed=mixed, cot=cot, out_weight=out_weight, out_bias=out_bias, gain2=norm2_gain,
        shift2=norm2_shift, up=up_weight, up_bias=up_bias, down=down_weight, down_bias=down_bias, own=own, shared_q=shared_q,
        shared_kv=shared_kv, own_mixed=own_mixed, shared_mixed=shared_mixed, own_log=own_log, shared_log=shared_log, weight=qkv_weight, normed=normed, ids=ids, gain1=norm1_gain)
    output, d_patch, *pieces = backward(inputs, head_dim, shares, custom)
    counts = time_table.shape[0], freq_table.shape[0]
    if custom:
        *rest, time_grad, freq_grad = assemble(pieces, features, up_weight.shape[1], shares, *counts)
        return (output, d_patch, *rest, time_grad.T, freq_grad)
    return (output, d_patch) + reduce_native(pieces, *counts)


def solution(mesh):
    clip_spec, row_spec, one = P("dp", "seq", None), P("dp", "seq"), P("dp")
    matrix = P("dp", None)
    return jax.shard_map(
        shards,
        mesh=mesh,
        in_specs=(clip_spec, clip_spec, row_spec, row_spec, one) + (P(),) * 15,
        out_specs=(clip_spec, clip_spec, matrix, one, one, matrix, one, one, one, one, one, matrix, one, matrix, one, P(None, "dp"), P(None, "dp")),
        check_vma=False,
    )
```

```python
import functools
import math

import jax
import jax.numpy as jnp
from jax import lax
from jax.experimental import pallas as pl
from jax.experimental.pallas import tpu as pltpu
from jax.sharding import PartitionSpec as P

HEADS = 12
EPS = 1e-06
NEGATIVE = -1000000000.0
FREQ_ROW = 104
TABLE_ROWS = 128
SMALL_ROWS = 32 + TABLE_ROWS
TILES = 3
CHUNKS = 2
UP_SPLIT = (False, True, False)
PAIR_SPLIT = (True, True, False)
F32 = jnp.float32
BF16 = jnp.bfloat16
NN = (((1,), (0,)), ((), ()))
NT = (((1,), (1,)), ((), ()))
TN = (((0,), (0,)), ((), ()))
MIB = 1 << 20


def mm(left, right, dims=NN):
    return lax.dot_general(left, right, dims, preferred_element_type=F32)


def params(limit=60):
    return pltpu.CompilerParams(vmem_limit_bytes=limit * MIB)


def row_sum(values):
    return jnp.sum(values, 0, keepdims=True)


def normalize(values):
    center = values - jnp.mean(values, -1, keepdims=True)
    rstd = lax.rsqrt(jnp.mean(center * center, -1, keepdims=True) + EPS)
    return center * rstd, rstd


def norm_back(d_out, gain, xhat, rstd):
    u = d_out * gain
    inner = jnp.mean(u * xhat, -1, keepdims=True)
    return rstd * (u - jnp.mean(u, -1, keepdims=True) - xhat * inner)


def gelu_parts(h):
    half = 0.5 * (1.0 + lax.erf(h * (1.0 / math.sqrt(2.0))))
    return half, half + h * jnp.exp(h * h * -0.5) * (1.0 / math.sqrt(2.0 * math.pi))


def split_high_low(values):
    high = values.astype(BF16)
    return high, (values - high.astype(F32)).astype(BF16)


def one_hot(time_row, freq_row):
    spot = lax.broadcasted_iota(jnp.int32, (TABLE_ROWS, time_row.shape[1]), 0)
    hit = (spot == time_row) | (spot == freq_row + FREQ_ROW)
    return jnp.where(hit, 1.0, 0.0).astype(BF16)


ROWS = 224
OWN = 352
SHARED = 176
WORK = OWN + SHARED
KEYS = 2 * OWN
TALL = WORK + SHARED
SHARED_MOVES = (
    (0, 2, 176, 48, 3, 384), (1, 2, 176, 48, 3, 432), (2, 2, 176, 48, 3, 480), (3, 2, 0, 32, 3, 352),
    (0, 2, 0, 176, 0, 352), (1, 2, 0, 176, 1, 352), (2, 2, 0, 176, 2, 352),
)
OWN_MOVES = (
    (2, 0, 0, 128, 0, 224), (2, 0, 128, 96, 1, 224), (3, 0, 0, 32, 1, 320), (0, 1, 0, 224, 2, 0), (1, 1, 0, 224, 3, 0),
    (2, 1, 128, 96, 3, 224), (2, 1, 0, 128, 2, 224), (3, 1, 0, 32, 3, 320), (0, 0, 0, 224, 0, 0), (1, 0, 0, 224, 1, 0),
)
MIRROR_MOVES = (
    (0, 2, 0, 176, 2, 528), (1, 2, 0, 176, 3, 528), (2, 2, 0, 176, 0, 528), (0, 2, 176, 48, 1, 560), (2, 2, 176, 48, 1, 656),
    (1, 2, 176, 48, 1, 608), (3, 2, 0, 32, 1, 528),
)
MOVES = SHARED_MOVES + OWN_MOVES
ALL_MOVES = MOVES + MIRROR_MOVES
UNUSED = (3, 32)


def seq_place():
    s = lax.axis_index("seq")
    return s, s // 2, lax.rem(s, 2)


def seq_peer(s):
    return {"seq": s}


def greet_group(s):
    barrier = pltpu.get_barrier_semaphore()
    for ahead in range(1, 4):
        pl.semaphore_signal(barrier, inc=1, device_id=seq_peer(lax.rem(s + ahead, 4)), device_id_type=pl.DeviceIdType.MESH)
    pl.semaphore_wait(barrier, 3)


class Mover:
    def __init__(self, s, at_home, at_work, send, recv, back=False):
        self.s, self.at_home, self.at_work, self.send, self.recv, self.back = s, at_home, at_work, send, recv, back

    def ends(self, move):
        home, clip, first, count, work, spot = move
        a, b = self.at_home.at[clip, pl.ds(first, count)], self.at_work.at[pl.ds(spot, count)]
        return (work, b, home, a) if self.back else (home, a, work, b)

    def each(self, moves, which, act, near=True):
        for device in range(4):
            chosen = [m for m in moves if self.ends(m)[which] == device and (near or self.ends(m)[0] != self.ends(m)[2])]
            if not chosen:
                continue

            @pl.when(self.s == device)
            def _(chosen=chosen):
                for m in chosen:
                    src_device, src, dst_device, dst = self.ends(m)
                    slot = ALL_MOVES.index(m)
                    if src_device == dst_device:
                        act(False, pltpu.make_async_copy(src, dst, self.recv.at[slot]))
                    else:
                        act(True, pltpu.make_async_remote_copy(
                            src_ref=src, dst_ref=dst, send_sem=self.send.at[slot], recv_sem=self.recv.at[slot],
                            device_id=seq_peer(dst_device), device_id_type=pl.DeviceIdType.MESH))

    def start(self, moves):
        self.each(moves, 0, lambda far, made: made.start())

    def wait(self, moves):
        self.each(moves, 2, lambda far, made: made.wait_recv() if far else made.wait())

    def drain(self, moves):
        self.each(moves, 0, lambda far, made: made.wait_send(), False)


class Sender:
    def __init__(self, send, recv):
        self.send, self.recv, self.used = send, recv, 0

    def far(self, source, target, peer, begin=True):
        made = pltpu.make_async_remote_copy(
            src_ref=source, dst_ref=target, send_sem=self.send.at[self.used], recv_sem=self.recv.at[self.used],
            device_id=seq_peer(peer), device_id_type=pl.DeviceIdType.MESH)
        self.used += 1
        if begin:
            made.start()
        return made

    def near(self, source, target, begin=True):
        made = pltpu.make_async_copy(source, target, self.recv.at[self.used])
        self.used += 1
        if begin:
            made.start()
        return made


def wait_all(copies):
    for made in copies:
        made.wait()


def shift_between(spot, cuts):
    slot = spot
    for low, high, shift in cuts:
        slot = jnp.where((spot >= low) & (spot < high), spot + shift, slot)
    return slot


def own_slots(spot):
    return shift_between(spot, ((224, 352, 224), (352, 576, -128)))


def shared_slots(spot):
    return shift_between(spot, ((176, 352, 48), (352, 528, 96), (528, 560, 144), (560, 608, -384), (608, 656, -208), (656, 704, -32)))


def span(first, size):
    return pl.ds(pl.multiple_of(first, 16), size)


def lane_parts(value):
    high, rest = split_high_low(value)
    low = (value - high.astype(F32) - rest.astype(F32)).astype(BF16)
    return high, rest, low


def with_lanes(base, lane, first, columns):
    for i, column in enumerate(columns):
        base = jnp.where(lane == first + i, column, base)
    return base


def attend(query, keys, values, key_ok, mixed_out, log_out, head_dim):
    count = query.shape[1]
    lane = lax.broadcasted_iota(jnp.int32, (1, 128), 1)
    head = lane // head_dim
    scale = BF16(1.0 / math.sqrt(head_dim))
    key_bias = jnp.where(key_ok, 0.0, NEGATIVE).astype(BF16)
    per_pair = 128 // head_dim
    units = [(first, h) for first in range(0, count, OWN) for h in range(per_pair)]
    log_out[...] = jnp.zeros_like(log_out)

    def pair(p, _):
        k, v = keys[p], values[p]
        biased = [with_lanes(k, lane, free_lane(h, head_dim), (key_bias,)) for h in range(per_pair)]
        counted = [with_lanes(v, lane, free_lane(h, head_dim), (BF16(1),)) for h in range(per_pair)]

        def score(unit):
            first, h = unit
            q = jnp.where(head == h, query[p, first:first + OWN] * scale, BF16(0))
            return mm(with_lanes(q, lane, free_lane(h, head_dim), (BF16(1),)), biased[h], NT)

        ready = score(units[0])
        for i, (first, h) in enumerate(units):
            scores = ready
            if i + 1 < len(units):
                ready = score(units[i + 1])
            rows = slice(first, first + OWN)
            highest = jnp.max(scores, -1, keepdims=True)
            powers = jnp.exp(scores - highest)
            out = mm(powers.astype(BF16), counted[h])
            first_free = free_lane(h, head_dim)
            total = out[:, first_free:first_free + 1]
            out = out * (1.0 / total)
            mixed = out if h == 0 else jnp.where(head == h, out, mixed)
            log_out[rows] = jnp.where(lane == per_pair * p + h, highest + jnp.log(total), log_out[rows])
            if h == per_pair - 1:
                mixed_out[p, rows] = mixed.astype(BF16)
        return 0

    lax.fori_loop(0, query.shape[0], pair, 0)


def free_lane(h, head_dim):
    return (h + 1) * head_dim % 128


def forward_body(head_dim, lengths, patches, cot, time_ids, freq_ids, time_table, freq_table, gain, shift, weight, query_bias, value_bias,
                 x_hbm, n_hbm, own_hbm, shared_q_hbm, shared_kv_hbm, own_log_hbm, own_mixed_hbm, shared_log, shared_mixed, mixed_out, cot_out,
                 id_out, valid_out,
                 x_out, n_out, own_out, shared_q_out, shared_kv_out, own_log, own_mixed, work, table_f32, table, ids, matrix, own_stage, shared_stage, mirror_stage,
                 patch_send, patch_recv, cot_send, cot_recv, send, recv, weight_sem):
    s, x, c = seq_place()
    features = x_out.shape[1]
    groups = own_out.shape[1]
    other = 1 - c
    loads = [pltpu.make_async_copy(weight.at[:, pl.ds(p * features, features)], matrix.at[:, pl.ds(p * features, features)], weight_sem.at[p])
             for p in range(3)]
    for load in loads:
        load.start()
    greet_group(s)
    patch_mover = Mover(s, patches, work, patch_send, patch_recv)
    cot_mover = Mover(s, cot, cot_out, cot_send, cot_recv)
    sender = Sender(send, recv)
    id_copies = []
    for i, source in enumerate((time_ids, freq_ids)):
        id_copies.append(sender.near(source, ids.at[s, i]))
        for ahead in range(1, 4):
            id_copies.append(sender.far(source, ids.at[s, i], lax.rem(s + ahead, 4)))
    patch_mover.start(ALL_MOVES)

    table_f32[...] = jnp.zeros_like(table_f32)
    table_f32[0:time_table.shape[0], :] = time_table[...]
    table_f32[FREQ_ROW:FREQ_ROW + freq_table.shape[0], :] = freq_table[...]
    high, low = split_high_low(table_f32[...])
    table[0:TABLE_ROWS, :] = high
    table[TABLE_ROWS:, :] = low
    spot = lax.broadcasted_iota(jnp.int32, (WORK, 1), 0)
    place = jnp.where(spot < OWN, jnp.where(spot < ROWS, spot + ROWS * c, spot + ROWS + 128 * c), shared_slots(spot - OWN + SHARED * s))
    limit = jnp.where(spot < OWN, jnp.where(x == 0, lengths[0], lengths[1]), lengths[2])
    valid_out[...] = jnp.broadcast_to(jnp.where(place < limit, 1.0, 0.0), valid_out.shape)
    id_out[...] = jnp.zeros_like(id_out)
    wait_all(id_copies)
    for device in range(4):
        @pl.when(s == device)
        def _(device=device):
            for home, clip, first, count, target, at in ALL_MOVES:
                if target == device:
                    for i in range(2):
                        id_out[i:i + 1, at:at + count] = ids[home, i, clip:clip + 1, first:first + count]

    bias = (query_bias[...].reshape(1, features), None, value_bias[...].reshape(1, features))

    def project(first, count, stage, own=True):
        rows = slice(first, first + count)
        hot = one_hot(id_out[0:1, rows], id_out[1:2, rows])
        value = work[rows].astype(F32) + mm(jnp.concatenate([hot, hot], 0), table[...], TN)
        if own:
            x_out[rows] = value
        xhat, _ = normalize(value)
        normed = (xhat * gain[...].reshape(1, features) + shift[...].reshape(1, features)).astype(BF16)
        n_out[c, rows] = normed
        for part in range(0 if own else 1, 3):
            out = mm(normed, matrix[:, part * features:(part + 1) * features])
            if bias[part] is not None:
                out = out + bias[part]
            out = out.astype(BF16)
            for g in range(2 * groups):
                stage[part if own else part - 1, g] = out[:, g * 128:(g + 1) * 128]

    patch_mover.wait(SHARED_MOVES)
    wait_all(loads)
    project(OWN, SHARED, shared_stage)
    q_rows, kv_rows = span(SHARED * c, SHARED), span(SHARED * s, SHARED)
    mine, theirs = pl.ds(groups * c, groups), pl.ds(groups * other, groups)
    mirror_rows = span(SHARED * (2 * (1 - x) + c), SHARED)
    partner = 2 * x + other
    shared_copies = [
        sender.far(shared_stage.at[0, theirs], shared_q_out.at[:, q_rows], partner),
        sender.far(shared_stage.at[1:3, theirs], shared_kv_out.at[:, :, kv_rows], partner),
        sender.near(shared_stage.at[0, mine], shared_q_out.at[:, q_rows]),
        sender.near(shared_stage.at[1:3, mine], shared_kv_out.at[:, :, kv_rows]),
    ]
    patch_mover.wait(OWN_MOVES)
    project(0, OWN, own_stage)
    own_rows = span(OWN * c, OWN)
    saves = [sender.near(x_out, x_hbm)]
    own_copies = [
        sender.far(own_stage.at[:, theirs], own_out.at[:, :, own_rows], partner),
        sender.near(own_stage.at[:, mine], own_out.at[:, :, own_rows]),
    ]
    cot_mover.start(MOVES)
    patch_mover.wait(MIRROR_MOVES)
    project(WORK, SHARED, mirror_stage, False)
    shared_copies += [
        sender.far(mirror_stage.at[:, theirs], shared_kv_out.at[:, :, mirror_rows], partner),
        sender.near(mirror_stage.at[:, mine], shared_kv_out.at[:, :, mirror_rows]),
    ]
    normed_copy = sender.far(n_out.at[c], n_out.at[c], partner)
    wait_all(own_copies)
    saves.append(sender.near(own_out, own_hbm))
    key_spot = lax.broadcasted_iota(jnp.int32, (KEYS, 1), 0)
    attend(own_out.at[0], own_out.at[1], own_out.at[2], own_slots(key_spot) < jnp.where(x == 0, lengths[0], lengths[1]),
           own_mixed, own_log, head_dim)
    mixed_copies = [
        sender.far(own_mixed.at[:, span(OWN * other, OWN)], mixed_out.at[mine, 0:OWN], partner),
        sender.near(own_mixed.at[:, own_rows], mixed_out.at[mine, 0:OWN]),
    ]
    wait_all(shared_copies + [normed_copy])
    saves += [sender.near(a, b) for a, b in ((n_out, n_hbm), (shared_q_out, shared_q_hbm), (shared_kv_out, shared_kv_hbm),
                                             (own_mixed, own_mixed_hbm), (own_log, own_log_hbm))]
    attend(shared_q_out, shared_kv_out.at[0], shared_kv_out.at[1], shared_slots(key_spot) < lengths[2],
           shared_mixed, shared_log, head_dim)
    mixed_copies += [
        sender.far(shared_mixed.at[:, span(SHARED * other, SHARED)], mixed_out.at[mine, OWN:WORK], partner),
        sender.near(shared_mixed.at[:, q_rows], mixed_out.at[mine, OWN:WORK]),
    ]
    wait_all(mixed_copies + saves)
    cot_mover.wait(MOVES)
    patch_mover.drain(ALL_MOVES)
    cot_mover.drain(MOVES)


def forward(lengths, patches, cot, time_ids, freq_ids, time_table, freq_table, gain, shift, weight, query_bias, value_bias, head_dim):
    features = patches.shape[2]
    groups = features // 256
    anywhere, vmem = pl.BlockSpec(memory_space=pl.ANY), pl.BlockSpec(memory_space=pltpu.VMEM)
    lanes = lambda *lead: jax.ShapeDtypeStruct(lead + (128,), BF16)
    saved = [
        jax.ShapeDtypeStruct((WORK, features), F32),
        jax.ShapeDtypeStruct((2, TALL, features), BF16),
        lanes(3, groups, KEYS),
        lanes(groups, OWN),
        lanes(2, groups, KEYS),
        jax.ShapeDtypeStruct((KEYS, 128), F32),
        lanes(groups, KEYS),
    ]
    dma = pltpu.SemaphoreType.DMA
    return pl.pallas_call(
        functools.partial(forward_body, head_dim),
        in_specs=[pl.BlockSpec(memory_space=pltpu.SMEM)] + [anywhere] * 4 + [vmem] * 4 + [anywhere] + [vmem] * 2,
        out_specs=[anywhere] * 7 + [vmem] * 6,
        out_shape=saved + [
            jax.ShapeDtypeStruct((OWN, 128), F32),
            lanes(groups, OWN),
            lanes(2 * groups, WORK),
            jax.ShapeDtypeStruct((WORK, features), BF16),
            jax.ShapeDtypeStruct((8, TALL), jnp.int32),
            jax.ShapeDtypeStruct((WORK, 128), F32),
        ],
        scratch_shapes=[pltpu.VMEM(a.shape, a.dtype) for a in saved] + [
            pltpu.VMEM((TALL, features), BF16),
            pltpu.VMEM((TABLE_ROWS, features), F32),
            pltpu.VMEM((2 * TABLE_ROWS, features), BF16),
            pltpu.VMEM((4, 2) + time_ids.shape, jnp.int32),
            pltpu.VMEM(weight.shape, BF16),
            pltpu.VMEM((3, 2 * groups, OWN, 128), BF16),
            pltpu.VMEM((3, 2 * groups, SHARED, 128), BF16),
            pltpu.VMEM((2, 2 * groups, SHARED, 128), BF16),
            dma((len(ALL_MOVES),)), dma((len(ALL_MOVES),)), dma((len(MOVES),)), dma((len(MOVES),)), dma((40,)), dma((40,)), dma((3,)),
        ],
        compiler_params=pltpu.CompilerParams(collective_id=1, has_side_effects=True, vmem_limit_bytes=60 * MIB),
    )(lengths, patches, cot, time_ids, freq_ids, time_table, freq_table, gain, shift, weight, query_bias, value_bias)


def attend_back(p, query, keys, values, d_mixed, mixed, logs, key_ok, d_query, d_keys, d_values, head_dim, block, tick):
    count = query.shape[1]
    lane = lax.broadcasted_iota(jnp.int32, (1, 128), 1)
    head = lane // head_dim
    scale = BF16(1.0 / math.sqrt(head_dim))
    key_bias = jnp.where(key_ok, 0.0, NEGATIVE).astype(BF16)
    k, v = keys[p], values[p]
    k_t = (k * scale).T
    per_pair = 128 // head_dim
    one = BF16(1)
    k_wide = [with_lanes(k, lane, free_lane(h, head_dim), (key_bias, one, one, one)) for h in range(per_pair)]
    v_wide = [with_lanes(v, lane, free_lane(h, head_dim), (one, one, one)) for h in range(per_pair)]
    total_k = jnp.zeros((KEYS, 128), F32)
    total_v = jnp.zeros((KEYS, 128), F32)
    units = [(first, min(first + block, count), h) for first in range(0, count, block) for h in range(per_pair)]

    def products(unit):
        first, last, h = unit
        rows = slice(first, last)
        d_m = d_mixed[p, rows]
        q_head = jnp.where(head == h, query[p, rows] * scale, BF16(0))
        m_head = jnp.where(head == h, d_m, BF16(0))
        delta = jnp.sum(m_head.astype(F32) * mixed[p, rows].astype(F32), -1, keepdims=True)
        at = per_pair * p + h
        q_wide = with_lanes(q_head, lane, free_lane(h, head_dim), (one,) + lane_parts(-logs[rows, at:at + 1]))
        m_wide = with_lanes(m_head, lane, free_lane(h, head_dim), lane_parts(-delta))
        return q_head, m_head, mm(k_wide[h], q_wide, NT), mm(v_wide[h], m_wide, NT)

    ready = products(units[0])
    parts = []
    for i, (first, last, h) in enumerate(units):
        q_head, m_head, scores, d_probs = ready
        if i + 1 < len(units):
            ready = products(units[i + 1])
        probs = jnp.exp(scores)
        d_scores = (probs * d_probs).astype(BF16)
        total_v = total_v + mm(probs.astype(BF16), m_head)
        total_k = total_k + mm(d_scores, q_head)
        parts.append(mm(k_t[h * head_dim:(h + 1) * head_dim], d_scores))
        if h == per_pair - 1:
            d_query[p, first:last] = jnp.concatenate(parts, 0).T.astype(BF16)
            parts = []
            tick(first // block)
    d_keys[p] = total_k.astype(BF16)
    d_values[p] = total_v.astype(BF16)


class Flow:
    def __init__(self, source, result, refs, place, single):
        self.source, self.result, self.single = source, result, single
        self.split = len(source.shape) == (4 if single else 5)
        self.got, self.x_got, self.y_got, self.z_got, self.send, self.recv = refs
        self.z, self.y, self.x, self.c = place
        self.open = {}
        if self.split:
            self.stages = [self.begin, self.cores_x, self.x_y, self.y_z, self.z_fill, self.fill_cores, self.end]
        else:
            self.stages = [self.begin, self.cores_y, self.y_z, self.z_x, self.x_cores, self.end]
        if single:
            self.stages = [self.to_x if self.split else self.to_y] + self.stages[2:]
        self.used = 0
        self.done = 0

    def advance(self):
        self.stages[self.done]()
        self.done += 1

    def copy(self, key, ends):
        slot = self.used
        self.used += 1

        def make():
            source, target, (z, y, x, c) = ends()
            return pltpu.make_async_remote_copy(
                src_ref=source, dst_ref=target, send_sem=self.send.at[slot], recv_sem=self.recv.at[slot],
                device_id=(z * 2 + y, x * 2 + c), device_id_type=pl.DeviceIdType.MESH)

        make().start()
        self.open.setdefault(key, []).append(make)

    def wait(self, key):
        for make in self.open.pop(key):
            make().wait()

    def at(self, z, y):
        row = self.row(z * 2 + y)
        return row.at[self.x] if self.split else row

    def row(self, i):
        return self.source.at[i] if self.single else self.source.at[i, self.c]

    def begin(self):
        self.copy("core", lambda: (self.source.at[:, 1 - self.c], self.got, (self.z, self.y, self.x, 1 - self.c)))

    def cores(self):
        self.wait("core")

        def add(i, _):
            self.source[i, self.c] = self.source[i, self.c] + self.got[i]
            return 0

        lax.fori_loop(0, self.got.shape[0], add, 0)

    def cores_x(self):
        self.cores()
        self.to_x()

    def to_x(self):
        part = lambda: self.source.at[:, 1 - self.x] if self.single else self.source.at[:, self.c, 1 - self.x]
        self.copy("x", lambda: (part(), self.x_got, (self.z, self.y, 1 - self.x, self.c)))

    def cores_y(self):
        self.cores()
        self.to_y()

    def to_y(self):
        for z in range(4):
            self.copy("y", lambda z=z: (self.at(z, 1 - self.y), self.y_got.at[z], (self.z, 1 - self.y, self.x, self.c)))

    def x_y(self):
        self.wait("x")

        def add(i, _):
            spot = self.row(i).at[self.x]
            spot[...] = spot[...] + self.x_got[i]
            return 0

        lax.fori_loop(0, self.source.shape[0], add, 0)
        self.to_y()

    def y_z(self):
        self.wait("y")

        def add(z, _):
            spot = self.at(z, self.y)
            spot[...] = spot[...] + self.y_got[z]
            return 0

        lax.fori_loop(0, 4, add, 0)
        for ahead in range(1, 4):
            def ends(ahead=ahead):
                z = lax.rem(self.z + ahead, 4)
                return self.at(z, self.y), self.z_got.at[ahead - 1], (z, self.y, self.x, self.c)

            self.copy("z", ends)

    def z_sum(self):
        self.wait("z")
        total = self.at(self.z, self.y)[...].astype(F32)
        for i in range(3):
            total = total + self.z_got[i].astype(F32)
        return total.astype(BF16)

    def z_fill(self):
        self.result[self.c, self.x] = self.z_sum()
        spot = lambda: self.result.at[self.c, self.x]
        self.copy("fill", lambda: (spot(), spot(), (self.z, self.y, 1 - self.x, self.c)))

    def fill_cores(self):
        self.wait("fill")
        self.to_core()

    def z_x(self):
        spot = self.at(self.z, self.y)
        spot[...] = self.z_sum()
        self.copy("x", lambda: (self.at(self.z, self.y), self.x_got, (self.z, self.y, 1 - self.x, self.c)))

    def x_cores(self):
        self.wait("x")
        self.result[self.c] = self.at(self.z, self.y)[...] + self.x_got[...]
        self.to_core()

    def to_core(self):
        spot = lambda: self.result.at[self.c]
        self.copy("end", lambda: (spot(), spot(), (self.z, self.y, self.x, 1 - self.c)))

    def end(self):
        self.wait("end")


FLOW_REFS = 6
FLOW_NAMES = ("D0", "D1", "D2", "E0", "E1", "E2", "U0", "U1", "U2", "O", "Q0", "Q1", "Q2", "S")
SCHEDULE = {
    "d0": ("E0", "D0",),
    "u0": ("U0",),
    "0c": ("E0",),
    "1b0": ("D0",),
    "d1": ("D1", "U0",),
    "u1": ("U1", "E0", "D1", "E1",),
    "2b1": ("U1",),
    "d2": ("D2", "D0",),
    "2e0": ("E2",),
    "2e1": ("E1",),
    "u2": ("U0",),
    "2c": ("D2", "E2",),
    "e": ("O", "E1", "D1",),
    "s01": ("U1", "R",),
    "s20": ("E2",),
    "s21": ("O", "U2",),
    "o00": ("U0",),
    "o01": ("D0",),
    "q0": ("D2", "D1", "Q0", "U2", "U1",),
    "q1": ("D0", "Q1",),
    "o20": ("O",),
    "q2": ("D2", "Q2", "E0",),
    "m": ("U2",),
    "n": ("Q0", "O",),
    "f0": ("D1", "E2", "E1", "U1", "Q1",),
    "f1": ("Q2", "D2",),
    "f2": ("S", "U0", "E1", "Q1",),
    "tail": ("Q0", "S", "D1", "E2", "E1", "S", "Q2", "Q1", "U1", "U2", "U1", "O", "D0", "D1", "Q2", "E2", "Q0", "D2", "E0", "S", "U2", "Q0", "O", "U0", "D2", "Q1", "S", "Q0", "Q2", "Q1", "E0", "S", "D0", "U2",),
}


def flow_scratch(name, shape):
    single = name[0] == "Q"
    shares, tail = shape[0], shape[1 if single else 2:]
    block = tail[-2:]
    first = (shares,) + block if len(tail) == 3 else block
    slots = 16
    return [pltpu.VMEM((8, 128) if single else (shares,) + tail, BF16), pltpu.VMEM(first, BF16), pltpu.VMEM((4,) + block, BF16), pltpu.VMEM((3,) + block, BF16),
            pltpu.SemaphoreType.DMA((slots,)), pltpu.SemaphoreType.DMA((slots,))]


def result_shape(name, shape):
    return (2,) + shape[1:] if name[0] == "Q" else shape[1:]


def place_of():
    d, s = lax.axis_index("dp"), lax.axis_index("seq")
    return d // 2, lax.rem(d, 2), s // 2, lax.rem(s, 2)


def greet(place):
    z, y, x, c = place
    peers = [(z, y, x, 1 - c), (z, y, 1 - x, c), (z, 1 - y, x, c)] + [(lax.rem(z + i, 4), y, x, c) for i in range(1, 4)]
    peers.append((z, y, 1 - x, 1 - c))
    barrier = pltpu.get_barrier_semaphore()
    for pz, py, px, pc in peers:
        pl.semaphore_signal(barrier, inc=1, device_id=(pz * 2 + py, px * 2 + pc), device_id_type=pl.DeviceIdType.MESH)
    pl.semaphore_wait(barrier, len(peers))


def piece_shapes(shares, features, hidden):
    share = features // shares
    width, tile = hidden // shares // TILES, hidden // TILES
    halved = (shares, 2, 2, features // 8, width)
    whole = (shares, 2, features // 4, width)
    up = tuple((shares, 2, 2, share, tile // 4) if split else (shares, 2, share, tile // 2) for split in UP_SPLIT)
    pairs = tuple((shares, 2, share // 2, features // 2) if split else (shares, share, features // 2) for split in PAIR_SPLIT)
    out = (shares, 2, share, features // 2)
    return (halved,) * TILES + (whole,) * TILES + up + (out,) + pairs + ((shares, 2, SMALL_ROWS // 2, -(-share // 128) * 128),)


def middle_part(env, out_weight, up, down, mixed, x1, n2, n2_t, dm, dm_t, acc, d_n2, act_all, d_hidden_all, slope_all, load_sem,
                weight_sem):
    total, features = x1.shape
    hidden = env.up.shape[1]
    tile = hidden // TILES
    shares = env.shares
    reach = hidden // shares
    width = reach // TILES
    share = features // shares
    line = lambda ref: ref[...].reshape(1, ref.shape[0])
    blocks = [slice(i, i + SHARED) for i in range(0, total, SHARED)]

    def weight_loads(j):
        made = []
        for d in range(shares):
            first = d * reach + j * width
            k = 2 * (shares * (j % 2) + d)
            made.append(pltpu.make_async_copy(env.up.at[:, pl.ds(first, width)], up.at[j % 2, :, pl.ds(d * width, width)], weight_sem.at[k]))
            made.append(pltpu.make_async_copy(env.down.at[pl.ds(first, width)], down.at[j % 2, pl.ds(d * width, width)], weight_sem.at[k + 1]))
        return made

    first_loads = [pltpu.make_async_copy(env.out_weight, out_weight, load_sem.at[0]), pltpu.make_async_copy(env.x, x1, load_sem.at[1]),
                   pltpu.make_async_copy(env.cot, dm, load_sem.at[2])]
    for g in range(env.mixed.shape[0]):
        first_loads.append(pltpu.make_async_copy(env.mixed.at[g], mixed.at[:, pl.ds(g * 128, 128)], load_sem.at[3 + g]))
    pending = {0: weight_loads(0), 1: weight_loads(1)}
    for made in first_loads + pending[0]:
        made.start()
    env.greet()
    wait_all(first_loads)
    for made in pending[1]:
        made.start()
    x1[...] = x1[...] + (mm(mixed[...], out_weight[...]) + line(env.out_bias))
    for rows in blocks:
        after = x1[rows]
        xhat, _ = normalize(after)
        n2[rows] = (xhat * line(env.gain2) + line(env.shift2)).astype(BF16)
        dm[rows] = (dm[rows].astype(F32) * env.valid[rows, 0:1]).astype(BF16)
    n2_t[...] = n2[...].T
    dm_t[...] = dm[...].T
    env.small[7:8, :] = row_sum(dm[...].astype(F32))
    for j in range(TILES):
        up_j, down_j = up.at[j % 2], down.at[j % 2]
        wait_all(pending[j])
        tile_bias = jnp.concatenate([env.up_bias[d * reach + j * width:d * reach + (j + 1) * width].reshape(1, width) for d in range(shares)], 1)
        chunk = tile // CHUNKS
        parts = [slice(i, i + chunk) for i in range(0, tile, chunk)]
        forth = lambda cols: mm(n2[...], up_j[:, cols])
        back = lambda cols: mm(dm[...], down_j[cols], NT)
        ready = forth(parts[0])
        for i, cols in enumerate(parts):
            h = ready + tile_bias[:, cols]
            if i + 1 < len(parts):
                ready = forth(parts[i + 1])
            half, slope = gelu_parts(h)
            act_all[:, cols] = (h * half).astype(BF16)
            slope_all[:, cols] = slope
            env.tick(f"{j}b{i}")
        halved, whole = env.pieces[j], env.pieces[TILES + j]
        high = halved.shape[3]
        for core in range(2):
            rows = slice(core * (features // 2), (core + 1) * (features // 2))
            out = mm(dm_t[rows], act_all[...]).astype(BF16)
            for d in range(shares):
                cols = slice(d * width, (d + 1) * width)
                for half_x in range(2):
                    halved[d, core, half_x] = out[half_x * high:(half_x + 1) * high, cols]
                whole[d, core] = out[2 * high:, cols]
        env.tick(f"d{j}")
        sums = []
        ready = back(parts[0])
        for i, cols in enumerate(parts):
            d_act = ready
            if i + 1 < len(parts):
                ready = back(parts[i + 1])
            d_hidden = (slope_all[:, cols] * d_act).astype(BF16)
            d_hidden_all[:, cols] = d_hidden
            sums.append(row_sum(d_hidden.astype(F32)))
            env.tick(f"{j}e{i}")
        bias_sum = jnp.concatenate(sums, 1)
        for d in range(shares):
            env.up_bias_grad[:, d * reach + j * width:d * reach + (j + 1) * width] = bias_sum[:, d * width:(d + 1) * width]
        out = mm(n2_t[...], d_hidden_all[...]).astype(BF16)
        g_up = env.pieces[2 * TILES + j]
        for d in range(shares):
            rows = slice(d * share, (d + 1) * share)
            for core in range(2):
                first = core * (tile // 2)
                if UP_SPLIT[j]:
                    for half_x in range(2):
                        g_up[d, core, half_x] = out[rows, first + half_x * (tile // 4):first + (half_x + 1) * (tile // 4)]
                else:
                    g_up[d, core] = out[rows, first:first + tile // 2]
        env.tick(f"u{j}")
        forward_sum, backward_sum = mm(act_all[...], down_j[...]), mm(d_hidden_all[...], up_j[...], NT)
        acc[...] = acc[...] + forward_sum if j else forward_sum
        d_n2[...] = d_n2[...] + backward_sum if j else backward_sum
        env.tick(f"{j}c")
        if j + 2 < TILES:
            pending[j + 2] = weight_loads(j + 2)
            for made in pending[j + 2]:
                made.start()
    sums = [jnp.zeros((1, features), F32)] * 3
    for rows in blocks:
        after = x1[rows]
        env.out_work[rows] = (env.valid[rows, 0:1] * (after + (acc[rows] + line(env.down_bias)))).astype(BF16)
        xhat, rstd = normalize(after)
        d_norm = d_n2[rows]
        d_x1 = dm[rows].astype(F32) + norm_back(d_norm, line(env.gain2), xhat, rstd)
        env.d_x1[rows] = d_x1
        d_a = d_x1.astype(BF16)
        n2[rows] = d_a
        sums = [a + row_sum(b) for a, b in zip(sums, (d_a.astype(F32), d_norm * xhat, d_norm))]
    d_mixed = mm(n2[...], out_weight[...], NT).astype(BF16)
    for g in range(features // 128):
        env.d_mixed[g] = d_mixed[:, g * 128:(g + 1) * 128]
    env.after_middle()
    out = mm(mixed[...].T, n2[...]).astype(BF16)
    g_out = env.pieces[3 * TILES]
    for d in range(shares):
        for core in range(2):
            g_out[d, core] = out[d * share:(d + 1) * share, core * (features // 2):(core + 1) * (features // 2)]
    for row, value in zip((2, 5, 6), sums):
        env.small[row:row + 1, :] = value
    env.tick("e")


def attention_part(env, matrix, own, shared_q, shared_kv, own_mixed, shared_mixed, own_d, shared_dq, shared_dkv, joined, normed, normed_t, pair_d, x_in,
                   d_work, d_mirror, weight_sem):
    s, x, c = env.s, env.x_at, env.c
    other = 1 - c
    total, features = x_in.shape
    groups = own.shape[1]
    partner, across = 2 * x + other, 2 * (1 - x) + c
    mine = pl.ds(groups * c, groups)
    own_rows = span(OWN * c, OWN)
    sender = env.sender
    loads = [pltpu.make_async_copy(a, b, weight_sem.at[i]) for i, (a, b) in enumerate((
        (env.shared_q, shared_q), (env.shared_kv, shared_kv), (env.shared_mixed, shared_mixed), (env.own, own), (env.own_mixed, own_mixed), (env.weight, matrix), (env.x, x_in)))]
    at = 0
    for rows in (slice(0, OWN), slice(OWN, WORK), slice(WORK, TALL)):
        for core in range(2):
            count = rows.stop - rows.start
            loads.append(pltpu.make_async_copy(env.normed.at[core, rows], normed.at[pl.ds(at, count)], weight_sem.at[len(loads)]))
            at += count
    for load in loads:
        load.start()
    key_spot = lax.broadcasted_iota(jnp.int32, (KEYS, 1), 0)
    shared_dm_copies, own_dm_copies = env.exchange_copies()
    wait_all(shared_dm_copies + loads[0:3])
    for p in range(groups):
        attend_back(p, shared_q, shared_kv.at[0], shared_kv.at[1], env.shared_dm, shared_mixed, env.shared_log, shared_slots(key_spot) < env.lengths[2],
                    shared_dq, shared_dkv.at[0], shared_dkv.at[1], env.head_dim, 256, lambda i: env.tick(f"s{p}{i}"))
    shared_copies = []
    for to, peer in ((other, partner), (c, None)):
        ends = [(shared_dq.at[:, span(SHARED * to, SHARED)], env.joined_lanes.at[0, mine, OWN:WORK])]
        for chip, rows in ((x, slice(OWN, WORK)), (1 - x, slice(WORK, TALL))):
            ends.append((shared_dkv.at[:, :, span(OWN * chip + SHARED * to, SHARED)], env.joined_lanes.at[1:3, mine, rows]))
        shared_copies += [sender.near(*pair) if peer is None else sender.far(*pair, peer) for pair in ends]
    wait_all(own_dm_copies + loads[3:5] + loads[7:])
    normed_t[...] = normed[...].T
    share = features // env.shares
    pair_d[KEYS + OWN:, 0:128] = jnp.zeros((OWN, 128), BF16)
    for p in range(groups):
        attend_back(p, own.at[0], own.at[1], own.at[2], env.own_dm, own_mixed, env.own_log,
                    own_slots(key_spot) < jnp.where(x == 0, env.lengths[0], env.lengths[1]),
                    own_d.at[0], own_d.at[1], own_d.at[2], env.head_dim, 256, lambda i: env.tick(f"o{p}{i}"))
        here, there = span(OWN * x, OWN), span(OWN * (1 - x), OWN)
        pair_d[KEYS:KEYS + OWN, 0:128] = shared_dq[p]
        for part in range(3):
            cols = slice(part * 128, (part + 1) * 128)
            pair_d[0:KEYS, cols] = own_d[part, p]
            if part:
                pair_d[KEYS:KEYS + OWN, cols] = shared_dkv[part - 1, p, here]
                pair_d[KEYS + OWN:, cols] = shared_dkv[part - 1, p, there]
        out = mm(normed_t[...], pair_d[...]).astype(BF16)
        piece = env.pieces[3 * TILES + 1 + p]
        for d in range(env.shares):
            if PAIR_SPLIT[p]:
                for half_x in range(2):
                    first = (2 * d + half_x) * (share // 2)
                    piece[d, half_x] = out[first:first + share // 2]
            else:
                piece[d] = out[d * share:(d + 1) * share]
        env.tick(f"q{p}")
    own_copies = [
        sender.far(own_d.at[:, :, span(OWN * other, OWN)], env.joined_lanes.at[:, mine, 0:OWN], partner),
        sender.near(own_d.at[:, :, own_rows], env.joined_lanes.at[:, mine, 0:OWN]),
    ]
    wait_all(loads[5:7])
    wait_all(own_copies + shared_copies)
    blocks = [slice(i, i + SHARED) for i in range(0, total, SHARED)]
    joined[WORK:TALL, 0:features] = jnp.zeros((SHARED, features), BF16)
    for part in range(3):
        height = TALL if part else WORK
        for g in range(2 * groups):
            at = (part * 2 * groups + g) * 128
            joined[0:height, at:at + 128] = env.joined_lanes[part, g, 0:height]
    d_mirror[...] = mm(joined[WORK:TALL, features:], matrix[:, features:], NT).astype(BF16)
    mirror_copy = sender.far(d_mirror, env.other_mirror, across)
    env.tick("m")
    packed = env.pieces[-1]
    sums = [jnp.zeros((1, features), F32)] * 4
    tables = jnp.zeros((TABLE_ROWS, 2 * features), F32)
    d_norms = mm(joined[0:WORK], matrix[...], NT)
    env.tick("n")
    for i, rows in enumerate(blocks):
        d_norm = d_norms[rows]
        if rows.start == OWN:
            mirror_copy.wait()
            d_norm = d_norm + env.other_mirror[...].astype(F32)
        xhat, rstd = normalize(x_in[rows])
        terms = (joined[rows, 0:features].astype(F32), joined[rows, 2 * features:].astype(F32), d_norm * xhat, d_norm)
        sums = [a + row_sum(b) for a, b in zip(sums, terms)]
        d_x = env.d_x1[rows] + norm_back(d_norm, env.gain1[...].reshape(1, features), xhat, rstd)
        high, low = split_high_low(d_x)
        d_work[rows] = high
        tables = tables + mm(one_hot(env.ids[0:1, rows], env.ids[1:2, rows]), jnp.concatenate([high, low], 1))
        if i < 2:
            env.tick(f"f{i}")
    d_mover = Mover(s, env.d_patches, d_work, env.d_send, env.d_recv, True)
    sums[1] = sums[1] + row_sum(joined[WORK:TALL, 2 * features:].astype(F32))
    d_mover.start(MOVES)
    small = env.small
    small[16:16 + TABLE_ROWS, :] = tables[:, 0:features] + tables[:, features:]
    for row, value in zip((0, 1, 3, 4), sums):
        small[row:row + 1, :] = value
    repeat = env.up_bias_grad.shape[1] // features
    height = packed.shape[2]
    if share != packed.shape[3]:
        packed[...] = jnp.zeros_like(packed)
    for d in range(env.shares):
        for r in range(repeat):
            first = (d * repeat + r) * share
            small[8 + r:9 + r, d * share:(d + 1) * share] = env.up_bias_grad[:, first:first + share]
        for core in range(2):
            packed[d, core, :, 0:share] = small[core * height:(core + 1) * height, d * share:(d + 1) * share].astype(BF16)
    env.tick("f2")
    env.tick("tail")
    for mover in (env.out_mover, d_mover):
        mover.wait(MOVES)
        mover.drain(MOVES)


class Env:
    pass


BACK_INPUTS = ("lengths", "valid", "x", "mixed", "cot", "out_weight", "out_bias", "gain2", "shift2", "up", "up_bias", "down", "down_bias",
               "own", "shared_q", "shared_kv", "own_mixed", "shared_mixed", "own_log", "shared_log", "weight", "normed", "ids", "gain1")
IN_VMEM = ("valid", "out_bias", "gain2", "shift2", "up_bias", "down_bias", "own_log", "shared_log", "ids", "gain1")
BACK_SCRATCH = ("d_mixed", "own_dm", "shared_dm", "other_mirror", "joined_lanes", "d_x1", "out_work", "small", "up_bias_grad", "zeros",
                "out_send", "out_recv", "d_send", "d_recv", "send", "recv", "dm_send", "dm_recv", "zero_sem")


def backward_body(head_dim, shares, custom, features, hidden, *refs):
    env = Env()
    refs = list(refs)
    take = lambda count: [refs.pop(0) for _ in range(count)]
    for name, ref in zip(BACK_INPUTS, take(len(BACK_INPUTS))):
        setattr(env, name, ref)
    count = len(FLOW_NAMES)
    env.output, env.d_patches = take(2)
    outs = take(count)
    for name, ref in zip(BACK_SCRATCH, take(len(BACK_SCRATCH))):
        setattr(env, name, ref)
    env.head_dim, env.shares = head_dim, shares
    env.s, env.x_at, env.c = seq_place()
    flows = {}
    if custom:
        place = place_of()
        env.pieces = take(count)
        for i, name in enumerate(FLOW_NAMES):
            flows[name] = Flow(env.pieces[i], outs[i], take(FLOW_REFS), place, name[0] == "Q")
        env.greet = lambda: greet(place)
    else:
        env.pieces = outs
        env.greet = lambda: greet_group(env.s)

    def tick(point):
        for name in SCHEDULE.get(point, ()):
            if name == "R":
                env.out_mover.start(MOVES)
            elif custom:
                flows[name].advance()

    env.tick = tick
    env.sender = Sender(env.send, env.recv)
    env.out_mover = Mover(env.s, env.output, env.out_work, env.out_send, env.out_recv, True)
    env.zeros[...] = jnp.zeros_like(env.zeros)
    env.small[...] = jnp.zeros_like(env.small)

    def fill(act):
        @pl.when(env.s == UNUSED[0])
        def _():
            for i, array in enumerate((env.output, env.d_patches)):
                for clip in range(3):
                    act(pltpu.make_async_copy(env.zeros, array.at[clip, pl.ds(UNUSED[1], ROWS - UNUSED[1])], env.zero_sem.at[3 * i + clip]))

    fill(lambda made: made.start())

    groups = features // 256

    def exchange_copies():
        other = 1 - env.c
        partner = 2 * env.x_at + other
        mine, theirs = pl.ds(groups * env.c, groups), pl.ds(groups * other, groups)
        places = ((env.shared_dm.at[:, span(SHARED * env.c, SHARED)], slice(OWN, WORK)), (env.own_dm.at[:, span(OWN * env.c, OWN)], slice(0, OWN)))
        sender = Sender(env.dm_send, env.dm_recv)
        return [[sender.far(env.d_mixed.at[theirs, rows], place, partner, False), sender.near(env.d_mixed.at[mine, rows], place, False)]
                for place, rows in places]

    def after_middle():
        for made in sum(exchange_copies(), []):
            made.start()

    env.exchange_copies = exchange_copies
    env.after_middle = after_middle
    tile = hidden // TILES
    dma = pltpu.SemaphoreType.DMA
    wide, tall = lambda kind: pltpu.VMEM((WORK, features), kind), pltpu.VMEM((features, WORK), BF16)
    lanes = lambda *lead: pltpu.VMEM(lead + (128,), BF16)
    pl.run_scoped(
        functools.partial(middle_part, env), pltpu.VMEM((features, features), BF16), pltpu.VMEM((2, features, tile), BF16),
        pltpu.VMEM((2, tile, features), BF16), wide(BF16), wide(F32), wide(BF16), tall, wide(BF16), tall, wide(F32), wide(F32),
        pltpu.VMEM((WORK, tile), BF16), pltpu.VMEM((WORK, tile), BF16), pltpu.VMEM((WORK, tile), F32), dma((3 + 2 * groups,)), dma((4 * shares,)))
    pl.run_scoped(
        functools.partial(attention_part, env), pltpu.VMEM((features, 3 * features), BF16), lanes(3, groups, KEYS), lanes(groups, OWN),
        lanes(2, groups, KEYS), lanes(groups, KEYS), lanes(groups, OWN), lanes(3, groups, KEYS), lanes(groups, OWN), lanes(2, groups, KEYS),
        pltpu.VMEM((TALL, 3 * features), BF16), pltpu.VMEM((2 * KEYS, features), BF16), pltpu.VMEM((features, 2 * KEYS), BF16),
        pltpu.VMEM((2 * KEYS, 384), BF16), wide(F32), wide(BF16), pltpu.VMEM((SHARED, features), BF16), dma((13,)))
    fill(lambda made: made.wait())
    assert all(flow.done == len(flow.stages) for flow in flows.values())


def backward(inputs, head_dim, shares, custom):
    features, hidden = inputs["up"].shape
    groups = features // 256
    anywhere, vmem = pl.BlockSpec(memory_space=pl.ANY), pl.BlockSpec(memory_space=pltpu.VMEM)
    dma = pltpu.SemaphoreType.DMA
    lanes = lambda *lead: pltpu.VMEM(lead + (128,), BF16)
    moves = len(MOVES)
    shapes = piece_shapes(shares, features, hidden)
    specs = [vmem if name in IN_VMEM else anywhere for name in BACK_INPUTS]
    specs[0] = pl.BlockSpec(memory_space=pltpu.SMEM)
    scratch = [
        lanes(2 * groups, WORK), lanes(groups, KEYS), lanes(groups, OWN), pltpu.VMEM((SHARED, features), BF16), lanes(3, 2 * groups, TALL),
        pltpu.VMEM((WORK, features), F32), pltpu.VMEM((WORK, features), BF16), pltpu.VMEM((SMALL_ROWS, features), F32),
        pltpu.VMEM((1, hidden), F32), pltpu.VMEM((ROWS - UNUSED[1], features), BF16),
        dma((moves,)), dma((moves,)), dma((moves,)), dma((moves,)), dma((24,)), dma((24,)), dma((4,)), dma((4,)), dma((6,)),
    ]
    if custom:
        scratch += [pltpu.VMEM(shape, BF16) for shape in shapes]
        scratch += [ref for name, shape in zip(FLOW_NAMES, shapes) for ref in flow_scratch(name, shape)]
    rows = jax.ShapeDtypeStruct((3, ROWS, features), BF16)
    return pl.pallas_call(
        functools.partial(backward_body, head_dim, shares, custom, features, hidden),
        in_specs=specs,
        out_specs=[anywhere] * 2 + [vmem] * len(shapes),
        out_shape=[rows, rows] + [jax.ShapeDtypeStruct(result_shape(name, shape) if custom else shape, BF16) for name, shape in zip(FLOW_NAMES, shapes)],
        scratch_shapes=scratch,
        compiler_params=pltpu.CompilerParams(collective_id=0, has_side_effects=True, vmem_limit_bytes=63 * MIB),
    )(*(inputs[name] for name in BACK_INPUTS))


def assemble_body(time_count, freq_count, *refs):
    count = len(FLOW_NAMES)
    pieces = refs[0:count]
    outs = refs[count:]
    halved, whole, up = pieces[0:TILES], pieces[TILES:2 * TILES], pieces[2 * TILES:3 * TILES]
    out, *pairs, packed = pieces[3 * TILES:]
    (qkv_out, qb, vb, out_out, ob, n1g, n1s, n2g, n2s, up_out, up_b, down_out, db, time_out, freq_out) = outs
    third = qkv_out.shape[1] // 3
    for core in range(2):
        for p, pair in enumerate(pairs):
            for part in range(3):
                first = part * third + core * (third // 2) + p * 128
                cols = slice(part * 128, (part + 1) * 128)
                if PAIR_SPLIT[p]:
                    high = pair.shape[2]
                    for half_x in range(2):
                        qkv_out[half_x * high:(half_x + 1) * high, first:first + 128] = pair[core, half_x, :, cols].astype(F32)
                else:
                    qkv_out[:, first:first + 128] = pair[core, :, cols].astype(F32)
        cols = out.shape[2]
        out_out[:, core * cols:(core + 1) * cols] = out[core].astype(F32)
    width = whole[0].shape[2]
    half = down_out.shape[1] // 2
    for j in range(TILES):
        for core in range(2):
            grad = jnp.concatenate([halved[j][core, 0], halved[j][core, 1], whole[j][core]], 0)
            down_out[j * width:(j + 1) * width, core * half:(core + 1) * half] = grad.astype(F32).T
            if UP_SPLIT[j]:
                grad = jnp.concatenate([up[j][core, 0], up[j][core, 1]], 1)
            else:
                grad = up[j][core]
            blocks = grad.shape[1] // width
            for k in range(blocks):
                first = ((core * blocks + k) * TILES + j) * width
                up_out[:, first:first + width] = grad[:, k * width:(k + 1) * width].astype(F32)
    small = jnp.concatenate([packed[0], packed[1]], 0).astype(F32)
    share = qb.shape[0]
    for row, ref in ((0, qb), (1, vb), (2, ob), (3, n1g), (4, n1s), (5, n2g), (6, n2s), (7, db)):
        ref[...] = small[row, 0:share]
    for r in range(up_b.shape[0] // share):
        up_b[r * share:(r + 1) * share] = small[8 + r, 0:share]
    time_out[...] = small[16:16 + TABLE_ROWS].T[0:share, 0:time_count]
    freq_out[...] = small[16 + FREQ_ROW:16 + FREQ_ROW + freq_count, 0:share]


def assemble(pieces, features, hidden, shares, time_count, freq_count):
    share = features // shares
    line = (share,)
    shapes = [(share, 3 * features), line, line, (share, features), line, line, line, line, line, (share, hidden), (hidden // shares,),
              (hidden // shares, features), line, (share, time_count), (freq_count, share)]
    return pl.pallas_call(
        functools.partial(assemble_body, time_count, freq_count),
        out_shape=[jax.ShapeDtypeStruct(shape, F32) for shape in shapes],
        compiler_params=params(),
    )(*pieces)


def reduce_native(pieces, time_count, freq_count):
    def total(part, axis):
        return lax.psum(lax.psum_scatter(part, "dp", scatter_dimension=axis, tiled=True), "seq").astype(F32)

    pieces = [p[0] for p in pieces]
    down = jnp.concatenate([jnp.concatenate([part for c in range(2) for part in (a[c, 0], a[c, 1], b[c])], 0)
                            for a, b in zip(pieces[0:TILES], pieces[TILES:2 * TILES])], 1)
    ups = []
    for piece, split in zip(pieces[2 * TILES:3 * TILES], UP_SPLIT):
        ups += [part for c in range(2) for part in ((piece[c, 0], piece[c, 1]) if split else (piece[c],))]
    up = jnp.concatenate(ups, 1)
    out, *pairs, packed = pieces[3 * TILES:]
    here = lax.rem(lax.axis_index("seq"), 2)
    pairs = [jnp.concatenate([p[0], p[1]], 0) if split else p for p, split in zip(pairs, PAIR_SPLIT)]
    qkv = jnp.concatenate([jnp.where(here == core, p[:, part * 128:(part + 1) * 128], BF16(0))
                           for part in range(3) for core in range(2) for p in pairs], 1)
    small = packed.reshape(SMALL_ROWS, -1)
    repeat = up.shape[1] // small.shape[1]
    up_bias = total(small[8:8 + repeat].reshape(-1), 0)
    small = total(small, 1)
    return (
        total(qkv, 0), small[0], small[1], total(jnp.concatenate([out[0], out[1]], 1), 0), small[2], small[3], small[4], small[5], small[6],
        total(up, 0), up_bias, total(down, 1).T, small[7], small[16:16 + time_count], small[16 + FREQ_ROW:16 + FREQ_ROW + freq_count],
    )


def shards(
    patches,
    cotangent,
    time_ids,
    freq_ids,
    lengths,
    qkv_weight,
    query_bias,
    value_bias,
    out_weight,
    out_bias,
    norm1_gain,
    norm1_shift,
    norm2_gain,
    norm2_shift,
    up_weight,
    up_bias,
    down_weight,
    down_bias,
    time_table,
    freq_table,
):
    features = patches.shape[2]
    head_dim = features // HEADS
    assert patches.shape[:2] == (3, ROWS) and lax.axis_size("seq") == 4
    custom = lax.axis_size("dp") == 8
    shares = 8 if custom else 1
    x, normed, own, shared_q, shared_kv, own_log, own_mixed, shared_log, shared_mixed, mixed, cot, ids, valid = forward(
        lengths, patches, cotangent, time_ids, freq_ids, time_table, freq_table, norm1_gain, norm1_shift, qkv_weight, query_bias, value_bias,
        head_dim
    )
    inputs = dict(
        lengths=lengths, valid=valid, x=x, mixed=mixed, cot=cot, out_weight=out_weight, out_bias=out_bias, gain2=norm2_gain,
        shift2=norm2_shift, up=up_weight, up_bias=up_bias, down=down_weight, down_bias=down_bias, own=own, shared_q=shared_q,
        shared_kv=shared_kv, own_mixed=own_mixed, shared_mixed=shared_mixed, own_log=own_log, shared_log=shared_log, weight=qkv_weight, normed=normed, ids=ids, gain1=norm1_gain)
    output, d_patch, *pieces = backward(inputs, head_dim, shares, custom)
    counts = time_table.shape[0], freq_table.shape[0]
    if custom:
        *rest, time_grad, freq_grad = assemble(pieces, features, up_weight.shape[1], shares, *counts)
        return (output, d_patch, *rest, time_grad.T, freq_grad)
    return (output, d_patch) + reduce_native(pieces, *counts)


def solution(mesh):
    clip_spec, row_spec, one = P("dp", "seq", None), P("dp", "seq"), P("dp")
    matrix = P("dp", None)
    return jax.shard_map(
        shards,
        mesh=mesh,
        in_specs=(clip_spec, clip_spec, row_spec, row_spec, one) + (P(),) * 15,
        out_specs=(clip_spec, clip_spec, matrix, one, one, matrix, one, one, one, one, one, matrix, one, matrix, one, P(None, "dp"), P(None, "dp")),
        check_vma=False,
    )
```

```python
import functools
import math

import jax
import jax.numpy as jnp
from jax import lax
from jax.experimental import pallas as pl
from jax.experimental.pallas import tpu as pltpu
from jax.sharding import PartitionSpec as P

HEADS = 12
EPS = 1e-06
NEGATIVE = -1000000000.0
FREQ_ROW = 104
TABLE_ROWS = 128
SMALL_ROWS = 32 + TABLE_ROWS
TILES = 3
CHUNKS = 2
UP_SPLIT = (False, True, False)
PAIR_SPLIT = (True, True, False)
F32 = jnp.float32
BF16 = jnp.bfloat16
NN = (((1,), (0,)), ((), ()))
NT = (((1,), (1,)), ((), ()))
TN = (((0,), (0,)), ((), ()))
MIB = 1 << 20


def mm(left, right, dims=NN):
    return lax.dot_general(left, right, dims, preferred_element_type=F32)


def params(limit=60):
    return pltpu.CompilerParams(vmem_limit_bytes=limit * MIB)


def row_sum(values):
    return jnp.sum(values, 0, keepdims=True)


def normalize(values):
    center = values - jnp.mean(values, -1, keepdims=True)
    rstd = lax.rsqrt(jnp.mean(center * center, -1, keepdims=True) + EPS)
    return center * rstd, rstd


def norm_back(d_out, gain, xhat, rstd):
    u = d_out * gain
    inner = jnp.mean(u * xhat, -1, keepdims=True)
    return rstd * (u - jnp.mean(u, -1, keepdims=True) - xhat * inner)


def gelu_parts(h):
    half = 0.5 * (1.0 + lax.erf(h * (1.0 / math.sqrt(2.0))))
    return half, half + h * jnp.exp(h * h * -0.5) * (1.0 / math.sqrt(2.0 * math.pi))


def split_high_low(values):
    high = values.astype(BF16)
    return high, (values - high.astype(F32)).astype(BF16)


def one_hot(time_row, freq_row):
    spot = lax.broadcasted_iota(jnp.int32, (TABLE_ROWS, time_row.shape[1]), 0)
    hit = (spot == time_row) | (spot == freq_row + FREQ_ROW)
    return jnp.where(hit, 1.0, 0.0).astype(BF16)


ROWS = 224
OWN = 352
SHARED = 176
WORK = OWN + SHARED
KEYS = 2 * OWN
TALL = WORK + SHARED
SHARED_MOVES = (
    (0, 2, 176, 48, 3, 384), (1, 2, 176, 48, 3, 432), (2, 2, 176, 48, 3, 480), (3, 2, 0, 32, 3, 352),
    (0, 2, 0, 176, 0, 352), (1, 2, 0, 176, 1, 352), (2, 2, 0, 176, 2, 352),
)
OWN_MOVES = (
    (2, 0, 0, 128, 0, 224), (2, 0, 128, 96, 1, 224), (3, 0, 0, 32, 1, 320), (0, 1, 0, 224, 2, 0), (1, 1, 0, 224, 3, 0),
    (2, 1, 128, 96, 3, 224), (2, 1, 0, 128, 2, 224), (3, 1, 0, 32, 3, 320), (0, 0, 0, 224, 0, 0), (1, 0, 0, 224, 1, 0),
)
MIRROR_MOVES = (
    (0, 2, 0, 176, 2, 528), (1, 2, 0, 176, 3, 528), (2, 2, 0, 176, 0, 528), (0, 2, 176, 48, 1, 560), (2, 2, 176, 48, 1, 656),
    (1, 2, 176, 48, 1, 608), (3, 2, 0, 32, 1, 528),
)
MOVES = SHARED_MOVES + OWN_MOVES
ALL_MOVES = MOVES + MIRROR_MOVES
UNUSED = (3, 32)


def seq_place():
    s = lax.axis_index("seq")
    return s, s // 2, lax.rem(s, 2)


def seq_peer(s):
    return {"seq": s}


def greet_group(s):
    barrier = pltpu.get_barrier_semaphore()
    for ahead in range(1, 4):
        pl.semaphore_signal(barrier, inc=1, device_id=seq_peer(lax.rem(s + ahead, 4)), device_id_type=pl.DeviceIdType.MESH)
    pl.semaphore_wait(barrier, 3)


class Mover:
    def __init__(self, s, at_home, at_work, send, recv, back=False):
        self.s, self.at_home, self.at_work, self.send, self.recv, self.back = s, at_home, at_work, send, recv, back

    def ends(self, move):
        home, clip, first, count, work, spot = move
        a, b = self.at_home.at[clip, pl.ds(first, count)], self.at_work.at[pl.ds(spot, count)]
        return (work, b, home, a) if self.back else (home, a, work, b)

    def each(self, moves, which, act, near=True):
        for device in range(4):
            chosen = [m for m in moves if self.ends(m)[which] == device and (near or self.ends(m)[0] != self.ends(m)[2])]
            if not chosen:
                continue

            @pl.when(self.s == device)
            def _(chosen=chosen):
                for m in chosen:
                    src_device, src, dst_device, dst = self.ends(m)
                    slot = ALL_MOVES.index(m)
                    if src_device == dst_device:
                        act(False, pltpu.make_async_copy(src, dst, self.recv.at[slot]))
                    else:
                        act(True, pltpu.make_async_remote_copy(
                            src_ref=src, dst_ref=dst, send_sem=self.send.at[slot], recv_sem=self.recv.at[slot],
                            device_id=seq_peer(dst_device), device_id_type=pl.DeviceIdType.MESH))

    def start(self, moves):
        self.each(moves, 0, lambda far, made: made.start())

    def wait(self, moves):
        self.each(moves, 2, lambda far, made: made.wait_recv() if far else made.wait())

    def drain(self, moves):
        self.each(moves, 0, lambda far, made: made.wait_send(), False)


class Sender:
    def __init__(self, send, recv):
        self.send, self.recv, self.used = send, recv, 0

    def far(self, source, target, peer, begin=True):
        made = pltpu.make_async_remote_copy(
            src_ref=source, dst_ref=target, send_sem=self.send.at[self.used], recv_sem=self.recv.at[self.used],
            device_id=seq_peer(peer), device_id_type=pl.DeviceIdType.MESH)
        self.used += 1
        if begin:
            made.start()
        return made

    def near(self, source, target, begin=True):
        made = pltpu.make_async_copy(source, target, self.recv.at[self.used])
        self.used += 1
        if begin:
            made.start()
        return made


def wait_all(copies):
    for made in copies:
        made.wait()


def shift_between(spot, cuts):
    slot = spot
    for low, high, shift in cuts:
        slot = jnp.where((spot >= low) & (spot < high), spot + shift, slot)
    return slot


def own_slots(spot):
    return shift_between(spot, ((224, 352, 224), (352, 576, -128)))


def shared_slots(spot):
    return shift_between(spot, ((176, 352, 48), (352, 528, 96), (528, 560, 144), (560, 608, -384), (608, 656, -208), (656, 704, -32)))


def span(first, size):
    return pl.ds(pl.multiple_of(first, 16), size)


def lane_parts(value):
    high, rest = split_high_low(value)
    low = (value - high.astype(F32) - rest.astype(F32)).astype(BF16)
    return high, rest, low


def with_lanes(base, lane, first, columns):
    for i, column in enumerate(columns):
        base = jnp.where(lane == first + i, column, base)
    return base


def attend(query, keys, values, key_ok, mixed_out, log_out, head_dim):
    count = query.shape[1]
    lane = lax.broadcasted_iota(jnp.int32, (1, 128), 1)
    head = lane // head_dim
    scale = BF16(1.0 / math.sqrt(head_dim))
    key_bias = jnp.where(key_ok, 0.0, NEGATIVE).astype(BF16)
    per_pair = 128 // head_dim
    units = [(first, h) for first in range(0, count, OWN) for h in range(per_pair)]
    log_out[...] = jnp.zeros_like(log_out)

    def pair(p, _):
        k, v = keys[p], values[p]
        biased = [with_lanes(k, lane, free_lane(h, head_dim), (key_bias,)) for h in range(per_pair)]
        counted = [with_lanes(v, lane, free_lane(h, head_dim), (BF16(1),)) for h in range(per_pair)]

        def score(unit):
            first, h = unit
            q = jnp.where(head == h, query[p, first:first + OWN] * scale, BF16(0))
            return mm(with_lanes(q, lane, free_lane(h, head_dim), (BF16(1),)), biased[h], NT)

        ready = score(units[0])
        for i, (first, h) in enumerate(units):
            scores = ready
            if i + 1 < len(units):
                ready = score(units[i + 1])
            rows = slice(first, first + OWN)
            highest = jnp.max(scores, -1, keepdims=True)
            powers = jnp.exp(scores - highest)
            out = mm(powers.astype(BF16), counted[h])
            first_free = free_lane(h, head_dim)
            total = out[:, first_free:first_free + 1]
            out = out * (1.0 / total)
            mixed = out if h == 0 else jnp.where(head == h, out, mixed)
            log_out[rows] = jnp.where(lane == per_pair * p + h, highest + jnp.log(total), log_out[rows])
            if h == per_pair - 1:
                mixed_out[p, rows] = mixed.astype(BF16)
        return 0

    lax.fori_loop(0, query.shape[0], pair, 0)


def free_lane(h, head_dim):
    return (h + 1) * head_dim % 128


def forward_body(head_dim, lengths, patches, cot, time_ids, freq_ids, time_table, freq_table, gain, shift, weight, query_bias, value_bias,
                 x_hbm, n_hbm, own_hbm, shared_q_hbm, shared_kv_hbm, own_log_hbm, own_mixed_hbm, shared_log, shared_mixed, mixed_out, cot_out,
                 id_out, valid_out,
                 x_out, n_out, own_out, shared_q_out, shared_kv_out, own_log, own_mixed, work, table_f32, table, ids, matrix, own_stage, shared_stage, mirror_stage,
                 patch_send, patch_recv, cot_send, cot_recv, send, recv, weight_sem):
    s, x, c = seq_place()
    features = x_out.shape[1]
    groups = own_out.shape[1]
    other = 1 - c
    loads = [pltpu.make_async_copy(weight.at[:, pl.ds(p * features, features)], matrix.at[:, pl.ds(p * features, features)], weight_sem.at[p])
             for p in range(3)]
    for load in loads:
        load.start()
    greet_group(s)
    patch_mover = Mover(s, patches, work, patch_send, patch_recv)
    cot_mover = Mover(s, cot, cot_out, cot_send, cot_recv)
    sender = Sender(send, recv)
    id_copies = []
    for i, source in enumerate((time_ids, freq_ids)):
        id_copies.append(sender.near(source, ids.at[s, i]))
        for ahead in range(1, 4):
            id_copies.append(sender.far(source, ids.at[s, i], lax.rem(s + ahead, 4)))
    patch_mover.start(ALL_MOVES)

    table_f32[...] = jnp.zeros_like(table_f32)
    table_f32[0:time_table.shape[0], :] = time_table[...]
    table_f32[FREQ_ROW:FREQ_ROW + freq_table.shape[0], :] = freq_table[...]
    high, low = split_high_low(table_f32[...])
    table[0:TABLE_ROWS, :] = high
    table[TABLE_ROWS:, :] = low
    spot = lax.broadcasted_iota(jnp.int32, (WORK, 1), 0)
    place = jnp.where(spot < OWN, jnp.where(spot < ROWS, spot + ROWS * c, spot + ROWS + 128 * c), shared_slots(spot - OWN + SHARED * s))
    limit = jnp.where(spot < OWN, jnp.where(x == 0, lengths[0], lengths[1]), lengths[2])
    valid_out[...] = jnp.broadcast_to(jnp.where(place < limit, 1.0, 0.0), valid_out.shape)
    id_out[...] = jnp.zeros_like(id_out)
    wait_all(id_copies)
    for device in range(4):
        @pl.when(s == device)
        def _(device=device):
            for home, clip, first, count, target, at in ALL_MOVES:
                if target == device:
                    for i in range(2):
                        id_out[i:i + 1, at:at + count] = ids[home, i, clip:clip + 1, first:first + count]

    bias = (query_bias[...].reshape(1, features), None, value_bias[...].reshape(1, features))

    def project(first, count, stage, own=True):
        rows = slice(first, first + count)
        hot = one_hot(id_out[0:1, rows], id_out[1:2, rows])
        value = work[rows].astype(F32) + mm(jnp.concatenate([hot, hot], 0), table[...], TN)
        if own:
            x_out[rows] = value
        xhat, _ = normalize(value)
        normed = (xhat * gain[...].reshape(1, features) + shift[...].reshape(1, features)).astype(BF16)
        n_out[c, rows] = normed
        for part in range(0 if own else 1, 3):
            out = mm(normed, matrix[:, part * features:(part + 1) * features])
            if bias[part] is not None:
                out = out + bias[part]
            out = out.astype(BF16)
            for g in range(2 * groups):
                stage[part if own else part - 1, g] = out[:, g * 128:(g + 1) * 128]

    patch_mover.wait(SHARED_MOVES)
    wait_all(loads)
    project(OWN, SHARED, shared_stage)
    q_rows, kv_rows = span(SHARED * c, SHARED), span(SHARED * s, SHARED)
    mine, theirs = pl.ds(groups * c, groups), pl.ds(groups * other, groups)
    mirror_rows = span(SHARED * (2 * (1 - x) + c), SHARED)
    partner = 2 * x + other
    shared_copies = [
        sender.far(shared_stage.at[0, theirs], shared_q_out.at[:, q_rows], partner),
        sender.far(shared_stage.at[1:3, theirs], shared_kv_out.at[:, :, kv_rows], partner),
        sender.near(shared_stage.at[0, mine], shared_q_out.at[:, q_rows]),
        sender.near(shared_stage.at[1:3, mine], shared_kv_out.at[:, :, kv_rows]),
    ]
    patch_mover.wait(OWN_MOVES)
    project(0, OWN, own_stage)
    own_rows = span(OWN * c, OWN)
    saves = [sender.near(x_out, x_hbm)]
    own_copies = [
        sender.far(own_stage.at[:, theirs], own_out.at[:, :, own_rows], partner),
        sender.near(own_stage.at[:, mine], own_out.at[:, :, own_rows]),
    ]
    cot_mover.start(MOVES)
    patch_mover.wait(MIRROR_MOVES)
    project(WORK, SHARED, mirror_stage, False)
    shared_copies += [
        sender.far(mirror_stage.at[:, theirs], shared_kv_out.at[:, :, mirror_rows], partner),
        sender.near(mirror_stage.at[:, mine], shared_kv_out.at[:, :, mirror_rows]),
    ]
    normed_copy = sender.far(n_out.at[c], n_out.at[c], partner)
    wait_all(own_copies)
    saves.append(sender.near(own_out, own_hbm))
    key_spot = lax.broadcasted_iota(jnp.int32, (KEYS, 1), 0)
    attend(own_out.at[0], own_out.at[1], own_out.at[2], own_slots(key_spot) < jnp.where(x == 0, lengths[0], lengths[1]),
           own_mixed, own_log, head_dim)
    mixed_copies = [
        sender.far(own_mixed.at[:, span(OWN * other, OWN)], mixed_out.at[mine, 0:OWN], partner),
        sender.near(own_mixed.at[:, own_rows], mixed_out.at[mine, 0:OWN]),
    ]
    wait_all(shared_copies + [normed_copy])
    saves += [sender.near(a, b) for a, b in ((n_out, n_hbm), (shared_q_out, shared_q_hbm), (shared_kv_out, shared_kv_hbm),
                                             (own_mixed, own_mixed_hbm), (own_log, own_log_hbm))]
    attend(shared_q_out, shared_kv_out.at[0], shared_kv_out.at[1], shared_slots(key_spot) < lengths[2],
           shared_mixed, shared_log, head_dim)
    mixed_copies += [
        sender.far(shared_mixed.at[:, span(SHARED * other, SHARED)], mixed_out.at[mine, OWN:WORK], partner),
        sender.near(shared_mixed.at[:, q_rows], mixed_out.at[mine, OWN:WORK]),
    ]
    wait_all(mixed_copies + saves)
    cot_mover.wait(MOVES)
    patch_mover.drain(ALL_MOVES)
    cot_mover.drain(MOVES)


def forward(lengths, patches, cot, time_ids, freq_ids, time_table, freq_table, gain, shift, weight, query_bias, value_bias, head_dim):
    features = patches.shape[2]
    groups = features // 256
    anywhere, vmem = pl.BlockSpec(memory_space=pl.ANY), pl.BlockSpec(memory_space=pltpu.VMEM)
    lanes = lambda *lead: jax.ShapeDtypeStruct(lead + (128,), BF16)
    saved = [
        jax.ShapeDtypeStruct((WORK, features), F32),
        jax.ShapeDtypeStruct((2, TALL, features), BF16),
        lanes(3, groups, KEYS),
        lanes(groups, OWN),
        lanes(2, groups, KEYS),
        jax.ShapeDtypeStruct((KEYS, 128), F32),
        lanes(groups, KEYS),
    ]
    dma = pltpu.SemaphoreType.DMA
    return pl.pallas_call(
        functools.partial(forward_body, head_dim),
        in_specs=[pl.BlockSpec(memory_space=pltpu.SMEM)] + [anywhere] * 4 + [vmem] * 4 + [anywhere] + [vmem] * 2,
        out_specs=[anywhere] * 7 + [vmem] * 6,
        out_shape=saved + [
            jax.ShapeDtypeStruct((OWN, 128), F32),
            lanes(groups, OWN),
            lanes(2 * groups, WORK),
            jax.ShapeDtypeStruct((WORK, features), BF16),
            jax.ShapeDtypeStruct((8, TALL), jnp.int32),
            jax.ShapeDtypeStruct((WORK, 128), F32),
        ],
        scratch_shapes=[pltpu.VMEM(a.shape, a.dtype) for a in saved] + [
            pltpu.VMEM((TALL, features), BF16),
            pltpu.VMEM((TABLE_ROWS, features), F32),
            pltpu.VMEM((2 * TABLE_ROWS, features), BF16),
            pltpu.VMEM((4, 2) + time_ids.shape, jnp.int32),
            pltpu.VMEM(weight.shape, BF16),
            pltpu.VMEM((3, 2 * groups, OWN, 128), BF16),
            pltpu.VMEM((3, 2 * groups, SHARED, 128), BF16),
            pltpu.VMEM((2, 2 * groups, SHARED, 128), BF16),
            dma((len(ALL_MOVES),)), dma((len(ALL_MOVES),)), dma((len(MOVES),)), dma((len(MOVES),)), dma((40,)), dma((40,)), dma((3,)),
        ],
        compiler_params=pltpu.CompilerParams(collective_id=1, has_side_effects=True, vmem_limit_bytes=60 * MIB),
    )(lengths, patches, cot, time_ids, freq_ids, time_table, freq_table, gain, shift, weight, query_bias, value_bias)


def attend_back(p, query, keys, values, d_mixed, mixed, logs, key_ok, d_query, d_keys, d_values, head_dim, block, tick):
    count = query.shape[1]
    lane = lax.broadcasted_iota(jnp.int32, (1, 128), 1)
    head = lane // head_dim
    scale = BF16(1.0 / math.sqrt(head_dim))
    key_bias = jnp.where(key_ok, 0.0, NEGATIVE).astype(BF16)
    k, v = keys[p], values[p]
    k_t = (k * scale).T
    per_pair = 128 // head_dim
    one = BF16(1)
    k_wide = [with_lanes(k, lane, free_lane(h, head_dim), (key_bias, one, one, one)) for h in range(per_pair)]
    v_wide = [with_lanes(v, lane, free_lane(h, head_dim), (one, one, one)) for h in range(per_pair)]
    total_k = jnp.zeros((KEYS, 128), F32)
    total_v = jnp.zeros((KEYS, 128), F32)
    units = [(first, min(first + block, count), h) for first in range(0, count, block) for h in range(per_pair)]

    def products(unit):
        first, last, h = unit
        rows = slice(first, last)
        d_m = d_mixed[p, rows]
        q_head = jnp.where(head == h, query[p, rows] * scale, BF16(0))
        m_head = jnp.where(head == h, d_m, BF16(0))
        delta = jnp.sum(m_head.astype(F32) * mixed[p, rows].astype(F32), -1, keepdims=True)
        at = per_pair * p + h
        q_wide = with_lanes(q_head, lane, free_lane(h, head_dim), (one,) + lane_parts(-logs[rows, at:at + 1]))
        m_wide = with_lanes(m_head, lane, free_lane(h, head_dim), lane_parts(-delta))
        return q_head, m_head, mm(k_wide[h], q_wide, NT), mm(v_wide[h], m_wide, NT)

    ready = products(units[0])
    parts = []
    for i, (first, last, h) in enumerate(units):
        q_head, m_head, scores, d_probs = ready
        if i + 1 < len(units):
            ready = products(units[i + 1])
        probs = jnp.exp(scores)
        d_scores = (probs * d_probs).astype(BF16)
        total_v = total_v + mm(probs.astype(BF16), m_head)
        total_k = total_k + mm(d_scores, q_head)
        parts.append(mm(k_t[h * head_dim:(h + 1) * head_dim], d_scores))
        if h == per_pair - 1:
            d_query[p, first:last] = jnp.concatenate(parts, 0).T.astype(BF16)
            parts = []
            tick(first // block)
    d_keys[p] = total_k.astype(BF16)
    d_values[p] = total_v.astype(BF16)


class Flow:
    def __init__(self, source, result, refs, place, single):
        self.source, self.result, self.single = source, result, single
        self.split = len(source.shape) == (4 if single else 5)
        self.got, self.x_got, self.y_got, self.z_got, self.send, self.recv = refs
        self.z, self.y, self.x, self.c = place
        self.open = {}
        if self.split:
            self.stages = [self.begin, self.cores_x, self.x_y, self.y_z, self.z_fill, self.fill_cores, self.end]
        else:
            self.stages = [self.begin, self.cores_y, self.y_z, self.z_x, self.x_cores, self.end]
        if single:
            self.stages = [self.to_x if self.split else self.to_y] + self.stages[2:]
        self.used = 0
        self.done = 0

    def advance(self):
        self.stages[self.done]()
        self.done += 1

    def copy(self, key, ends):
        slot = self.used
        self.used += 1

        def make():
            source, target, (z, y, x, c) = ends()
            return pltpu.make_async_remote_copy(
                src_ref=source, dst_ref=target, send_sem=self.send.at[slot], recv_sem=self.recv.at[slot],
                device_id=(z * 2 + y, x * 2 + c), device_id_type=pl.DeviceIdType.MESH)

        make().start()
        self.open.setdefault(key, []).append(make)

    def wait(self, key):
        for make in self.open.pop(key):
            make().wait()

    def at(self, z, y):
        row = self.row(z * 2 + y)
        return row.at[self.x] if self.split else row

    def row(self, i):
        return self.source.at[i] if self.single else self.source.at[i, self.c]

    def begin(self):
        self.copy("core", lambda: (self.source.at[:, 1 - self.c], self.got, (self.z, self.y, self.x, 1 - self.c)))

    def cores(self):
        self.wait("core")

        def add(i, _):
            self.source[i, self.c] = self.source[i, self.c] + self.got[i]
            return 0

        lax.fori_loop(0, self.got.shape[0], add, 0)

    def cores_x(self):
        self.cores()
        self.to_x()

    def to_x(self):
        part = lambda: self.source.at[:, 1 - self.x] if self.single else self.source.at[:, self.c, 1 - self.x]
        self.copy("x", lambda: (part(), self.x_got, (self.z, self.y, 1 - self.x, self.c)))

    def cores_y(self):
        self.cores()
        self.to_y()

    def to_y(self):
        for z in range(4):
            self.copy("y", lambda z=z: (self.at(z, 1 - self.y), self.y_got.at[z], (self.z, 1 - self.y, self.x, self.c)))

    def x_y(self):
        self.wait("x")

        def add(i, _):
            spot = self.row(i).at[self.x]
            spot[...] = spot[...] + self.x_got[i]
            return 0

        lax.fori_loop(0, self.source.shape[0], add, 0)
        self.to_y()

    def y_z(self):
        self.wait("y")

        def add(z, _):
            spot = self.at(z, self.y)
            spot[...] = spot[...] + self.y_got[z]
            return 0

        lax.fori_loop(0, 4, add, 0)
        for ahead in range(1, 4):
            def ends(ahead=ahead):
                z = lax.rem(self.z + ahead, 4)
                return self.at(z, self.y), self.z_got.at[ahead - 1], (z, self.y, self.x, self.c)

            self.copy("z", ends)

    def z_sum(self):
        self.wait("z")
        total = self.at(self.z, self.y)[...].astype(F32)
        for i in range(3):
            total = total + self.z_got[i].astype(F32)
        return total.astype(BF16)

    def z_fill(self):
        self.result[self.c, self.x] = self.z_sum()
        spot = lambda: self.result.at[self.c, self.x]
        self.copy("fill", lambda: (spot(), spot(), (self.z, self.y, 1 - self.x, self.c)))

    def fill_cores(self):
        self.wait("fill")
        self.to_core()

    def z_x(self):
        spot = self.at(self.z, self.y)
        spot[...] = self.z_sum()
        self.copy("x", lambda: (self.at(self.z, self.y), self.x_got, (self.z, self.y, 1 - self.x, self.c)))

    def x_cores(self):
        self.wait("x")
        self.result[self.c] = self.at(self.z, self.y)[...] + self.x_got[...]
        self.to_core()

    def to_core(self):
        spot = lambda: self.result.at[self.c]
        self.copy("end", lambda: (spot(), spot(), (self.z, self.y, self.x, 1 - self.c)))

    def end(self):
        self.wait("end")


FLOW_REFS = 6
FLOW_NAMES = ("D0", "D1", "D2", "E0", "E1", "E2", "U0", "U1", "U2", "O", "Q0", "Q1", "Q2", "S")
SCHEDULE = {
    "d0": ("E0", "D0",),
    "u0": ("U0",),
    "0c": ("E0",),
    "1b0": ("D0",),
    "d1": ("D1", "U0",),
    "u1": ("U1", "E0", "D1", "E1",),
    "2b1": ("U1",),
    "d2": ("D2", "D0",),
    "2e0": ("E2",),
    "2e1": ("E1",),
    "u2": ("U0",),
    "2c": ("D2", "E2",),
    "e": ("O", "E1", "D1",),
    "s01": ("U1", "R",),
    "s20": ("E2",),
    "s21": ("O", "U2",),
    "o00": ("U0",),
    "o01": ("D0",),
    "q0": ("D2", "D1", "Q0", "U2", "U1",),
    "q1": ("D0", "Q1",),
    "o20": ("O",),
    "q2": ("D2", "Q2", "E0",),
    "m": ("U2",),
    "n": ("Q0", "O",),
    "f0": ("D1", "E2", "E1", "U1", "Q1",),
    "f1": ("Q2", "D2",),
    "f2": ("S", "U0", "E1", "Q1",),
    "tail": ("Q0", "S", "D1", "E2", "E1", "S", "Q2", "Q1", "U1", "U2", "U1", "O", "D0", "D1", "Q2", "E2", "Q0", "D2", "E0", "S", "U2", "Q0", "O", "U0", "D2", "Q1", "S", "Q0", "Q2", "Q1", "E0", "S", "D0", "U2",),
}


def flow_scratch(name, shape):
    single = name[0] == "Q"
    shares, tail = shape[0], shape[1 if single else 2:]
    block = tail[-2:]
    first = (shares,) + block if len(tail) == 3 else block
    slots = 16
    return [pltpu.VMEM((8, 128) if single else (shares,) + tail, BF16), pltpu.VMEM(first, BF16), pltpu.VMEM((4,) + block, BF16), pltpu.VMEM((3,) + block, BF16),
            pltpu.SemaphoreType.DMA((slots,)), pltpu.SemaphoreType.DMA((slots,))]


def result_shape(name, shape):
    return (2,) + shape[1:] if name[0] == "Q" else shape[1:]


def place_of():
    d, s = lax.axis_index("dp"), lax.axis_index("seq")
    return d // 2, lax.rem(d, 2), s // 2, lax.rem(s, 2)


def greet(place):
    z, y, x, c = place
    peers = [(z, y, x, 1 - c), (z, y, 1 - x, c), (z, 1 - y, x, c)] + [(lax.rem(z + i, 4), y, x, c) for i in range(1, 4)]
    peers.append((z, y, 1 - x, 1 - c))
    barrier = pltpu.get_barrier_semaphore()
    for pz, py, px, pc in peers:
        pl.semaphore_signal(barrier, inc=1, device_id=(pz * 2 + py, px * 2 + pc), device_id_type=pl.DeviceIdType.MESH)
    pl.semaphore_wait(barrier, len(peers))


def piece_shapes(shares, features, hidden):
    share = features // shares
    width, tile = hidden // shares // TILES, hidden // TILES
    halved = (shares, 2, 2, features // 8, width)
    whole = (shares, 2, features // 4, width)
    up = tuple((shares, 2, 2, share, tile // 4) if split else (shares, 2, share, tile // 2) for split in UP_SPLIT)
    pairs = tuple((shares, 2, share // 2, features // 2) if split else (shares, share, features // 2) for split in PAIR_SPLIT)
    out = (shares, 2, share, features // 2)
    return (halved,) * TILES + (whole,) * TILES + up + (out,) + pairs + ((shares, 2, SMALL_ROWS // 2, -(-share // 128) * 128),)


def middle_part(env, out_weight, up, down, mixed, x1, n2, n2_t, dm, dm_t, acc, d_n2, act_all, d_hidden_all, slope_all, load_sem,
                weight_sem):
    total, features = x1.shape
    hidden = env.up.shape[1]
    tile = hidden // TILES
    shares = env.shares
    reach = hidden // shares
    width = reach // TILES
    share = features // shares
    line = lambda ref: ref[...].reshape(1, ref.shape[0])
    blocks = [slice(i, i + SHARED) for i in range(0, total, SHARED)]

    def weight_loads(j):
        made = []
        for d in range(shares):
            first = d * reach + j * width
            k = 2 * (shares * (j % 2) + d)
            made.append(pltpu.make_async_copy(env.up.at[:, pl.ds(first, width)], up.at[j % 2, :, pl.ds(d * width, width)], weight_sem.at[k]))
            made.append(pltpu.make_async_copy(env.down.at[pl.ds(first, width)], down.at[j % 2, pl.ds(d * width, width)], weight_sem.at[k + 1]))
        return made

    first_loads = [pltpu.make_async_copy(env.out_weight, out_weight, load_sem.at[0]), pltpu.make_async_copy(env.x, x1, load_sem.at[1]),
                   pltpu.make_async_copy(env.cot, dm, load_sem.at[2])]
    for g in range(env.mixed.shape[0]):
        first_loads.append(pltpu.make_async_copy(env.mixed.at[g], mixed.at[:, pl.ds(g * 128, 128)], load_sem.at[3 + g]))
    pending = {0: weight_loads(0), 1: weight_loads(1)}
    for made in first_loads + pending[0] + pending[1]:
        made.start()
    env.greet()
    wait_all(first_loads)
    x1[...] = x1[...] + (mm(mixed[...], out_weight[...]) + line(env.out_bias))
    for rows in blocks:
        after = x1[rows]
        xhat, _ = normalize(after)
        n2[rows] = (xhat * line(env.gain2) + line(env.shift2)).astype(BF16)
        dm[rows] = (dm[rows].astype(F32) * env.valid[rows, 0:1]).astype(BF16)
    n2_t[...] = n2[...].T
    dm_t[...] = dm[...].T
    acc[...] = jnp.zeros_like(acc)
    d_n2[...] = jnp.zeros_like(d_n2)
    env.small[7:8, :] = row_sum(dm[...].astype(F32))
    for j in range(TILES):
        up_j, down_j = up.at[j % 2], down.at[j % 2]
        wait_all(pending[j])
        tile_bias = jnp.concatenate([env.up_bias[d * reach + j * width:d * reach + (j + 1) * width].reshape(1, width) for d in range(shares)], 1)
        chunk = tile // CHUNKS
        parts = [slice(i, i + chunk) for i in range(0, tile, chunk)]
        forth = lambda cols: mm(n2[...], up_j[:, cols])
        back = lambda cols: mm(dm[...], down_j[cols], NT)
        ready = forth(parts[0])
        for i, cols in enumerate(parts):
            h = ready + tile_bias[:, cols]
            if i + 1 < len(parts):
                ready = forth(parts[i + 1])
            half, slope = gelu_parts(h)
            act_all[:, cols] = (h * half).astype(BF16)
            slope_all[:, cols] = slope
            env.tick(f"{j}b{i}")
        halved, whole = env.pieces[j], env.pieces[TILES + j]
        high = halved.shape[3]
        for core in range(2):
            rows = slice(core * (features // 2), (core + 1) * (features // 2))
            out = mm(dm_t[rows], act_all[...]).astype(BF16)
            for d in range(shares):
                cols = slice(d * width, (d + 1) * width)
                for half_x in range(2):
                    halved[d, core, half_x] = out[half_x * high:(half_x + 1) * high, cols]
                whole[d, core] = out[2 * high:, cols]
        env.tick(f"d{j}")
        sums = []
        ready = back(parts[0])
        for i, cols in enumerate(parts):
            d_act = ready
            if i + 1 < len(parts):
                ready = back(parts[i + 1])
            d_hidden = (slope_all[:, cols] * d_act).astype(BF16)
            d_hidden_all[:, cols] = d_hidden
            sums.append(row_sum(d_hidden.astype(F32)))
            env.tick(f"{j}e{i}")
        bias_sum = jnp.concatenate(sums, 1)
        for d in range(shares):
            env.up_bias_grad[:, d * reach + j * width:d * reach + (j + 1) * width] = bias_sum[:, d * width:(d + 1) * width]
        out = mm(n2_t[...], d_hidden_all[...]).astype(BF16)
        g_up = env.pieces[2 * TILES + j]
        for d in range(shares):
            rows = slice(d * share, (d + 1) * share)
            for core in range(2):
                first = core * (tile // 2)
                if UP_SPLIT[j]:
                    for half_x in range(2):
                        g_up[d, core, half_x] = out[rows, first + half_x * (tile // 4):first + (half_x + 1) * (tile // 4)]
                else:
                    g_up[d, core] = out[rows, first:first + tile // 2]
        env.tick(f"u{j}")
        acc[...] += mm(act_all[...], down_j[...])
        d_n2[...] += mm(d_hidden_all[...], up_j[...], NT)
        env.tick(f"{j}c")
        if j + 2 < TILES:
            pending[j + 2] = weight_loads(j + 2)
            for made in pending[j + 2]:
                made.start()
    sums = [jnp.zeros((1, features), F32)] * 3
    for rows in blocks:
        after = x1[rows]
        env.out_work[rows] = (env.valid[rows, 0:1] * (after + (acc[rows] + line(env.down_bias)))).astype(BF16)
        xhat, rstd = normalize(after)
        d_norm = d_n2[rows]
        d_x1 = dm[rows].astype(F32) + norm_back(d_norm, line(env.gain2), xhat, rstd)
        env.d_x1[rows] = d_x1
        d_a = d_x1.astype(BF16)
        n2[rows] = d_a
        sums = [a + row_sum(b) for a, b in zip(sums, (d_a.astype(F32), d_norm * xhat, d_norm))]
    d_mixed = mm(n2[...], out_weight[...], NT).astype(BF16)
    for g in range(features // 128):
        env.d_mixed[g] = d_mixed[:, g * 128:(g + 1) * 128]
    env.after_middle()
    out = mm(mixed[...].T, n2[...]).astype(BF16)
    g_out = env.pieces[3 * TILES]
    for d in range(shares):
        for core in range(2):
            g_out[d, core] = out[d * share:(d + 1) * share, core * (features // 2):(core + 1) * (features // 2)]
    for row, value in zip((2, 5, 6), sums):
        env.small[row:row + 1, :] = value
    env.tick("e")


def attention_part(env, matrix, own, shared_q, shared_kv, own_mixed, shared_mixed, own_d, shared_dq, shared_dkv, joined, normed, normed_t, pair_d, x_in,
                   d_work, d_mirror, weight_sem):
    s, x, c = env.s, env.x_at, env.c
    other = 1 - c
    total, features = x_in.shape
    groups = own.shape[1]
    partner, across = 2 * x + other, 2 * (1 - x) + c
    mine = pl.ds(groups * c, groups)
    own_rows = span(OWN * c, OWN)
    sender = env.sender
    loads = [pltpu.make_async_copy(a, b, weight_sem.at[i]) for i, (a, b) in enumerate((
        (env.shared_q, shared_q), (env.shared_kv, shared_kv), (env.shared_mixed, shared_mixed), (env.own, own), (env.own_mixed, own_mixed), (env.weight, matrix), (env.x, x_in)))]
    at = 0
    for rows in (slice(0, OWN), slice(OWN, WORK), slice(WORK, TALL)):
        for core in range(2):
            count = rows.stop - rows.start
            loads.append(pltpu.make_async_copy(env.normed.at[core, rows], normed.at[pl.ds(at, count)], weight_sem.at[len(loads)]))
            at += count
    for load in loads:
        load.start()
    key_spot = lax.broadcasted_iota(jnp.int32, (KEYS, 1), 0)
    shared_dm_copies, own_dm_copies = env.exchange_copies()
    wait_all(shared_dm_copies + loads[0:3])
    for p in range(groups):
        attend_back(p, shared_q, shared_kv.at[0], shared_kv.at[1], env.shared_dm, shared_mixed, env.shared_log, shared_slots(key_spot) < env.lengths[2],
                    shared_dq, shared_dkv.at[0], shared_dkv.at[1], env.head_dim, 256, lambda i: env.tick(f"s{p}{i}"))
    shared_copies = []
    for to, peer in ((other, partner), (c, None)):
        ends = [(shared_dq.at[:, span(SHARED * to, SHARED)], env.joined_lanes.at[0, mine, OWN:WORK])]
        for chip, rows in ((x, slice(OWN, WORK)), (1 - x, slice(WORK, TALL))):
            ends.append((shared_dkv.at[:, :, span(OWN * chip + SHARED * to, SHARED)], env.joined_lanes.at[1:3, mine, rows]))
        shared_copies += [sender.near(*pair) if peer is None else sender.far(*pair, peer) for pair in ends]
    wait_all(own_dm_copies + loads[3:5] + loads[7:])
    normed_t[...] = normed[...].T
    share = features // env.shares
    pair_d[KEYS + OWN:, 0:128] = jnp.zeros((OWN, 128), BF16)
    for p in range(groups):
        attend_back(p, own.at[0], own.at[1], own.at[2], env.own_dm, own_mixed, env.own_log,
                    own_slots(key_spot) < jnp.where(x == 0, env.lengths[0], env.lengths[1]),
                    own_d.at[0], own_d.at[1], own_d.at[2], env.head_dim, 256, lambda i: env.tick(f"o{p}{i}"))
        here, there = span(OWN * x, OWN), span(OWN * (1 - x), OWN)
        pair_d[KEYS:KEYS + OWN, 0:128] = shared_dq[p]
        for part in range(3):
            cols = slice(part * 128, (part + 1) * 128)
            pair_d[0:KEYS, cols] = own_d[part, p]
            if part:
                pair_d[KEYS:KEYS + OWN, cols] = shared_dkv[part - 1, p, here]
                pair_d[KEYS + OWN:, cols] = shared_dkv[part - 1, p, there]
        out = mm(normed_t[...], pair_d[...]).astype(BF16)
        piece = env.pieces[3 * TILES + 1 + p]
        for d in range(env.shares):
            if PAIR_SPLIT[p]:
                for half_x in range(2):
                    first = (2 * d + half_x) * (share // 2)
                    piece[d, half_x] = out[first:first + share // 2]
            else:
                piece[d] = out[d * share:(d + 1) * share]
        env.tick(f"q{p}")
    own_copies = [
        sender.far(own_d.at[:, :, span(OWN * other, OWN)], env.joined_lanes.at[:, mine, 0:OWN], partner),
        sender.near(own_d.at[:, :, own_rows], env.joined_lanes.at[:, mine, 0:OWN]),
    ]
    wait_all(loads[5:7])
    wait_all(own_copies + shared_copies)
    blocks = [slice(i, i + SHARED) for i in range(0, total, SHARED)]
    joined[WORK:TALL, 0:features] = jnp.zeros((SHARED, features), BF16)
    for part in range(3):
        height = TALL if part else WORK
        for g in range(2 * groups):
            at = (part * 2 * groups + g) * 128
            joined[0:height, at:at + 128] = env.joined_lanes[part, g, 0:height]
    d_mirror[...] = mm(joined[WORK:TALL, features:], matrix[:, features:], NT).astype(BF16)
    mirror_copy = sender.far(d_mirror, env.other_mirror, across)
    env.tick("m")
    packed = env.pieces[-1]
    sums = [jnp.zeros((1, features), F32)] * 4
    tables = jnp.zeros((TABLE_ROWS, 2 * features), F32)
    d_norms = mm(joined[0:WORK], matrix[...], NT)
    env.tick("n")
    for i, rows in enumerate(blocks):
        d_norm = d_norms[rows]
        if rows.start == OWN:
            mirror_copy.wait()
            d_norm = d_norm + env.other_mirror[...].astype(F32)
        xhat, rstd = normalize(x_in[rows])
        terms = (joined[rows, 0:features].astype(F32), joined[rows, 2 * features:].astype(F32), d_norm * xhat, d_norm)
        sums = [a + row_sum(b) for a, b in zip(sums, terms)]
        d_x = env.d_x1[rows] + norm_back(d_norm, env.gain1[...].reshape(1, features), xhat, rstd)
        high, low = split_high_low(d_x)
        d_work[rows] = high
        tables = tables + mm(one_hot(env.ids[0:1, rows], env.ids[1:2, rows]), jnp.concatenate([high, low], 1))
        if i < 2:
            env.tick(f"f{i}")
    d_mover = Mover(s, env.d_patches, d_work, env.d_send, env.d_recv, True)
    sums[1] = sums[1] + row_sum(joined[WORK:TALL, 2 * features:].astype(F32))
    d_mover.start(MOVES)
    small = env.small
    small[16:16 + TABLE_ROWS, :] = tables[:, 0:features] + tables[:, features:]
    for row, value in zip((0, 1, 3, 4), sums):
        small[row:row + 1, :] = value
    repeat = env.up_bias_grad.shape[1] // features
    height = packed.shape[2]
    if share != packed.shape[3]:
        packed[...] = jnp.zeros_like(packed)
    for d in range(env.shares):
        for r in range(repeat):
            first = (d * repeat + r) * share
            small[8 + r:9 + r, d * share:(d + 1) * share] = env.up_bias_grad[:, first:first + share]
        for core in range(2):
            packed[d, core, :, 0:share] = small[core * height:(core + 1) * height, d * share:(d + 1) * share].astype(BF16)
    env.tick("f2")
    env.tick("tail")
    for mover in (env.out_mover, d_mover):
        mover.wait(MOVES)
        mover.drain(MOVES)


class Env:
    pass


BACK_INPUTS = ("lengths", "valid", "x", "mixed", "cot", "out_weight", "out_bias", "gain2", "shift2", "up", "up_bias", "down", "down_bias",
               "own", "shared_q", "shared_kv", "own_mixed", "shared_mixed", "own_log", "shared_log", "weight", "normed", "ids", "gain1")
IN_VMEM = ("valid", "out_bias", "gain2", "shift2", "up_bias", "down_bias", "own_log", "shared_log", "ids", "gain1")
BACK_SCRATCH = ("d_mixed", "own_dm", "shared_dm", "other_mirror", "joined_lanes", "d_x1", "out_work", "small", "up_bias_grad", "zeros",
                "out_send", "out_recv", "d_send", "d_recv", "send", "recv", "dm_send", "dm_recv", "zero_sem")


def backward_body(head_dim, shares, custom, features, hidden, *refs):
    env = Env()
    refs = list(refs)
    take = lambda count: [refs.pop(0) for _ in range(count)]
    for name, ref in zip(BACK_INPUTS, take(len(BACK_INPUTS))):
        setattr(env, name, ref)
    count = len(FLOW_NAMES)
    env.output, env.d_patches = take(2)
    outs = take(count)
    for name, ref in zip(BACK_SCRATCH, take(len(BACK_SCRATCH))):
        setattr(env, name, ref)
    env.head_dim, env.shares = head_dim, shares
    env.s, env.x_at, env.c = seq_place()
    flows = {}
    if custom:
        place = place_of()
        env.pieces = take(count)
        for i, name in enumerate(FLOW_NAMES):
            flows[name] = Flow(env.pieces[i], outs[i], take(FLOW_REFS), place, name[0] == "Q")
        env.greet = lambda: greet(place)
    else:
        env.pieces = outs
        env.greet = lambda: greet_group(env.s)

    def tick(point):
        for name in SCHEDULE.get(point, ()):
            if name == "R":
                env.out_mover.start(MOVES)
            elif custom:
                flows[name].advance()

    env.tick = tick
    env.sender = Sender(env.send, env.recv)
    env.out_mover = Mover(env.s, env.output, env.out_work, env.out_send, env.out_recv, True)
    env.zeros[...] = jnp.zeros_like(env.zeros)
    env.small[...] = jnp.zeros_like(env.small)

    def fill(act):
        @pl.when(env.s == UNUSED[0])
        def _():
            for i, array in enumerate((env.output, env.d_patches)):
                for clip in range(3):
                    act(pltpu.make_async_copy(env.zeros, array.at[clip, pl.ds(UNUSED[1], ROWS - UNUSED[1])], env.zero_sem.at[3 * i + clip]))

    fill(lambda made: made.start())

    groups = features // 256

    def exchange_copies():
        other = 1 - env.c
        partner = 2 * env.x_at + other
        mine, theirs = pl.ds(groups * env.c, groups), pl.ds(groups * other, groups)
        places = ((env.shared_dm.at[:, span(SHARED * env.c, SHARED)], slice(OWN, WORK)), (env.own_dm.at[:, span(OWN * env.c, OWN)], slice(0, OWN)))
        sender = Sender(env.dm_send, env.dm_recv)
        return [[sender.far(env.d_mixed.at[theirs, rows], place, partner, False), sender.near(env.d_mixed.at[mine, rows], place, False)]
                for place, rows in places]

    def after_middle():
        for made in sum(exchange_copies(), []):
            made.start()

    env.exchange_copies = exchange_copies
    env.after_middle = after_middle
    tile = hidden // TILES
    dma = pltpu.SemaphoreType.DMA
    wide, tall = lambda kind: pltpu.VMEM((WORK, features), kind), pltpu.VMEM((features, WORK), BF16)
    lanes = lambda *lead: pltpu.VMEM(lead + (128,), BF16)
    pl.run_scoped(
        functools.partial(middle_part, env), pltpu.VMEM((features, features), BF16), pltpu.VMEM((2, features, tile), BF16),
        pltpu.VMEM((2, tile, features), BF16), wide(BF16), wide(F32), wide(BF16), tall, wide(BF16), tall, wide(F32), wide(F32),
        pltpu.VMEM((WORK, tile), BF16), pltpu.VMEM((WORK, tile), BF16), pltpu.VMEM((WORK, tile), F32), dma((3 + 2 * groups,)), dma((4 * shares,)))
    pl.run_scoped(
        functools.partial(attention_part, env), pltpu.VMEM((features, 3 * features), BF16), lanes(3, groups, KEYS), lanes(groups, OWN),
        lanes(2, groups, KEYS), lanes(groups, KEYS), lanes(groups, OWN), lanes(3, groups, KEYS), lanes(groups, OWN), lanes(2, groups, KEYS),
        pltpu.VMEM((TALL, 3 * features), BF16), pltpu.VMEM((2 * KEYS, features), BF16), pltpu.VMEM((features, 2 * KEYS), BF16),
        pltpu.VMEM((2 * KEYS, 384), BF16), wide(F32), wide(BF16), pltpu.VMEM((SHARED, features), BF16), dma((13,)))
    fill(lambda made: made.wait())
    assert all(flow.done == len(flow.stages) for flow in flows.values())


def backward(inputs, head_dim, shares, custom):
    features, hidden = inputs["up"].shape
    groups = features // 256
    anywhere, vmem = pl.BlockSpec(memory_space=pl.ANY), pl.BlockSpec(memory_space=pltpu.VMEM)
    dma = pltpu.SemaphoreType.DMA
    lanes = lambda *lead: pltpu.VMEM(lead + (128,), BF16)
    moves = len(MOVES)
    shapes = piece_shapes(shares, features, hidden)
    specs = [vmem if name in IN_VMEM else anywhere for name in BACK_INPUTS]
    specs[0] = pl.BlockSpec(memory_space=pltpu.SMEM)
    scratch = [
        lanes(2 * groups, WORK), lanes(groups, KEYS), lanes(groups, OWN), pltpu.VMEM((SHARED, features), BF16), lanes(3, 2 * groups, TALL),
        pltpu.VMEM((WORK, features), F32), pltpu.VMEM((WORK, features), BF16), pltpu.VMEM((SMALL_ROWS, features), F32),
        pltpu.VMEM((1, hidden), F32), pltpu.VMEM((ROWS - UNUSED[1], features), BF16),
        dma((moves,)), dma((moves,)), dma((moves,)), dma((moves,)), dma((24,)), dma((24,)), dma((4,)), dma((4,)), dma((6,)),
    ]
    if custom:
        scratch += [pltpu.VMEM(shape, BF16) for shape in shapes]
        scratch += [ref for name, shape in zip(FLOW_NAMES, shapes) for ref in flow_scratch(name, shape)]
    rows = jax.ShapeDtypeStruct((3, ROWS, features), BF16)
    return pl.pallas_call(
        functools.partial(backward_body, head_dim, shares, custom, features, hidden),
        in_specs=specs,
        out_specs=[anywhere] * 2 + [vmem] * len(shapes),
        out_shape=[rows, rows] + [jax.ShapeDtypeStruct(result_shape(name, shape) if custom else shape, BF16) for name, shape in zip(FLOW_NAMES, shapes)],
        scratch_shapes=scratch,
        compiler_params=pltpu.CompilerParams(collective_id=0, has_side_effects=True, vmem_limit_bytes=63 * MIB),
    )(*(inputs[name] for name in BACK_INPUTS))


def assemble_body(time_count, freq_count, *refs):
    count = len(FLOW_NAMES)
    pieces = refs[0:count]
    outs = refs[count:]
    halved, whole, up = pieces[0:TILES], pieces[TILES:2 * TILES], pieces[2 * TILES:3 * TILES]
    out, *pairs, packed = pieces[3 * TILES:]
    (qkv_out, qb, vb, out_out, ob, n1g, n1s, n2g, n2s, up_out, up_b, down_out, db, time_out, freq_out) = outs
    third = qkv_out.shape[1] // 3
    for core in range(2):
        for p, pair in enumerate(pairs):
            for part in range(3):
                first = part * third + core * (third // 2) + p * 128
                cols = slice(part * 128, (part + 1) * 128)
                if PAIR_SPLIT[p]:
                    high = pair.shape[2]
                    for half_x in range(2):
                        qkv_out[half_x * high:(half_x + 1) * high, first:first + 128] = pair[core, half_x, :, cols].astype(F32)
                else:
                    qkv_out[:, first:first + 128] = pair[core, :, cols].astype(F32)
        cols = out.shape[2]
        out_out[:, core * cols:(core + 1) * cols] = out[core].astype(F32)
    width = whole[0].shape[2]
    half = down_out.shape[1] // 2
    for j in range(TILES):
        for core in range(2):
            grad = jnp.concatenate([halved[j][core, 0], halved[j][core, 1], whole[j][core]], 0)
            down_out[j * width:(j + 1) * width, core * half:(core + 1) * half] = grad.astype(F32).T
            if UP_SPLIT[j]:
                grad = jnp.concatenate([up[j][core, 0], up[j][core, 1]], 1)
            else:
                grad = up[j][core]
            blocks = grad.shape[1] // width
            for k in range(blocks):
                first = ((core * blocks + k) * TILES + j) * width
                up_out[:, first:first + width] = grad[:, k * width:(k + 1) * width].astype(F32)
    small = jnp.concatenate([packed[0], packed[1]], 0).astype(F32)
    share = qb.shape[0]
    for row, ref in ((0, qb), (1, vb), (2, ob), (3, n1g), (4, n1s), (5, n2g), (6, n2s), (7, db)):
        ref[...] = small[row, 0:share]
    for r in range(up_b.shape[0] // share):
        up_b[r * share:(r + 1) * share] = small[8 + r, 0:share]
    time_out[...] = small[16:16 + TABLE_ROWS].T[0:share, 0:time_count]
    freq_out[...] = small[16 + FREQ_ROW:16 + FREQ_ROW + freq_count, 0:share]


def assemble(pieces, features, hidden, shares, time_count, freq_count):
    share = features // shares
    line = (share,)
    shapes = [(share, 3 * features), line, line, (share, features), line, line, line, line, line, (share, hidden), (hidden // shares,),
              (hidden // shares, features), line, (share, time_count), (freq_count, share)]
    return pl.pallas_call(
        functools.partial(assemble_body, time_count, freq_count),
        out_shape=[jax.ShapeDtypeStruct(shape, F32) for shape in shapes],
        compiler_params=params(),
    )(*pieces)


def reduce_native(pieces, time_count, freq_count):
    def total(part, axis):
        return lax.psum(lax.psum_scatter(part, "dp", scatter_dimension=axis, tiled=True), "seq").astype(F32)

    pieces = [p[0] for p in pieces]
    down = jnp.concatenate([jnp.concatenate([part for c in range(2) for part in (a[c, 0], a[c, 1], b[c])], 0)
                            for a, b in zip(pieces[0:TILES], pieces[TILES:2 * TILES])], 1)
    ups = []
    for piece, split in zip(pieces[2 * TILES:3 * TILES], UP_SPLIT):
        ups += [part for c in range(2) for part in ((piece[c, 0], piece[c, 1]) if split else (piece[c],))]
    up = jnp.concatenate(ups, 1)
    out, *pairs, packed = pieces[3 * TILES:]
    here = lax.rem(lax.axis_index("seq"), 2)
    pairs = [jnp.concatenate([p[0], p[1]], 0) if split else p for p, split in zip(pairs, PAIR_SPLIT)]
    qkv = jnp.concatenate([jnp.where(here == core, p[:, part * 128:(part + 1) * 128], BF16(0))
                           for part in range(3) for core in range(2) for p in pairs], 1)
    small = packed.reshape(SMALL_ROWS, -1)
    repeat = up.shape[1] // small.shape[1]
    up_bias = total(small[8:8 + repeat].reshape(-1), 0)
    small = total(small, 1)
    return (
        total(qkv, 0), small[0], small[1], total(jnp.concatenate([out[0], out[1]], 1), 0), small[2], small[3], small[4], small[5], small[6],
        total(up, 0), up_bias, total(down, 1).T, small[7], small[16:16 + time_count], small[16 + FREQ_ROW:16 + FREQ_ROW + freq_count],
    )


def shards(
    patches,
    cotangent,
    time_ids,
    freq_ids,
    lengths,
    qkv_weight,
    query_bias,
    value_bias,
    out_weight,
    out_bias,
    norm1_gain,
    norm1_shift,
    norm2_gain,
    norm2_shift,
    up_weight,
    up_bias,
    down_weight,
    down_bias,
    time_table,
    freq_table,
):
    features = patches.shape[2]
    head_dim = features // HEADS
    assert patches.shape[:2] == (3, ROWS) and lax.axis_size("seq") == 4
    custom = lax.axis_size("dp") == 8
    shares = 8 if custom else 1
    x, normed, own, shared_q, shared_kv, own_log, own_mixed, shared_log, shared_mixed, mixed, cot, ids, valid = forward(
        lengths, patches, cotangent, time_ids, freq_ids, time_table, freq_table, norm1_gain, norm1_shift, qkv_weight, query_bias, value_bias,
        head_dim
    )
    inputs = dict(
        lengths=lengths, valid=valid, x=x, mixed=mixed, cot=cot, out_weight=out_weight, out_bias=out_bias, gain2=norm2_gain,
        shift2=norm2_shift, up=up_weight, up_bias=up_bias, down=down_weight, down_bias=down_bias, own=own, shared_q=shared_q,
        shared_kv=shared_kv, own_mixed=own_mixed, shared_mixed=shared_mixed, own_log=own_log, shared_log=shared_log, weight=qkv_weight, normed=normed, ids=ids, gain1=norm1_gain)
    output, d_patch, *pieces = backward(inputs, head_dim, shares, custom)
    counts = time_table.shape[0], freq_table.shape[0]
    if custom:
        *rest, time_grad, freq_grad = assemble(pieces, features, up_weight.shape[1], shares, *counts)
        return (output, d_patch, *rest, time_grad.T, freq_grad)
    return (output, d_patch) + reduce_native(pieces, *counts)


def solution(mesh):
    clip_spec, row_spec, one = P("dp", "seq", None), P("dp", "seq"), P("dp")
    matrix = P("dp", None)
    return jax.shard_map(
        shards,
        mesh=mesh,
        in_specs=(clip_spec, clip_spec, row_spec, row_spec, one) + (P(),) * 15,
        out_specs=(clip_spec, clip_spec, matrix, one, one, matrix, one, one, one, one, one, matrix, one, matrix, one, P(None, "dp"), P(None, "dp")),
        check_vma=False,
    )
```

```python
import functools
import math

import jax
import jax.numpy as jnp
from jax import lax
from jax.experimental import pallas as pl
from jax.experimental.pallas import tpu as pltpu
from jax.sharding import PartitionSpec as P

HEADS = 12
EPS = 1e-06
NEGATIVE = -1000000000.0
FREQ_ROW = 104
TABLE_ROWS = 128
SMALL_ROWS = 32 + TABLE_ROWS
TILES = 3
CHUNKS = 2
UP_SPLIT = (False, True, False)
PAIR_SPLIT = (True, True, False)
F32 = jnp.float32
BF16 = jnp.bfloat16
NN = (((1,), (0,)), ((), ()))
NT = (((1,), (1,)), ((), ()))
TN = (((0,), (0,)), ((), ()))
MIB = 1 << 20


def mm(left, right, dims=NN):
    return lax.dot_general(left, right, dims, preferred_element_type=F32)


def params(limit=60):
    return pltpu.CompilerParams(vmem_limit_bytes=limit * MIB)


def row_sum(values):
    return jnp.sum(values, 0, keepdims=True)


def normalize(values):
    center = values - jnp.mean(values, -1, keepdims=True)
    rstd = lax.rsqrt(jnp.mean(center * center, -1, keepdims=True) + EPS)
    return center * rstd, rstd


def norm_back(d_out, gain, xhat, rstd):
    u = d_out * gain
    inner = jnp.mean(u * xhat, -1, keepdims=True)
    return rstd * (u - jnp.mean(u, -1, keepdims=True) - xhat * inner)


def gelu_parts(h):
    half = 0.5 * (1.0 + lax.erf(h * (1.0 / math.sqrt(2.0))))
    return half, half + h * jnp.exp(h * h * -0.5) * (1.0 / math.sqrt(2.0 * math.pi))


def split_high_low(values):
    high = values.astype(BF16)
    return high, (values - high.astype(F32)).astype(BF16)


def one_hot(time_row, freq_row):
    spot = lax.broadcasted_iota(jnp.int32, (TABLE_ROWS, time_row.shape[1]), 0)
    hit = (spot == time_row) | (spot == freq_row + FREQ_ROW)
    return jnp.where(hit, 1.0, 0.0).astype(BF16)


ROWS = 224
OWN = 352
SHARED = 176
WORK = OWN + SHARED
KEYS = 2 * OWN
TALL = WORK + SHARED
SHARED_MOVES = (
    (0, 2, 176, 48, 3, 384), (1, 2, 176, 48, 3, 432), (2, 2, 176, 48, 3, 480), (3, 2, 0, 32, 3, 352),
    (0, 2, 0, 176, 0, 352), (1, 2, 0, 176, 1, 352), (2, 2, 0, 176, 2, 352),
)
OWN_MOVES = (
    (2, 0, 0, 128, 0, 224), (2, 0, 128, 96, 1, 224), (3, 0, 0, 32, 1, 320), (0, 1, 0, 224, 2, 0), (1, 1, 0, 224, 3, 0),
    (2, 1, 128, 96, 3, 224), (2, 1, 0, 128, 2, 224), (3, 1, 0, 32, 3, 320), (0, 0, 0, 224, 0, 0), (1, 0, 0, 224, 1, 0),
)
MIRROR_MOVES = (
    (0, 2, 0, 176, 2, 528), (1, 2, 0, 176, 3, 528), (2, 2, 0, 176, 0, 528), (0, 2, 176, 48, 1, 560), (2, 2, 176, 48, 1, 656),
    (1, 2, 176, 48, 1, 608), (3, 2, 0, 32, 1, 528),
)
MOVES = SHARED_MOVES + OWN_MOVES
ALL_MOVES = MOVES + MIRROR_MOVES
UNUSED = (3, 32)


def seq_place():
    s = lax.axis_index("seq")
    return s, s // 2, lax.rem(s, 2)


def seq_peer(s):
    return {"seq": s}


def greet_group(s):
    barrier = pltpu.get_barrier_semaphore()
    for ahead in range(1, 4):
        pl.semaphore_signal(barrier, inc=1, device_id=seq_peer(lax.rem(s + ahead, 4)), device_id_type=pl.DeviceIdType.MESH)
    pl.semaphore_wait(barrier, 3)


class Mover:
    def __init__(self, s, at_home, at_work, send, recv, back=False):
        self.s, self.at_home, self.at_work, self.send, self.recv, self.back = s, at_home, at_work, send, recv, back

    def ends(self, move):
        home, clip, first, count, work, spot = move
        a, b = self.at_home.at[clip, pl.ds(first, count)], self.at_work.at[pl.ds(spot, count)]
        return (work, b, home, a) if self.back else (home, a, work, b)

    def each(self, moves, which, act, near=True):
        for device in range(4):
            chosen = [m for m in moves if self.ends(m)[which] == device and (near or self.ends(m)[0] != self.ends(m)[2])]
            if not chosen:
                continue

            @pl.when(self.s == device)
            def _(chosen=chosen):
                for m in chosen:
                    src_device, src, dst_device, dst = self.ends(m)
                    slot = ALL_MOVES.index(m)
                    if src_device == dst_device:
                        act(False, pltpu.make_async_copy(src, dst, self.recv.at[slot]))
                    else:
                        act(True, pltpu.make_async_remote_copy(
                            src_ref=src, dst_ref=dst, send_sem=self.send.at[slot], recv_sem=self.recv.at[slot],
                            device_id=seq_peer(dst_device), device_id_type=pl.DeviceIdType.MESH))

    def start(self, moves):
        self.each(moves, 0, lambda far, made: made.start())

    def wait(self, moves):
        self.each(moves, 2, lambda far, made: made.wait_recv() if far else made.wait())

    def drain(self, moves):
        self.each(moves, 0, lambda far, made: made.wait_send(), False)


class Sender:
    def __init__(self, send, recv):
        self.send, self.recv, self.used = send, recv, 0

    def far(self, source, target, peer, begin=True):
        made = pltpu.make_async_remote_copy(
            src_ref=source, dst_ref=target, send_sem=self.send.at[self.used], recv_sem=self.recv.at[self.used],
            device_id=seq_peer(peer), device_id_type=pl.DeviceIdType.MESH)
        self.used += 1
        if begin:
            made.start()
        return made

    def near(self, source, target, begin=True):
        made = pltpu.make_async_copy(source, target, self.recv.at[self.used])
        self.used += 1
        if begin:
            made.start()
        return made


def wait_all(copies):
    for made in copies:
        made.wait()


def shift_between(spot, cuts):
    slot = spot
    for low, high, shift in cuts:
        slot = jnp.where((spot >= low) & (spot < high), spot + shift, slot)
    return slot


def own_slots(spot):
    return shift_between(spot, ((224, 352, 224), (352, 576, -128)))


def shared_slots(spot):
    return shift_between(spot, ((176, 352, 48), (352, 528, 96), (528, 560, 144), (560, 608, -384), (608, 656, -208), (656, 704, -32)))


def span(first, size):
    return pl.ds(pl.multiple_of(first, 16), size)


def lane_parts(value):
    high, rest = split_high_low(value)
    low = (value - high.astype(F32) - rest.astype(F32)).astype(BF16)
    return high, rest, low


def with_lanes(base, lane, first, columns):
    for i, column in enumerate(columns):
        base = jnp.where(lane == first + i, column, base)
    return base


def attend(query, keys, values, key_ok, mixed_out, log_out, head_dim):
    count = query.shape[1]
    lane = lax.broadcasted_iota(jnp.int32, (1, 128), 1)
    head = lane // head_dim
    scale = BF16(1.0 / math.sqrt(head_dim))
    key_bias = jnp.where(key_ok, 0.0, NEGATIVE).astype(BF16)
    per_pair = 128 // head_dim
    units = [(first, h) for first in range(0, count, OWN) for h in range(per_pair)]
    log_out[...] = jnp.zeros_like(log_out)

    def pair(p, _):
        k, v = keys[p], values[p]
        biased = [with_lanes(k, lane, free_lane(h, head_dim), (key_bias,)) for h in range(per_pair)]
        counted = [with_lanes(v, lane, free_lane(h, head_dim), (BF16(1),)) for h in range(per_pair)]

        def score(unit):
            first, h = unit
            q = jnp.where(head == h, query[p, first:first + OWN] * scale, BF16(0))
            return mm(with_lanes(q, lane, free_lane(h, head_dim), (BF16(1),)), biased[h], NT)

        ready = score(units[0])
        for i, (first, h) in enumerate(units):
            scores = ready
            if i + 1 < len(units):
                ready = score(units[i + 1])
            rows = slice(first, first + OWN)
            highest = jnp.max(scores, -1, keepdims=True)
            powers = jnp.exp(scores - highest)
            out = mm(powers.astype(BF16), counted[h])
            first_free = free_lane(h, head_dim)
            total = out[:, first_free:first_free + 1]
            out = out * (1.0 / total)
            mixed = out if h == 0 else jnp.where(head == h, out, mixed)
            log_out[rows] = jnp.where(lane == per_pair * p + h, highest + jnp.log(total), log_out[rows])
            if h == per_pair - 1:
                mixed_out[p, rows] = mixed.astype(BF16)
        return 0

    lax.fori_loop(0, query.shape[0], pair, 0)


def free_lane(h, head_dim):
    return (h + 1) * head_dim % 128


def forward_body(head_dim, lengths, patches, cot, time_ids, freq_ids, time_table, freq_table, gain, shift, weight, query_bias, value_bias,
                 x_hbm, n_hbm, own_hbm, shared_q_hbm, shared_kv_hbm, own_log_hbm, own_mixed_hbm, shared_log, shared_mixed, mixed_out, cot_out,
                 id_out, valid_out,
                 x_out, n_out, own_out, shared_q_out, shared_kv_out, own_log, own_mixed, work, table_f32, table, ids, matrix, own_stage, shared_stage, mirror_stage,
                 patch_send, patch_recv, cot_send, cot_recv, send, recv, weight_sem):
    s, x, c = seq_place()
    features = x_out.shape[1]
    groups = own_out.shape[1]
    other = 1 - c
    loads = [pltpu.make_async_copy(weight.at[:, pl.ds(p * features, features)], matrix.at[:, pl.ds(p * features, features)], weight_sem.at[p])
             for p in range(3)]
    for load in loads:
        load.start()
    greet_group(s)
    patch_mover = Mover(s, patches, work, patch_send, patch_recv)
    cot_mover = Mover(s, cot, cot_out, cot_send, cot_recv)
    sender = Sender(send, recv)
    id_copies = []
    for i, source in enumerate((time_ids, freq_ids)):
        id_copies.append(sender.near(source, ids.at[s, i]))
        for ahead in range(1, 4):
            id_copies.append(sender.far(source, ids.at[s, i], lax.rem(s + ahead, 4)))
    patch_mover.start(ALL_MOVES)

    table_f32[...] = jnp.zeros_like(table_f32)
    table_f32[0:time_table.shape[0], :] = time_table[...]
    table_f32[FREQ_ROW:FREQ_ROW + freq_table.shape[0], :] = freq_table[...]
    high, low = split_high_low(table_f32[...])
    table[0:TABLE_ROWS, :] = high
    table[TABLE_ROWS:, :] = low
    spot = lax.broadcasted_iota(jnp.int32, (WORK, 1), 0)
    place = jnp.where(spot < OWN, jnp.where(spot < ROWS, spot + ROWS * c, spot + ROWS + 128 * c), shared_slots(spot - OWN + SHARED * s))
    limit = jnp.where(spot < OWN, jnp.where(x == 0, lengths[0], lengths[1]), lengths[2])
    valid_out[...] = jnp.broadcast_to(jnp.where(place < limit, 1.0, 0.0), valid_out.shape)
    id_out[...] = jnp.zeros_like(id_out)
    wait_all(id_copies)
    for device in range(4):
        @pl.when(s == device)
        def _(device=device):
            for home, clip, first, count, target, at in ALL_MOVES:
                if target == device:
                    for i in range(2):
                        id_out[i:i + 1, at:at + count] = ids[home, i, clip:clip + 1, first:first + count]

    bias = (query_bias[...].reshape(1, features), None, value_bias[...].reshape(1, features))

    def project(first, count, stage, own=True):
        rows = slice(first, first + count)
        hot = one_hot(id_out[0:1, rows], id_out[1:2, rows])
        value = work[rows].astype(F32) + mm(jnp.concatenate([hot, hot], 0), table[...], TN)
        if own:
            x_out[rows] = value
        xhat, _ = normalize(value)
        normed = (xhat * gain[...].reshape(1, features) + shift[...].reshape(1, features)).astype(BF16)
        n_out[c, rows] = normed
        for part in range(0 if own else 1, 3):
            out = mm(normed, matrix[:, part * features:(part + 1) * features])
            if bias[part] is not None:
                out = out + bias[part]
            out = out.astype(BF16)
            for g in range(2 * groups):
                stage[part if own else part - 1, g] = out[:, g * 128:(g + 1) * 128]

    patch_mover.wait(SHARED_MOVES)
    wait_all(loads)
    project(OWN, SHARED, shared_stage)
    q_rows, kv_rows = span(SHARED * c, SHARED), span(SHARED * s, SHARED)
    mine, theirs = pl.ds(groups * c, groups), pl.ds(groups * other, groups)
    mirror_rows = span(SHARED * (2 * (1 - x) + c), SHARED)
    partner = 2 * x + other
    shared_copies = [
        sender.far(shared_stage.at[0, theirs], shared_q_out.at[:, q_rows], partner),
        sender.far(shared_stage.at[1:3, theirs], shared_kv_out.at[:, :, kv_rows], partner),
        sender.near(shared_stage.at[0, mine], shared_q_out.at[:, q_rows]),
        sender.near(shared_stage.at[1:3, mine], shared_kv_out.at[:, :, kv_rows]),
    ]
    patch_mover.wait(OWN_MOVES)
    project(0, OWN, own_stage)
    own_rows = span(OWN * c, OWN)
    saves = [sender.near(x_out, x_hbm)]
    own_copies = [
        sender.far(own_stage.at[:, theirs], own_out.at[:, :, own_rows], partner),
        sender.near(own_stage.at[:, mine], own_out.at[:, :, own_rows]),
    ]
    cot_mover.start(MOVES)
    patch_mover.wait(MIRROR_MOVES)
    project(WORK, SHARED, mirror_stage, False)
    shared_copies += [
        sender.far(mirror_stage.at[:, theirs], shared_kv_out.at[:, :, mirror_rows], partner),
        sender.near(mirror_stage.at[:, mine], shared_kv_out.at[:, :, mirror_rows]),
    ]
    normed_copy = sender.far(n_out.at[c], n_out.at[c], partner)
    wait_all(own_copies)
    saves.append(sender.near(own_out, own_hbm))
    key_spot = lax.broadcasted_iota(jnp.int32, (KEYS, 1), 0)
    attend(own_out.at[0], own_out.at[1], own_out.at[2], own_slots(key_spot) < jnp.where(x == 0, lengths[0], lengths[1]),
           own_mixed, own_log, head_dim)
    mixed_copies = [
        sender.far(own_mixed.at[:, span(OWN * other, OWN)], mixed_out.at[mine, 0:OWN], partner),
        sender.near(own_mixed.at[:, own_rows], mixed_out.at[mine, 0:OWN]),
    ]
    wait_all(shared_copies + [normed_copy])
    saves += [sender.near(a, b) for a, b in ((n_out, n_hbm), (shared_q_out, shared_q_hbm), (shared_kv_out, shared_kv_hbm),
                                             (own_mixed, own_mixed_hbm), (own_log, own_log_hbm))]
    attend(shared_q_out, shared_kv_out.at[0], shared_kv_out.at[1], shared_slots(key_spot) < lengths[2],
           shared_mixed, shared_log, head_dim)
    mixed_copies += [
        sender.far(shared_mixed.at[:, span(SHARED * other, SHARED)], mixed_out.at[mine, OWN:WORK], partner),
        sender.near(shared_mixed.at[:, q_rows], mixed_out.at[mine, OWN:WORK]),
    ]
    wait_all(mixed_copies + saves)
    cot_mover.wait(MOVES)
    patch_mover.drain(ALL_MOVES)
    cot_mover.drain(MOVES)


def forward(lengths, patches, cot, time_ids, freq_ids, time_table, freq_table, gain, shift, weight, query_bias, value_bias, head_dim):
    features = patches.shape[2]
    groups = features // 256
    anywhere, vmem = pl.BlockSpec(memory_space=pl.ANY), pl.BlockSpec(memory_space=pltpu.VMEM)
    lanes = lambda *lead: jax.ShapeDtypeStruct(lead + (128,), BF16)
    saved = [
        jax.ShapeDtypeStruct((WORK, features), F32),
        jax.ShapeDtypeStruct((2, TALL, features), BF16),
        lanes(3, groups, KEYS),
        lanes(groups, OWN),
        lanes(2, groups, KEYS),
        jax.ShapeDtypeStruct((KEYS, 128), F32),
        lanes(groups, KEYS),
    ]
    dma = pltpu.SemaphoreType.DMA
    return pl.pallas_call(
        functools.partial(forward_body, head_dim),
        in_specs=[pl.BlockSpec(memory_space=pltpu.SMEM)] + [anywhere] * 4 + [vmem] * 4 + [anywhere] + [vmem] * 2,
        out_specs=[anywhere] * 7 + [vmem] * 6,
        out_shape=saved + [
            jax.ShapeDtypeStruct((OWN, 128), F32),
            lanes(groups, OWN),
            lanes(2 * groups, WORK),
            jax.ShapeDtypeStruct((WORK, features), BF16),
            jax.ShapeDtypeStruct((8, TALL), jnp.int32),
            jax.ShapeDtypeStruct((WORK, 128), F32),
        ],
        scratch_shapes=[pltpu.VMEM(a.shape, a.dtype) for a in saved] + [
            pltpu.VMEM((TALL, features), BF16),
            pltpu.VMEM((TABLE_ROWS, features), F32),
            pltpu.VMEM((2 * TABLE_ROWS, features), BF16),
            pltpu.VMEM((4, 2) + time_ids.shape, jnp.int32),
            pltpu.VMEM(weight.shape, BF16),
            pltpu.VMEM((3, 2 * groups, OWN, 128), BF16),
            pltpu.VMEM((3, 2 * groups, SHARED, 128), BF16),
            pltpu.VMEM((2, 2 * groups, SHARED, 128), BF16),
            dma((len(ALL_MOVES),)), dma((len(ALL_MOVES),)), dma((len(MOVES),)), dma((len(MOVES),)), dma((40,)), dma((40,)), dma((3,)),
        ],
        compiler_params=pltpu.CompilerParams(collective_id=1, has_side_effects=True, vmem_limit_bytes=60 * MIB),
    )(lengths, patches, cot, time_ids, freq_ids, time_table, freq_table, gain, shift, weight, query_bias, value_bias)


def attend_back(p, query, keys, values, d_mixed, mixed, logs, key_ok, d_query, d_keys, d_values, head_dim, block, tick):
    count = query.shape[1]
    lane = lax.broadcasted_iota(jnp.int32, (1, 128), 1)
    head = lane // head_dim
    scale = BF16(1.0 / math.sqrt(head_dim))
    key_bias = jnp.where(key_ok, 0.0, NEGATIVE).astype(BF16)
    k, v = keys[p], values[p]
    k_t = (k * scale).T
    per_pair = 128 // head_dim
    one = BF16(1)
    k_wide = [with_lanes(k, lane, free_lane(h, head_dim), (key_bias, one, one, one)) for h in range(per_pair)]
    v_wide = [with_lanes(v, lane, free_lane(h, head_dim), (one, one, one)) for h in range(per_pair)]
    total_k = jnp.zeros((KEYS, 128), F32)
    total_v = jnp.zeros((KEYS, 128), F32)
    units = [(first, min(first + block, count), h) for first in range(0, count, block) for h in range(per_pair)]

    def products(unit):
        first, last, h = unit
        rows = slice(first, last)
        d_m = d_mixed[p, rows]
        q_head = jnp.where(head == h, query[p, rows] * scale, BF16(0))
        m_head = jnp.where(head == h, d_m, BF16(0))
        delta = jnp.sum(m_head.astype(F32) * mixed[p, rows].astype(F32), -1, keepdims=True)
        at = per_pair * p + h
        q_wide = with_lanes(q_head, lane, free_lane(h, head_dim), (one,) + lane_parts(-logs[rows, at:at + 1]))
        m_wide = with_lanes(m_head, lane, free_lane(h, head_dim), lane_parts(-delta))
        return q_head, m_head, mm(k_wide[h], q_wide, NT), mm(v_wide[h], m_wide, NT)

    ready = products(units[0])
    parts = []
    for i, (first, last, h) in enumerate(units):
        q_head, m_head, scores, d_probs = ready
        if i + 1 < len(units):
            ready = products(units[i + 1])
        probs = jnp.exp(scores)
        d_scores = (probs * d_probs).astype(BF16)
        total_v = total_v + mm(probs.astype(BF16), m_head)
        total_k = total_k + mm(d_scores, q_head)
        parts.append(mm(k_t[h * head_dim:(h + 1) * head_dim], d_scores))
        if h == per_pair - 1:
            d_query[p, first:last] = jnp.concatenate(parts, 0).T.astype(BF16)
            parts = []
            tick(first // block)
    d_keys[p] = total_k.astype(BF16)
    d_values[p] = total_v.astype(BF16)


class Flow:
    def __init__(self, source, result, refs, place, single):
        self.source, self.result, self.single = source, result, single
        self.split = len(source.shape) == (4 if single else 5)
        self.got, self.x_got, self.y_got, self.z_got, self.send, self.recv = refs
        self.z, self.y, self.x, self.c = place
        self.open = {}
        if self.split:
            self.stages = [self.begin, self.cores_x, self.x_y, self.y_z, self.z_fill, self.fill_cores, self.end]
        else:
            self.stages = [self.begin, self.cores_y, self.y_z, self.z_x, self.x_cores, self.end]
        if single:
            self.stages = [self.to_x if self.split else self.to_y] + self.stages[2:]
        self.used = 0
        self.done = 0

    def advance(self):
        self.stages[self.done]()
        self.done += 1

    def copy(self, key, ends):
        slot = self.used
        self.used += 1

        def make():
            source, target, (z, y, x, c) = ends()
            return pltpu.make_async_remote_copy(
                src_ref=source, dst_ref=target, send_sem=self.send.at[slot], recv_sem=self.recv.at[slot],
                device_id=(z * 2 + y, x * 2 + c), device_id_type=pl.DeviceIdType.MESH)

        make().start()
        self.open.setdefault(key, []).append(make)

    def wait(self, key):
        for make in self.open.pop(key):
            make().wait()

    def at(self, z, y):
        row = self.row(z * 2 + y)
        return row.at[self.x] if self.split else row

    def row(self, i):
        return self.source.at[i] if self.single else self.source.at[i, self.c]

    def begin(self):
        self.copy("core", lambda: (self.source.at[:, 1 - self.c], self.got, (self.z, self.y, self.x, 1 - self.c)))

    def cores(self):
        self.wait("core")

        def add(i, _):
            self.source[i, self.c] = self.source[i, self.c] + self.got[i]
            return 0

        lax.fori_loop(0, self.got.shape[0], add, 0)

    def cores_x(self):
        self.cores()
        self.to_x()

    def to_x(self):
        part = lambda: self.source.at[:, 1 - self.x] if self.single else self.source.at[:, self.c, 1 - self.x]
        self.copy("x", lambda: (part(), self.x_got, (self.z, self.y, 1 - self.x, self.c)))

    def cores_y(self):
        self.cores()
        self.to_y()

    def to_y(self):
        for z in range(4):
            self.copy("y", lambda z=z: (self.at(z, 1 - self.y), self.y_got.at[z], (self.z, 1 - self.y, self.x, self.c)))

    def x_y(self):
        self.wait("x")

        def add(i, _):
            spot = self.row(i).at[self.x]
            spot[...] = spot[...] + self.x_got[i]
            return 0

        lax.fori_loop(0, self.source.shape[0], add, 0)
        self.to_y()

    def y_z(self):
        self.wait("y")

        def add(z, _):
            spot = self.at(z, self.y)
            spot[...] = spot[...] + self.y_got[z]
            return 0

        lax.fori_loop(0, 4, add, 0)
        for ahead in range(1, 4):
            def ends(ahead=ahead):
                z = lax.rem(self.z + ahead, 4)
                return self.at(z, self.y), self.z_got.at[ahead - 1], (z, self.y, self.x, self.c)

            self.copy("z", ends)

    def z_sum(self):
        self.wait("z")
        total = self.at(self.z, self.y)[...].astype(F32)
        for i in range(3):
            total = total + self.z_got[i].astype(F32)
        return total.astype(BF16)

    def z_fill(self):
        self.result[self.c, self.x] = self.z_sum()
        spot = lambda: self.result.at[self.c, self.x]
        self.copy("fill", lambda: (spot(), spot(), (self.z, self.y, 1 - self.x, self.c)))

    def fill_cores(self):
        self.wait("fill")
        self.to_core()

    def z_x(self):
        spot = self.at(self.z, self.y)
        spot[...] = self.z_sum()
        self.copy("x", lambda: (self.at(self.z, self.y), self.x_got, (self.z, self.y, 1 - self.x, self.c)))

    def x_cores(self):
        self.wait("x")
        self.result[self.c] = self.at(self.z, self.y)[...] + self.x_got[...]
        self.to_core()

    def to_core(self):
        spot = lambda: self.result.at[self.c]
        self.copy("end", lambda: (spot(), spot(), (self.z, self.y, self.x, 1 - self.c)))

    def end(self):
        self.wait("end")


FLOW_REFS = 6
FLOW_NAMES = ("D0", "D1", "D2", "E0", "E1", "E2", "U0", "U1", "U2", "O", "Q0", "Q1", "Q2", "S")
SCHEDULE = {
    "d0": ("E0", "D0",),
    "0c": ("U0", "E0",),
    "1b1": ("D0",),
    "d1": ("D1", "U0",),
    "u1": ("U1", "D1",),
    "2b1": ("U1", "E0",),
    "d2": ("E2", "D2", "D0",),
    "u2": ("D1", "U2", "U0", "E2",),
    "2c": ("D2",),
    "e": ("U2", "R", "E0", "D0",),
    "s10": ("E2", "E1", "O", "U1",),
    "s21": ("D1",),
    "o02": ("O", "U2", "E2",),
    "q0": ("Q0",),
    "q1": ("Q1", "U1", "D2", "E1",),
    "o22": ("D1", "O", "D0", "U2",),
    "q2": ("Q0", "Q2",),
    "m": ("E1", "D2",),
    "f0": ("Q1", "U0", "Q0", "U1",),
    "f1": ("Q2", "E1", "O",),
    "f2": ("U1", "Q1", "D2", "S", "S", "Q2",),
    "tail": ("D0", "Q0", "E1", "D1", "E0", "S", "U0", "O", "Q1", "S", "Q2", "E2", "D2", "Q1", "U2", "D0", "Q0", "E0", "U0", "S", "O", "U1", "S", "Q1", "Q2", "U2", "E1", "D2", "E2", "Q0", "D1",),
}


def flow_scratch(name, shape):
    single = name[0] == "Q"
    shares, tail = shape[0], shape[1 if single else 2:]
    block = tail[-2:]
    first = (shares,) + block if len(tail) == 3 else block
    slots = 16
    return [pltpu.VMEM((8, 128) if single else (shares,) + tail, BF16), pltpu.VMEM(first, BF16), pltpu.VMEM((4,) + block, BF16), pltpu.VMEM((3,) + block, BF16),
            pltpu.SemaphoreType.DMA((slots,)), pltpu.SemaphoreType.DMA((slots,))]


def result_shape(name, shape):
    return (2,) + shape[1:] if name[0] == "Q" else shape[1:]


def place_of():
    d, s = lax.axis_index("dp"), lax.axis_index("seq")
    return d // 2, lax.rem(d, 2), s // 2, lax.rem(s, 2)


def greet(place):
    z, y, x, c = place
    peers = [(z, y, x, 1 - c), (z, y, 1 - x, c), (z, 1 - y, x, c)] + [(lax.rem(z + i, 4), y, x, c) for i in range(1, 4)]
    peers.append((z, y, 1 - x, 1 - c))
    barrier = pltpu.get_barrier_semaphore()
    for pz, py, px, pc in peers:
        pl.semaphore_signal(barrier, inc=1, device_id=(pz * 2 + py, px * 2 + pc), device_id_type=pl.DeviceIdType.MESH)
    pl.semaphore_wait(barrier, len(peers))


def piece_shapes(shares, features, hidden):
    share = features // shares
    width, tile = hidden // shares // TILES, hidden // TILES
    halved = (shares, 2, 2, features // 8, width)
    whole = (shares, 2, features // 4, width)
    up = tuple((shares, 2, 2, share, tile // 4) if split else (shares, 2, share, tile // 2) for split in UP_SPLIT)
    pairs = tuple((shares, 2, share // 2, features // 2) if split else (shares, share, features // 2) for split in PAIR_SPLIT)
    out = (shares, 2, share, features // 2)
    return (halved,) * TILES + (whole,) * TILES + up + (out,) + pairs + ((shares, 2, SMALL_ROWS // 2, -(-share // 128) * 128),)


def middle_part(env, out_weight, up, down, mixed, x1, n2, n2_t, dm, dm_t, acc, d_n2, act_all, d_hidden_all, slope_all, load_sem,
                weight_sem):
    total, features = x1.shape
    hidden = env.up.shape[1]
    tile = hidden // TILES
    shares = env.shares
    reach = hidden // shares
    width = reach // TILES
    share = features // shares
    line = lambda ref: ref[...].reshape(1, ref.shape[0])
    blocks = [slice(i, i + SHARED) for i in range(0, total, SHARED)]

    def weight_loads(j):
        made = []
        for d in range(shares):
            first = d * reach + j * width
            k = 2 * (shares * (j % 2) + d)
            made.append(pltpu.make_async_copy(env.up.at[:, pl.ds(first, width)], up.at[j % 2, :, pl.ds(d * width, width)], weight_sem.at[k]))
            made.append(pltpu.make_async_copy(env.down.at[pl.ds(first, width)], down.at[j % 2, pl.ds(d * width, width)], weight_sem.at[k + 1]))
        return made

    first_loads = [pltpu.make_async_copy(env.out_weight, out_weight, load_sem.at[0]), pltpu.make_async_copy(env.x, x1, load_sem.at[1]),
                   pltpu.make_async_copy(env.cot, dm, load_sem.at[2])]
    for g in range(env.mixed.shape[0]):
        first_loads.append(pltpu.make_async_copy(env.mixed.at[g], mixed.at[:, pl.ds(g * 128, 128)], load_sem.at[3 + g]))
    pending = {0: weight_loads(0), 1: weight_loads(1)}
    for made in first_loads + pending[0] + pending[1]:
        made.start()
    env.greet()
    wait_all(first_loads)
    x1[...] = x1[...] + (mm(mixed[...], out_weight[...]) + line(env.out_bias))
    for rows in blocks:
        after = x1[rows]
        xhat, _ = normalize(after)
        n2[rows] = (xhat * line(env.gain2) + line(env.shift2)).astype(BF16)
        dm[rows] = (dm[rows].astype(F32) * env.valid[rows, 0:1]).astype(BF16)
    n2_t[...] = n2[...].T
    dm_t[...] = dm[...].T
    acc[...] = jnp.zeros_like(acc)
    d_n2[...] = jnp.zeros_like(d_n2)
    env.small[7:8, :] = row_sum(dm[...].astype(F32))
    for j in range(TILES):
        up_j, down_j = up.at[j % 2], down.at[j % 2]
        wait_all(pending[j])
        tile_bias = jnp.concatenate([env.up_bias[d * reach + j * width:d * reach + (j + 1) * width].reshape(1, width) for d in range(shares)], 1)
        chunk = tile // CHUNKS
        parts = [slice(i, i + chunk) for i in range(0, tile, chunk)]
        forth = lambda cols: mm(n2[...], up_j[:, cols])
        back = lambda cols: mm(dm[...], down_j[cols], NT)
        ready = forth(parts[0])
        for i, cols in enumerate(parts):
            h = ready + tile_bias[:, cols]
            if i + 1 < len(parts):
                ready = forth(parts[i + 1])
            half, slope = gelu_parts(h)
            act_all[:, cols] = (h * half).astype(BF16)
            slope_all[:, cols] = slope
            env.tick(f"{j}b{i}")
        halved, whole = env.pieces[j], env.pieces[TILES + j]
        high = halved.shape[3]
        for core in range(2):
            rows = slice(core * (features // 2), (core + 1) * (features // 2))
            out = mm(dm_t[rows], act_all[...]).astype(BF16)
            for d in range(shares):
                cols = slice(d * width, (d + 1) * width)
                for half_x in range(2):
                    halved[d, core, half_x] = out[half_x * high:(half_x + 1) * high, cols]
                whole[d, core] = out[2 * high:, cols]
        env.tick(f"d{j}")
        sums = []
        ready = back(parts[0])
        for i, cols in enumerate(parts):
            d_act = ready
            if i + 1 < len(parts):
                ready = back(parts[i + 1])
            d_hidden = (slope_all[:, cols] * d_act).astype(BF16)
            d_hidden_all[:, cols] = d_hidden
            sums.append(row_sum(d_hidden.astype(F32)))
            env.tick(f"{j}e{i}")
        bias_sum = jnp.concatenate(sums, 1)
        for d in range(shares):
            env.up_bias_grad[:, d * reach + j * width:d * reach + (j + 1) * width] = bias_sum[:, d * width:(d + 1) * width]
        out = mm(n2_t[...], d_hidden_all[...]).astype(BF16)
        g_up = env.pieces[2 * TILES + j]
        for d in range(shares):
            rows = slice(d * share, (d + 1) * share)
            for core in range(2):
                first = core * (tile // 2)
                if UP_SPLIT[j]:
                    for half_x in range(2):
                        g_up[d, core, half_x] = out[rows, first + half_x * (tile // 4):first + (half_x + 1) * (tile // 4)]
                else:
                    g_up[d, core] = out[rows, first:first + tile // 2]
        env.tick(f"u{j}")
        acc[...] += mm(act_all[...], down_j[...])
        d_n2[...] += mm(d_hidden_all[...], up_j[...], NT)
        env.tick(f"{j}c")
        if j + 2 < TILES:
            pending[j + 2] = weight_loads(j + 2)
            for made in pending[j + 2]:
                made.start()
    sums = [jnp.zeros((1, features), F32)] * 3
    for rows in blocks:
        after = x1[rows]
        env.out_work[rows] = (env.valid[rows, 0:1] * (after + (acc[rows] + line(env.down_bias)))).astype(BF16)
        xhat, rstd = normalize(after)
        d_norm = d_n2[rows]
        d_x1 = dm[rows].astype(F32) + norm_back(d_norm, line(env.gain2), xhat, rstd)
        env.d_x1[rows] = d_x1
        d_a = d_x1.astype(BF16)
        n2[rows] = d_a
        sums = [a + row_sum(b) for a, b in zip(sums, (d_a.astype(F32), d_norm * xhat, d_norm))]
    d_mixed = mm(n2[...], out_weight[...], NT).astype(BF16)
    for g in range(features // 128):
        env.d_mixed[g] = d_mixed[:, g * 128:(g + 1) * 128]
    env.after_middle()
    out = mm(mixed[...].T, n2[...]).astype(BF16)
    g_out = env.pieces[3 * TILES]
    for d in range(shares):
        for core in range(2):
            g_out[d, core] = out[d * share:(d + 1) * share, core * (features // 2):(core + 1) * (features // 2)]
    for row, value in zip((2, 5, 6), sums):
        env.small[row:row + 1, :] = value
    env.tick("e")


def attention_part(env, matrix, own, shared_q, shared_kv, own_mixed, shared_mixed, own_d, shared_dq, shared_dkv, joined, normed, normed_t, pair_d, x_in,
                   d_work, d_mirror, weight_sem):
    s, x, c = env.s, env.x_at, env.c
    other = 1 - c
    total, features = x_in.shape
    groups = own.shape[1]
    partner, across = 2 * x + other, 2 * (1 - x) + c
    mine = pl.ds(groups * c, groups)
    own_rows = span(OWN * c, OWN)
    sender = env.sender
    loads = [pltpu.make_async_copy(a, b, weight_sem.at[i]) for i, (a, b) in enumerate((
        (env.shared_q, shared_q), (env.shared_kv, shared_kv), (env.shared_mixed, shared_mixed), (env.own, own), (env.own_mixed, own_mixed), (env.weight, matrix), (env.x, x_in)))]
    at = 0
    for rows in (slice(0, OWN), slice(OWN, WORK), slice(WORK, TALL)):
        for core in range(2):
            count = rows.stop - rows.start
            loads.append(pltpu.make_async_copy(env.normed.at[core, rows], normed.at[pl.ds(at, count)], weight_sem.at[len(loads)]))
            at += count
    for load in loads:
        load.start()
    key_spot = lax.broadcasted_iota(jnp.int32, (KEYS, 1), 0)
    shared_dm_copies, own_dm_copies = env.exchange_copies()
    wait_all(shared_dm_copies + loads[0:3])
    for p in range(groups):
        attend_back(p, shared_q, shared_kv.at[0], shared_kv.at[1], env.shared_dm, shared_mixed, env.shared_log, shared_slots(key_spot) < env.lengths[2],
                    shared_dq, shared_dkv.at[0], shared_dkv.at[1], env.head_dim, 256, lambda i: env.tick(f"s{p}{i}"))
    shared_copies = []
    for to, peer in ((other, partner), (c, None)):
        ends = [(shared_dq.at[:, span(SHARED * to, SHARED)], env.joined_lanes.at[0, mine, OWN:WORK])]
        for chip, rows in ((x, slice(OWN, WORK)), (1 - x, slice(WORK, TALL))):
            ends.append((shared_dkv.at[:, :, span(OWN * chip + SHARED * to, SHARED)], env.joined_lanes.at[1:3, mine, rows]))
        shared_copies += [sender.near(*pair) if peer is None else sender.far(*pair, peer) for pair in ends]
    wait_all(own_dm_copies + loads[3:5] + loads[7:])
    normed_t[...] = normed[...].T
    share = features // env.shares
    pair_d[KEYS + OWN:, 0:128] = jnp.zeros((OWN, 128), BF16)
    for p in range(groups):
        attend_back(p, own.at[0], own.at[1], own.at[2], env.own_dm, own_mixed, env.own_log,
                    own_slots(key_spot) < jnp.where(x == 0, env.lengths[0], env.lengths[1]),
                    own_d.at[0], own_d.at[1], own_d.at[2], env.head_dim, 256, lambda i: env.tick(f"o{p}{i}"))
        here, there = span(OWN * x, OWN), span(OWN * (1 - x), OWN)
        pair_d[KEYS:KEYS + OWN, 0:128] = shared_dq[p]
        for part in range(3):
            cols = slice(part * 128, (part + 1) * 128)
            pair_d[0:KEYS, cols] = own_d[part, p]
            if part:
                pair_d[KEYS:KEYS + OWN, cols] = shared_dkv[part - 1, p, here]
                pair_d[KEYS + OWN:, cols] = shared_dkv[part - 1, p, there]
        out = mm(normed_t[...], pair_d[...]).astype(BF16)
        piece = env.pieces[3 * TILES + 1 + p]
        for d in range(env.shares):
            if PAIR_SPLIT[p]:
                for half_x in range(2):
                    first = (2 * d + half_x) * (share // 2)
                    piece[d, half_x] = out[first:first + share // 2]
            else:
                piece[d] = out[d * share:(d + 1) * share]
        env.tick(f"q{p}")
    own_copies = [
        sender.far(own_d.at[:, :, span(OWN * other, OWN)], env.joined_lanes.at[:, mine, 0:OWN], partner),
        sender.near(own_d.at[:, :, own_rows], env.joined_lanes.at[:, mine, 0:OWN]),
    ]
    wait_all(loads[5:7])
    wait_all(own_copies + shared_copies)
    blocks = [slice(i, i + SHARED) for i in range(0, total, SHARED)]
    joined[WORK:TALL, 0:features] = jnp.zeros((SHARED, features), BF16)
    for part in range(3):
        height = TALL if part else WORK
        for g in range(2 * groups):
            at = (part * 2 * groups + g) * 128
            joined[0:height, at:at + 128] = env.joined_lanes[part, g, 0:height]
    d_mirror[...] = mm(joined[WORK:TALL, features:], matrix[:, features:], NT).astype(BF16)
    mirror_copy = sender.far(d_mirror, env.other_mirror, across)
    env.tick("m")
    packed = env.pieces[-1]
    sums = [jnp.zeros((1, features), F32)] * 4
    tables = jnp.zeros((TABLE_ROWS, 2 * features), F32)
    d_norms = mm(joined[0:WORK], matrix[...], NT)
    env.tick("n")
    for i, rows in enumerate(blocks):
        d_norm = d_norms[rows]
        if rows.start == OWN:
            mirror_copy.wait()
            d_norm = d_norm + env.other_mirror[...].astype(F32)
        xhat, rstd = normalize(x_in[rows])
        terms = (joined[rows, 0:features].astype(F32), joined[rows, 2 * features:].astype(F32), d_norm * xhat, d_norm)
        sums = [a + row_sum(b) for a, b in zip(sums, terms)]
        d_x = env.d_x1[rows] + norm_back(d_norm, env.gain1[...].reshape(1, features), xhat, rstd)
        high, low = split_high_low(d_x)
        d_work[rows] = high
        tables = tables + mm(one_hot(env.ids[0:1, rows], env.ids[1:2, rows]), jnp.concatenate([high, low], 1))
        if i < 2:
            env.tick(f"f{i}")
    d_mover = Mover(s, env.d_patches, d_work, env.d_send, env.d_recv, True)
    sums[1] = sums[1] + row_sum(joined[WORK:TALL, 2 * features:].astype(F32))
    d_mover.start(MOVES)
    small = env.small
    small[16:16 + TABLE_ROWS, :] = tables[:, 0:features] + tables[:, features:]
    for row, value in zip((0, 1, 3, 4), sums):
        small[row:row + 1, :] = value
    repeat = env.up_bias_grad.shape[1] // features
    height = packed.shape[2]
    if share != packed.shape[3]:
        packed[...] = jnp.zeros_like(packed)
    for d in range(env.shares):
        for r in range(repeat):
            first = (d * repeat + r) * share
            small[8 + r:9 + r, d * share:(d + 1) * share] = env.up_bias_grad[:, first:first + share]
        for core in range(2):
            packed[d, core, :, 0:share] = small[core * height:(core + 1) * height, d * share:(d + 1) * share].astype(BF16)
    env.tick("f2")
    env.tick("tail")
    for mover in (env.out_mover, d_mover):
        mover.wait(MOVES)
        mover.drain(MOVES)


class Env:
    pass


BACK_INPUTS = ("lengths", "valid", "x", "mixed", "cot", "out_weight", "out_bias", "gain2", "shift2", "up", "up_bias", "down", "down_bias",
               "own", "shared_q", "shared_kv", "own_mixed", "shared_mixed", "own_log", "shared_log", "weight", "normed", "ids", "gain1")
IN_VMEM = ("valid", "out_bias", "gain2", "shift2", "up_bias", "down_bias", "own_log", "shared_log", "ids", "gain1")
BACK_SCRATCH = ("d_mixed", "own_dm", "shared_dm", "other_mirror", "joined_lanes", "d_x1", "out_work", "small", "up_bias_grad", "zeros",
                "out_send", "out_recv", "d_send", "d_recv", "send", "recv", "dm_send", "dm_recv", "zero_sem")


def backward_body(head_dim, shares, custom, features, hidden, *refs):
    env = Env()
    refs = list(refs)
    take = lambda count: [refs.pop(0) for _ in range(count)]
    for name, ref in zip(BACK_INPUTS, take(len(BACK_INPUTS))):
        setattr(env, name, ref)
    count = len(FLOW_NAMES)
    env.output, env.d_patches = take(2)
    outs = take(count)
    for name, ref in zip(BACK_SCRATCH, take(len(BACK_SCRATCH))):
        setattr(env, name, ref)
    env.head_dim, env.shares = head_dim, shares
    env.s, env.x_at, env.c = seq_place()
    flows = {}
    if custom:
        place = place_of()
        env.pieces = take(count)
        for i, name in enumerate(FLOW_NAMES):
            flows[name] = Flow(env.pieces[i], outs[i], take(FLOW_REFS), place, name[0] == "Q")
        env.greet = lambda: greet(place)
    else:
        env.pieces = outs
        env.greet = lambda: greet_group(env.s)

    def tick(point):
        for name in SCHEDULE.get(point, ()):
            if name == "R":
                env.out_mover.start(MOVES)
            elif custom:
                flows[name].advance()

    env.tick = tick
    env.sender = Sender(env.send, env.recv)
    env.out_mover = Mover(env.s, env.output, env.out_work, env.out_send, env.out_recv, True)
    env.zeros[...] = jnp.zeros_like(env.zeros)
    env.small[...] = jnp.zeros_like(env.small)

    def fill(act):
        @pl.when(env.s == UNUSED[0])
        def _():
            for i, array in enumerate((env.output, env.d_patches)):
                for clip in range(3):
                    act(pltpu.make_async_copy(env.zeros, array.at[clip, pl.ds(UNUSED[1], ROWS - UNUSED[1])], env.zero_sem.at[3 * i + clip]))

    fill(lambda made: made.start())

    groups = features // 256

    def exchange_copies():
        other = 1 - env.c
        partner = 2 * env.x_at + other
        mine, theirs = pl.ds(groups * env.c, groups), pl.ds(groups * other, groups)
        places = ((env.shared_dm.at[:, span(SHARED * env.c, SHARED)], slice(OWN, WORK)), (env.own_dm.at[:, span(OWN * env.c, OWN)], slice(0, OWN)))
        sender = Sender(env.dm_send, env.dm_recv)
        return [[sender.far(env.d_mixed.at[theirs, rows], place, partner, False), sender.near(env.d_mixed.at[mine, rows], place, False)]
                for place, rows in places]

    def after_middle():
        for made in sum(exchange_copies(), []):
            made.start()

    env.exchange_copies = exchange_copies
    env.after_middle = after_middle
    tile = hidden // TILES
    dma = pltpu.SemaphoreType.DMA
    wide, tall = lambda kind: pltpu.VMEM((WORK, features), kind), pltpu.VMEM((features, WORK), BF16)
    lanes = lambda *lead: pltpu.VMEM(lead + (128,), BF16)
    pl.run_scoped(
        functools.partial(middle_part, env), pltpu.VMEM((features, features), BF16), pltpu.VMEM((2, features, tile), BF16),
        pltpu.VMEM((2, tile, features), BF16), wide(BF16), wide(F32), wide(BF16), tall, wide(BF16), tall, wide(F32), wide(F32),
        pltpu.VMEM((WORK, tile), BF16), pltpu.VMEM((WORK, tile), BF16), pltpu.VMEM((WORK, tile), F32), dma((3 + 2 * groups,)), dma((4 * shares,)))
    pl.run_scoped(
        functools.partial(attention_part, env), pltpu.VMEM((features, 3 * features), BF16), lanes(3, groups, KEYS), lanes(groups, OWN),
        lanes(2, groups, KEYS), lanes(groups, KEYS), lanes(groups, OWN), lanes(3, groups, KEYS), lanes(groups, OWN), lanes(2, groups, KEYS),
        pltpu.VMEM((TALL, 3 * features), BF16), pltpu.VMEM((2 * KEYS, features), BF16), pltpu.VMEM((features, 2 * KEYS), BF16),
        pltpu.VMEM((2 * KEYS, 384), BF16), wide(F32), wide(BF16), pltpu.VMEM((SHARED, features), BF16), dma((13,)))
    fill(lambda made: made.wait())
    assert all(flow.done == len(flow.stages) for flow in flows.values())


def backward(inputs, head_dim, shares, custom):
    features, hidden = inputs["up"].shape
    groups = features // 256
    anywhere, vmem = pl.BlockSpec(memory_space=pl.ANY), pl.BlockSpec(memory_space=pltpu.VMEM)
    dma = pltpu.SemaphoreType.DMA
    lanes = lambda *lead: pltpu.VMEM(lead + (128,), BF16)
    moves = len(MOVES)
    shapes = piece_shapes(shares, features, hidden)
    specs = [vmem if name in IN_VMEM else anywhere for name in BACK_INPUTS]
    specs[0] = pl.BlockSpec(memory_space=pltpu.SMEM)
    scratch = [
        lanes(2 * groups, WORK), lanes(groups, KEYS), lanes(groups, OWN), pltpu.VMEM((SHARED, features), BF16), lanes(3, 2 * groups, TALL),
        pltpu.VMEM((WORK, features), F32), pltpu.VMEM((WORK, features), BF16), pltpu.VMEM((SMALL_ROWS, features), F32),
        pltpu.VMEM((1, hidden), F32), pltpu.VMEM((ROWS - UNUSED[1], features), BF16),
        dma((moves,)), dma((moves,)), dma((moves,)), dma((moves,)), dma((24,)), dma((24,)), dma((4,)), dma((4,)), dma((6,)),
    ]
    if custom:
        scratch += [pltpu.VMEM(shape, BF16) for shape in shapes]
        scratch += [ref for name, shape in zip(FLOW_NAMES, shapes) for ref in flow_scratch(name, shape)]
    rows = jax.ShapeDtypeStruct((3, ROWS, features), BF16)
    return pl.pallas_call(
        functools.partial(backward_body, head_dim, shares, custom, features, hidden),
        in_specs=specs,
        out_specs=[anywhere] * 2 + [vmem] * len(shapes),
        out_shape=[rows, rows] + [jax.ShapeDtypeStruct(result_shape(name, shape) if custom else shape, BF16) for name, shape in zip(FLOW_NAMES, shapes)],
        scratch_shapes=scratch,
        compiler_params=pltpu.CompilerParams(collective_id=0, has_side_effects=True, vmem_limit_bytes=63 * MIB),
    )(*(inputs[name] for name in BACK_INPUTS))


def assemble_body(time_count, freq_count, *refs):
    count = len(FLOW_NAMES)
    pieces = refs[0:count]
    outs = refs[count:]
    halved, whole, up = pieces[0:TILES], pieces[TILES:2 * TILES], pieces[2 * TILES:3 * TILES]
    out, *pairs, packed = pieces[3 * TILES:]
    (qkv_out, qb, vb, out_out, ob, n1g, n1s, n2g, n2s, up_out, up_b, down_out, db, time_out, freq_out) = outs
    third = qkv_out.shape[1] // 3
    for core in range(2):
        for p, pair in enumerate(pairs):
            for part in range(3):
                first = part * third + core * (third // 2) + p * 128
                cols = slice(part * 128, (part + 1) * 128)
                if PAIR_SPLIT[p]:
                    high = pair.shape[2]
                    for half_x in range(2):
                        qkv_out[half_x * high:(half_x + 1) * high, first:first + 128] = pair[core, half_x, :, cols].astype(F32)
                else:
                    qkv_out[:, first:first + 128] = pair[core, :, cols].astype(F32)
        cols = out.shape[2]
        out_out[:, core * cols:(core + 1) * cols] = out[core].astype(F32)
    width = whole[0].shape[2]
    half = down_out.shape[1] // 2
    for j in range(TILES):
        for core in range(2):
            grad = jnp.concatenate([halved[j][core, 0], halved[j][core, 1], whole[j][core]], 0)
            down_out[j * width:(j + 1) * width, core * half:(core + 1) * half] = grad.astype(F32).T
            if UP_SPLIT[j]:
                grad = jnp.concatenate([up[j][core, 0], up[j][core, 1]], 1)
            else:
                grad = up[j][core]
            blocks = grad.shape[1] // width
            for k in range(blocks):
                first = ((core * blocks + k) * TILES + j) * width
                up_out[:, first:first + width] = grad[:, k * width:(k + 1) * width].astype(F32)
    small = jnp.concatenate([packed[0], packed[1]], 0).astype(F32)
    share = qb.shape[0]
    for row, ref in ((0, qb), (1, vb), (2, ob), (3, n1g), (4, n1s), (5, n2g), (6, n2s), (7, db)):
        ref[...] = small[row, 0:share]
    for r in range(up_b.shape[0] // share):
        up_b[r * share:(r + 1) * share] = small[8 + r, 0:share]
    time_out[...] = small[16:16 + TABLE_ROWS].T[0:share, 0:time_count]
    freq_out[...] = small[16 + FREQ_ROW:16 + FREQ_ROW + freq_count, 0:share]


def assemble(pieces, features, hidden, shares, time_count, freq_count):
    share = features // shares
    line = (share,)
    shapes = [(share, 3 * features), line, line, (share, features), line, line, line, line, line, (share, hidden), (hidden // shares,),
              (hidden // shares, features), line, (share, time_count), (freq_count, share)]
    return pl.pallas_call(
        functools.partial(assemble_body, time_count, freq_count),
        out_shape=[jax.ShapeDtypeStruct(shape, F32) for shape in shapes],
        compiler_params=params(),
    )(*pieces)


def reduce_native(pieces, time_count, freq_count):
    def total(part, axis):
        return lax.psum(lax.psum_scatter(part, "dp", scatter_dimension=axis, tiled=True), "seq").astype(F32)

    pieces = [p[0] for p in pieces]
    down = jnp.concatenate([jnp.concatenate([part for c in range(2) for part in (a[c, 0], a[c, 1], b[c])], 0)
                            for a, b in zip(pieces[0:TILES], pieces[TILES:2 * TILES])], 1)
    ups = []
    for piece, split in zip(pieces[2 * TILES:3 * TILES], UP_SPLIT):
        ups += [part for c in range(2) for part in ((piece[c, 0], piece[c, 1]) if split else (piece[c],))]
    up = jnp.concatenate(ups, 1)
    out, *pairs, packed = pieces[3 * TILES:]
    here = lax.rem(lax.axis_index("seq"), 2)
    pairs = [jnp.concatenate([p[0], p[1]], 0) if split else p for p, split in zip(pairs, PAIR_SPLIT)]
    qkv = jnp.concatenate([jnp.where(here == core, p[:, part * 128:(part + 1) * 128], BF16(0))
                           for part in range(3) for core in range(2) for p in pairs], 1)
    small = packed.reshape(SMALL_ROWS, -1)
    repeat = up.shape[1] // small.shape[1]
    up_bias = total(small[8:8 + repeat].reshape(-1), 0)
    small = total(small, 1)
    return (
        total(qkv, 0), small[0], small[1], total(jnp.concatenate([out[0], out[1]], 1), 0), small[2], small[3], small[4], small[5], small[6],
        total(up, 0), up_bias, total(down, 1).T, small[7], small[16:16 + time_count], small[16 + FREQ_ROW:16 + FREQ_ROW + freq_count],
    )


def shards(
    patches,
    cotangent,
    time_ids,
    freq_ids,
    lengths,
    qkv_weight,
    query_bias,
    value_bias,
    out_weight,
    out_bias,
    norm1_gain,
    norm1_shift,
    norm2_gain,
    norm2_shift,
    up_weight,
    up_bias,
    down_weight,
    down_bias,
    time_table,
    freq_table,
):
    features = patches.shape[2]
    head_dim = features // HEADS
    assert patches.shape[:2] == (3, ROWS) and lax.axis_size("seq") == 4
    custom = lax.axis_size("dp") == 8
    shares = 8 if custom else 1
    x, normed, own, shared_q, shared_kv, own_log, own_mixed, shared_log, shared_mixed, mixed, cot, ids, valid = forward(
        lengths, patches, cotangent, time_ids, freq_ids, time_table, freq_table, norm1_gain, norm1_shift, qkv_weight, query_bias, value_bias,
        head_dim
    )
    inputs = dict(
        lengths=lengths, valid=valid, x=x, mixed=mixed, cot=cot, out_weight=out_weight, out_bias=out_bias, gain2=norm2_gain,
        shift2=norm2_shift, up=up_weight, up_bias=up_bias, down=down_weight, down_bias=down_bias, own=own, shared_q=shared_q,
        shared_kv=shared_kv, own_mixed=own_mixed, shared_mixed=shared_mixed, own_log=own_log, shared_log=shared_log, weight=qkv_weight, normed=normed, ids=ids, gain1=norm1_gain)
    output, d_patch, *pieces = backward(inputs, head_dim, shares, custom)
    counts = time_table.shape[0], freq_table.shape[0]
    if custom:
        *rest, time_grad, freq_grad = assemble(pieces, features, up_weight.shape[1], shares, *counts)
        return (output, d_patch, *rest, time_grad.T, freq_grad)
    return (output, d_patch) + reduce_native(pieces, *counts)


def solution(mesh):
    clip_spec, row_spec, one = P("dp", "seq", None), P("dp", "seq"), P("dp")
    matrix = P("dp", None)
    return jax.shard_map(
        shards,
        mesh=mesh,
        in_specs=(clip_spec, clip_spec, row_spec, row_spec, one) + (P(),) * 15,
        out_specs=(clip_spec, clip_spec, matrix, one, one, matrix, one, one, one, one, one, matrix, one, matrix, one, P(None, "dp"), P(None, "dp")),
        check_vma=False,
    )
```
